32 devices in a mesh: head: 4 (over y, x), seq: 8 (over z, core).
Axes of the slice: x: 2, y: 2, z: 4, core: 2. Of those that a mesh axis runs over, the one named last changes fastest.
Arguments:
- tokens: bfloat16 [8, 1024, 2048], P('seq'), may hold values from -6 to 6
- cotangent: bfloat16 [8, 1024, 2048], P('seq'), may hold values from -6 to 6
- counts: int32 [8], P('seq'), may hold values from 0 to 1, as said below
- pads: int32 [8], P('seq'), may hold values from 0 to 256, as said below
- norm1_gain: bfloat16 [2048], P('seq'), may hold values from 0.5 to 1.5
- w_query: bfloat16 [2048, 2048], P('seq', 'head'), may hold values from -0.125 to 0.125
- w_key: bfloat16 [2048, 2048], P('seq', 'head'), may hold values from -0.125 to 0.125
- w_value: bfloat16 [2048, 2048], P('seq', 'head'), may hold values from -0.125 to 0.125
- w_gate_out: bfloat16 [2048, 2048], P('seq', 'head'), may hold values from -0.125 to 0.125
- w_forget: bfloat16 [2048, 256], P('seq', 'head'), may hold values from -0.125 to 0.125
- forget_bias: bfloat16 [256], P(('head', 'seq')), may hold values from -1 to 7
- out_gain: bfloat16 [2048], P(('head', 'seq')), may hold values from 0.5 to 1.5
- w_out: bfloat16 [2048, 2048], P('head', 'seq'), may hold values from -0.25 to 0.25
- norm2_gain: bfloat16 [2048], P('seq'), may hold values from 0.5 to 1.5
- w_gate: bfloat16 [2048, 5632], P('seq', 'head'), may hold values from -0.125 to 0.125
- w_up: bfloat16 [2048, 5632], P('seq', 'head'), may hold values from -0.125 to 0.125
- w_down: bfloat16 [5632, 2048], P('head', 'seq'), may hold values from -0.15625 to 0.15625
Outputs:
- outputs: bfloat16 [8, 1024, 2048], P('seq')
- input_grad: float32 [8, 1024, 2048], P('seq')
- norm1_gain_grad: float32 [2048], P('seq')
- w_query_grad: float32 [2048, 2048], P('seq', 'head')
- w_key_grad: float32 [2048, 2048], P('seq', 'head')
- w_value_grad: float32 [2048, 2048], P('seq', 'head')
- w_gate_out_grad: float32 [2048, 2048], P('seq', 'head')
- w_forget_grad: float32 [2048, 256], P('seq', 'head')
- forget_bias_grad: float32 [256], P(('head', 'seq'))
- out_gain_grad: float32 [2048], P(('head', 'seq'))
- w_out_grad: float32 [2048, 2048], P('head', 'seq')
- norm2_gain_grad: float32 [2048], P('seq')
- w_gate_grad: float32 [2048, 5632], P('seq', 'head')
- w_up_grad: float32 [2048, 5632], P('seq', 'head')
- w_down_grad: float32 [5632, 2048], P('head', 'seq')
- rms_stats: float32 [3], replicated
The draws below stay inside these ranges and needn't reach their ends.
Inputs may be any that keep to these rules, and one draw needn't show every extreme that they name: Index i of seq holds counts[i] live sequence slots, its first ones; index 0 holds 1. `pads`: the last sequence slot has 256 padded positions.
All inputs are finite; a program needn't handle non-finite values.
Results may differ from the reference program's by a relative error of at most 0.017.
Values may be sent and summed in bfloat16 or wider, within the bound.
A program may use at most 320 MiB of HBM per device.

```python
import jax
import jax.numpy as jnp
from jax import lax

D = 2048
HEADS = 4
SLOTS = 64
FF = 5632
LEN = 1024
BLOCK = 64
SEQ_DEV = 1
SEQS = 8


def draw_counts(key, part):
    raw = jax.random.randint(key, (SEQS // SEQ_DEV,), 0, SEQ_DEV + 1, dtype=jnp.int32)
    return raw.at[0].set(SEQ_DEV)


def draw_pads(key, part):
    raw = jax.random.randint(key, (SEQS,), 0, LEN // 4 + 1, dtype=jnp.int32)
    return raw.at[SEQS - 1].set(LEN // 4)


def draw_forget_bias(key, part):
    values = jax.random.uniform(key, (HEADS * SLOTS,), jnp.float32, -1.0, 6.0)
    return values.astype(jnp.bfloat16)


def block_scale(own_key, shape, cuts, low, high):
    loudness, own = 1.0, jax.random.fold_in(own_key, 6)
    for axis_at, shards_of in cuts:
        heights = jnp.exp(jax.random.uniform(jax.random.fold_in(own, axis_at), (shards_of,), jnp.float32, low / len(cuts), high / len(cuts)))
        loudness = loudness * jnp.repeat(heights, shape[axis_at] // shards_of).reshape([-1 if axis == axis_at else 1 for axis in range(len(shape))])
    return loudness


def noise(own_key, extent, deviation, limit, cuts=(), kind=jnp.bfloat16):
    values = deviation * jax.random.normal(own_key, extent, jnp.float32)
    if cuts:
        values = values * block_scale(own_key, extent, cuts, -0.22, 0.18)
    return jnp.clip(values, -limit, limit).astype(kind)


def setup_inputs(seed: int = 0) -> dict:
    keys = jax.random.split(jax.random.key(seed), 18)
    return {
        "tokens": noise(keys[0], (SEQS, LEN, D), 1.0, 6.0, ((0, 8),)),
        "cotangent": noise(keys[1], (SEQS, LEN, D), 1.0, 6.0, ((0, 8),)),
        "counts": draw_counts(jax.random.fold_in(keys[17], 71), 0),
        "pads": draw_pads(jax.random.fold_in(keys[17], 71), 0),
        "norm1_gain": jnp.clip(1.0 + 0.1 * jax.random.normal(keys[4], (D,), jnp.float32), 0.5, 1.5).astype(jnp.bfloat16),
        "w_query": noise(keys[5], (D, D), D ** -0.5, 0.125, ((0, 8), (1, 4))),
        "w_key": noise(keys[6], (D, D), D ** -0.5, 0.125, ((0, 8), (1, 4))),
        "w_value": noise(keys[7], (D, D), D ** -0.5, 0.125, ((0, 8), (1, 4))),
        "w_gate_out": noise(keys[8], (D, D), D ** -0.5, 0.125, ((0, 8), (1, 4))),
        "w_forget": noise(keys[9], (D, HEADS * SLOTS), D ** -0.5, 0.125, ((0, 8), (1, 4))),
        "forget_bias": draw_forget_bias(jax.random.fold_in(keys[17], 71), 0),
        "out_gain": jnp.clip(1.0 + 0.1 * jax.random.normal(keys[11], (D,), jnp.float32), 0.5, 1.5).astype(jnp.bfloat16),
        "w_out": noise(keys[12], (D, D), (D // 4) ** -0.5, 0.25, ((0, 4), (1, 8))),
        "norm2_gain": jnp.clip(1.0 + 0.1 * jax.random.normal(keys[13], (D,), jnp.float32), 0.5, 1.5).astype(jnp.bfloat16),
        "w_gate": noise(keys[14], (D, FF), D ** -0.5, 0.125, ((0, 8), (1, 4))),
        "w_up": noise(keys[15], (D, FF), D ** -0.5, 0.125, ((0, 8), (1, 4))),
        "w_down": noise(keys[16], (FF, D), (FF // 4) ** -0.5, 0.15625, ((0, 4), (1, 8))),
    }


EPSILON = 1e-06
DAMPING = 8.0
FULL_PRECISION = lax.Precision.HIGHEST

@jax.custom_vjp
def low(v):
    return lax.optimization_barrier(v.astype(jnp.bfloat16)).astype(jnp.float32)

@jax.custom_vjp
def low_back(v):
    return v

def low_keep(v):
    return (low(v), None)

def low_pass(kept, grad):
    return (grad,)

def back_keep(v):
    return (v, None)

def back_low(kept, grad):
    return (low(grad),)
low.defvjp(low_keep, low_pass)
low_back.defvjp(back_keep, back_low)

def matmul(left, right):
    return jnp.dot(left, right, precision=FULL_PRECISION)

def mix_block(states, block_in):
    state_k, state_v = states
    queries, key_rows, value_rows, log_keep = block_in
    steps_n = queries.shape[0]
    scaled = queries * queries.shape[1] ** (-0.5)
    cumlog = jnp.cumsum(log_keep, axis=0)
    keep_in = -jnp.expm1(log_keep)
    lower = jnp.arange(steps_n)[:, None] >= jnp.arange(steps_n)[None, :]
    lower3 = lower[:, :, None]
    spread = cumlog[:, None, :] - cumlog[None, :, :]
    weighted = jnp.where(lower3, jnp.exp(jnp.where(lower3, spread, 0.0)), 0.0) * keep_in[None, :, :]
    fade_in = jnp.exp(cumlog)
    inner_qk = matmul(scaled, key_rows.T)
    scores = jnp.einsum('ts,tsj->tj', inner_qk, weighted, precision=FULL_PRECISION) + fade_in * matmul(scaled, state_k.T)
    slot_probs = jax.nn.softmax(scores, axis=-1)
    mixing = jnp.einsum('tj,tsj->ts', slot_probs, weighted, precision=FULL_PRECISION)
    output = matmul(mixing, value_rows) + matmul(slot_probs * fade_in, state_v)
    tail_keep = jnp.exp(cumlog[-1][None, :] - cumlog) * keep_in
    new_k = fade_in[-1][:, None] * state_k + matmul(tail_keep.T, key_rows)
    new_v = fade_in[-1][:, None] * state_v + matmul(tail_keep.T, value_rows)
    return ((new_k, new_v), output)

def skipped(states, block_in):
    return (states, jnp.zeros((block_in[2].shape[0], block_in[2].shape[1]), jnp.float32))

def mixer(queries, key_rows, value_rows, log_keep, live_blocks, skip_dead):
    total_rows, head_width = queries.shape
    slot_count = log_keep.shape[1]
    num_blocks = total_rows // BLOCK
    inputs = (queries.reshape(num_blocks, BLOCK, head_width), key_rows.reshape(num_blocks, BLOCK, head_width), value_rows.reshape(num_blocks, BLOCK, head_width), log_keep.reshape(num_blocks, BLOCK, slot_count), live_blocks)

    def step(states, packed):
        block_in = (packed[0], packed[1], packed[2], packed[3])
        if skip_dead:
            return lax.cond(packed[4], mix_block, skipped, states, block_in)
        return mix_block(states, block_in)
    start = (jnp.zeros((slot_count, head_width), jnp.float32), jnp.zeros((slot_count, head_width), jnp.float32))
    _, outs = lax.scan(jax.checkpoint(step), start, inputs)
    return outs.reshape(total_rows, head_width)

def layer(seq_rows, live_rows, weights):
    norm1_gain, w_query, w_key, w_value, w_gate_out, w_forget, forget_bias, out_gain, w_out, norm2_gain, w_gate, w_up, w_down = weights
    normed1 = low(seq_rows * lax.rsqrt(lax.optimization_barrier(jnp.mean(seq_rows * seq_rows, axis=-1, keepdims=True)) + EPSILON) * norm1_gain)
    queries = low(low_back(matmul(normed1, w_query)))
    key_rows = low(low_back(matmul(normed1, w_key)))
    value_rows = low(low_back(matmul(normed1, w_value)))
    gate_pre = low_back(matmul(normed1, w_gate_out))
    forget_pre = low_back(matmul(normed1, w_forget) + forget_bias)
    log_keep = jax.nn.log_sigmoid(forget_pre) / DAMPING
    head_width = queries.shape[1] // HEADS
    slot_count = log_keep.shape[1] // HEADS
    live_blocks = jnp.ones((seq_rows.shape[0] // BLOCK,), dtype=bool)
    pieces = []
    for head_idx in range(HEADS):
        columns = slice(head_idx * head_width, (head_idx + 1) * head_width)
        slot_cols = slice(head_idx * slot_count, (head_idx + 1) * slot_count)
        mixed = mixer(queries[:, columns], key_rows[:, columns], value_rows[:, columns], log_keep[:, slot_cols], live_blocks, False)
        unit_mixed = mixed * lax.rsqrt(lax.optimization_barrier(jnp.mean(mixed * mixed, axis=-1, keepdims=True)) + EPSILON)
        pieces.append(unit_mixed * out_gain[columns] * jax.nn.silu(gate_pre[:, columns]))
    gated = low(jnp.concatenate(pieces, axis=1))
    attended = low_back(matmul(gated, w_out))
    residual = seq_rows + attended
    normed2 = low(residual * lax.rsqrt(lax.optimization_barrier(jnp.mean(residual * residual, axis=-1, keepdims=True)) + EPSILON) * norm2_gain)
    hidden = low(jax.nn.silu(low_back(matmul(normed2, w_gate))) * low_back(matmul(normed2, w_up)))
    ffn_out = low_back(matmul(hidden, w_down))
    return (live_rows[:, None] * (residual + ffn_out), attended, ffn_out)

def reference(tokens, cotangent, counts, pads, norm1_gain, w_query, w_key, w_value, w_gate_out, w_forget, forget_bias, out_gain, w_out, norm2_gain, w_gate, w_up, w_down):
    seq_ids = jnp.arange(SEQS)
    owner = seq_ids // SEQ_DEV
    place = seq_ids % SEQ_DEV
    live_len = jnp.where(place < counts[owner], LEN - pads, 0)
    live_rows = (jnp.arange(LEN)[None, :] < live_len[:, None]).astype(jnp.float32)
    weights = tuple((weight.astype(jnp.float32) for weight in (norm1_gain, w_query, w_key, w_value, w_gate_out, w_forget, forget_bias, out_gain, w_out, norm2_gain, w_gate, w_up, w_down)))

    def forward(tokens_f, *weights_f):

        def one_seq(weights_c, packed):
            rows_in, live_in = packed
            out_rows, attended, ffn_out = layer(rows_in, live_in, weights_c)
            mask = live_in[:, None]
            sums = jnp.stack([jnp.sum(mask * rows_in * rows_in), jnp.sum(mask * attended * attended), jnp.sum(mask * ffn_out * ffn_out)])
            return (weights_c, (out_rows, sums))
        _, (outs, sums) = lax.scan(jax.checkpoint(one_seq), tuple(weights_f), (tokens_f, live_rows))
        return (outs, lax.optimization_barrier(jnp.sum(sums, axis=0)))
    outs, pullback, sums = jax.vjp(forward, tokens.astype(jnp.float32), *weights, has_aux=True)
    grads = pullback(cotangent.astype(jnp.float32))
    total = jnp.sum(live_rows)
    rms_stats = jnp.sqrt(sums / (total * D))
    return (outs.astype(jnp.bfloat16), grads[0], grads[1], grads[2], grads[3], grads[4], grads[5], grads[6], grads[7], grads[8], grads[9], grads[10], grads[11], grads[12], grads[13], rms_stats)
```

```python
import functools

import jax
import jax.numpy as jnp
import numpy as np
from jax import lax
from jax.experimental import pallas as pl
from jax.experimental.pallas import tpu as pltpu
from jax.sharding import PartitionSpec as P

EPSILON = 1e-06
DAMPING = 8.0
TILE = 128
BLOCKS = 4
HALVES = (64, 32, 16, 8, 4, 2, 1)
NT = (((1,), (1,)), ((), ()))
NN = (((1,), (0,)), ((), ()))
TN = (((0,), (0,)), ((), ()))


def rel_tile(rows, i, h):
    per = rows // BLOCKS // TILE
    return (i // per ^ h[0]) * per + i % per


def mm(left, right, dims):
    return lax.dot_general(left, right, dims, preferred_element_type=jnp.float32)


def span_matrix():
    r = np.arange(TILE)[:, None]
    t = np.arange(TILE)[None, :]
    parts = []
    for h in HALVES:
        base = t // (2 * h) * (2 * h)
        upper = t % (2 * h) >= h
        parts.append(upper & (r >= base + h) & (r <= t))
        parts.append(~upper & (r > t) & (r <= base + h - 1))
    parts.append(r <= t)
    parts.append(r > t)
    return np.concatenate(parts, axis=1).astype(np.float32)


def level_of():
    s = lax.broadcasted_iota(jnp.int32, (TILE, TILE), 0)
    t = lax.broadcasted_iota(jnp.int32, (TILE, TILE), 1)
    return jnp.where(s < t, s ^ t, jnp.where(s == t, 0, -1))


def level_masks():
    x = level_of()
    masks = [(x >= h) & (x < 2 * h) for h in HALVES]
    masks.append(x == 0)
    return masks


def decays(log_keep, keep_in, spans):
    slots = log_keep.shape[0]
    high = log_keep.astype(jnp.bfloat16)
    rest = log_keep - high.astype(jnp.float32)
    mid = rest.astype(jnp.bfloat16)
    both = mm(jnp.concatenate([high, mid], axis=0), spans, NN)
    grown = jnp.exp(both[:slots] + both[slots:])
    n = len(HALVES)
    ones = jnp.ones_like(keep_in)
    e_parts = [grown[:, (2 * i) * TILE : (2 * i + 1) * TILE] for i in range(n)] + [ones]
    f_bare = [grown[:, (2 * i + 1) * TILE : (2 * i + 2) * TILE] for i in range(n)] + [ones]
    e_all = grown[:, 2 * n * TILE : (2 * n + 1) * TILE]
    f_all = grown[:, (2 * n + 1) * TILE : (2 * n + 2) * TILE]
    total = e_all[:, TILE - 1 : TILE]
    return e_parts, f_bare, e_all, f_all, total


def norm_gate(mixed, gain, gate_pre):
    scale = lax.rsqrt(jnp.mean(mixed * mixed, axis=-1, keepdims=True) + EPSILON)
    unit = mixed * scale
    return scale, unit


def fwd_kernel(h_ref, q_ref, k_ref, v_ref, g_ref, lk_ref, w_ref, gain_ref, spans_ref,
               gated_ref, mixed_ref, probs_ref, kst_ref, vst_ref, kacc, vacc):
    @pl.when(pl.program_id(0) == 0)
    def _():
        kacc[...] = jnp.zeros_like(kacc)
        vacc[...] = jnp.zeros_like(vacc)
    width = q_ref.shape[1]
    root = width ** -0.5
    q, k, v = q_ref[...], k_ref[...], v_ref[...]
    keep_in = w_ref[...]
    e_parts, f_bare, e_all, f_all, total = decays(lk_ref[...], keep_in, spans_ref[...])
    masks = level_masks()
    kst, vst = kacc[...], vacc[...]
    kst_b, vst_b = kst.astype(jnp.bfloat16), vst.astype(jnp.bfloat16)
    kst_ref[0] = kst_b
    vst_ref[0] = vst_b
    inner = mm(k, q, NT) * root
    inner_b = inner.astype(jnp.bfloat16)
    zero_b = jnp.zeros_like(inner_b)
    f_parts = [(bare * keep_in).astype(jnp.bfloat16) for bare in f_bare]
    scores = e_all * (mm(kst_b, q, NT) * root)
    for mask, grow, fade in zip(masks, e_parts, f_parts):
        scores += grow * mm(fade, jnp.where(mask, inner_b, zero_b), NN)
    top = jnp.max(scores, axis=0, keepdims=True)
    raised = jnp.exp(scores - top)
    probs = raised / jnp.sum(raised, axis=0, keepdims=True)
    probs_ref[...] = probs
    mixing = jnp.zeros((TILE, TILE), jnp.float32)
    for mask, grow, fade in zip(masks, e_parts, f_parts):
        mixing = jnp.where(mask, mm(fade, (probs * grow).astype(jnp.bfloat16), TN), mixing)
    mixed = mm(mixing.astype(jnp.bfloat16), v, TN) + mm((probs * e_all).astype(jnp.bfloat16), vst_b, TN)
    tail = (f_all * keep_in).astype(jnp.bfloat16)
    kacc[...] = total * kst + mm(tail, k, NN)
    vacc[...] = total * vst + mm(tail, v, NN)
    mixed_ref[...] = mixed
    scale = lax.rsqrt(jnp.mean(mixed * mixed, axis=-1, keepdims=True) + EPSILON)
    gate = g_ref[...].astype(jnp.float32)
    swish = gate * jax.nn.sigmoid(gate)
    gated_ref[...] = (mixed * scale * gain_ref[...] * swish).astype(jnp.bfloat16)


def rec_fwd(head, qkvg, log_keep_t, keep_in_t, gain):
    rows, wide = qkvg.shape
    width = wide // 4
    slots = log_keep_t.shape[0]
    tiles = rows // TILE
    spans = jnp.asarray(span_matrix(), jnp.bfloat16)
    place = functools.partial(rel_tile, rows)
    col = lambda j: pl.BlockSpec((TILE, width), lambda i, h: (place(i, h), j))
    lane = pl.BlockSpec((slots, TILE), lambda i, h: (0, place(i, h)))
    state = pl.BlockSpec((1, slots, width), lambda i, h: (i, 0, 0))
    return pl.pallas_call(
        fwd_kernel,
        grid_spec=pltpu.PrefetchScalarGridSpec(
            num_scalar_prefetch=1,
            grid=(tiles,),
            in_specs=[col(0), col(1), col(2), col(3), lane, lane,
                      pl.BlockSpec((1, width), lambda i, h: (0, 0)),
                      pl.BlockSpec(spans.shape, lambda i, h: (0, 0))],
            out_specs=[col(0), col(0), lane, state, state],
            scratch_shapes=[pltpu.VMEM((slots, width), jnp.float32)] * 2,
        ),
        out_shape=[
            jax.ShapeDtypeStruct((rows, width), jnp.bfloat16),
            jax.ShapeDtypeStruct((rows, width), jnp.float32),
            jax.ShapeDtypeStruct((slots, rows), jnp.float32),
            jax.ShapeDtypeStruct((tiles, slots, width), jnp.bfloat16),
            jax.ShapeDtypeStruct((tiles, slots, width), jnp.bfloat16),
        ],
        compiler_params=pltpu.CompilerParams(dimension_semantics=("arbitrary",), vmem_limit_bytes=32 << 20),
        cost_estimate=pl.CostEstimate(flops=5 * 10**9, bytes_accessed=10 << 20, transcendentals=0),
        name="slot_fwd",
    )(head, qkvg, qkvg, qkvg, qkvg, log_keep_t, keep_in_t, gain, spans)


def bwd_kernel(h_ref, q_ref, k_ref, v_ref, g_ref, lk_ref, w_ref, fpre_ref, gain_ref, spans_ref,
               mixed_ref, probs_ref, kst_ref, vst_ref, dg_ref,
               dproj_ref, dgain_ref, dbias_ref, dk_acc, dv_acc, cross):
    step = pl.program_id(0)
    width = q_ref.shape[1]
    slots = lk_ref.shape[0]

    @pl.when(step == 0)
    def _():
        dk_acc[...] = jnp.zeros_like(dk_acc)
        dv_acc[...] = jnp.zeros_like(dv_acc)
        cross[...] = jnp.zeros_like(cross)
        dgain_ref[...] = jnp.zeros_like(dgain_ref)
        dbias_ref[...] = jnp.zeros_like(dbias_ref)
    root = width ** -0.5
    q, k, v = q_ref[...], k_ref[...], v_ref[...]
    mixed = mixed_ref[...]
    gate = g_ref[...].astype(jnp.float32)
    gain = gain_ref[...]
    d_gated = dg_ref[...].astype(jnp.float32)
    scale = lax.rsqrt(jnp.mean(mixed * mixed, axis=-1, keepdims=True) + EPSILON)
    unit = mixed * scale
    sigma = jax.nn.sigmoid(gate)
    swish = gate * sigma
    slope = sigma * (1.0 + gate * (1.0 - sigma))
    dproj_ref[:, 3 * width : 4 * width] = (d_gated * unit * gain * slope).astype(jnp.bfloat16)
    d_normed = d_gated * swish
    dgain_ref[...] += jnp.sum(d_normed * unit, axis=0, keepdims=True)
    c = d_normed * gain
    d_mixed = scale * (c - unit * jnp.mean(c * unit, axis=-1, keepdims=True))
    d_out = d_mixed.astype(jnp.bfloat16)

    log_keep, keep_in = lk_ref[...], w_ref[...]
    e_parts, f_bare, e_all, f_all, total = decays(log_keep, keep_in, spans_ref[...])
    masks = level_masks()
    probs = probs_ref[...]
    kst, vst = kst_ref[0], vst_ref[0]
    dkst, dvst = dk_acc[...], dv_acc[...]
    dkst_b, dvst_b = dkst.astype(jnp.bfloat16), dvst.astype(jnp.bfloat16)

    inner_b = (mm(k, q, NT) * root).astype(jnp.bfloat16)
    d_mixing_b = mm(v, d_out, NT).astype(jnp.bfloat16)
    pair = jnp.concatenate([inner_b, d_mixing_b], axis=1)
    zero_b = jnp.zeros_like(pair)
    masks2 = [jnp.concatenate([mask, mask], axis=1) for mask in masks]
    pairs = [jnp.where(mask, pair, zero_b) for mask in masks2]
    f_parts = [(bare * keep_in).astype(jnp.bfloat16) for bare in f_bare]
    both = [mm(fade, two, NN) for fade, two in zip(f_parts, pairs)]
    s_state = mm(kst, q, NT) * root
    p_state = mm(vst, d_out, NT)
    d_probs = e_all * p_state
    for grow, two in zip(e_parts, both):
        d_probs += grow * two[:, TILE:]
    d_scores = probs * (d_probs - jnp.sum(probs * d_probs, axis=0, keepdims=True))

    xy_all = jnp.concatenate([d_scores * e_all, probs * e_all], axis=1).astype(jnp.bfloat16)
    xy_parts = [jnp.concatenate([d_scores * grow, probs * grow], axis=1).astype(jnp.bfloat16) for grow in e_parts]
    x0 = xy_all[:, :TILE]
    y0 = xy_all[:, TILE:]
    change = x0.astype(jnp.float32) * s_state + y0.astype(jnp.float32) * p_state
    into = jnp.zeros((slots, TILE), jnp.float32)
    d_both = jnp.zeros((TILE, 2 * TILE), jnp.float32)
    for i, (grow, bare, fade, two, xy, part, mask) in enumerate(
        zip(e_parts, f_bare, f_parts, both, xy_parts, pairs, masks2)
    ):
        z = mm(xy, part, NT)
        into += bare * z
        if i < len(HALVES):
            mass = xy.astype(jnp.float32) * two
            change += mass[:, :TILE] + mass[:, TILE:] - fade.astype(jnp.float32) * z
        d_both = jnp.where(mask, mm(fade, xy, TN), d_both)
    d_both_b = d_both.astype(jnp.bfloat16)
    d_inner, mixing = d_both_b[:, :TILE], d_both_b[:, TILE:]
    tail = (f_all * keep_in).astype(jnp.bfloat16)
    z_state = mm(dkst_b, k, NT) + mm(dvst_b, v, NT)
    into += f_all * z_state
    change -= tail.astype(jnp.float32) * z_state

    dproj_ref[:, :width] = (root * (mm(d_inner, k, TN) + mm(x0, kst, TN))).astype(jnp.bfloat16)
    dproj_ref[:, width : 2 * width] = (root * mm(d_inner, q, NN) + mm(tail, dkst_b, TN)).astype(jnp.bfloat16)
    dproj_ref[:, 2 * width : 3 * width] = (mm(mixing, d_out, NN) + mm(tail, dvst_b, TN)).astype(jnp.bfloat16)

    later = (lax.broadcasted_iota(jnp.int32, (TILE, TILE), 0) >= lax.broadcasted_iota(jnp.int32, (TILE, TILE), 1)).astype(jnp.bfloat16)
    high = change.astype(jnp.bfloat16)
    rest = change - high.astype(jnp.float32)
    mid = rest.astype(jnp.bfloat16)
    low = (rest - mid.astype(jnp.float32)).astype(jnp.bfloat16)
    sums = mm(jnp.concatenate([high, mid, low], axis=0), later, NN)
    d_log_keep = sums[:slots] + sums[slots : 2 * slots] + sums[2 * slots :] + cross[...] - jnp.exp(log_keep) * into
    d_forget = (d_log_keep * jax.nn.sigmoid(-fpre_ref[...]) / DAMPING).astype(jnp.bfloat16)
    dbias_ref[...] += jnp.sum(d_forget.astype(jnp.float32), axis=1, keepdims=True)
    turned = jnp.transpose(d_forget.astype(jnp.float32))
    dproj_ref[:, 4 * width :] = jnp.concatenate([turned, jnp.zeros_like(turned)], axis=1).astype(jnp.bfloat16)

    dkst_new = total * dkst + root * mm(x0, q, NN)
    dvst_new = total * dvst + mm(y0, d_out, NN)
    dk_acc[...] = dkst_new
    dv_acc[...] = dvst_new
    cross[...] = jnp.sum(kst.astype(jnp.float32) * dkst_new + vst.astype(jnp.float32) * dvst_new, axis=1, keepdims=True)


def rec_bwd(head, qkvg, log_keep_t, keep_in_t, forget_pre_t, gain, mixed, probs, kst, vst, d_gated):
    rows, wide = qkvg.shape
    width = wide // 4
    slots = log_keep_t.shape[0]
    tiles = rows // TILE
    last = tiles - 1
    spans = jnp.asarray(span_matrix(), jnp.bfloat16)
    place = lambda i, h: rel_tile(rows, last - i, h)
    col = lambda j: pl.BlockSpec((TILE, width), lambda i, h: (place(i, h), j))
    lane = pl.BlockSpec((slots, TILE), lambda i, h: (0, place(i, h)))
    state = pl.BlockSpec((1, slots, width), lambda i, h: (last - i, 0, 0))
    wide_out = 4 * width + 2 * slots
    return pl.pallas_call(
        bwd_kernel,
        grid_spec=pltpu.PrefetchScalarGridSpec(
            num_scalar_prefetch=1,
            grid=(tiles,),
            in_specs=[col(0), col(1), col(2), col(3), lane, lane, lane,
                      pl.BlockSpec((1, width), lambda i, h: (0, 0)),
                      pl.BlockSpec(spans.shape, lambda i, h: (0, 0)),
                      col(0), lane, state, state, col(0)],
            out_specs=[pl.BlockSpec((TILE, wide_out), lambda i, h: (place(i, h), 0)),
                       pl.BlockSpec((1, width), lambda i, h: (0, 0)),
                       pl.BlockSpec((slots, 1), lambda i, h: (0, 0))],
            scratch_shapes=[pltpu.VMEM((slots, width), jnp.float32)] * 2 + [pltpu.VMEM((slots, 1), jnp.float32)],
        ),
        out_shape=[
            jax.ShapeDtypeStruct((rows, wide_out), jnp.bfloat16),
            jax.ShapeDtypeStruct((1, width), jnp.float32),
            jax.ShapeDtypeStruct((slots, 1), jnp.float32),
        ],
        compiler_params=pltpu.CompilerParams(dimension_semantics=("arbitrary",), vmem_limit_bytes=40 << 20),
        cost_estimate=pl.CostEstimate(flops=8 * 10**9, bytes_accessed=16 << 20, transcendentals=0),
        name="slot_bwd",
    )(head, qkvg, qkvg, qkvg, qkvg, log_keep_t, keep_in_t, forget_pre_t, gain, spans, mixed, probs, kst, vst, d_gated)


def swap(value, bit):
    return lax.ppermute(value, "head", [(i, i ^ bit) for i in range(BLOCKS)])


def rows_of(array, blocks):
    size = array.shape[0] // BLOCKS
    return jnp.concatenate([array[k * size : (k + 1) * size] for k in blocks], axis=0)


def head_scatter(left, right):
    size = left.shape[0] // BLOCKS
    half = right.shape[0] // 2
    first, second = right[:half], right[half:]
    send_a = mm(rows_of(left, (1, 3)), first, NT).astype(jnp.bfloat16)
    send_b = mm(rows_of(left, (2, 3)), second, NT).astype(jnp.bfloat16)
    got_a, got_b = swap(send_a, 1), swap(send_b, 2)
    sum_a = mm(rows_of(left, (0, 2)), first, NT) + got_a.astype(jnp.float32)
    sum_b = mm(rows_of(left, (0, 1)), second, NT) + got_b.astype(jnp.float32)
    more_a = swap(sum_a[size:].astype(jnp.bfloat16), 2)
    more_b = swap(sum_b[size:].astype(jnp.bfloat16), 1)
    return jnp.concatenate(
        [sum_a[:size] + more_a.astype(jnp.float32), sum_b[:size] + more_b.astype(jnp.float32)], axis=1
    )


def head_gather(own):
    size, width = own.shape
    half = width // 2
    a, b = own[:, :half], own[:, half:]
    a_one, b_two = swap(a, 1), swap(b, 2)
    a_rest = swap(jnp.concatenate([a, a_one], axis=0), 2)
    b_rest = swap(jnp.concatenate([b, b_two], axis=0), 1)
    side_a = jnp.concatenate([a, a_one, a_rest], axis=0)
    side_b = jnp.concatenate([b, b_rest[:size], b_two, b_rest[size:]], axis=0)
    return jnp.concatenate([side_a, side_b], axis=1)


def turn(array, head_pos):
    blocks = array.reshape((BLOCKS, array.shape[0] // BLOCKS) + array.shape[1:])
    picked = [lax.dynamic_index_in_dim(blocks, head_pos ^ k, 0, keepdims=False) for k in range(BLOCKS)]
    return jnp.concatenate(picked, axis=0)


def rms_scale(values):
    return lax.rsqrt(jnp.mean(values * values, axis=-1, keepdims=True) + EPSILON)


def norm_back(scaled_grad, unit_rows, scale_rows):
    return scale_rows * (
        scaled_grad - unit_rows * jnp.mean(scaled_grad * unit_rows, axis=-1, keepdims=True)
    )


def silu_slope(values):
    sigma = jax.nn.sigmoid(values)
    return sigma * (1.0 + values * (1.0 - sigma))


def on_device(seq_count, tokens, cotangent, counts, pads, norm1_gain, w_query, w_key, w_value, w_gate_out,
              w_forget, forget_bias, out_gain, w_out, norm2_gain, w_gate, w_up, w_down):
    f32, b16 = jnp.float32, jnp.bfloat16
    rows, model_width = tokens.shape[1:]
    head_pos = lax.axis_index("head")
    head_arr = head_pos.reshape(1).astype(jnp.int32)
    width, slots, hidden_width = w_query.shape[1], w_forget.shape[1], w_gate.shape[1]
    share = w_query.shape[0]
    extra = slots
    size = rows // BLOCKS

    small = jnp.concatenate([out_gain, forget_bias])
    small = jnp.pad(small, (0, share - small.shape[0]))
    columns = jnp.stack([norm1_gain, norm2_gain, small], axis=1)
    columns = jnp.pad(columns, ((0, 0), (0, extra - 3)))
    own_mix = jnp.concatenate(
        [w_query, w_key, w_value, w_gate_out, w_forget, columns, w_out.T], axis=1
    )
    mix = lax.all_gather(own_mix, "seq", axis=0, tiled=True)
    own_gu = jnp.concatenate([w_gate, w_up], axis=1)
    gu_weight = lax.all_gather(own_gu, "seq", axis=0, tiled=True)
    down_weight = lax.all_gather(w_down.T, "seq", axis=0, tiled=True)

    wide = 4 * width
    in_weight = mix[:, : wide + slots + extra]
    out_weight = mix[:, wide + slots + extra :]
    gains = mix[:, wide + slots : wide + slots + 3].astype(f32)
    gain_one, gain_two = gains[:, 0], gains[:, 1]
    small_all = gains[:, 2].reshape(seq_count, share)
    n_gain, n_bias = out_gain.shape[0], forget_bias.shape[0]
    gain_head = small_all[:, :n_gain].reshape(1, width)
    bias = small_all[:, n_gain : n_gain + n_bias].reshape(slots, 1)

    x_rel = turn(tokens[0], head_pos)
    cot_rel = turn(cotangent[0], head_pos)
    block_of = jnp.arange(BLOCKS, dtype=jnp.int32) ^ head_pos
    position = (block_of[:, None] * size + jnp.arange(size, dtype=jnp.int32)[None, :]).reshape(rows, 1)
    live_len = jnp.where(counts[0] > 0, rows - pads[0], 0)
    live = (position < live_len).astype(f32)
    live_own = live[:size]

    x_f = x_rel.astype(f32)
    normed1 = (x_f * rms_scale(x_f) * gain_one).astype(b16)
    qkvg = mm(normed1, in_weight[:, :wide], NN).astype(b16)
    forget_t = lax.dot_general(
        in_weight[:, wide : wide + slots], normed1, (((0,), (1,)), ((), ())), preferred_element_type=f32
    ) + bias
    log_keep = jax.nn.log_sigmoid(forget_t) / DAMPING
    keep_in = -jnp.expm1(log_keep)
    gated, mixed, probs, kst, vst = rec_fwd(head_arr, qkvg, log_keep, keep_in, gain_head)

    attended = head_scatter(gated, out_weight)
    x_own = x_rel[:size].astype(f32)
    residual = x_own + attended
    scale_two = rms_scale(residual)
    unit_two = residual * scale_two
    normed2 = head_gather((unit_two * gain_two).astype(b16))
    gu = mm(normed2, gu_weight, NN)
    gate_h, up_h = gu[:, :hidden_width], gu[:, hidden_width:]
    hidden = (jax.nn.silu(gate_h) * up_h).astype(b16)

    grad_rows = cot_rel.astype(f32) * live
    grad_ffn = grad_rows.astype(b16)
    grad_down = lax.psum_scatter(mm(grad_ffn, hidden, TN).astype(b16), "seq", scatter_dimension=0, tiled=True)
    grad_hidden = mm(grad_ffn, down_weight, NN)
    grad_gu = jnp.concatenate(
        [(grad_hidden * up_h * silu_slope(gate_h)).astype(b16), (grad_hidden * jax.nn.silu(gate_h)).astype(b16)],
        axis=1,
    )
    grad_normed2 = head_scatter(grad_gu, gu_weight)
    grad_gu_w = lax.psum_scatter(mm(normed2, grad_gu, TN).astype(b16), "seq", scatter_dimension=0, tiled=True)
    grad_gain_two = jnp.sum(grad_normed2 * unit_two, axis=0)
    grad_residual = grad_rows[:size] + norm_back(grad_normed2 * gain_two, unit_two, scale_two)
    grad_att = head_gather(grad_residual.astype(b16))
    grad_gated = mm(grad_att, out_weight, NN)
    grad_out = lax.psum_scatter(mm(grad_att, gated, TN).astype(b16), "seq", scatter_dimension=0, tiled=True)
    grad_in, grad_gain_head, grad_bias = rec_bwd(
        head_arr, qkvg, log_keep, keep_in, forget_t, gain_head, mixed, probs, kst, vst, grad_gated
    )

    ffn_out = head_scatter(hidden, down_weight)
    out_own = (live_own * (residual + ffn_out)).astype(b16)
    outputs = turn(head_gather(out_own), head_pos)
    stats = jnp.stack([
        jnp.sum(live_own * x_own * x_own),
        jnp.sum(live_own * attended * attended),
        jnp.sum(live_own * ffn_out * ffn_out),
        jnp.sum(live_own),
    ])

    grad_in_w = mm(normed1, grad_in, TN)
    gain_one_part = jnp.sum(grad_in_w * in_weight.astype(f32), axis=1) / gain_one
    shared = jnp.concatenate([grad_gain_two, gain_one_part, stats])
    shared = shared + swap(shared, 1)
    shared = shared + swap(shared, 2)
    stats = shared[2 * model_width :]
    stats_high = stats.astype(b16).astype(f32)
    eight = jnp.concatenate([stats_high, stats - stats_high])
    third = jnp.concatenate(
        [
            grad_gain_head.reshape(seq_count, n_gain),
            grad_bias.reshape(seq_count, n_bias),
            jnp.broadcast_to(eight, (seq_count, 8)),
            jnp.zeros((seq_count, share - n_gain - n_bias - 8), f32),
        ],
        axis=1,
    ).reshape(model_width)
    columns = jnp.stack([shared[model_width : 2 * model_width], shared[:model_width], third], axis=1)
    columns = jnp.pad(columns, ((0, 0), (wide + slots, extra - 3)))
    grad_in_w = lax.psum_scatter((grad_in_w + columns).astype(b16), "seq", scatter_dimension=0, tiled=True)

    grad_normed1 = head_scatter(grad_in, in_weight)
    scale_one = rms_scale(x_own)
    input_own = grad_residual + norm_back(grad_normed1 * gain_one, x_own * scale_one, scale_one)
    input_grad = turn(head_gather(input_own.astype(b16)), head_pos).astype(f32)

    done = grad_in_w.astype(f32)
    tail = done[:, wide + slots : wide + slots + 3]
    small = tail[:, 2]
    sums = small[n_gain + n_bias : n_gain + n_bias + 4] + small[n_gain + n_bias + 4 : n_gain + n_bias + 8]
    rms_stats = jnp.sqrt(sums[:3] / (sums[3] * model_width))
    grad_gu_w = grad_gu_w.astype(f32)
    return (
        outputs[None],
        input_grad[None],
        tail[:, 0],
        done[:, :width],
        done[:, width : 2 * width],
        done[:, 2 * width : 3 * width],
        done[:, 3 * width : wide],
        done[:, wide : wide + slots],
        small[n_gain : n_gain + n_bias],
        small[:n_gain],
        grad_out.astype(f32).T,
        tail[:, 1],
        grad_gu_w[:, :hidden_width],
        grad_gu_w[:, hidden_width:],
        grad_down.astype(f32).T,
        rms_stats,
    )


def solution(mesh):
    both = P("seq", "head")
    flat = P(("head", "seq"))
    rows = P("seq", None, None)
    return jax.shard_map(
        functools.partial(on_device, mesh.shape["seq"]),
        mesh=mesh,
        in_specs=(rows, rows, P("seq"), P("seq"), P("seq"), both, both, both, both, both, flat, flat,
                  P("head", "seq"), P("seq"), both, both, P("head", "seq")),
        out_specs=(rows, rows, P("seq"), both, both, both, both, both, flat, flat, P("head", "seq"), P("seq"),
                   both, both, P("head", "seq"), P()),
        check_vma=False,
    )
```

```python
import functools

import jax
import jax.numpy as jnp
import numpy as np
from jax import lax
from jax.experimental import pallas as pl
from jax.experimental.pallas import tpu as pltpu
from jax.sharding import PartitionSpec as P

EPSILON = 1e-06
DAMPING = 8.0
TILE = 128
BLOCKS = 4
HALVES = (64, 32, 16, 8, 4, 2, 1)
NT = (((1,), (1,)), ((), ()))
NN = (((1,), (0,)), ((), ()))
TN = (((0,), (0,)), ((), ()))


def rel_tile(rows, i, h):
    per = rows // BLOCKS // TILE
    return (i // per ^ h[0]) * per + i % per


def mm(left, right, dims):
    return lax.dot_general(left, right, dims, preferred_element_type=jnp.float32)


def span_matrix():
    r = np.arange(TILE)[:, None]
    t = np.arange(TILE)[None, :]
    parts = []
    for h in HALVES:
        base = t // (2 * h) * (2 * h)
        upper = t % (2 * h) >= h
        parts.append(upper & (r >= base + h) & (r <= t))
        parts.append(~upper & (r > t) & (r <= base + h - 1))
    parts.append(r <= t)
    parts.append(r > t)
    return np.concatenate(parts, axis=1).astype(np.float32)


def level_of():
    s = lax.broadcasted_iota(jnp.int32, (TILE, TILE), 0)
    t = lax.broadcasted_iota(jnp.int32, (TILE, TILE), 1)
    return jnp.where(s < t, s ^ t, jnp.where(s == t, 0, -1))


def level_masks():
    x = level_of()
    masks = [(x >= h) & (x < 2 * h) for h in HALVES]
    masks.append(x == 0)
    return masks


def decays(log_keep, keep_in, spans):
    slots = log_keep.shape[0]
    high = log_keep.astype(jnp.bfloat16)
    rest = log_keep - high.astype(jnp.float32)
    mid = rest.astype(jnp.bfloat16)
    both = mm(jnp.concatenate([high, mid], axis=0), spans, NN)
    grown = jnp.exp(both[:slots] + both[slots:])
    n = len(HALVES)
    ones = jnp.ones_like(keep_in)
    e_parts = [grown[:, (2 * i) * TILE : (2 * i + 1) * TILE] for i in range(n)] + [ones]
    f_bare = [grown[:, (2 * i + 1) * TILE : (2 * i + 2) * TILE] for i in range(n)] + [ones]
    e_all = grown[:, 2 * n * TILE : (2 * n + 1) * TILE]
    f_all = grown[:, (2 * n + 1) * TILE : (2 * n + 2) * TILE]
    total = e_all[:, TILE - 1 : TILE]
    return e_parts, f_bare, e_all, f_all, total


def norm_gate(mixed, gain, gate_pre):
    scale = lax.rsqrt(jnp.mean(mixed * mixed, axis=-1, keepdims=True) + EPSILON)
    unit = mixed * scale
    return scale, unit


def fwd_kernel(h_ref, q_ref, k_ref, v_ref, g_ref, lk_ref, w_ref, gain_ref, spans_ref,
               gated_ref, mixed_ref, probs_ref, kst_ref, vst_ref, kacc, vacc):
    @pl.when(pl.program_id(0) == 0)
    def _():
        kacc[...] = jnp.zeros_like(kacc)
        vacc[...] = jnp.zeros_like(vacc)
    width = q_ref.shape[1]
    root = width ** -0.5
    q, k, v = q_ref[...], k_ref[...], v_ref[...]
    keep_in = w_ref[...]
    e_parts, f_bare, e_all, f_all, total = decays(lk_ref[...], keep_in, spans_ref[...])
    masks = level_masks()
    kst, vst = kacc[...], vacc[...]
    kst_b, vst_b = kst.astype(jnp.bfloat16), vst.astype(jnp.bfloat16)
    kst_ref[0] = kst_b
    vst_ref[0] = vst_b
    inner = mm(k, q, NT) * root
    inner_b = inner.astype(jnp.bfloat16)
    zero_b = jnp.zeros_like(inner_b)
    f_parts = [(bare * keep_in).astype(jnp.bfloat16) for bare in f_bare]
    scores = e_all * (mm(kst_b, q, NT) * root)
    for mask, grow, fade in zip(masks, e_parts, f_parts):
        scores += grow * mm(fade, jnp.where(mask, inner_b, zero_b), NN)
    top = jnp.max(scores, axis=0, keepdims=True)
    raised = jnp.exp(scores - top)
    probs = raised / jnp.sum(raised, axis=0, keepdims=True)
    probs_ref[...] = probs
    mixing = jnp.zeros((TILE, TILE), jnp.float32)
    for mask, grow, fade in zip(masks, e_parts, f_parts):
        mixing = jnp.where(mask, mm(fade, (probs * grow).astype(jnp.bfloat16), TN), mixing)
    mixed = mm(mixing.astype(jnp.bfloat16), v, TN) + mm((probs * e_all).astype(jnp.bfloat16), vst_b, TN)
    tail = (f_all * keep_in).astype(jnp.bfloat16)
    kacc[...] = total * kst + mm(tail, k, NN)
    vacc[...] = total * vst + mm(tail, v, NN)
    mixed_ref[...] = mixed
    scale = lax.rsqrt(jnp.mean(mixed * mixed, axis=-1, keepdims=True) + EPSILON)
    gate = g_ref[...].astype(jnp.float32)
    swish = gate * jax.nn.sigmoid(gate)
    gated_ref[...] = (mixed * scale * gain_ref[...] * swish).astype(jnp.bfloat16)


def rec_fwd(head, qkvg, log_keep_t, keep_in_t, gain):
    rows, wide = qkvg.shape
    width = wide // 4
    slots = log_keep_t.shape[0]
    tiles = rows // TILE
    spans = jnp.asarray(span_matrix(), jnp.bfloat16)
    place = functools.partial(rel_tile, rows)
    col = lambda j: pl.BlockSpec((TILE, width), lambda i, h: (place(i, h), j))
    lane = pl.BlockSpec((slots, TILE), lambda i, h: (0, place(i, h)))
    state = pl.BlockSpec((1, slots, width), lambda i, h: (i, 0, 0))
    return pl.pallas_call(
        fwd_kernel,
        grid_spec=pltpu.PrefetchScalarGridSpec(
            num_scalar_prefetch=1,
            grid=(tiles,),
            in_specs=[col(0), col(1), col(2), col(3), lane, lane,
                      pl.BlockSpec((1, width), lambda i, h: (0, 0)),
                      pl.BlockSpec(spans.shape, lambda i, h: (0, 0))],
            out_specs=[col(0), col(0), lane, state, state],
            scratch_shapes=[pltpu.VMEM((slots, width), jnp.float32)] * 2,
        ),
        out_shape=[
            jax.ShapeDtypeStruct((rows, width), jnp.bfloat16),
            jax.ShapeDtypeStruct((rows, width), jnp.float32),
            jax.ShapeDtypeStruct((slots, rows), jnp.float32),
            jax.ShapeDtypeStruct((tiles, slots, width), jnp.bfloat16),
            jax.ShapeDtypeStruct((tiles, slots, width), jnp.bfloat16),
        ],
        compiler_params=pltpu.CompilerParams(dimension_semantics=("arbitrary",), vmem_limit_bytes=32 << 20),
        cost_estimate=pl.CostEstimate(flops=5 * 10**9, bytes_accessed=10 << 20, transcendentals=0),
        name="slot_fwd",
    )(head, qkvg, qkvg, qkvg, qkvg, log_keep_t, keep_in_t, gain, spans)


def bwd_kernel(h_ref, q_ref, k_ref, v_ref, g_ref, lk_ref, w_ref, fpre_ref, gain_ref, spans_ref,
               mixed_ref, probs_ref, kst_ref, vst_ref, dg_ref,
               dproj_ref, dgain_ref, dbias_ref, dk_acc, dv_acc, cross):
    step = pl.program_id(0)
    width = q_ref.shape[1]
    slots = lk_ref.shape[0]

    @pl.when(step == 0)
    def _():
        dk_acc[...] = jnp.zeros_like(dk_acc)
        dv_acc[...] = jnp.zeros_like(dv_acc)
        cross[...] = jnp.zeros_like(cross)
        dgain_ref[...] = jnp.zeros_like(dgain_ref)
        dbias_ref[...] = jnp.zeros_like(dbias_ref)
    root = width ** -0.5
    q, k, v = q_ref[...], k_ref[...], v_ref[...]
    mixed = mixed_ref[...]
    gate = g_ref[...].astype(jnp.float32)
    gain = gain_ref[...]
    d_gated = dg_ref[...].astype(jnp.float32)
    scale = lax.rsqrt(jnp.mean(mixed * mixed, axis=-1, keepdims=True) + EPSILON)
    unit = mixed * scale
    sigma = jax.nn.sigmoid(gate)
    swish = gate * sigma
    slope = sigma * (1.0 + gate * (1.0 - sigma))
    dproj_ref[:, 3 * width : 4 * width] = (d_gated * unit * gain * slope).astype(jnp.bfloat16)
    d_normed = d_gated * swish
    dgain_ref[...] += jnp.sum(d_normed * unit, axis=0, keepdims=True)
    c = d_normed * gain
    d_mixed = scale * (c - unit * jnp.mean(c * unit, axis=-1, keepdims=True))
    d_out = d_mixed.astype(jnp.bfloat16)

    log_keep, keep_in = lk_ref[...], w_ref[...]
    e_parts, f_bare, e_all, f_all, total = decays(log_keep, keep_in, spans_ref[...])
    masks = level_masks()
    probs = probs_ref[...]
    kst, vst = kst_ref[0], vst_ref[0]
    dkst, dvst = dk_acc[...], dv_acc[...]
    dkst_b, dvst_b = dkst.astype(jnp.bfloat16), dvst.astype(jnp.bfloat16)

    inner_b = (mm(k, q, NT) * root).astype(jnp.bfloat16)
    d_mixing_b = mm(v, d_out, NT).astype(jnp.bfloat16)
    pair = jnp.concatenate([inner_b, d_mixing_b], axis=1)
    zero_b = jnp.zeros_like(pair)
    masks2 = [jnp.concatenate([mask, mask], axis=1) for mask in masks]
    pairs = [jnp.where(mask, pair, zero_b) for mask in masks2]
    f_parts = [(bare * keep_in).astype(jnp.bfloat16) for bare in f_bare]
    both = [mm(fade, two, NN) for fade, two in zip(f_parts, pairs)]
    s_state = mm(kst, q, NT) * root
    p_state = mm(vst, d_out, NT)
    d_probs = e_all * p_state
    for grow, two in zip(e_parts, both):
        d_probs += grow * two[:, TILE:]
    d_scores = probs * (d_probs - jnp.sum(probs * d_probs, axis=0, keepdims=True))

    xy_all = jnp.concatenate([d_scores * e_all, probs * e_all], axis=1).astype(jnp.bfloat16)
    xy_parts = [jnp.concatenate([d_scores * grow, probs * grow], axis=1).astype(jnp.bfloat16) for grow in e_parts]
    x0 = xy_all[:, :TILE]
    y0 = xy_all[:, TILE:]
    change = x0.astype(jnp.float32) * s_state + y0.astype(jnp.float32) * p_state
    into = jnp.zeros((slots, TILE), jnp.float32)
    d_both = jnp.zeros((TILE, 2 * TILE), jnp.float32)
    for i, (grow, bare, fade, two, xy, part, mask) in enumerate(
        zip(e_parts, f_bare, f_parts, both, xy_parts, pairs, masks2)
    ):
        z = mm(xy, part, NT)
        into += bare * z
        if i < len(HALVES):
            mass = xy.astype(jnp.float32) * two
            change += mass[:, :TILE] + mass[:, TILE:] - fade.astype(jnp.float32) * z
        d_both = jnp.where(mask, mm(fade, xy, TN), d_both)
    d_both_b = d_both.astype(jnp.bfloat16)
    d_inner, mixing = d_both_b[:, :TILE], d_both_b[:, TILE:]
    tail = (f_all * keep_in).astype(jnp.bfloat16)
    z_state = mm(dkst_b, k, NT) + mm(dvst_b, v, NT)
    into += f_all * z_state
    change -= tail.astype(jnp.float32) * z_state

    dproj_ref[:, :width] = (root * (mm(d_inner, k, TN) + mm(x0, kst, TN))).astype(jnp.bfloat16)
    dproj_ref[:, width : 2 * width] = (root * mm(d_inner, q, NN) + mm(tail, dkst_b, TN)).astype(jnp.bfloat16)
    dproj_ref[:, 2 * width : 3 * width] = (mm(mixing, d_out, NN) + mm(tail, dvst_b, TN)).astype(jnp.bfloat16)

    later = (lax.broadcasted_iota(jnp.int32, (TILE, TILE), 0) >= lax.broadcasted_iota(jnp.int32, (TILE, TILE), 1)).astype(jnp.bfloat16)
    high = change.astype(jnp.bfloat16)
    rest = change - high.astype(jnp.float32)
    mid = rest.astype(jnp.bfloat16)
    low = (rest - mid.astype(jnp.float32)).astype(jnp.bfloat16)
    sums = mm(jnp.concatenate([high, mid, low], axis=0), later, NN)
    d_log_keep = sums[:slots] + sums[slots : 2 * slots] + sums[2 * slots :] + cross[...] - jnp.exp(log_keep) * into
    d_forget = (d_log_keep * jax.nn.sigmoid(-fpre_ref[...]) / DAMPING).astype(jnp.bfloat16)
    dbias_ref[...] += jnp.sum(d_forget.astype(jnp.float32), axis=1, keepdims=True)
    turned = jnp.transpose(d_forget.astype(jnp.float32))
    dproj_ref[:, 4 * width :] = jnp.concatenate([turned, jnp.zeros_like(turned)], axis=1).astype(jnp.bfloat16)

    dkst_new = total * dkst + root * mm(x0, q, NN)
    dvst_new = total * dvst + mm(y0, d_out, NN)
    dk_acc[...] = dkst_new
    dv_acc[...] = dvst_new
    cross[...] = jnp.sum(kst.astype(jnp.float32) * dkst_new + vst.astype(jnp.float32) * dvst_new, axis=1, keepdims=True)


def rec_bwd(head, qkvg, log_keep_t, keep_in_t, forget_pre_t, gain, mixed, probs, kst, vst, d_gated):
    rows, wide = qkvg.shape
    width = wide // 4
    slots = log_keep_t.shape[0]
    tiles = rows // TILE
    last = tiles - 1
    spans = jnp.asarray(span_matrix(), jnp.bfloat16)
    place = lambda i, h: rel_tile(rows, last - i, h)
    col = lambda j: pl.BlockSpec((TILE, width), lambda i, h: (place(i, h), j))
    lane = pl.BlockSpec((slots, TILE), lambda i, h: (0, place(i, h)))
    state = pl.BlockSpec((1, slots, width), lambda i, h: (last - i, 0, 0))
    wide_out = 4 * width + 2 * slots
    return pl.pallas_call(
        bwd_kernel,
        grid_spec=pltpu.PrefetchScalarGridSpec(
            num_scalar_prefetch=1,
            grid=(tiles,),
            in_specs=[col(0), col(1), col(2), col(3), lane, lane, lane,
                      pl.BlockSpec((1, width), lambda i, h: (0, 0)),
                      pl.BlockSpec(spans.shape, lambda i, h: (0, 0)),
                      col(0), lane, state, state, col(0)],
            out_specs=[pl.BlockSpec((TILE, wide_out), lambda i, h: (place(i, h), 0)),
                       pl.BlockSpec((1, width), lambda i, h: (0, 0)),
                       pl.BlockSpec((slots, 1), lambda i, h: (0, 0))],
            scratch_shapes=[pltpu.VMEM((slots, width), jnp.float32)] * 2 + [pltpu.VMEM((slots, 1), jnp.float32)],
        ),
        out_shape=[
            jax.ShapeDtypeStruct((rows, wide_out), jnp.bfloat16),
            jax.ShapeDtypeStruct((1, width), jnp.float32),
            jax.ShapeDtypeStruct((slots, 1), jnp.float32),
        ],
        compiler_params=pltpu.CompilerParams(dimension_semantics=("arbitrary",), vmem_limit_bytes=40 << 20),
        cost_estimate=pl.CostEstimate(flops=8 * 10**9, bytes_accessed=16 << 20, transcendentals=0),
        name="slot_bwd",
    )(head, qkvg, qkvg, qkvg, qkvg, log_keep_t, keep_in_t, forget_pre_t, gain, spans, mixed, probs, kst, vst, d_gated)


MESH = pl.DeviceIdType.MESH
CHUNK = 32


def neighbours():
    head = lax.axis_index("head")
    return {"head": head + 1 - 2 * (head % 2)}, {"head": (head + 2) % BLOCKS}


def greet(targets):
    barrier = pltpu.get_barrier_semaphore()
    for target in targets:
        pl.semaphore_signal(barrier, inc=1, device_id=target, device_id_type=MESH)
    pl.semaphore_wait(barrier, len(targets))


def weight_tiles(pairs, out_ref, stage, turned, sem, watch=None):
    tile = turned.shape[0]

    def copy(i):
        return pltpu.make_async_copy(
            stage.at[i % 2], out_ref.at[pl.ds(pl.multiple_of(i * tile, tile), tile), :], sem.at[i % 2]
        )

    def body(i, carry):
        @pl.when(i >= 2)
        def _():
            copy(i - 2).wait()

        here = pl.ds(pl.multiple_of(i * tile, tile), tile)
        for left_ref, right_ref, column in pairs:
            turned[...] = jnp.transpose(left_ref[:, here])
            width = right_ref.shape[1]

            def chunk(at, cols):
                value = mm(turned[...], right_ref[:, pl.ds(at, cols)], NN)
                stage[i % 2, :, pl.ds(column + at, cols)] = value.astype(jnp.bfloat16)
                if watch is not None:
                    watch(here, column, at, cols, value)

            def step(c, carry):
                chunk(pl.multiple_of(c * 256, 256), 256)
                return carry

            lax.fori_loop(0, width // 256, step, 0)
            if width % 256:
                chunk(width // 256 * 256, width % 256)
        copy(i).start()
        return carry

    count = out_ref.shape[0] // tile
    lax.fori_loop(0, count, body, 0)
    copy(count - 2).wait()
    copy(count - 1).wait()


def scatter_kernel(finish, filler, n_side, n_out, skip, window, left_ref, right_ref, *rest):
    side, rest = rest[:n_side], rest[n_side:]
    outs, (acc, send, got, send_sem, got_sem, *spare) = rest[:n_out], rest[n_out:]
    size, half = send.shape[1:]
    depth = left_ref.shape[1]
    cols = 256
    to_x, to_y = neighbours()
    if window:
        right_buf, right_sem = spare
        fetch = pltpu.make_async_copy(right_ref.at[:, pl.ds(0, depth)], right_buf, right_sem.at[0])
        fetch.start()
        greet((to_x, to_y))
        fetch.wait()
        right_ref = right_buf
    else:
        greet((to_x, to_y))

    def part(block, side_at, store):
        def body(c, carry):
            at = pl.multiple_of(c * cols, cols)
            value = mm(
                left_ref[block * size : (block + 1) * size, :],
                right_ref[pl.ds(side_at * half + at, cols), skip : skip + depth],
                NT,
            )
            store(at, value)
            return carry

        lax.fori_loop(0, half // cols, body, 0)

    def copy(slot, target):
        return pltpu.make_async_remote_copy(
            src_ref=send.at[slot], dst_ref=got.at[slot], send_sem=send_sem.at[slot], recv_sem=got_sem.at[slot],
            device_id=target, device_id_type=MESH,
        )

    targets = (to_x, to_y, to_x, to_y, to_y, to_x)
    copies = [copy(slot, target) for slot, target in enumerate(targets)]

    def keep(slot):
        def store(at, value):
            send[slot, :, pl.ds(at, cols)] = value.astype(jnp.bfloat16)
        return store

    def keep_sum(slot, arrived):
        def store(at, value):
            send[slot, :, pl.ds(at, cols)] = (value + got[arrived, :, pl.ds(at, cols)].astype(jnp.float32)).astype(jnp.bfloat16)
        return store

    def own(side_at):
        def store(at, value):
            acc[:, pl.ds(side_at * half + at, cols)] = value
        return store

    for slot, (block, side_at) in enumerate(((3, 0), (3, 1), (1, 0), (2, 1))):
        part(block, side_at, keep(slot))
        copies[slot].start()
    part(0, 0, own(0))
    part(0, 1, own(1))
    for slot, arrived, block, side_at in ((4, 0, 2, 0), (5, 1, 1, 1)):
        copies[arrived].wait_recv()
        part(block, side_at, keep_sum(slot, arrived))
        copies[slot].start()
    if filler is not None:
        filler(left_ref, right_ref, side, outs, spare)
    for slot in (2, 3, 4, 5):
        copies[slot].wait_recv()

    def rows(i, carry):
        at = pl.multiple_of(i * CHUNK, CHUNK)
        here = pl.ds(at, CHUNK)
        sum_a = acc[here, :half] + got[2, here, :].astype(jnp.float32) + got[4, here, :].astype(jnp.float32)
        sum_b = acc[here, half:] + got[3, here, :].astype(jnp.float32) + got[5, here, :].astype(jnp.float32)
        finish(here, jnp.concatenate([sum_a, sum_b], axis=1), side, outs, i)
        return carry

    lax.fori_loop(0, size // CHUNK, rows, 0)
    for one in copies:
        one.wait_send()


WHOLE = pl.BlockSpec(memory_space=pltpu.VMEM)


def head_scatter(left, right, side, out_shapes, finish, number, skip=0, filler=None, far=None, window=False):
    size, half = left.shape[0] // BLOCKS, right.shape[0] // 2
    out_specs, scratch, right_spec = [WHOLE] * len(out_shapes), [], WHOLE
    if window:
        right_spec = pl.BlockSpec(memory_space=pl.ANY)
        scratch = [pltpu.VMEM((2 * half, left.shape[1]), jnp.bfloat16), pltpu.SemaphoreType.DMA((1,))]
    if far is not None:
        out_shapes, out_specs = [*out_shapes, far], [*out_specs, pl.BlockSpec(memory_space=pl.ANY)]
        scratch = [
            pltpu.VMEM((2, 256, far.shape[1]), jnp.bfloat16),
            pltpu.VMEM((256, left.shape[0]), jnp.bfloat16),
            pltpu.SemaphoreType.DMA((2,)),
        ]
    return pl.pallas_call(
        functools.partial(scatter_kernel, finish, filler, len(side), len(out_shapes), skip, window),
        in_specs=[WHOLE, right_spec] + [WHOLE] * len(side),
        out_specs=out_specs,
        out_shape=out_shapes,
        scratch_shapes=[
            pltpu.VMEM((size, 2 * half), jnp.float32),
            pltpu.VMEM((6, size, half), jnp.bfloat16),
            pltpu.VMEM((6, size, half), jnp.bfloat16),
            pltpu.SemaphoreType.DMA((6,)),
            pltpu.SemaphoreType.DMA((6,)),
            *scratch,
        ],
        compiler_params=pltpu.CompilerParams(collective_id=number, has_side_effects=True, vmem_limit_bytes=56 << 20),
        cost_estimate=pl.CostEstimate(flops=10**9, bytes_accessed=1 << 20, transcendentals=0),
        name="head_scatter%d" % number,
    )(left, right, *side)


def fill_gu(left_ref, right_ref, side, outs, spare):
    weight_tiles([(side[-1], left_ref, 0)], outs[-1], *spare)


def fill_mix(skip, left_ref, right_ref, side, outs, spare):
    normed_ref, att_ref, gated_ref = side[-3:]
    part_ref = outs[-2]
    part_ref[...] = jnp.zeros_like(part_ref)

    def watch(here, column, at, cols, value):
        if column:
            weight = right_ref[here, pl.ds(column + at, cols)].astype(jnp.float32)
            part_ref[here, :] += jnp.sum(value * weight, axis=1, keepdims=True)

    weight_tiles([(att_ref, gated_ref, 0), (normed_ref, left_ref, skip)], outs[-1], *spare, watch=watch)


def gather_kernel(own_ref, out_ref, send_sem, got_sem):
    half = own_ref.shape[1] // 2
    to_x, to_y = neighbours()
    greet((to_x, to_y))

    def copy(slot, src, block, side_at, target):
        here = pl.ds(side_at * half, half)
        return pltpu.make_async_remote_copy(
            src_ref=src.at[:, here], dst_ref=out_ref.at[block, :, here],
            send_sem=send_sem.at[slot], recv_sem=got_sem.at[slot], device_id=target, device_id_type=MESH,
        )

    copies = [
        copy(0, own_ref, 1, 0, to_x),
        copy(1, own_ref, 2, 1, to_y),
        copy(2, own_ref, 1, 1, to_x),
        copy(3, own_ref, 2, 0, to_y),
        copy(4, out_ref.at[1], 3, 0, to_y),
        copy(5, out_ref.at[2], 3, 1, to_x),
    ]
    for one in copies[:4]:
        one.start()
    out_ref[0] = own_ref[...]
    for first, second in ((0, 4), (1, 5)):
        copies[first].wait_recv()
        copies[second].start()
    for one in copies[2:]:
        one.wait_recv()
    for one in copies:
        one.wait_send()


def head_gather(own, number):
    size, width = own.shape
    return pl.pallas_call(
        gather_kernel,
        in_specs=[WHOLE],
        out_specs=WHOLE,
        out_shape=jax.ShapeDtypeStruct((BLOCKS, size, width), own.dtype),
        scratch_shapes=[pltpu.SemaphoreType.DMA((6,)), pltpu.SemaphoreType.DMA((6,))],
        compiler_params=pltpu.CompilerParams(collective_id=number, has_side_effects=True, vmem_limit_bytes=24 << 20),
        cost_estimate=pl.CostEstimate(flops=10**9, bytes_accessed=1 << 20, transcendentals=0),
        name="head_gather%d" % number,
    )(own)


def unit_of(values):
    scale = lax.rsqrt(jnp.mean(values * values, axis=-1, keepdims=True) + EPSILON)
    return scale, values * scale


def finish_mixer(here, total, side, outs, i):
    x_ref, gain_ref = side
    residual_ref, normed_ref = outs
    residual = x_ref[here, :].astype(jnp.float32) + total
    residual_ref[here, :] = residual
    normed_ref[here, :] = (unit_of(residual)[1] * gain_ref[...]).astype(jnp.bfloat16)


def finish_norm_two(here, total, side, outs, i):
    residual_ref, cot_ref, live_ref, gain_ref = side[:4]
    grad_ref, low_ref, gain_grad_ref = outs[:3]
    scale, unit = unit_of(residual_ref[here, :])
    gained = jnp.sum(total * unit, axis=0, keepdims=True)

    @pl.when(i == 0)
    def _():
        gain_grad_ref[...] = jnp.zeros_like(gain_grad_ref)

    gain_grad_ref[...] += gained
    c = total * gain_ref[...]
    grad = cot_ref[here, :].astype(jnp.float32) * live_ref[here, :] + scale * (
        c - unit * jnp.mean(c * unit, axis=-1, keepdims=True)
    )
    grad_ref[here, :] = grad
    low_ref[here, :] = grad.astype(jnp.bfloat16)


def finish_norm_one(here, total, side, outs, i):
    x_ref, grad_ref, gain_ref = side[:3]
    scale, unit = unit_of(x_ref[here, :].astype(jnp.float32))
    c = total * gain_ref[...]
    outs[0][here, :] = (
        grad_ref[here, :] + scale * (c - unit * jnp.mean(c * unit, axis=-1, keepdims=True))
    ).astype(jnp.bfloat16)


def finish_ffn(here, total, side, outs, i):
    residual_ref, live_ref = side
    out_ref, square_ref = outs
    live = live_ref[here, :]

    @pl.when(i == 0)
    def _():
        square_ref[...] = jnp.zeros_like(square_ref)

    square_ref[...] += jnp.sum(live * total * total, axis=0, keepdims=True)
    out_ref[here, :] = (live * (residual_ref[here, :] + total)).astype(jnp.bfloat16)


def ffn_fwd_kernel(x_ref, w_ref, gu_ref, hidden_ref):
    def body(i, carry):
        here = pl.ds(pl.multiple_of(i * 256, 256), 256)
        value = mm(x_ref[here, :], w_ref[...], NN)
        gu_ref[here, :] = value.astype(jnp.bfloat16)
        gate, up = value[:, :128], value[:, 128:]
        hidden_ref[here, :] = (gate * jax.nn.sigmoid(gate) * up).astype(jnp.bfloat16)
        return carry

    lax.fori_loop(0, x_ref.shape[0] // 256, body, 0)


def ffn_fwd(x, weight):
    rows, width = x.shape
    wide = weight.shape[1]
    return pl.pallas_call(
        ffn_fwd_kernel,
        grid=(wide // 256,),
        in_specs=[pl.BlockSpec((rows, width), lambda j: (0, 0)), pl.BlockSpec((width, 256), lambda j: (0, j))],
        out_specs=[pl.BlockSpec((rows, 256), lambda j: (0, j)), pl.BlockSpec((rows, 128), lambda j: (0, j))],
        out_shape=[
            jax.ShapeDtypeStruct((rows, wide), jnp.bfloat16),
            jax.ShapeDtypeStruct((rows, wide // 2), jnp.bfloat16),
        ],
        compiler_params=pltpu.CompilerParams(dimension_semantics=("arbitrary",), vmem_limit_bytes=32 << 20),
        cost_estimate=pl.CostEstimate(flops=10**9, bytes_accessed=1 << 20, transcendentals=0),
        name="ffn_fwd",
    )(x, weight)


def ffn_bwd_kernel(grad_ref, w_ref, gu_ref, out_ref):
    def body(i, carry):
        here = pl.ds(pl.multiple_of(i * 256, 256), 256)
        value = mm(grad_ref[here, :], w_ref[...], NN)
        for p in range(2):
            grad = value[:, p * 128 : (p + 1) * 128]
            gate = gu_ref[here, p * 256 : p * 256 + 128].astype(jnp.float32)
            up = gu_ref[here, p * 256 + 128 : (p + 1) * 256].astype(jnp.float32)
            sigma = jax.nn.sigmoid(gate)
            swish = gate * sigma
            out_ref[here, p * 256 : p * 256 + 128] = (grad * up * (sigma + swish * (1.0 - sigma))).astype(jnp.bfloat16)
            out_ref[here, p * 256 + 128 : (p + 1) * 256] = (grad * swish).astype(jnp.bfloat16)
        return carry

    lax.fori_loop(0, grad_ref.shape[0] // 256, body, 0)


def ffn_bwd(grad, weight, gu):
    rows, width = grad.shape
    wide = gu.shape[1]
    return pl.pallas_call(
        ffn_bwd_kernel,
        grid=(pl.cdiv(wide, 512),),
        in_specs=[
            pl.BlockSpec((rows, width), lambda j: (0, 0)),
            pl.BlockSpec((width, 256), lambda j: (0, j)),
            pl.BlockSpec((rows, 512), lambda j: (0, j)),
        ],
        out_specs=pl.BlockSpec((rows, 512), lambda j: (0, j)),
        out_shape=jax.ShapeDtypeStruct((rows, wide), jnp.bfloat16),
        compiler_params=pltpu.CompilerParams(dimension_semantics=("arbitrary",), vmem_limit_bytes=32 << 20),
        cost_estimate=pl.CostEstimate(flops=10**9, bytes_accessed=1 << 20, transcendentals=0),
        name="ffn_bwd",
    )(grad, weight, gu)


def weight_grad_kernel(left_ref, right_ref, out_ref):
    turned = jnp.transpose(left_ref[...])
    width = right_ref.shape[1]

    def chunk(at, cols):
        out_ref[:, pl.ds(at, cols)] = mm(turned, right_ref[:, pl.ds(at, cols)], NN).astype(jnp.bfloat16)

    def step(c, carry):
        chunk(pl.multiple_of(c * 256, 256), 256)
        return carry

    lax.fori_loop(0, width // 256, step, 0)
    if width % 256:
        chunk(width // 256 * 256, width % 256)


def weight_grad(left, right):
    rows, high = left.shape
    width = right.shape[1]
    return pl.pallas_call(
        weight_grad_kernel,
        grid=(high // 256,),
        in_specs=[pl.BlockSpec((rows, 256), lambda i: (0, i)), pl.BlockSpec((rows, width), lambda i: (0, 0))],
        out_specs=pl.BlockSpec((256, width), lambda i: (i, 0)),
        out_shape=jax.ShapeDtypeStruct((high, width), jnp.bfloat16),
        compiler_params=pltpu.CompilerParams(dimension_semantics=("arbitrary",), vmem_limit_bytes=32 << 20),
        cost_estimate=pl.CostEstimate(flops=10**9, bytes_accessed=1 << 20, transcendentals=0),
        name="weight_grad",
    )(left, right)


def add_last_kernel(base_ref, more_ref, out_ref):
    out_ref[...] = (base_ref[...].astype(jnp.float32) + more_ref[...]).astype(jnp.bfloat16)


def add_last(base, more):
    high, cols = more.shape
    last = base.shape[1] // cols - 1
    return pl.pallas_call(
        add_last_kernel,
        grid=(1,),
        in_specs=[pl.BlockSpec((high, cols), lambda i: (0, last)), pl.BlockSpec((high, cols), lambda i: (0, 0))],
        out_specs=pl.BlockSpec((high, cols), lambda i: (0, last)),
        out_shape=jax.ShapeDtypeStruct(base.shape, base.dtype),
        input_output_aliases={0: 0},
        compiler_params=pltpu.CompilerParams(dimension_semantics=("arbitrary",), vmem_limit_bytes=16 << 20),
        cost_estimate=pl.CostEstimate(flops=10**6, bytes_accessed=1 << 20, transcendentals=0),
        name="add_last",
    )(base, more)


def swap(value, bit):
    return lax.ppermute(value, "head", [(i, i ^ bit) for i in range(BLOCKS)])


def after(values, *earlier):
    return lax.optimization_barrier((values, earlier))[0]


def turn(array, head_pos):
    blocks = array.reshape((BLOCKS, array.shape[0] // BLOCKS) + array.shape[1:])
    picked = [lax.dynamic_index_in_dim(blocks, head_pos ^ k, 0, keepdims=False) for k in range(BLOCKS)]
    return jnp.concatenate(picked, axis=0)


def rms_scale(values):
    return lax.rsqrt(jnp.mean(values * values, axis=-1, keepdims=True) + EPSILON)


def on_device(seq_count, tokens, cotangent, counts, pads, norm1_gain, w_query, w_key, w_value, w_gate_out,
              w_forget, forget_bias, out_gain, w_out, norm2_gain, w_gate, w_up, w_down):
    f32, b16 = jnp.float32, jnp.bfloat16
    rows, model_width = tokens.shape[1:]
    head_pos = lax.axis_index("head")
    head_arr = head_pos.reshape(1).astype(jnp.int32)
    width, slots, hidden_width = w_query.shape[1], w_forget.shape[1], w_gate.shape[1]
    share = w_query.shape[0]
    extra = slots
    size = rows // BLOCKS

    small = jnp.concatenate([out_gain, forget_bias])
    small = jnp.pad(small, (0, share - small.shape[0]))
    columns = jnp.stack([norm1_gain, norm2_gain, small], axis=1)
    columns = jnp.pad(columns, ((0, 0), (0, extra - 3)))
    wide = 4 * width
    own_mix = jnp.concatenate([w_out.T, w_query, w_key, w_value, w_gate_out, w_forget, columns], axis=1)
    mix = lax.all_gather(own_mix, "seq", axis=0, tiled=True)
    own_gu = jnp.stack([w_gate.reshape(share, -1, 128), w_up.reshape(share, -1, 128)], axis=2).reshape(share, -1)
    gu_weight = lax.all_gather(own_gu, "seq", axis=0, tiled=True)
    down_weight = lax.all_gather(w_down.T, "seq", axis=0, tiled=True)

    skip = width
    f_at, extra_at = skip + wide, skip + wide + slots
    gains = mix[:, extra_at : extra_at + 3].astype(f32)
    gain_one, gain_two = gains[:, 0], gains[:, 1]
    small_all = gains[:, 2].reshape(seq_count, share)
    n_gain, n_bias = out_gain.shape[0], forget_bias.shape[0]
    gain_head = small_all[:, :n_gain].reshape(1, width)
    bias = small_all[:, n_gain : n_gain + n_bias].reshape(slots, 1)

    x_rel = turn(tokens[0], head_pos)
    cot_rel = turn(cotangent[0], head_pos)
    block_of = jnp.arange(BLOCKS, dtype=jnp.int32) ^ head_pos
    position = (block_of[:, None] * size + jnp.arange(size, dtype=jnp.int32)[None, :]).reshape(rows, 1)
    live_len = jnp.where(counts[0] > 0, rows - pads[0], 0)
    live = (position < live_len).astype(f32)
    live_own = live[:size]

    x_f = x_rel.astype(f32)
    normed1 = (x_f * rms_scale(x_f) * gain_one).astype(b16)
    qkvg = mm(normed1, mix[:, skip:f_at], NN).astype(b16)
    forget_t = lax.dot_general(
        mix[:, f_at:extra_at], normed1, (((0,), (1,)), ((), ())), preferred_element_type=f32
    ) + bias
    log_keep = jax.nn.log_sigmoid(forget_t) / DAMPING
    keep_in = -jnp.expm1(log_keep)
    gated, mixed, probs, kst, vst = rec_fwd(head_arr, qkvg, log_keep, keep_in, gain_head)

    row_one, row_two = gain_one[None], gain_two[None]
    x_own = x_rel[:size]
    cot_own = cot_rel[:size]
    tall = lambda kind: jax.ShapeDtypeStruct((size, model_width), kind)
    line = jax.ShapeDtypeStruct((1, model_width), f32)
    residual, normed_own = head_scatter(
        gated, mix, (x_own, row_two), [tall(f32), tall(b16)], finish_mixer, 0, window=True
    )
    normed2 = head_gather(normed_own, 1).reshape(rows, model_width)
    gu, hidden = ffn_fwd(normed2, gu_weight)

    grad_ffn = (cot_rel.astype(f32) * live).astype(b16)
    grad_down = weight_grad(grad_ffn, hidden)
    down_weight = after(down_weight, grad_down)
    grad_down = lax.psum_scatter(grad_down, "seq", scatter_dimension=0, tiled=True)
    grad_gu = ffn_bwd(grad_ffn, down_weight, gu)
    grad_residual, grad_low, grad_gain_two, grad_gu_w = head_scatter(
        grad_gu, gu_weight, (residual, cot_own, live_own, row_two, normed2), [tall(f32), tall(b16), line],
        finish_norm_two, 2, filler=fill_gu, far=jax.ShapeDtypeStruct(gu_weight.shape, b16),
    )
    grad_gu_w = lax.psum_scatter(grad_gu_w, "seq", scatter_dimension=0, tiled=True)
    grad_att = head_gather(grad_low, 3).reshape(rows, model_width)
    grad_gated = mm(after(grad_att, grad_down), mix[:, :width], NN)
    grad_in, grad_gain_head, grad_bias = rec_bwd(
        head_arr, qkvg, log_keep, keep_in, forget_t, gain_head, mixed, probs, kst, vst, grad_gated
    )
    input_own, gain_one_part, grad_mix = head_scatter(
        grad_in, mix, (x_own, grad_residual, row_one, normed1, grad_att, gated),
        [tall(b16), jax.ShapeDtypeStruct((model_width, 1), f32)], finish_norm_one, 6,
        skip=skip, filler=functools.partial(fill_mix, skip), far=jax.ShapeDtypeStruct(mix.shape, b16),
    )
    shared = jnp.stack([grad_gain_two[0], gain_one_part[:, 0] / gain_one])
    shared = shared + swap(shared, 1)
    shared = shared + swap(shared, 2)
    third = jnp.concatenate(
        [
            grad_gain_head.reshape(seq_count, n_gain),
            grad_bias.reshape(seq_count, n_bias),
            jnp.zeros((seq_count, share - n_gain - n_bias), f32),
        ],
        axis=1,
    ).reshape(model_width)
    columns = jnp.stack([shared[1], shared[0], third], axis=1)
    grad_mix = add_last(grad_mix, jnp.pad(columns, ((0, 0), (slots, extra - 3))))
    hidden = after(hidden, grad_mix)
    grad_mix = lax.psum_scatter(grad_mix, "seq", scatter_dimension=0, tiled=True)

    out_own, ffn_squares = head_scatter(hidden, down_weight, (residual, live_own), [tall(b16), line], finish_ffn, 4)
    x_own_f = x_own.astype(f32)
    attended = residual - x_own_f
    stats = jnp.stack([
        jnp.sum(live_own * x_own_f * x_own_f),
        jnp.sum(live_own * attended * attended),
        jnp.sum(ffn_squares),
        jnp.sum(live_own),
    ])
    sums = lax.psum(stats, ("head", "seq"))
    out_own, input_own = after((out_own, input_own), grad_gu_w)
    outputs = turn(head_gather(out_own, 5).reshape(rows, model_width), head_pos)
    input_grad = turn(head_gather(input_own, 7).reshape(rows, model_width), head_pos).astype(f32)

    done = grad_mix.astype(f32)
    tail = done[:, extra_at : extra_at + 3]
    small = tail[:, 2]
    rms_stats = jnp.sqrt(sums[:3] / (sums[3] * model_width))
    pairs = grad_gu_w.astype(f32).reshape(share, -1, 2, 128)
    return (
        outputs[None],
        input_grad[None],
        tail[:, 0],
        done[:, skip : skip + width],
        done[:, skip + width : skip + 2 * width],
        done[:, skip + 2 * width : skip + 3 * width],
        done[:, skip + 3 * width : f_at],
        done[:, f_at:extra_at],
        small[n_gain : n_gain + n_bias],
        small[:n_gain],
        done[:, :width].T,
        tail[:, 1],
        pairs[:, :, 0].reshape(share, -1),
        pairs[:, :, 1].reshape(share, -1),
        grad_down.astype(f32).T,
        rms_stats,
    )


def solution(mesh):
    both = P("seq", "head")
    flat = P(("head", "seq"))
    rows = P("seq", None, None)
    return jax.shard_map(
        functools.partial(on_device, mesh.shape["seq"]),
        mesh=mesh,
        in_specs=(rows, rows, P("seq"), P("seq"), P("seq"), both, both, both, both, both, flat, flat,
                  P("head", "seq"), P("seq"), both, both, P("head", "seq")),
        out_specs=(rows, rows, P("seq"), both, both, both, both, both, flat, flat, P("head", "seq"), P("seq"),
                   both, both, P("head", "seq"), P()),
        check_vma=False,
    )
```

```python
import functools

import jax
import jax.numpy as jnp
import numpy as np
from jax import lax
from jax.experimental import pallas as pl
from jax.experimental.pallas import tpu as pltpu
from jax.sharding import PartitionSpec as P

EPSILON = 1e-06
DAMPING = 8.0
TILE = 128
BLOCKS = 4
HALVES = (64, 32, 16, 8, 4, 2, 1)
NT = (((1,), (1,)), ((), ()))
NN = (((1,), (0,)), ((), ()))
TN = (((0,), (0,)), ((), ()))


def rel_tile(rows, i, h):
    per = rows // BLOCKS // TILE
    return (i // per ^ h[0]) * per + i % per


def mm(left, right, dims):
    return lax.dot_general(left, right, dims, preferred_element_type=jnp.float32)


def span_matrix():
    r = np.arange(TILE)[:, None]
    t = np.arange(TILE)[None, :]
    parts = []
    for h in HALVES:
        base = t // (2 * h) * (2 * h)
        upper = t % (2 * h) >= h
        parts.append(upper & (r >= base + h) & (r <= t))
        parts.append(~upper & (r > t) & (r <= base + h - 1))
    parts.append(r <= t)
    parts.append(r > t)
    return np.concatenate(parts, axis=1).astype(np.float32)


def level_of():
    s = lax.broadcasted_iota(jnp.int32, (TILE, TILE), 0)
    t = lax.broadcasted_iota(jnp.int32, (TILE, TILE), 1)
    return jnp.where(s < t, s ^ t, jnp.where(s == t, 0, -1))


def level_masks():
    x = level_of()
    masks = [(x >= h) & (x < 2 * h) for h in HALVES]
    masks.append(x == 0)
    return masks


def decays(log_keep, keep_in, spans):
    slots = log_keep.shape[0]
    high = log_keep.astype(jnp.bfloat16)
    rest = log_keep - high.astype(jnp.float32)
    mid = rest.astype(jnp.bfloat16)
    both = mm(jnp.concatenate([high, mid], axis=0), spans, NN)
    grown = jnp.exp(both[:slots] + both[slots:])
    n = len(HALVES)
    ones = jnp.ones_like(keep_in)
    e_parts = [grown[:, (2 * i) * TILE : (2 * i + 1) * TILE] for i in range(n)] + [ones]
    f_bare = [grown[:, (2 * i + 1) * TILE : (2 * i + 2) * TILE] for i in range(n)] + [ones]
    e_all = grown[:, 2 * n * TILE : (2 * n + 1) * TILE]
    f_all = grown[:, (2 * n + 1) * TILE : (2 * n + 2) * TILE]
    total = e_all[:, TILE - 1 : TILE]
    return e_parts, f_bare, e_all, f_all, total


def norm_gate(mixed, gain, gate_pre):
    scale = lax.rsqrt(jnp.mean(mixed * mixed, axis=-1, keepdims=True) + EPSILON)
    unit = mixed * scale
    return scale, unit


def fwd_kernel(h_ref, q_ref, k_ref, v_ref, g_ref, lk_ref, w_ref, gain_ref, spans_ref,
               gated_ref, mixed_ref, probs_ref, kst_ref, vst_ref, kacc, vacc):
    @pl.when(pl.program_id(0) == 0)
    def _():
        kacc[...] = jnp.zeros_like(kacc)
        vacc[...] = jnp.zeros_like(vacc)
    width = q_ref.shape[1]
    root = width ** -0.5
    q, k, v = q_ref[...], k_ref[...], v_ref[...]
    keep_in = w_ref[...]
    e_parts, f_bare, e_all, f_all, total = decays(lk_ref[...], keep_in, spans_ref[...])
    masks = level_masks()
    kst, vst = kacc[...], vacc[...]
    kst_b, vst_b = kst.astype(jnp.bfloat16), vst.astype(jnp.bfloat16)
    kst_ref[0] = kst_b
    vst_ref[0] = vst_b
    inner = mm(k, q, NT) * root
    inner_b = inner.astype(jnp.bfloat16)
    zero_b = jnp.zeros_like(inner_b)
    f_parts = [(bare * keep_in).astype(jnp.bfloat16) for bare in f_bare]
    scores = e_all * (mm(kst_b, q, NT) * root)
    for mask, grow, fade in zip(masks, e_parts, f_parts):
        scores += grow * mm(fade, jnp.where(mask, inner_b, zero_b), NN)
    top = jnp.max(scores, axis=0, keepdims=True)
    raised = jnp.exp(scores - top)
    probs = raised / jnp.sum(raised, axis=0, keepdims=True)
    probs_ref[...] = probs
    mixing = jnp.zeros((TILE, TILE), jnp.float32)
    for mask, grow, fade in zip(masks, e_parts, f_parts):
        mixing = jnp.where(mask, mm(fade, (probs * grow).astype(jnp.bfloat16), TN), mixing)
    mixed = mm(mixing.astype(jnp.bfloat16), v, TN) + mm((probs * e_all).astype(jnp.bfloat16), vst_b, TN)
    tail = (f_all * keep_in).astype(jnp.bfloat16)
    kacc[...] = total * kst + mm(tail, k, NN)
    vacc[...] = total * vst + mm(tail, v, NN)
    mixed_ref[...] = mixed
    scale = lax.rsqrt(jnp.mean(mixed * mixed, axis=-1, keepdims=True) + EPSILON)
    gate = g_ref[...].astype(jnp.float32)
    swish = gate * jax.nn.sigmoid(gate)
    gated_ref[...] = (mixed * scale * gain_ref[...] * swish).astype(jnp.bfloat16)


def rec_fwd(head, qkvg, log_keep_t, keep_in_t, gain):
    rows, wide = qkvg.shape
    width = wide // 4
    slots = log_keep_t.shape[0]
    tiles = rows // TILE
    spans = jnp.asarray(span_matrix(), jnp.bfloat16)
    place = functools.partial(rel_tile, rows)
    col = lambda j: pl.BlockSpec((TILE, width), lambda i, h: (place(i, h), j))
    lane = pl.BlockSpec((slots, TILE), lambda i, h: (0, place(i, h)))
    state = pl.BlockSpec((1, slots, width), lambda i, h: (i, 0, 0))
    return pl.pallas_call(
        fwd_kernel,
        grid_spec=pltpu.PrefetchScalarGridSpec(
            num_scalar_prefetch=1,
            grid=(tiles,),
            in_specs=[col(0), col(1), col(2), col(3), lane, lane,
                      pl.BlockSpec((1, width), lambda i, h: (0, 0)),
                      pl.BlockSpec(spans.shape, lambda i, h: (0, 0))],
            out_specs=[col(0), col(0), lane, state, state],
            scratch_shapes=[pltpu.VMEM((slots, width), jnp.float32)] * 2,
        ),
        out_shape=[
            jax.ShapeDtypeStruct((rows, width), jnp.bfloat16),
            jax.ShapeDtypeStruct((rows, width), jnp.float32),
            jax.ShapeDtypeStruct((slots, rows), jnp.float32),
            jax.ShapeDtypeStruct((tiles, slots, width), jnp.bfloat16),
            jax.ShapeDtypeStruct((tiles, slots, width), jnp.bfloat16),
        ],
        compiler_params=pltpu.CompilerParams(dimension_semantics=("arbitrary",), vmem_limit_bytes=60 << 20),
        cost_estimate=pl.CostEstimate(flops=5 * 10**9, bytes_accessed=10 << 20, transcendentals=0),
        name="slot_fwd",
    )(head, qkvg, qkvg, qkvg, qkvg, log_keep_t, keep_in_t, gain, spans)


def bwd_kernel(h_ref, q_ref, k_ref, v_ref, g_ref, lk_ref, w_ref, fpre_ref, gain_ref, spans_ref,
               mixed_ref, probs_ref, kst_ref, vst_ref, dg_ref,
               dproj_ref, dgain_ref, dbias_ref, dk_acc, dv_acc, cross):
    step = pl.program_id(0)
    width = q_ref.shape[1]
    slots = lk_ref.shape[0]

    @pl.when(step == 0)
    def _():
        dk_acc[...] = jnp.zeros_like(dk_acc)
        dv_acc[...] = jnp.zeros_like(dv_acc)
        cross[...] = jnp.zeros_like(cross)
        dgain_ref[...] = jnp.zeros_like(dgain_ref)
        dbias_ref[...] = jnp.zeros_like(dbias_ref)
    root = width ** -0.5
    q, k, v = q_ref[...], k_ref[...], v_ref[...]
    mixed = mixed_ref[...]
    gate = g_ref[...].astype(jnp.float32)
    gain = gain_ref[...]
    d_gated = dg_ref[...].astype(jnp.float32)
    scale = lax.rsqrt(jnp.mean(mixed * mixed, axis=-1, keepdims=True) + EPSILON)
    unit = mixed * scale
    sigma = jax.nn.sigmoid(gate)
    swish = gate * sigma
    slope = sigma * (1.0 + gate * (1.0 - sigma))
    dproj_ref[:, 3 * width : 4 * width] = (d_gated * unit * gain * slope).astype(jnp.bfloat16)
    d_normed = d_gated * swish
    dgain_ref[...] += jnp.sum(d_normed * unit, axis=0, keepdims=True)
    c = d_normed * gain
    d_mixed = scale * (c - unit * jnp.mean(c * unit, axis=-1, keepdims=True))
    d_out = d_mixed.astype(jnp.bfloat16)

    log_keep, keep_in = lk_ref[...], w_ref[...]
    e_parts, f_bare, e_all, f_all, total = decays(log_keep, keep_in, spans_ref[...])
    masks = level_masks()
    probs = probs_ref[...]
    kst, vst = kst_ref[0], vst_ref[0]
    dkst, dvst = dk_acc[...], dv_acc[...]
    dkst_b, dvst_b = dkst.astype(jnp.bfloat16), dvst.astype(jnp.bfloat16)

    inner_b = (mm(k, q, NT) * root).astype(jnp.bfloat16)
    d_mixing_b = mm(v, d_out, NT).astype(jnp.bfloat16)
    pair = jnp.concatenate([inner_b, d_mixing_b], axis=1)
    zero_b = jnp.zeros_like(pair)
    masks2 = [jnp.concatenate([mask, mask], axis=1) for mask in masks]
    pairs = [jnp.where(mask, pair, zero_b) for mask in masks2]
    f_parts = [(bare * keep_in).astype(jnp.bfloat16) for bare in f_bare]
    both = [mm(fade, two, NN) for fade, two in zip(f_parts, pairs)]
    s_state = mm(kst, q, NT) * root
    p_state = mm(vst, d_out, NT)
    d_probs = e_all * p_state
    for grow, two in zip(e_parts, both):
        d_probs += grow * two[:, TILE:]
    d_scores = probs * (d_probs - jnp.sum(probs * d_probs, axis=0, keepdims=True))

    xy_all = jnp.concatenate([d_scores * e_all, probs * e_all], axis=1).astype(jnp.bfloat16)
    xy_parts = [jnp.concatenate([d_scores * grow, probs * grow], axis=1).astype(jnp.bfloat16) for grow in e_parts]
    x0 = xy_all[:, :TILE]
    y0 = xy_all[:, TILE:]
    change = x0.astype(jnp.float32) * s_state + y0.astype(jnp.float32) * p_state
    into = jnp.zeros((slots, TILE), jnp.float32)
    d_both = jnp.zeros((TILE, 2 * TILE), jnp.float32)
    for i, (grow, bare, fade, two, xy, part, mask) in enumerate(
        zip(e_parts, f_bare, f_parts, both, xy_parts, pairs, masks2)
    ):
        z = mm(xy, part, NT)
        into += bare * z
        if i < len(HALVES):
            mass = xy.astype(jnp.float32) * two
            change += mass[:, :TILE] + mass[:, TILE:] - fade.astype(jnp.float32) * z
        d_both = jnp.where(mask, mm(fade, xy, TN), d_both)
    d_both_b = d_both.astype(jnp.bfloat16)
    d_inner, mixing = d_both_b[:, :TILE], d_both_b[:, TILE:]
    tail = (f_all * keep_in).astype(jnp.bfloat16)
    z_state = mm(dkst_b, k, NT) + mm(dvst_b, v, NT)
    into += f_all * z_state
    change -= tail.astype(jnp.float32) * z_state

    dproj_ref[:, :width] = (root * (mm(d_inner, k, TN) + mm(x0, kst, TN))).astype(jnp.bfloat16)
    dproj_ref[:, width : 2 * width] = (root * mm(d_inner, q, NN) + mm(tail, dkst_b, TN)).astype(jnp.bfloat16)
    dproj_ref[:, 2 * width : 3 * width] = (mm(mixing, d_out, NN) + mm(tail, dvst_b, TN)).astype(jnp.bfloat16)

    later = (lax.broadcasted_iota(jnp.int32, (TILE, TILE), 0) >= lax.broadcasted_iota(jnp.int32, (TILE, TILE), 1)).astype(jnp.bfloat16)
    high = change.astype(jnp.bfloat16)
    rest = change - high.astype(jnp.float32)
    mid = rest.astype(jnp.bfloat16)
    low = (rest - mid.astype(jnp.float32)).astype(jnp.bfloat16)
    sums = mm(jnp.concatenate([high, mid, low], axis=0), later, NN)
    d_log_keep = sums[:slots] + sums[slots : 2 * slots] + sums[2 * slots :] + cross[...] - jnp.exp(log_keep) * into
    d_forget = (d_log_keep * jax.nn.sigmoid(-fpre_ref[...]) / DAMPING).astype(jnp.bfloat16)
    dbias_ref[...] += jnp.sum(d_forget.astype(jnp.float32), axis=1, keepdims=True)
    turned = jnp.transpose(d_forget.astype(jnp.float32))
    dproj_ref[:, 4 * width :] = jnp.concatenate([turned, jnp.zeros_like(turned)], axis=1).astype(jnp.bfloat16)

    dkst_new = total * dkst + root * mm(x0, q, NN)
    dvst_new = total * dvst + mm(y0, d_out, NN)
    dk_acc[...] = dkst_new
    dv_acc[...] = dvst_new
    cross[...] = jnp.sum(kst.astype(jnp.float32) * dkst_new + vst.astype(jnp.float32) * dvst_new, axis=1, keepdims=True)


def rec_bwd(head, qkvg, log_keep_t, keep_in_t, forget_pre_t, gain, mixed, probs, kst, vst, d_gated):
    rows, wide = qkvg.shape
    width = wide // 4
    slots = log_keep_t.shape[0]
    tiles = rows // TILE
    last = tiles - 1
    spans = jnp.asarray(span_matrix(), jnp.bfloat16)
    place = lambda i, h: rel_tile(rows, last - i, h)
    col = lambda j: pl.BlockSpec((TILE, width), lambda i, h: (place(i, h), j))
    lane = pl.BlockSpec((slots, TILE), lambda i, h: (0, place(i, h)))
    state = pl.BlockSpec((1, slots, width), lambda i, h: (last - i, 0, 0))
    wide_out = 4 * width + 2 * slots
    return pl.pallas_call(
        bwd_kernel,
        grid_spec=pltpu.PrefetchScalarGridSpec(
            num_scalar_prefetch=1,
            grid=(tiles,),
            in_specs=[col(0), col(1), col(2), col(3), lane, lane, lane,
                      pl.BlockSpec((1, width), lambda i, h: (0, 0)),
                      pl.BlockSpec(spans.shape, lambda i, h: (0, 0)),
                      col(0), lane, state, state, col(0)],
            out_specs=[pl.BlockSpec((TILE, wide_out), lambda i, h: (place(i, h), 0)),
                       pl.BlockSpec((1, width), lambda i, h: (0, 0)),
                       pl.BlockSpec((slots, 1), lambda i, h: (0, 0))],
            scratch_shapes=[pltpu.VMEM((slots, width), jnp.float32)] * 2 + [pltpu.VMEM((slots, 1), jnp.float32)],
        ),
        out_shape=[
            jax.ShapeDtypeStruct((rows, wide_out), jnp.bfloat16),
            jax.ShapeDtypeStruct((1, width), jnp.float32),
            jax.ShapeDtypeStruct((slots, 1), jnp.float32),
        ],
        compiler_params=pltpu.CompilerParams(dimension_semantics=("arbitrary",), vmem_limit_bytes=60 << 20),
        cost_estimate=pl.CostEstimate(flops=8 * 10**9, bytes_accessed=16 << 20, transcendentals=0),
        name="slot_bwd",
    )(head, qkvg, qkvg, qkvg, qkvg, log_keep_t, keep_in_t, forget_pre_t, gain, spans, mixed, probs, kst, vst, d_gated)


MESH = pl.DeviceIdType.MESH
CHUNK = 32


def neighbours():
    head = lax.axis_index("head")
    return {"head": head + 1 - 2 * (head % 2)}, {"head": (head + 2) % BLOCKS}


def flipped(index, bit):
    return index + bit - 2 * bit * (index // bit % 2)


def other_core():
    return {"seq": flipped(lax.axis_index("seq"), 1)}


def greet(targets):
    barrier = pltpu.get_barrier_semaphore()
    for target in targets:
        pl.semaphore_signal(barrier, inc=1, device_id=target, device_id_type=MESH)
    pl.semaphore_wait(barrier, len(targets))


LIMIT = 60 << 20
FAR = pl.BlockSpec(memory_space=pl.ANY)
WHOLE = pl.BlockSpec(memory_space=pltpu.VMEM)


class Loads:
    def __init__(self, sem):
        self.sem, self.copies = sem, []

    def add(self, src, dst):
        copy = pltpu.make_async_copy(src, dst, self.sem.at[len(self.copies)])
        copy.start()
        self.copies.append(copy)
        return copy


class Scatter:
    order = (0, 2, 1, 3)

    def __init__(self, left, right, acc, mid, send, got, send_sem, got_sem):
        self.left, self.right, self.acc, self.mid, self.send, self.got = left, right, acc, mid, send, got
        self.size, self.cols = send.shape[1:]
        to_x, to_y = neighbours()
        self.copies = []
        for u in range(2):
            for k, to in enumerate((to_x, to_x, to_y, to_y, to_y, to_x)):
                slot = 6 * u + k
                self.copies.append(
                    pltpu.make_async_remote_copy(
                        src_ref=send.at[slot], dst_ref=got.at[slot], send_sem=send_sem.at[slot],
                        recv_sem=got_sem.at[slot], device_id=to, device_id_type=MESH,
                    )
                )

    def first(self, loads, watch=None):
        size, cols = self.size, self.cols
        for part, load in zip(self.order, loads):
            load.wait()
            value = mm(self.left[...], self.right[part * cols : (part + 1) * cols, :], NT)
            side_at, u = part // 2, part % 2
            here = slice(part * cols, (part + 1) * cols)
            slot = 6 * u + 2 * side_at
            near_block, mid_block = (1, 2) if side_at == 0 else (2, 1)
            self.acc[:, here] = value[:size]
            self.mid[:, here] = value[mid_block * size : (mid_block + 1) * size]
            self.send[slot] = value[3 * size :].astype(jnp.bfloat16)
            self.copies[slot].start()
            self.send[slot + 1] = value[near_block * size : (near_block + 1) * size].astype(jnp.bfloat16)
            self.copies[slot + 1].start()
            if watch is not None:
                watch(here, value)

    def second(self):
        cols = self.cols
        for part in self.order:
            side_at, u = part // 2, part % 2
            first, second = 6 * u + 2 * side_at, 6 * u + 4 + side_at
            here = slice(part * cols, (part + 1) * cols)
            self.copies[first].wait_recv()
            self.send[second] = (self.mid[:, here] + self.got[first].astype(jnp.float32)).astype(jnp.bfloat16)
            self.copies[second].start()

    def last(self, finish):
        for u in range(2):
            for k in (1, 3, 4, 5):
                self.copies[6 * u + k].wait_recv()
        cols = self.cols

        def rows(i, carry):
            here = pl.ds(pl.multiple_of(i * CHUNK, CHUNK), CHUNK)
            sums = []
            for part in range(4):
                side_at, u = part // 2, part % 2
                one, two = self.got[6 * u + 2 * side_at + 1, here, :], self.got[6 * u + 4 + side_at, here, :]
                own = self.acc[here, part * cols : (part + 1) * cols]
                sums.append(own + one.astype(jnp.float32) + two.astype(jnp.float32))
            finish(here, jnp.concatenate(sums, axis=1), i)
            return carry

        lax.fori_loop(0, self.size // CHUNK, rows, 0)

    def close(self):
        for one in self.copies:
            one.wait_send()


def scatter_scratch(rows, depth, high):
    size, cols = rows // BLOCKS, high // 4
    return [
        pltpu.VMEM((rows, depth), jnp.bfloat16),
        pltpu.VMEM((high, depth), jnp.bfloat16),
        pltpu.VMEM((size, high), jnp.float32),
        pltpu.VMEM((size, high), jnp.float32),
        pltpu.VMEM((12, size, cols), jnp.bfloat16),
        pltpu.VMEM((12, size, cols), jnp.bfloat16),
        pltpu.SemaphoreType.DMA((12,)),
        pltpu.SemaphoreType.DMA((12,)),
    ]


def load_parts(loads, right_far, right, skip):
    cols = right.shape[0] // 4
    parts = []
    for part in Scatter.order:
        here = pl.ds(part * cols, cols)
        parts.append(loads.add(right_far.at[here, pl.ds(skip, right.shape[1])], right.at[here, :]))
    return parts


def scatter_kernel(plan, *refs):
    n_far, n_near, n_out, skip, finish, filler = plan
    left_far, right_far, *more_far = refs[:n_far]
    near = refs[n_far : n_far + n_near]
    outs = refs[n_far + n_near : n_far + n_near + n_out]
    load_sem, *rest = refs[n_far + n_near + n_out :]
    scatter, spare = rest[:8], rest[8:]
    left, right = scatter[:2]
    loads = Loads(load_sem)
    load_left = loads.add(left_far, left)
    parts = load_parts(loads, right_far, right, skip)
    more = [(loads.add(src, dst), dst) for src, dst in zip(more_far, spare)]
    spare = spare[len(more_far) :]
    greet(neighbours() if filler is None else (*neighbours(), other_core()))
    sum_heads = Scatter(*scatter)
    load_left.wait()
    sum_heads.first(parts)
    sum_heads.second()
    for load, _ in more:
        load.wait()
    side = [dst for _, dst in more]
    if filler is not None:
        filler(left, right, side, outs, spare)
    sum_heads.last(lambda here, total, i: finish(here, total, side, near, outs, i))
    sum_heads.close()


def head_scatter(left, right, far, near, out_shapes, finish, number, filler=None, filled=(), scratch=()):
    rows, depth = left.shape
    plan = (2 + len(far), len(near), len(out_shapes) + len(filled), 0, finish, filler)
    return pl.pallas_call(
        functools.partial(scatter_kernel, plan),
        in_specs=[FAR] * (2 + len(far)) + [WHOLE] * len(near),
        out_specs=[WHOLE] * len(out_shapes) + [FAR] * len(filled),
        out_shape=[*out_shapes, *filled],
        scratch_shapes=[
            pltpu.SemaphoreType.DMA((5 + len(far),)),
            *scatter_scratch(rows, depth, right.shape[0]),
            *[pltpu.VMEM(one.shape, one.dtype) for one in far],
            *scratch,
        ],
        compiler_params=pltpu.CompilerParams(collective_id=number, has_side_effects=True, vmem_limit_bytes=LIMIT),
        cost_estimate=pl.CostEstimate(flops=10**9, bytes_accessed=1 << 20, transcendentals=0),
        name="head_scatter%d" % number,
    )(left, right, *far, *near)


STEP = 512


def weight_tiles(pairs, place, out_ref, room, land, store_sem, send_sem, got_sem):
    count = land.shape[0]
    share = land.shape[1]
    core = lax.axis_index("seq") % 2
    width = out_ref.shape[1]

    def swap_shard(p):
        return pltpu.make_async_remote_copy(
            src_ref=room.at[pl.ds((2 * p + 1 - core) * share, share), :], dst_ref=land.at[p],
            send_sem=send_sem.at[p], recv_sem=got_sem.at[p], device_id=other_core(), device_id_type=MESH,
        )

    def store(p):
        return pltpu.make_async_copy(land.at[p], out_ref.at[pl.ds(p * share, share), :], store_sem.at[p])

    def settle(p):
        swap_shard(p).wait_recv()
        own = room[pl.ds(pl.multiple_of((2 * p + core) * share, share), share), :]
        land[p] = (own.astype(jnp.float32) + land[p].astype(jnp.float32)).astype(jnp.bfloat16)
        store(p).start()

    per = STEP // (2 * share)
    for i in range(room.shape[0] // STEP):
        here = slice(i * STEP, (i + 1) * STEP)
        for turned, right, column in pairs:
            for at in range(0, right.shape[1], STEP):
                cols = min(STEP, right.shape[1] - at)
                value = mm(turned[here, :], right[:, at : at + cols], NN).astype(jnp.bfloat16)
                for src, dst, wide in place(column + at, cols):
                    room[here, dst : dst + wide] = value[:, src : src + wide]
        for p in range(i * per, (i + 1) * per):
            swap_shard(p).start()
        if i:
            for p in range((i - 1) * per, i * per):
                settle(p)
    for p in range(count - per, count):
        settle(p)
    for p in range(count):
        store(p).wait()
        swap_shard(p).wait_send()


def tile_scratch(high, width, share, room):
    count = high // (2 * share)
    return [pltpu.VMEM((high, width), jnp.bfloat16)] * room + [
        pltpu.VMEM((count, share, width), jnp.bfloat16),
        pltpu.SemaphoreType.DMA((count,)),
        pltpu.SemaphoreType.DMA((count,)),
        pltpu.SemaphoreType.DMA((count,)),
    ]


def fill_gu(left, right, side, outs, spare):
    half = left.shape[1] // 2

    def place(at, cols):
        return [(k, (at + k) // 256 * 128 + (at + k) // 128 % 2 * half, 128) for k in range(0, cols, 128)]

    weight_tiles([(side[0], left, 0)], place, outs[-1], right, *spare)


def fill_mix(left, right, side, outs, spare):
    att_t, gated, normed_t, grad_in = side[:4]
    place = lambda at, cols: [(0, at, cols)]
    weight_tiles([(att_t, gated, 0), (normed_t, grad_in, gated.shape[1])], place, outs[-1], *spare)


class Gather:
    def __init__(self, own, blocks, send_sem, got_sem):
        half = own.shape[1] // 2
        to_x, to_y = neighbours()

        def copy(slot, src, block, side_at, target):
            here = pl.ds(side_at * half, half)
            return pltpu.make_async_remote_copy(
                src_ref=src.at[:, here], dst_ref=blocks.at[block, :, here],
                send_sem=send_sem.at[slot], recv_sem=got_sem.at[slot], device_id=target, device_id_type=MESH,
            )

        self.copies = [
            copy(0, own, 1, 0, to_x),
            copy(1, own, 2, 1, to_y),
            copy(2, own, 1, 1, to_x),
            copy(3, own, 2, 0, to_y),
            copy(4, blocks.at[1], 3, 0, to_y),
            copy(5, blocks.at[2], 3, 1, to_x),
        ]

    def first(self):
        for one in self.copies[:4]:
            one.start()

    def second(self):
        for near, far in ((0, 4), (1, 5)):
            self.copies[near].wait_recv()
            self.copies[far].start()

    def last(self):
        for one in self.copies[2:]:
            one.wait_recv()
        for one in self.copies:
            one.wait_send()


def gather_kernel(plan, *refs):
    keep, product, also = plan
    refs = list(refs)
    own_ref = refs.pop(0)
    weight_far = refs.pop(0) if product else None
    also_far = refs.pop(0) if also else None
    out_ref = refs.pop(0) if keep else None
    turned_ref = refs.pop(0)
    product_ref = refs.pop(0) if product else None
    also_ref = refs.pop(0) if also else None
    blocks, turned_buf, send_sem, got_sem, out_sem, load_sem, *refs = refs
    size, half = own_ref.shape[0], own_ref.shape[1] // 2
    loads = Loads(load_sem)
    if product:
        weight = refs.pop(0)
        fetch = loads.add(weight_far.at[:, pl.ds(0, weight.shape[1])], weight)
    if also:
        also_buf, also_turned = refs
        fetch = loads.add(also_far, also_buf)
    greet(neighbours())
    gather = Gather(own_ref, blocks, send_sem, got_sem)
    gather.first()
    if product or also:
        fetch.wait()
    stores = []

    def store(src, dst):
        copy = pltpu.make_async_copy(src, dst, out_sem.at[len(stores)])
        copy.start()
        stores.append(copy)

    def use(block, side_at, src):
        here = slice(side_at * half, (side_at + 1) * half)
        rows = slice(block * size, (block + 1) * size)
        value = src[:, here]
        turned_buf[here, rows] = jnp.transpose(value)
        store(turned_buf.at[here, rows], turned_ref.at[here, rows])
        if keep:
            store(src.at[:, here], out_ref.at[block, :, here])
        if product:
            term = mm(value, weight[here, :], NN)
            if (block, side_at) in ((0, 0), (1, 0), (2, 1), (3, 0)):
                product_ref[rows, :] = term
            else:
                product_ref[rows, :] += term

    use(0, 0, own_ref)
    use(0, 1, own_ref)
    if also:
        also_turned[...] = jnp.transpose(also_buf[: also_buf.shape[0] // 2, :])
        middle = also_buf.shape[0] // 2
        store(also_turned, also_ref.at[:, pl.ds(0, middle)])
    gather.second()
    use(1, 0, blocks.at[1])
    use(2, 1, blocks.at[2])
    if also:
        stores[-1 - 4 * keep - 2 * (not keep)].wait()
        finished = len(stores) - 1 - 4 * keep - 2 * (not keep)
        also_turned[...] = jnp.transpose(also_buf[middle:, :])
        store(also_turned, also_ref.at[:, pl.ds(middle, middle)])
    for slot, block, side_at in ((2, 1, 1), (3, 2, 0), (4, 3, 0), (5, 3, 1)):
        gather.copies[slot].wait_recv()
        use(block, side_at, blocks.at[block])
    for at, one in enumerate(stores):
        if not also or at != finished:
            one.wait()
    for one in gather.copies:
        one.wait_send()


def head_gather(own, number, keep=True, weight=None, width=0, also=None):
    size, wide = own.shape
    rows = BLOCKS * size
    product = weight is not None
    extra = [one for one in (weight, also) if one is not None]
    out_shape, out_specs = [], []
    if keep:
        out_shape.append(jax.ShapeDtypeStruct((BLOCKS, size, wide), own.dtype))
        out_specs.append(FAR)
    out_shape.append(jax.ShapeDtypeStruct((wide, rows), own.dtype))
    out_specs.append(FAR)
    scratch = [
        pltpu.VMEM((BLOCKS, size, wide), own.dtype),
        pltpu.VMEM((wide, rows), own.dtype),
        pltpu.SemaphoreType.DMA((6,)),
        pltpu.SemaphoreType.DMA((6,)),
        pltpu.SemaphoreType.DMA((20,)),
        pltpu.SemaphoreType.DMA((2,)),
    ]
    if product:
        out_shape.append(jax.ShapeDtypeStruct((rows, width), jnp.float32))
        out_specs.append(WHOLE)
        scratch.append(pltpu.VMEM((wide, width), own.dtype))
    if also is not None:
        out_shape.append(jax.ShapeDtypeStruct(also.shape[::-1], also.dtype))
        out_specs.append(FAR)
        scratch += [pltpu.VMEM(also.shape, also.dtype), pltpu.VMEM((also.shape[1], also.shape[0] // 2), also.dtype)]
    return pl.pallas_call(
        functools.partial(gather_kernel, (keep, product, also is not None)),
        in_specs=[WHOLE] + [FAR] * len(extra),
        out_specs=out_specs,
        out_shape=out_shape,
        scratch_shapes=scratch,
        compiler_params=pltpu.CompilerParams(collective_id=number, has_side_effects=True, vmem_limit_bytes=LIMIT),
        cost_estimate=pl.CostEstimate(flops=10**9, bytes_accessed=1 << 20, transcendentals=0),
        name="head_gather%d" % number,
    )(own, *extra)


def unit_of(values):
    scale = lax.rsqrt(jnp.mean(values * values, axis=-1, keepdims=True) + EPSILON)
    return scale, values * scale


def finish_mixer(here, total, side, near, outs, i):
    x = side[0][here, :].astype(jnp.float32)
    gain, live = near[0][...], near[1][here, :]
    residual = x + total
    outs[0][here, :] = residual
    outs[1][here, :] = (unit_of(residual)[1] * gain).astype(jnp.bfloat16)
    add_row(outs[2], jnp.sum(live * x * x, axis=0, keepdims=True), i)
    add_row(outs[3], jnp.sum(live * total * total, axis=0, keepdims=True), i)


def add_row(ref, row, i):
    @pl.when(i == 0)
    def _():
        ref[...] = jnp.zeros_like(ref)

    ref[...] += row


def norm_back(total, gain, scale, unit):
    c = total * gain
    return scale * (c - unit * jnp.mean(c * unit, axis=-1, keepdims=True))


def finish_norm_two(here, total, side, near, outs, i):
    residual, cot = side[1][here, :], side[2][here, :].astype(jnp.float32)
    live, gain = near[0][here, :], near[1][...]
    scale, unit = unit_of(residual)
    add_row(outs[2], jnp.sum(total * unit, axis=0, keepdims=True), i)
    grad = cot * live + norm_back(total, gain, scale, unit)
    outs[0][here, :] = grad
    outs[1][here, :] = grad.astype(jnp.bfloat16)


def finish_ffn(here, total, side, near, outs, i):
    live = near[0][here, :]
    add_row(outs[1], jnp.sum(live * total * total, axis=0, keepdims=True), i)
    outs[0][here, :] = (live * (side[-1][here, :] + total)).astype(jnp.bfloat16)


SMALL = 8


def tail_kernel(skip, grad_far, mix_far, x_far, res_far, out_own, scale_ref, gain_ref, small_ref,
                outputs_far, input_far, total_ref, load_sem, store_sem, *rest):
    scatter = rest[:8]
    left, right = scatter[:2]
    x_buf, res_buf, gain_row, in_own, out_blocks, in_blocks, f_send, f_got, z_send, z_got, s_buf, s_send, s_got = rest[8:]
    loads = Loads(load_sem)
    load_left = loads.add(grad_far, left)
    parts = load_parts(loads, mix_far, right, skip)
    load_x = loads.add(x_far, x_buf)
    load_res = loads.add(res_far, res_buf)
    size = in_own.shape[0]
    seq = lax.axis_index("seq")
    hops = [*neighbours(), other_core()]
    bit = 2
    while bit < lax.axis_size("seq"):
        hops.append({"seq": flipped(seq, bit)})
        bit *= 2
    greet(hops)
    sum_heads = Scatter(*scatter)

    def watch(here, value):
        term = value * x_buf[:, here].astype(jnp.float32) * scale_ref[...]
        gain_row[:, here] = jnp.sum(term, axis=0, keepdims=True)

    f_gather = Gather(out_own, out_blocks, f_send, f_got)
    f_gather.first()
    load_left.wait()
    load_x.wait()
    sum_heads.first(parts, watch)
    sum_heads.second()

    is_last = lax.broadcasted_iota(jnp.int32, (SMALL, 1), 0) == SMALL - 1
    is_first = lax.broadcasted_iota(jnp.int32, (SMALL, 1), 0) == 0
    s_buf[0] = jnp.where(is_first, gain_row[...], small_ref[...])
    small = [
        pltpu.make_async_remote_copy(
            src_ref=s_buf.at[2 * k], dst_ref=s_buf.at[2 * k + 1], send_sem=s_send.at[k], recv_sem=s_got.at[k],
            device_id=hop, device_id_type=MESH,
        )
        for k, hop in enumerate(hops)
    ]

    def hop_done(k):
        small[k].wait_recv()
        arrived = s_buf[2 * k + 1]
        if k < 2:
            arrived = jnp.where(is_last, 0.0, arrived)
        if k + 1 < len(small):
            s_buf[2 * k + 2] = s_buf[2 * k] + arrived
            small[k + 1].start()
        else:
            total_ref[...] = s_buf[2 * k] + arrived

    small[0].start()
    load_res.wait()

    def finish(here, total, i):
        scale, unit = unit_of(x_buf[here, :].astype(jnp.float32))
        in_own[here, :] = (res_buf[here, :] + norm_back(total, gain_ref[...], scale, unit)).astype(jnp.bfloat16)

    f_gather.second()
    hop_done(0)
    sum_heads.last(finish)
    z_gather = Gather(in_own, in_blocks, z_send, z_got)
    z_gather.first()
    head = lax.axis_index("head")
    places = (head, flipped(head, 1), flipped(head, 2), BLOCKS - 1 - head)
    stores = []

    def store(src, far, k):
        copy = pltpu.make_async_copy(src, far.at[places[k]], store_sem.at[len(stores)])
        copy.start()
        stores.append(copy)

    store(out_own, outputs_far, 0)
    store(in_own, input_far, 0)
    hop_done(1)
    z_gather.second()
    for k in range(2, len(small)):
        hop_done(k)
    f_gather.last()
    for k in range(1, BLOCKS):
        store(out_blocks.at[k], outputs_far, k)
    z_gather.last()
    for k in range(1, BLOCKS):
        store(in_blocks.at[k], input_far, k)
    sum_heads.close()
    for one in small:
        one.wait_send()
    for one in stores:
        one.wait()


def tail_stage(hops, skip, grad_in, mix, x_rel, grad_residual, out_own, scale, gain, small, number):
    rows, depth = grad_in.shape
    size, high = out_own.shape
    blocks = jax.ShapeDtypeStruct((BLOCKS, size, high), jnp.bfloat16)
    sems = lambda n: pltpu.SemaphoreType.DMA((n,))
    return pl.pallas_call(
        functools.partial(tail_kernel, skip),
        in_specs=[FAR] * 4 + [WHOLE] * 4,
        out_specs=[FAR, FAR, WHOLE],
        out_shape=[blocks, blocks, jax.ShapeDtypeStruct((SMALL, high), jnp.float32)],
        scratch_shapes=[
            sems(7),
            sems(2 * BLOCKS),
            *scatter_scratch(rows, depth, high),
            pltpu.VMEM((rows, high), jnp.bfloat16),
            pltpu.VMEM((size, high), jnp.float32),
            pltpu.VMEM((1, high), jnp.float32),
            pltpu.VMEM((size, high), jnp.bfloat16),
            pltpu.VMEM((BLOCKS, size, high), jnp.bfloat16),
            pltpu.VMEM((BLOCKS, size, high), jnp.bfloat16),
            sems(6), sems(6), sems(6), sems(6),
            pltpu.VMEM((2 * hops, SMALL, high), jnp.float32),
            sems(hops), sems(hops),
        ],
        compiler_params=pltpu.CompilerParams(collective_id=number, has_side_effects=True, vmem_limit_bytes=LIMIT),
        cost_estimate=pl.CostEstimate(flops=10**9, bytes_accessed=1 << 20, transcendentals=0),
        name="tail_stage",
    )(grad_in, mix, x_rel, grad_residual, out_own, scale, gain, small)


def ffn_fwd_kernel(x_ref, w_ref, gu_ref, hidden_ref):
    value = mm(x_ref[...], w_ref[...], NN)
    gu_ref[...] = value.astype(jnp.bfloat16)
    gate, up = value[:, :128], value[:, 128:]
    hidden_ref[...] = (gate * jax.nn.sigmoid(gate) * up).astype(jnp.bfloat16)


def ffn_fwd(x, weight):
    rows, width = x.shape
    wide = weight.shape[1]
    return pl.pallas_call(
        ffn_fwd_kernel,
        grid=(wide // 256,),
        in_specs=[pl.BlockSpec((rows, width), lambda j: (0, 0)), pl.BlockSpec((width, 256), lambda j: (0, j))],
        out_specs=[pl.BlockSpec((rows, 256), lambda j: (0, j)), pl.BlockSpec((rows, 128), lambda j: (0, j))],
        out_shape=[
            jax.ShapeDtypeStruct((rows, wide), jnp.bfloat16),
            jax.ShapeDtypeStruct((rows, wide // 2), jnp.bfloat16),
        ],
        compiler_params=pltpu.CompilerParams(dimension_semantics=("arbitrary",), vmem_limit_bytes=LIMIT),
        cost_estimate=pl.CostEstimate(flops=10**9, bytes_accessed=1 << 20, transcendentals=0),
        name="ffn_fwd",
    )(x, weight)


def ffn_bwd_kernel(grad_ref, w_ref, gu_ref, out_ref):
    value = mm(grad_ref[...], w_ref[...], NN)
    for p in range(2):
        grad = value[:, p * 128 : (p + 1) * 128]
        gate = gu_ref[:, p * 256 : p * 256 + 128].astype(jnp.float32)
        up = gu_ref[:, p * 256 + 128 : (p + 1) * 256].astype(jnp.float32)
        sigma = jax.nn.sigmoid(gate)
        swish = gate * sigma
        out_ref[:, p * 256 : p * 256 + 128] = (grad * up * (sigma + swish * (1.0 - sigma))).astype(jnp.bfloat16)
        out_ref[:, p * 256 + 128 : (p + 1) * 256] = (grad * swish).astype(jnp.bfloat16)


def ffn_bwd(grad, weight, gu):
    rows, width = grad.shape
    wide = gu.shape[1]
    return pl.pallas_call(
        ffn_bwd_kernel,
        grid=(pl.cdiv(wide, 512),),
        in_specs=[
            pl.BlockSpec((rows, width), lambda j: (0, 0)),
            pl.BlockSpec((width, 256), lambda j: (0, j)),
            pl.BlockSpec((rows, 512), lambda j: (0, j)),
        ],
        out_specs=pl.BlockSpec((rows, 512), lambda j: (0, j)),
        out_shape=jax.ShapeDtypeStruct((rows, wide), jnp.bfloat16),
        compiler_params=pltpu.CompilerParams(dimension_semantics=("arbitrary",), vmem_limit_bytes=LIMIT),
        cost_estimate=pl.CostEstimate(flops=10**9, bytes_accessed=1 << 20, transcendentals=0),
        name="ffn_bwd",
    )(grad, weight, gu)


def after(values, *earlier):
    return lax.optimization_barrier((values, earlier))[0]


def turn(array, head_pos):
    blocks = array.reshape((BLOCKS, array.shape[0] // BLOCKS) + array.shape[1:])
    picked = [lax.dynamic_index_in_dim(blocks, head_pos ^ k, 0, keepdims=False) for k in range(BLOCKS)]
    return jnp.concatenate(picked, axis=0)


def rms_scale(values):
    return lax.rsqrt(jnp.mean(values * values, axis=-1, keepdims=True) + EPSILON)


def on_device(seq_count, tokens, cotangent, counts, pads, norm1_gain, w_query, w_key, w_value, w_gate_out,
              w_forget, forget_bias, out_gain, w_out, norm2_gain, w_gate, w_up, w_down):
    f32, b16 = jnp.float32, jnp.bfloat16
    rows, model_width = tokens.shape[1:]
    head_pos = lax.axis_index("head")
    head_arr = head_pos.reshape(1).astype(jnp.int32)
    width, slots, hidden_width = w_query.shape[1], w_forget.shape[1], w_gate.shape[1]
    share = w_query.shape[0]
    extra = slots
    size = rows // BLOCKS

    small = jnp.concatenate([out_gain, forget_bias])
    small = jnp.pad(small, (0, share - small.shape[0]))
    columns = jnp.stack([norm1_gain, norm2_gain, small], axis=1)
    columns = jnp.pad(columns, ((0, 0), (0, extra - 3)))
    wide = 4 * width
    narrow = jnp.concatenate([w_forget, columns], axis=1)
    own_mix = jnp.concatenate([w_out.T, w_query, w_key, w_value, w_gate_out, narrow], axis=1)
    mix = lax.all_gather(own_mix, "seq", axis=0, tiled=True)
    own_gu = jnp.stack([w_gate.reshape(share, -1, 128), w_up.reshape(share, -1, 128)], axis=2).reshape(share, -1)
    gu_weight = lax.all_gather(own_gu, "seq", axis=0, tiled=True)
    down_weight = lax.all_gather(w_down.T, "seq", axis=0, tiled=True)

    skip = width
    f_at, extra_at = skip + wide, skip + wide + slots
    gains = mix[:, extra_at : extra_at + 3].astype(f32)
    gain_one, gain_two = gains[:, 0], gains[:, 1]
    small_all = gains[:, 2].reshape(seq_count, share)
    n_gain, n_bias = out_gain.shape[0], forget_bias.shape[0]
    gain_head = small_all[:, :n_gain].reshape(1, width)
    bias = small_all[:, n_gain : n_gain + n_bias].reshape(slots, 1)

    x_rel = turn(tokens[0], head_pos)
    cot_rel = turn(cotangent[0], head_pos)
    block_of = jnp.arange(BLOCKS, dtype=jnp.int32) ^ head_pos
    position = (block_of[:, None] * size + jnp.arange(size, dtype=jnp.int32)[None, :]).reshape(rows, 1)
    live_len = jnp.where(counts[0] > 0, rows - pads[0], 0)
    live = (position < live_len).astype(f32)
    live_own = live[:size]

    x_f = x_rel.astype(f32)
    scale_one = rms_scale(x_f)
    normed1 = lax.optimization_barrier((x_f * scale_one * gain_one).astype(b16))
    grad_ffn = (cot_rel.astype(f32) * live).astype(b16)
    qkvg = mm(normed1, mix[:, skip:f_at], NN).astype(b16)
    forget_t = lax.dot_general(
        mix[:, f_at:extra_at], normed1, (((0,), (1,)), ((), ())), preferred_element_type=f32
    ) + bias
    log_keep = jax.nn.log_sigmoid(forget_t) / DAMPING
    keep_in = -jnp.expm1(log_keep)
    gated, mixed, probs, kst, vst = rec_fwd(head_arr, qkvg, log_keep, keep_in, gain_head)

    row_one, row_two = gain_one[None], gain_two[None]
    x_own = x_rel[:size]
    cot_own = cot_rel[:size]
    tall = lambda kind: jax.ShapeDtypeStruct((size, model_width), kind)
    line = jax.ShapeDtypeStruct((1, model_width), f32)
    seq_pos = lax.axis_index("seq")
    residual, normed_own, x_squares, mix_squares = head_scatter(
        gated, mix, [x_own], [row_two, live_own], [tall(f32), tall(b16), line, line], finish_mixer, 0
    )
    normed2, normed2_t, normed1_t = head_gather(normed_own, 1, also=normed1)
    gu, hidden = ffn_fwd(normed2.reshape(rows, model_width), gu_weight)

    grad_down = mm(grad_ffn, hidden, TN).astype(b16).reshape(-1, 2, share, hidden_width)
    core = seq_pos % 2
    kept = lax.dynamic_index_in_dim(grad_down, core, 1, keepdims=False)
    given = lax.dynamic_index_in_dim(grad_down, 1 - core, 1, keepdims=False)
    given = lax.ppermute(given, "seq", [(i, i ^ 1) for i in range(seq_count)])
    grad_down = (kept.astype(f32) + given.astype(f32)).astype(b16).reshape(-1, hidden_width)
    down_weight = after(down_weight, grad_down)
    lines = [list(range(c, seq_count, 2)) for c in range(2)]

    def line_scatter(array):
        return lax.psum_scatter(array, "seq", scatter_dimension=0, tiled=True, axis_index_groups=lines)

    grad_down = line_scatter(grad_down)
    grad_gu = ffn_bwd(grad_ffn, down_weight, gu)
    high = model_width // 2
    grad_residual, grad_low, grad_gain_two, grad_gu_w = head_scatter(
        grad_gu, gu_weight, [normed2_t, residual, cot_own], [live_own, row_two], [tall(f32), tall(b16), line],
        finish_norm_two, 2, filler=fill_gu, filled=[jax.ShapeDtypeStruct((high, gu_weight.shape[1]), b16)],
        scratch=tile_scratch(model_width, gu_weight.shape[1], share, 0),
    )
    grad_gu_w = line_scatter(grad_gu_w)
    grad_att_t, grad_gated = head_gather(grad_low, 3, keep=False, weight=mix, width=width)
    grad_gated = after(grad_gated, grad_down)
    grad_in, grad_gain_head, grad_bias = rec_bwd(
        head_arr, qkvg, log_keep, keep_in, forget_t, gain_head, mixed, probs, kst, vst, grad_gated
    )
    out_own, ffn_squares, grad_mix = head_scatter(
        hidden, down_weight, [grad_att_t, gated, normed1_t, grad_in, residual], [live_own],
        [tall(b16), line], finish_ffn, 4,
        filler=fill_mix, filled=[jax.ShapeDtypeStruct((high, mix.shape[1]), b16)],
        scratch=tile_scratch(model_width, mix.shape[1], share, 1),
    )
    grad_mix = line_scatter(grad_mix)
    live_row = jnp.full((1, model_width), jnp.sum(live_own) / model_width)
    own_row = jnp.concatenate([grad_gain_head.reshape(seq_count, n_gain), grad_bias.reshape(seq_count, n_bias)], axis=1)
    own_row = jnp.pad(own_row, ((0, 0), (0, share - n_gain - n_bias))).reshape(1, model_width)
    nothing = jnp.zeros((1, model_width), f32)
    small = jnp.concatenate(
        [nothing, grad_gain_two, x_squares, mix_squares, ffn_squares, live_row, nothing, own_row], axis=0
    )
    hops = 2 + seq_count.bit_length() - 1
    outputs, input_grad, small = tail_stage(
        hops, skip, grad_in, mix, x_rel, grad_residual, out_own, scale_one, row_one, small, 6
    )
    outputs = outputs.reshape(rows, model_width)
    input_grad = input_grad.reshape(rows, model_width).astype(f32)

    done = grad_mix.astype(f32)
    sums = jnp.sum(small[2:6], axis=1)
    rms_stats = jnp.sqrt(sums[:3] / (sums[3] * model_width))
    own = lax.dynamic_slice(small, (0, seq_pos * share), (SMALL, share))
    grad_gu_w = grad_gu_w.astype(f32)
    return (
        outputs[None],
        input_grad[None],
        own[0],
        done[:, skip : skip + width],
        done[:, skip + width : skip + 2 * width],
        done[:, skip + 2 * width : skip + 3 * width],
        done[:, skip + 3 * width : f_at],
        done[:, f_at:extra_at],
        own[SMALL - 1, n_gain : n_gain + n_bias],
        own[SMALL - 1, :n_gain],
        done[:, :width].T,
        own[1],
        grad_gu_w[:, :hidden_width],
        grad_gu_w[:, hidden_width:],
        grad_down.astype(f32).T,
        rms_stats,
    )


def solution(mesh):
    both = P("seq", "head")
    flat = P(("head", "seq"))
    rows = P("seq", None, None)
    return jax.shard_map(
        functools.partial(on_device, mesh.shape["seq"]),
        mesh=mesh,
        in_specs=(rows, rows, P("seq"), P("seq"), P("seq"), both, both, both, both, both, flat, flat,
                  P("head", "seq"), P("seq"), both, both, P("head", "seq")),
        out_specs=(rows, rows, P("seq"), both, both, both, both, both, flat, flat, P("head", "seq"), P("seq"),
                   both, both, P("head", "seq"), P()),
        check_vma=False,
    )
```

```python
import functools

import jax
import jax.numpy as jnp
import numpy as np
from jax import lax
from jax.experimental import pallas as pl
from jax.experimental.pallas import tpu as pltpu
from jax.sharding import PartitionSpec as P

EPSILON = 1e-06
DAMPING = 8.0
TILE = 128
BLOCKS = 4
HALVES = (64, 32, 16, 8, 4, 2, 1)
NT = (((1,), (1,)), ((), ()))
NN = (((1,), (0,)), ((), ()))
TN = (((0,), (0,)), ((), ()))


def rel_tile(rows, i, h):
    per = rows // BLOCKS // TILE
    return (i // per ^ h[0]) * per + i % per


def mm(left, right, dims):
    return lax.dot_general(left, right, dims, preferred_element_type=jnp.float32)


def span_matrix():
    r = np.arange(TILE)[:, None]
    t = np.arange(TILE)[None, :]
    parts = []
    for h in HALVES:
        base = t // (2 * h) * (2 * h)
        upper = t % (2 * h) >= h
        parts.append(upper & (r >= base + h) & (r <= t))
        parts.append(~upper & (r > t) & (r <= base + h - 1))
    parts.append(r <= t)
    parts.append(r > t)
    return np.concatenate(parts, axis=1).astype(np.float32)


def level_of():
    s = lax.broadcasted_iota(jnp.int32, (TILE, TILE), 0)
    t = lax.broadcasted_iota(jnp.int32, (TILE, TILE), 1)
    return jnp.where(s < t, s ^ t, jnp.where(s == t, 0, -1))


def level_masks():
    x = level_of()
    masks = [(x >= h) & (x < 2 * h) for h in HALVES]
    masks.append(x == 0)
    return masks


def decays(log_keep, keep_in, spans):
    slots = log_keep.shape[0]
    high = log_keep.astype(jnp.bfloat16)
    rest = log_keep - high.astype(jnp.float32)
    mid = rest.astype(jnp.bfloat16)
    both = mm(jnp.concatenate([high, mid], axis=0), spans, NN)
    grown = jnp.exp(both[:slots] + both[slots:])
    n = len(HALVES)
    ones = jnp.ones_like(keep_in)
    e_parts = [grown[:, (2 * i) * TILE : (2 * i + 1) * TILE] for i in range(n)] + [ones]
    f_bare = [grown[:, (2 * i + 1) * TILE : (2 * i + 2) * TILE] for i in range(n)] + [ones]
    e_all = grown[:, 2 * n * TILE : (2 * n + 1) * TILE]
    f_all = grown[:, (2 * n + 1) * TILE : (2 * n + 2) * TILE]
    total = e_all[:, TILE - 1 : TILE]
    return e_parts, f_bare, e_all, f_all, total


def norm_gate(mixed, gain, gate_pre):
    scale = lax.rsqrt(jnp.mean(mixed * mixed, axis=-1, keepdims=True) + EPSILON)
    unit = mixed * scale
    return scale, unit


def fwd_kernel(h_ref, q_ref, k_ref, v_ref, g_ref, lk_ref, w_ref, gain_ref, spans_ref,
               gated_ref, mixed_ref, probs_ref, kst_ref, vst_ref, kacc, vacc):
    @pl.when(pl.program_id(0) == 0)
    def _():
        kacc[...] = jnp.zeros_like(kacc)
        vacc[...] = jnp.zeros_like(vacc)
    width = q_ref.shape[1]
    root = width ** -0.5
    q, k, v = q_ref[...], k_ref[...], v_ref[...]
    keep_in = w_ref[...]
    e_parts, f_bare, e_all, f_all, total = decays(lk_ref[...], keep_in, spans_ref[...])
    masks = level_masks()
    kst, vst = kacc[...], vacc[...]
    kst_b, vst_b = kst.astype(jnp.bfloat16), vst.astype(jnp.bfloat16)
    kst_ref[0] = kst_b
    vst_ref[0] = vst_b
    inner = mm(k, q, NT) * root
    inner_b = inner.astype(jnp.bfloat16)
    zero_b = jnp.zeros_like(inner_b)
    f_parts = [(bare * keep_in).astype(jnp.bfloat16) for bare in f_bare]
    scores = e_all * (mm(kst_b, q, NT) * root)
    for mask, grow, fade in zip(masks, e_parts, f_parts):
        scores += grow * mm(fade, jnp.where(mask, inner_b, zero_b), NN)
    top = jnp.max(scores, axis=0, keepdims=True)
    raised = jnp.exp(scores - top)
    probs = raised / jnp.sum(raised, axis=0, keepdims=True)
    probs_ref[...] = probs
    mixing = jnp.zeros((TILE, TILE), jnp.float32)
    for mask, grow, fade in zip(masks, e_parts, f_parts):
        mixing = jnp.where(mask, mm(fade, (probs * grow).astype(jnp.bfloat16), TN), mixing)
    mixed = mm(mixing.astype(jnp.bfloat16), v, TN) + mm((probs * e_all).astype(jnp.bfloat16), vst_b, TN)
    tail = (f_all * keep_in).astype(jnp.bfloat16)
    kacc[...] = total * kst + mm(tail, k, NN)
    vacc[...] = total * vst + mm(tail, v, NN)
    mixed_ref[...] = mixed
    scale = lax.rsqrt(jnp.mean(mixed * mixed, axis=-1, keepdims=True) + EPSILON)
    gate = g_ref[...].astype(jnp.float32)
    swish = gate * jax.nn.sigmoid(gate)
    gated_ref[...] = (mixed * scale * gain_ref[...] * swish).astype(jnp.bfloat16)


def rec_fwd(head, qkvg, log_keep_t, keep_in_t, gain):
    rows, wide = qkvg.shape
    width = wide // 4
    slots = log_keep_t.shape[0]
    tiles = rows // TILE
    spans = jnp.asarray(span_matrix(), jnp.bfloat16)
    place = functools.partial(rel_tile, rows)
    col = lambda j: pl.BlockSpec((TILE, width), lambda i, h: (place(i, h), j))
    lane = pl.BlockSpec((slots, TILE), lambda i, h: (0, place(i, h)))
    state = pl.BlockSpec((1, slots, width), lambda i, h: (i, 0, 0))
    return pl.pallas_call(
        fwd_kernel,
        grid_spec=pltpu.PrefetchScalarGridSpec(
            num_scalar_prefetch=1,
            grid=(tiles,),
            in_specs=[col(0), col(1), col(2), col(3), lane, lane,
                      pl.BlockSpec((1, width), lambda i, h: (0, 0)),
                      pl.BlockSpec(spans.shape, lambda i, h: (0, 0))],
            out_specs=[col(0), col(0), lane, state, state],
            scratch_shapes=[pltpu.VMEM((slots, width), jnp.float32)] * 2,
        ),
        out_shape=[
            jax.ShapeDtypeStruct((rows, width), jnp.bfloat16),
            jax.ShapeDtypeStruct((rows, width), jnp.float32),
            jax.ShapeDtypeStruct((slots, rows), jnp.float32),
            jax.ShapeDtypeStruct((tiles, slots, width), jnp.bfloat16),
            jax.ShapeDtypeStruct((tiles, slots, width), jnp.bfloat16),
        ],
        compiler_params=pltpu.CompilerParams(dimension_semantics=("arbitrary",), vmem_limit_bytes=60 << 20),
        cost_estimate=pl.CostEstimate(flops=5 * 10**9, bytes_accessed=10 << 20, transcendentals=0),
        name="slot_fwd",
    )(head, qkvg, qkvg, qkvg, qkvg, log_keep_t, keep_in_t, gain, spans)


def bwd_tile(step, q_ref, k_ref, v_ref, g_ref, lk_ref, w_ref, fpre_ref, gain_ref, spans_ref,
               mixed_ref, probs_ref, kst_ref, vst_ref, dg_ref,
               dproj_ref, dgain_ref, dbias_ref, dk_acc, dv_acc, cross):
    width = q_ref.shape[1]
    slots = lk_ref.shape[0]

    @pl.when(step == 0)
    def _():
        dk_acc[...] = jnp.zeros_like(dk_acc)
        dv_acc[...] = jnp.zeros_like(dv_acc)
        cross[...] = jnp.zeros_like(cross)
        dgain_ref[...] = jnp.zeros_like(dgain_ref)
        dbias_ref[...] = jnp.zeros_like(dbias_ref)
    root = width ** -0.5
    q, k, v = q_ref[...], k_ref[...], v_ref[...]
    mixed = mixed_ref[...]
    gate = g_ref[...].astype(jnp.float32)
    gain = gain_ref[...]
    d_gated = dg_ref[...].astype(jnp.float32)
    scale = lax.rsqrt(jnp.mean(mixed * mixed, axis=-1, keepdims=True) + EPSILON)
    unit = mixed * scale
    sigma = jax.nn.sigmoid(gate)
    swish = gate * sigma
    slope = sigma * (1.0 + gate * (1.0 - sigma))
    dproj_ref[:, 3 * width : 4 * width] = (d_gated * unit * gain * slope).astype(jnp.bfloat16)
    d_normed = d_gated * swish
    dgain_ref[...] += jnp.sum(d_normed * unit, axis=0, keepdims=True)
    c = d_normed * gain
    d_mixed = scale * (c - unit * jnp.mean(c * unit, axis=-1, keepdims=True))
    d_out = d_mixed.astype(jnp.bfloat16)

    log_keep, keep_in = lk_ref[...], w_ref[...]
    e_parts, f_bare, e_all, f_all, total = decays(log_keep, keep_in, spans_ref[...])
    masks = level_masks()
    probs = probs_ref[...]
    kst, vst = kst_ref[0], vst_ref[0]
    dkst, dvst = dk_acc[...], dv_acc[...]
    dkst_b, dvst_b = dkst.astype(jnp.bfloat16), dvst.astype(jnp.bfloat16)

    inner_b = (mm(k, q, NT) * root).astype(jnp.bfloat16)
    d_mixing_b = mm(v, d_out, NT).astype(jnp.bfloat16)
    pair = jnp.concatenate([inner_b, d_mixing_b], axis=1)
    zero_b = jnp.zeros_like(pair)
    masks2 = [jnp.concatenate([mask, mask], axis=1) for mask in masks]
    pairs = [jnp.where(mask, pair, zero_b) for mask in masks2]
    f_parts = [(bare * keep_in).astype(jnp.bfloat16) for bare in f_bare]
    both = [mm(fade, two, NN) for fade, two in zip(f_parts, pairs)]
    s_state = mm(kst, q, NT) * root
    p_state = mm(vst, d_out, NT)
    d_probs = e_all * p_state
    for grow, two in zip(e_parts, both):
        d_probs += grow * two[:, TILE:]
    d_scores = probs * (d_probs - jnp.sum(probs * d_probs, axis=0, keepdims=True))

    xy_all = jnp.concatenate([d_scores * e_all, probs * e_all], axis=1).astype(jnp.bfloat16)
    xy_parts = [jnp.concatenate([d_scores * grow, probs * grow], axis=1).astype(jnp.bfloat16) for grow in e_parts]
    x0 = xy_all[:, :TILE]
    y0 = xy_all[:, TILE:]
    change = x0.astype(jnp.float32) * s_state + y0.astype(jnp.float32) * p_state
    into = jnp.zeros((slots, TILE), jnp.float32)
    d_both = jnp.zeros((TILE, 2 * TILE), jnp.float32)
    for i, (grow, bare, fade, two, xy, part, mask) in enumerate(
        zip(e_parts, f_bare, f_parts, both, xy_parts, pairs, masks2)
    ):
        z = mm(xy, part, NT)
        into += bare * z
        if i < len(HALVES):
            mass = xy.astype(jnp.float32) * two
            change += mass[:, :TILE] + mass[:, TILE:] - fade.astype(jnp.float32) * z
        d_both = jnp.where(mask, mm(fade, xy, TN), d_both)
    d_both_b = d_both.astype(jnp.bfloat16)
    d_inner, mixing = d_both_b[:, :TILE], d_both_b[:, TILE:]
    tail = (f_all * keep_in).astype(jnp.bfloat16)
    z_state = mm(dkst_b, k, NT) + mm(dvst_b, v, NT)
    into += f_all * z_state
    change -= tail.astype(jnp.float32) * z_state

    dproj_ref[:, :width] = (root * (mm(d_inner, k, TN) + mm(x0, kst, TN))).astype(jnp.bfloat16)
    dproj_ref[:, width : 2 * width] = (root * mm(d_inner, q, NN) + mm(tail, dkst_b, TN)).astype(jnp.bfloat16)
    dproj_ref[:, 2 * width : 3 * width] = (mm(mixing, d_out, NN) + mm(tail, dvst_b, TN)).astype(jnp.bfloat16)

    later = (lax.broadcasted_iota(jnp.int32, (TILE, TILE), 0) >= lax.broadcasted_iota(jnp.int32, (TILE, TILE), 1)).astype(jnp.bfloat16)
    high = change.astype(jnp.bfloat16)
    rest = change - high.astype(jnp.float32)
    mid = rest.astype(jnp.bfloat16)
    low = (rest - mid.astype(jnp.float32)).astype(jnp.bfloat16)
    sums = mm(jnp.concatenate([high, mid, low], axis=0), later, NN)
    d_log_keep = sums[:slots] + sums[slots : 2 * slots] + sums[2 * slots :] + cross[...] - jnp.exp(log_keep) * into
    d_forget = (d_log_keep * jax.nn.sigmoid(-fpre_ref[...]) / DAMPING).astype(jnp.bfloat16)
    dbias_ref[...] += jnp.sum(d_forget.astype(jnp.float32), axis=1, keepdims=True)
    turned = jnp.transpose(d_forget.astype(jnp.float32))
    dproj_ref[:, 4 * width :] = jnp.concatenate([turned, jnp.zeros_like(turned)], axis=1).astype(jnp.bfloat16)

    dkst_new = total * dkst + root * mm(x0, q, NN)
    dvst_new = total * dvst + mm(y0, d_out, NN)
    dk_acc[...] = dkst_new
    dv_acc[...] = dvst_new
    cross[...] = jnp.sum(kst.astype(jnp.float32) * dkst_new + vst.astype(jnp.float32) * dvst_new, axis=1, keepdims=True)


MESH = pl.DeviceIdType.MESH
CHUNK = 32


def neighbours():
    head = lax.axis_index("head")
    return {"head": head + 1 - 2 * (head % 2)}, {"head": (head + 2) % BLOCKS}


def flipped(index, bit):
    return index + bit - 2 * bit * (index // bit % 2)


def other_core():
    return {"seq": flipped(lax.axis_index("seq"), 1)}


def greet(targets):
    barrier = pltpu.get_barrier_semaphore()
    for target in targets:
        pl.semaphore_signal(barrier, inc=1, device_id=target, device_id_type=MESH)
    pl.semaphore_wait(barrier, len(targets))


LIMIT = 60 << 20
FAR = pl.BlockSpec(memory_space=pl.ANY)
WHOLE = pl.BlockSpec(memory_space=pltpu.VMEM)


class Loads:
    def __init__(self, sem):
        self.sem, self.copies = sem, []

    def add(self, src, dst):
        copy = pltpu.make_async_copy(src, dst, self.sem.at[len(self.copies)])
        copy.start()
        self.copies.append(copy)
        return copy


class Scatter:
    order = (0, 2, 1, 3)

    def __init__(self, left, right, acc, mid, send, got, send_sem, got_sem):
        self.left, self.right, self.acc, self.mid, self.send, self.got = left, right, acc, mid, send, got
        self.size, self.cols = send.shape[1:]
        to_x, to_y = neighbours()
        self.copies = []
        for u in range(2):
            for k, to in enumerate((to_x, to_x, to_y, to_y, to_y, to_x)):
                slot = 6 * u + k
                self.copies.append(
                    pltpu.make_async_remote_copy(
                        src_ref=send.at[slot], dst_ref=got.at[slot], send_sem=send_sem.at[slot],
                        recv_sem=got_sem.at[slot], device_id=to, device_id_type=MESH,
                    )
                )

    def first(self, loads, watch=None):
        size, cols = self.size, self.cols
        for part, load in zip(self.order, loads):
            load.wait()
            value = mm(self.left[...], self.right[part * cols : (part + 1) * cols, :], NT)
            side_at, u = part // 2, part % 2
            here = slice(part * cols, (part + 1) * cols)
            slot = 6 * u + 2 * side_at
            near_block, mid_block = (1, 2) if side_at == 0 else (2, 1)
            self.acc[:, here] = value[:size]
            self.mid[:, here] = value[mid_block * size : (mid_block + 1) * size]
            self.send[slot] = value[3 * size :].astype(jnp.bfloat16)
            self.copies[slot].start()
            self.send[slot + 1] = value[near_block * size : (near_block + 1) * size].astype(jnp.bfloat16)
            self.copies[slot + 1].start()
            if watch is not None:
                watch(here, value)

    def second(self, u):
        cols = self.cols
        for side_at in range(2):
            part = 2 * side_at + u
            first, second = 6 * u + 2 * side_at, 6 * u + 4 + side_at
            here = slice(part * cols, (part + 1) * cols)
            self.copies[first].wait_recv()
            self.send[second] = (self.mid[:, here] + self.got[first].astype(jnp.float32)).astype(jnp.bfloat16)
            self.copies[second].start()

    def last(self, finish):
        for u in range(2):
            for k in (1, 3, 4, 5):
                self.copies[6 * u + k].wait_recv()
        cols = self.cols

        def rows(i, carry):
            here = pl.ds(pl.multiple_of(i * CHUNK, CHUNK), CHUNK)
            sums = []
            for part in range(4):
                side_at, u = part // 2, part % 2
                one, two = self.got[6 * u + 2 * side_at + 1, here, :], self.got[6 * u + 4 + side_at, here, :]
                own = self.acc[here, part * cols : (part + 1) * cols]
                sums.append(own + one.astype(jnp.float32) + two.astype(jnp.float32))
            finish(here, jnp.concatenate(sums, axis=1), i)
            return carry

        lax.fori_loop(0, self.size // CHUNK, rows, 0)

    def close(self):
        for one in self.copies:
            one.wait_send()


def scatter_scratch(rows, depth, high):
    size, cols = rows // BLOCKS, high // 4
    return [
        pltpu.VMEM((rows, depth), jnp.bfloat16),
        pltpu.VMEM((high, depth), jnp.bfloat16),
        pltpu.VMEM((size, high), jnp.float32),
        pltpu.VMEM((size, high), jnp.float32),
        pltpu.VMEM((12, size, cols), jnp.bfloat16),
        pltpu.VMEM((12, size, cols), jnp.bfloat16),
        pltpu.SemaphoreType.DMA((12,)),
        pltpu.SemaphoreType.DMA((12,)),
    ]


def load_parts(loads, right_far, right, skip):
    cols = right.shape[0] // 4
    parts = []
    for part in Scatter.order:
        here = pl.ds(part * cols, cols)
        parts.append(loads.add(right_far.at[here, pl.ds(skip, right.shape[1])], right.at[here, :]))
    return parts


def scatter_kernel(plan, *refs):
    n_far, n_near, n_out, skip, finish, filler = plan
    left_far, right_far, *more_far = refs[:n_far]
    near = refs[n_far : n_far + n_near]
    outs = refs[n_far + n_near : n_far + n_near + n_out]
    load_sem, *rest = refs[n_far + n_near + n_out :]
    scatter, spare = rest[:8], rest[8:]
    left, right = scatter[:2]
    loads = Loads(load_sem)
    load_left = loads.add(left_far, left)
    parts = load_parts(loads, right_far, right, skip)
    more = [(loads.add(src, dst), dst) for src, dst in zip(more_far, spare)]
    spare = spare[len(more_far) :]
    greet(neighbours() if filler is None else (*neighbours(), other_core()))
    sum_heads = Scatter(*scatter)
    load_left.wait()
    sum_heads.first(parts)
    sum_heads.second(0)
    for load, _ in more:
        load.wait()
    side = [dst for _, dst in more]
    if filler is not None:
        steps = filler(left, right, side, outs, spare)
        next(steps)
        sum_heads.second(1)
        for _ in steps:
            pass
    else:
        sum_heads.second(1)
    sum_heads.last(lambda here, total, i: finish(here, total, side, near, outs, i))
    sum_heads.close()


def head_scatter(left, right, far, near, out_shapes, finish, number, filler=None, filled=(), scratch=()):
    rows, depth = left.shape
    plan = (2 + len(far), len(near), len(out_shapes) + len(filled), 0, finish, filler)
    return pl.pallas_call(
        functools.partial(scatter_kernel, plan),
        in_specs=[FAR] * (2 + len(far)) + [WHOLE] * len(near),
        out_specs=[WHOLE] * len(out_shapes) + [FAR] * len(filled),
        out_shape=[*out_shapes, *filled],
        scratch_shapes=[
            pltpu.SemaphoreType.DMA((5 + len(far),)),
            *scatter_scratch(rows, depth, right.shape[0]),
            *[pltpu.VMEM(one.shape, one.dtype) for one in far],
            *scratch,
        ],
        compiler_params=pltpu.CompilerParams(collective_id=number, has_side_effects=True, vmem_limit_bytes=LIMIT),
        cost_estimate=pl.CostEstimate(flops=10**9, bytes_accessed=1 << 20, transcendentals=0),
        name="head_scatter%d" % number,
    )(left, right, *far, *near)


STEP = 512


def weight_tiles(pairs, place, out_ref, room, land, store_sem, send_sem, got_sem, pause=None):
    count, share = land.shape[:2]
    high = 2 * count * share
    core = lax.axis_index("seq") % 2
    per = STEP // (2 * share)

    def row(p, at):
        return (2 * p + at) * share % room.shape[0]

    def swap_shard(p):
        return pltpu.make_async_remote_copy(
            src_ref=room.at[pl.ds(row(p, 0) + (1 - core) * share, share), :], dst_ref=land.at[p],
            send_sem=send_sem.at[p], recv_sem=got_sem.at[p], device_id=other_core(), device_id_type=MESH,
        )

    def store(p):
        return pltpu.make_async_copy(land.at[p], out_ref.at[pl.ds(p * share, share), :], store_sem.at[p])

    def settle(p):
        swap_shard(p).wait_recv()
        own = room[pl.ds(pl.multiple_of(row(p, 0) + core * share, share), share), :]
        land[p] = (own.astype(jnp.float32) + land[p].astype(jnp.float32)).astype(jnp.bfloat16)
        store(p).start()

    sent = []
    for i in range(high // STEP):
        here = slice(i * STEP, (i + 1) * STEP)
        there = slice(i * STEP % room.shape[0], i * STEP % room.shape[0] + STEP)
        if (i + 1) * STEP > room.shape[0]:
            for p in range((i - 2) * per, (i - 1) * per):
                swap_shard(p).wait_send()
                sent.append(p)
        for turned, right, column in pairs:
            for at in range(0, right.shape[1], STEP):
                cols = min(STEP, right.shape[1] - at)
                value = mm(turned[here, :], right[:, at : at + cols], NN).astype(jnp.bfloat16)
                for src, dst, wide in place(column + at, cols):
                    room[there, dst : dst + wide] = value[:, src : src + wide]
        for p in range(i * per, (i + 1) * per):
            swap_shard(p).start()
        if i:
            for p in range((i - 1) * per, i * per):
                settle(p)
        if i == pause:
            yield
    for p in range(count - per, count):
        settle(p)
    for p in range(count):
        store(p).wait()
        if p not in sent:
            swap_shard(p).wait_send()


def tile_scratch(high, width, share, room):
    count = high // (2 * share)
    return [pltpu.VMEM((2 * STEP, width), jnp.bfloat16)] * room + [
        pltpu.VMEM((count, share, width), jnp.bfloat16),
        pltpu.SemaphoreType.DMA((count,)),
        pltpu.SemaphoreType.DMA((count,)),
        pltpu.SemaphoreType.DMA((count,)),
    ]


def fill_gu(left, right, side, outs, spare):
    half = left.shape[1] // 2

    def place(at, cols):
        return [(k, (at + k) // 256 * 128 + (at + k) // 128 % 2 * half, 128) for k in range(0, cols, 128)]

    return weight_tiles([(side[0], left, 0)], place, outs[-1], right, *spare, pause=1)


def mixed_index(block):
    head = lax.axis_index("head")
    return (block + head) % 2 + 2 * ((block // 2 + head // 2) % 2)


def fill_mix(left, right, side, outs, spare):
    qkvg, d_gated, mixed, probs, kst, vst, log_keep, keep_in, forget, spans, gain, _, att_t, gated, normed_t = side
    grad_far, gain_grad, bias_grad, out_ref = outs[-2], outs[2], outs[3], outs[-1]
    grad_in, grad_sem, dk_acc, dv_acc, cross, *spare = spare
    width = gated.shape[1]
    tiles = qkvg.shape[0] // TILE
    per = tiles // BLOCKS

    def tile(i, carry):
        at = tiles - 1 - i
        rel = mixed_index(at // per) * per + at % per
        rows = pl.ds(pl.multiple_of(rel * TILE, TILE), TILE)
        bwd_tile(
            i, *[qkvg.at[rows, pl.ds(k * width, width)] for k in range(4)], log_keep.at[:, rows], keep_in.at[:, rows],
            forget.at[:, rows], gain, spans, mixed.at[rows, :], probs.at[:, rows], kst.at[pl.ds(at, 1)],
            vst.at[pl.ds(at, 1)], d_gated.at[rows, :], grad_in.at[rows, :], gain_grad, bias_grad, dk_acc, dv_acc, cross,
        )
        return carry

    lax.fori_loop(0, tiles, tile, 0)
    keep = pltpu.make_async_copy(grad_in, grad_far, grad_sem.at[0])
    keep.start()
    yield
    place = lambda at, cols: [(0, at, cols)]
    yield from weight_tiles([(att_t, gated, 0), (normed_t, grad_in, width)], place, out_ref, *spare)
    keep.wait()


class Gather:
    def __init__(self, own, blocks, send_sem, got_sem):
        half = own.shape[1] // 2
        to_x, to_y = neighbours()

        def copy(slot, src, block, side_at, target):
            here = pl.ds(side_at * half, half)
            return pltpu.make_async_remote_copy(
                src_ref=src.at[:, here], dst_ref=blocks.at[block, :, here],
                send_sem=send_sem.at[slot], recv_sem=got_sem.at[slot], device_id=target, device_id_type=MESH,
            )

        self.copies = [
            copy(0, own, 1, 0, to_x),
            copy(1, own, 2, 1, to_y),
            copy(2, own, 1, 1, to_x),
            copy(3, own, 2, 0, to_y),
            copy(4, blocks.at[1], 3, 0, to_y),
            copy(5, blocks.at[2], 3, 1, to_x),
        ]

    def first(self):
        for one in self.copies[:4]:
            one.start()

    def second(self):
        for near, far in ((0, 4), (1, 5)):
            self.copies[near].wait_recv()
            self.copies[far].start()

    def last(self):
        for one in self.copies[2:]:
            one.wait_recv()
        for one in self.copies:
            one.wait_send()


def gather_kernel(plan, *refs):
    keep, product, also = plan
    refs = list(refs)
    own_ref = refs.pop(0)
    weight_far = refs.pop(0) if product else None
    also_far = refs.pop(0) if also else None
    out_ref = refs.pop(0) if keep else None
    turned_ref = refs.pop(0)
    product_ref = refs.pop(0) if product else None
    also_ref = refs.pop(0) if also else None
    blocks, turned_buf, send_sem, got_sem, out_sem, load_sem, *refs = refs
    size, half = own_ref.shape[0], own_ref.shape[1] // 2
    loads = Loads(load_sem)
    if product:
        weight = refs.pop(0)
        fetch = loads.add(weight_far.at[:, pl.ds(0, weight.shape[1])], weight)
    if also:
        also_buf, also_turned = refs
        fetch = loads.add(also_far, also_buf)
    greet(neighbours())
    gather = Gather(own_ref, blocks, send_sem, got_sem)
    gather.first()
    if product or also:
        fetch.wait()
    stores = []

    def store(src, dst):
        copy = pltpu.make_async_copy(src, dst, out_sem.at[len(stores)])
        copy.start()
        stores.append(copy)

    def use(block, side_at, src):
        here = slice(side_at * half, (side_at + 1) * half)
        rows = slice(block * size, (block + 1) * size)
        value = src[:, here]
        turned_buf[here, rows] = jnp.transpose(value)
        store(turned_buf.at[here, rows], turned_ref.at[here, rows])
        if keep:
            store(src.at[:, here], out_ref.at[block, :, here])
        if product:
            term = mm(value, weight[here, :], NN)
            if (block, side_at) in ((0, 0), (1, 0), (2, 1), (3, 0)):
                product_ref[rows, :] = term
            else:
                product_ref[rows, :] += term

    use(0, 0, own_ref)
    use(0, 1, own_ref)
    if also:
        also_turned[...] = jnp.transpose(also_buf[: also_buf.shape[0] // 2, :])
        middle = also_buf.shape[0] // 2
        store(also_turned, also_ref.at[:, pl.ds(0, middle)])
    gather.second()
    use(1, 0, blocks.at[1])
    use(2, 1, blocks.at[2])
    if also:
        stores[-1 - 4 * keep - 2 * (not keep)].wait()
        finished = len(stores) - 1 - 4 * keep - 2 * (not keep)
        also_turned[...] = jnp.transpose(also_buf[middle:, :])
        store(also_turned, also_ref.at[:, pl.ds(middle, middle)])
    for slot, block, side_at in ((2, 1, 1), (3, 2, 0), (4, 3, 0), (5, 3, 1)):
        gather.copies[slot].wait_recv()
        use(block, side_at, blocks.at[block])
    for at, one in enumerate(stores):
        if not also or at != finished:
            one.wait()
    for one in gather.copies:
        one.wait_send()


def head_gather(own, number, keep=True, weight=None, width=0, also=None):
    size, wide = own.shape
    rows = BLOCKS * size
    product = weight is not None
    extra = [one for one in (weight, also) if one is not None]
    out_shape, out_specs = [], []
    if keep:
        out_shape.append(jax.ShapeDtypeStruct((BLOCKS, size, wide), own.dtype))
        out_specs.append(FAR)
    out_shape.append(jax.ShapeDtypeStruct((wide, rows), own.dtype))
    out_specs.append(FAR)
    scratch = [
        pltpu.VMEM((BLOCKS, size, wide), own.dtype),
        pltpu.VMEM((wide, rows), own.dtype),
        pltpu.SemaphoreType.DMA((6,)),
        pltpu.SemaphoreType.DMA((6,)),
        pltpu.SemaphoreType.DMA((20,)),
        pltpu.SemaphoreType.DMA((2,)),
    ]
    if product:
        out_shape.append(jax.ShapeDtypeStruct((rows, width), jnp.float32))
        out_specs.append(WHOLE)
        scratch.append(pltpu.VMEM((wide, width), own.dtype))
    if also is not None:
        out_shape.append(jax.ShapeDtypeStruct(also.shape[::-1], also.dtype))
        out_specs.append(FAR)
        scratch += [pltpu.VMEM(also.shape, also.dtype), pltpu.VMEM((also.shape[1], also.shape[0] // 2), also.dtype)]
    return pl.pallas_call(
        functools.partial(gather_kernel, (keep, product, also is not None)),
        in_specs=[WHOLE] + [FAR] * len(extra),
        out_specs=out_specs,
        out_shape=out_shape,
        scratch_shapes=scratch,
        compiler_params=pltpu.CompilerParams(collective_id=number, has_side_effects=True, vmem_limit_bytes=LIMIT),
        cost_estimate=pl.CostEstimate(flops=10**9, bytes_accessed=1 << 20, transcendentals=0),
        name="head_gather%d" % number,
    )(own, *extra)


def unit_of(values):
    scale = lax.rsqrt(jnp.mean(values * values, axis=-1, keepdims=True) + EPSILON)
    return scale, values * scale


def finish_mixer(here, total, side, near, outs, i):
    x = side[0][here, :].astype(jnp.float32)
    gain, live = near[0][...], near[1][here, :]
    residual = x + total
    outs[0][here, :] = residual
    outs[1][here, :] = (unit_of(residual)[1] * gain).astype(jnp.bfloat16)
    add_row(outs[2], jnp.sum(live * x * x, axis=0, keepdims=True), i)
    add_row(outs[3], jnp.sum(live * total * total, axis=0, keepdims=True), i)


def add_row(ref, row, i):
    @pl.when(i == 0)
    def _():
        ref[...] = jnp.zeros_like(ref)

    ref[...] += row


def norm_back(total, gain, scale, unit):
    c = total * gain
    return scale * (c - unit * jnp.mean(c * unit, axis=-1, keepdims=True))


def finish_norm_two(here, total, side, near, outs, i):
    residual, cot = side[1][here, :], side[2][here, :].astype(jnp.float32)
    live, gain = near[0][here, :], near[1][...]
    scale, unit = unit_of(residual)
    add_row(outs[2], jnp.sum(total * unit, axis=0, keepdims=True), i)
    grad = cot * live + norm_back(total, gain, scale, unit)
    outs[0][here, :] = grad
    outs[1][here, :] = grad.astype(jnp.bfloat16)


def finish_ffn(here, total, side, near, outs, i):
    live = near[0][here, :]
    add_row(outs[1], jnp.sum(live * total * total, axis=0, keepdims=True), i)
    outs[0][here, :] = (live * (side[11][here, :] + total)).astype(jnp.bfloat16)


SMALL = 8


def tail_kernel(skip, grad_far, mix_far, x_far, res_far, out_own, scale_ref, gain_ref, small_ref,
                outputs_far, input_far, total_ref, load_sem, store_sem, *rest):
    scatter = rest[:8]
    left, right = scatter[:2]
    x_buf, res_buf, gain_row, in_own, out_blocks, in_blocks, f_send, f_got, z_send, z_got, s_buf, s_send, s_got = rest[8:]
    loads = Loads(load_sem)
    load_left = loads.add(grad_far, left)
    parts = load_parts(loads, mix_far, right, skip)
    load_x = loads.add(x_far, x_buf)
    load_res = loads.add(res_far, res_buf)
    size = in_own.shape[0]
    seq = lax.axis_index("seq")
    hops = [*neighbours(), other_core()]
    bit = 2
    while bit < lax.axis_size("seq"):
        hops.append({"seq": flipped(seq, bit)})
        bit *= 2
    greet(hops)
    sum_heads = Scatter(*scatter)

    def watch(here, value):
        term = value * x_buf[:, here].astype(jnp.float32) * scale_ref[...]
        gain_row[:, here] = jnp.sum(term, axis=0, keepdims=True)

    f_gather = Gather(out_own, out_blocks, f_send, f_got)
    f_gather.first()
    load_left.wait()
    load_x.wait()
    sum_heads.first(parts, watch)
    sum_heads.second(0)
    sum_heads.second(1)

    is_last = lax.broadcasted_iota(jnp.int32, (SMALL, 1), 0) == SMALL - 1
    is_first = lax.broadcasted_iota(jnp.int32, (SMALL, 1), 0) == 0
    s_buf[0] = jnp.where(is_first, gain_row[...], small_ref[...])
    small = [
        pltpu.make_async_remote_copy(
            src_ref=s_buf.at[2 * k], dst_ref=s_buf.at[2 * k + 1], send_sem=s_send.at[k], recv_sem=s_got.at[k],
            device_id=hop, device_id_type=MESH,
        )
        for k, hop in enumerate(hops)
    ]

    def hop_done(k):
        small[k].wait_recv()
        arrived = s_buf[2 * k + 1]
        if k < 2:
            arrived = jnp.where(is_last, 0.0, arrived)
        if k + 1 < len(small):
            s_buf[2 * k + 2] = s_buf[2 * k] + arrived
            small[k + 1].start()
        else:
            total_ref[...] = s_buf[2 * k] + arrived

    small[0].start()
    load_res.wait()

    def finish(here, total, i):
        scale, unit = unit_of(x_buf[here, :].astype(jnp.float32))
        in_own[here, :] = (res_buf[here, :] + norm_back(total, gain_ref[...], scale, unit)).astype(jnp.bfloat16)

    f_gather.second()
    hop_done(0)
    sum_heads.last(finish)
    z_gather = Gather(in_own, in_blocks, z_send, z_got)
    z_gather.first()
    head = lax.axis_index("head")
    places = (head, flipped(head, 1), flipped(head, 2), BLOCKS - 1 - head)
    stores = []

    def store(src, far, k):
        copy = pltpu.make_async_copy(src, far.at[places[k]], store_sem.at[len(stores)])
        copy.start()
        stores.append(copy)

    store(out_own, outputs_far, 0)
    store(in_own, input_far, 0)
    hop_done(1)
    z_gather.second()
    for k in range(2, len(small)):
        hop_done(k)
    f_gather.last()
    for k in range(1, BLOCKS):
        store(out_blocks.at[k], outputs_far, k)
    z_gather.last()
    for k in range(1, BLOCKS):
        store(in_blocks.at[k], input_far, k)
    sum_heads.close()
    for one in small:
        one.wait_send()
    for one in stores:
        one.wait()


def tail_stage(hops, skip, grad_in, mix, x_rel, grad_residual, out_own, scale, gain, small, number):
    rows, depth = grad_in.shape
    size, high = out_own.shape
    blocks = jax.ShapeDtypeStruct((BLOCKS, size, high), jnp.bfloat16)
    sems = lambda n: pltpu.SemaphoreType.DMA((n,))
    return pl.pallas_call(
        functools.partial(tail_kernel, skip),
        in_specs=[FAR] * 4 + [WHOLE] * 4,
        out_specs=[FAR, FAR, WHOLE],
        out_shape=[blocks, blocks, jax.ShapeDtypeStruct((SMALL, high), jnp.float32)],
        scratch_shapes=[
            sems(7),
            sems(2 * BLOCKS),
            *scatter_scratch(rows, depth, high),
            pltpu.VMEM((rows, high), jnp.bfloat16),
            pltpu.VMEM((size, high), jnp.float32),
            pltpu.VMEM((1, high), jnp.float32),
            pltpu.VMEM((size, high), jnp.bfloat16),
            pltpu.VMEM((BLOCKS, size, high), jnp.bfloat16),
            pltpu.VMEM((BLOCKS, size, high), jnp.bfloat16),
            sems(6), sems(6), sems(6), sems(6),
            pltpu.VMEM((2 * hops, SMALL, high), jnp.float32),
            sems(hops), sems(hops),
        ],
        compiler_params=pltpu.CompilerParams(collective_id=number, has_side_effects=True, vmem_limit_bytes=LIMIT),
        cost_estimate=pl.CostEstimate(flops=10**9, bytes_accessed=1 << 20, transcendentals=0),
        name="tail_stage",
    )(grad_in, mix, x_rel, grad_residual, out_own, scale, gain, small)


def ffn_fwd_kernel(x_ref, w_ref, gu_ref, hidden_ref):
    value = mm(x_ref[...], w_ref[...], NN)
    gu_ref[...] = value.astype(jnp.bfloat16)
    gate, up = value[:, :128], value[:, 128:]
    hidden_ref[...] = (gate * jax.nn.sigmoid(gate) * up).astype(jnp.bfloat16)


def ffn_fwd(x, weight):
    rows, width = x.shape
    wide = weight.shape[1]
    return pl.pallas_call(
        ffn_fwd_kernel,
        grid=(wide // 256,),
        in_specs=[pl.BlockSpec((rows, width), lambda j: (0, 0)), pl.BlockSpec((width, 256), lambda j: (0, j))],
        out_specs=[pl.BlockSpec((rows, 256), lambda j: (0, j)), pl.BlockSpec((rows, 128), lambda j: (0, j))],
        out_shape=[
            jax.ShapeDtypeStruct((rows, wide), jnp.bfloat16),
            jax.ShapeDtypeStruct((rows, wide // 2), jnp.bfloat16),
        ],
        compiler_params=pltpu.CompilerParams(dimension_semantics=("arbitrary",), vmem_limit_bytes=LIMIT),
        cost_estimate=pl.CostEstimate(flops=10**9, bytes_accessed=1 << 20, transcendentals=0),
        name="ffn_fwd",
    )(x, weight)


def ffn_bwd_kernel(grad_ref, w_ref, gu_ref, out_ref):
    value = mm(grad_ref[...], w_ref[...], NN)
    for p in range(2):
        grad = value[:, p * 128 : (p + 1) * 128]
        gate = gu_ref[:, p * 256 : p * 256 + 128].astype(jnp.float32)
        up = gu_ref[:, p * 256 + 128 : (p + 1) * 256].astype(jnp.float32)
        sigma = jax.nn.sigmoid(gate)
        swish = gate * sigma
        out_ref[:, p * 256 : p * 256 + 128] = (grad * up * (sigma + swish * (1.0 - sigma))).astype(jnp.bfloat16)
        out_ref[:, p * 256 + 128 : (p + 1) * 256] = (grad * swish).astype(jnp.bfloat16)


def ffn_bwd(grad, weight, gu):
    rows, width = grad.shape
    wide = gu.shape[1]
    return pl.pallas_call(
        ffn_bwd_kernel,
        grid=(pl.cdiv(wide, 512),),
        in_specs=[
            pl.BlockSpec((rows, width), lambda j: (0, 0)),
            pl.BlockSpec((width, 256), lambda j: (0, j)),
            pl.BlockSpec((rows, 512), lambda j: (0, j)),
        ],
        out_specs=pl.BlockSpec((rows, 512), lambda j: (0, j)),
        out_shape=jax.ShapeDtypeStruct((rows, wide), jnp.bfloat16),
        compiler_params=pltpu.CompilerParams(dimension_semantics=("arbitrary",), vmem_limit_bytes=LIMIT),
        cost_estimate=pl.CostEstimate(flops=10**9, bytes_accessed=1 << 20, transcendentals=0),
        name="ffn_bwd",
    )(grad, weight, gu)


def after(values, *earlier):
    return lax.optimization_barrier((values, earlier))[0]


def turn(array, head_pos):
    blocks = array.reshape((BLOCKS, array.shape[0] // BLOCKS) + array.shape[1:])
    picked = [lax.dynamic_index_in_dim(blocks, head_pos ^ k, 0, keepdims=False) for k in range(BLOCKS)]
    return jnp.concatenate(picked, axis=0)


def rms_scale(values):
    return lax.rsqrt(jnp.mean(values * values, axis=-1, keepdims=True) + EPSILON)


def on_device(seq_count, tokens, cotangent, counts, pads, norm1_gain, w_query, w_key, w_value, w_gate_out,
              w_forget, forget_bias, out_gain, w_out, norm2_gain, w_gate, w_up, w_down):
    f32, b16 = jnp.float32, jnp.bfloat16
    rows, model_width = tokens.shape[1:]
    head_pos = lax.axis_index("head")
    head_arr = head_pos.reshape(1).astype(jnp.int32)
    width, slots, hidden_width = w_query.shape[1], w_forget.shape[1], w_gate.shape[1]
    share = w_query.shape[0]
    extra = slots
    size = rows // BLOCKS

    small = jnp.concatenate([out_gain, forget_bias])
    small = jnp.pad(small, (0, share - small.shape[0]))
    columns = jnp.stack([norm1_gain, norm2_gain, small], axis=1)
    columns = jnp.pad(columns, ((0, 0), (0, extra - 3)))
    wide = 4 * width
    narrow = jnp.concatenate([w_forget, columns], axis=1)
    own_mix = jnp.concatenate([w_out.T, w_query, w_key, w_value, w_gate_out, narrow], axis=1)
    mix = lax.all_gather(own_mix, "seq", axis=0, tiled=True)
    own_gu = jnp.stack([w_gate.reshape(share, -1, 128), w_up.reshape(share, -1, 128)], axis=2).reshape(share, -1)
    gu_weight = lax.all_gather(own_gu, "seq", axis=0, tiled=True)
    down_weight = lax.all_gather(w_down.T, "seq", axis=0, tiled=True)

    skip = width
    f_at, extra_at = skip + wide, skip + wide + slots
    gains = mix[:, extra_at : extra_at + 3].astype(f32)
    gain_one, gain_two = gains[:, 0], gains[:, 1]
    small_all = gains[:, 2].reshape(seq_count, share)
    n_gain, n_bias = out_gain.shape[0], forget_bias.shape[0]
    gain_head = small_all[:, :n_gain].reshape(1, width)
    bias = small_all[:, n_gain : n_gain + n_bias].reshape(slots, 1)

    x_rel = turn(tokens[0], head_pos)
    cot_rel = turn(cotangent[0], head_pos)
    block_of = jnp.arange(BLOCKS, dtype=jnp.int32) ^ head_pos
    position = (block_of[:, None] * size + jnp.arange(size, dtype=jnp.int32)[None, :]).reshape(rows, 1)
    live_len = jnp.where(counts[0] > 0, rows - pads[0], 0)
    live = (position < live_len).astype(f32)
    live_own = live[:size]

    x_f = x_rel.astype(f32)
    scale_one = rms_scale(x_f)
    normed1 = lax.optimization_barrier((x_f * scale_one * gain_one).astype(b16))
    grad_ffn = (cot_rel.astype(f32) * live).astype(b16)
    qkvg = mm(normed1, mix[:, skip:f_at], NN).astype(b16)
    forget_t = lax.dot_general(
        mix[:, f_at:extra_at], normed1, (((0,), (1,)), ((), ())), preferred_element_type=f32
    ) + bias
    log_keep = jax.nn.log_sigmoid(forget_t) / DAMPING
    keep_in = -jnp.expm1(log_keep)
    gated, mixed, probs, kst, vst = rec_fwd(head_arr, qkvg, log_keep, keep_in, gain_head)

    row_one, row_two = gain_one[None], gain_two[None]
    x_own = x_rel[:size]
    cot_own = cot_rel[:size]
    tall = lambda kind: jax.ShapeDtypeStruct((size, model_width), kind)
    line = jax.ShapeDtypeStruct((1, model_width), f32)
    seq_pos = lax.axis_index("seq")
    residual, normed_own, x_squares, mix_squares = head_scatter(
        gated, mix, [x_own], [row_two, live_own], [tall(f32), tall(b16), line, line], finish_mixer, 0
    )
    normed2, normed2_t, normed1_t = head_gather(normed_own, 1, also=normed1)
    gu, hidden = ffn_fwd(normed2.reshape(rows, model_width), gu_weight)

    grad_down = mm(grad_ffn, hidden, TN).astype(b16).reshape(-1, 2, share, hidden_width)
    core = seq_pos % 2
    kept = lax.dynamic_index_in_dim(grad_down, core, 1, keepdims=False)
    given = lax.dynamic_index_in_dim(grad_down, 1 - core, 1, keepdims=False)
    given = lax.ppermute(given, "seq", [(i, i ^ 1) for i in range(seq_count)])
    grad_down = (kept.astype(f32) + given.astype(f32)).astype(b16).reshape(-1, hidden_width)
    down_weight = after(down_weight, grad_down)
    lines = [list(range(c, seq_count, 2)) for c in range(2)]

    def line_scatter(array):
        return lax.psum_scatter(array, "seq", scatter_dimension=0, tiled=True, axis_index_groups=lines)

    grad_down = line_scatter(grad_down)
    grad_gu = ffn_bwd(grad_ffn, down_weight, gu)
    high = model_width // 2
    grad_residual, grad_low, grad_gain_two, grad_gu_w = head_scatter(
        grad_gu, gu_weight, [normed2_t, residual, cot_own], [live_own, row_two], [tall(f32), tall(b16), line],
        finish_norm_two, 2, filler=fill_gu, filled=[jax.ShapeDtypeStruct((high, gu_weight.shape[1]), b16)],
        scratch=tile_scratch(model_width, gu_weight.shape[1], share, 0),
    )
    grad_gu_w = line_scatter(grad_gu_w)
    grad_att_t, grad_gated = head_gather(grad_low, 3, keep=False, weight=mix, width=width)
    grad_gated = after(grad_gated, grad_down)
    wide_in = wide + slots + extra
    states = [pltpu.VMEM((slots, width), f32), pltpu.VMEM((slots, width), f32), pltpu.VMEM((slots, 1), f32)]
    out_own, ffn_squares, grad_gain_head, grad_bias, grad_in, grad_mix = head_scatter(
        hidden, down_weight,
        [qkvg, grad_gated, mixed, probs, kst, vst, log_keep, keep_in, forget_t, jnp.asarray(span_matrix(), b16), gain_head,
         residual, grad_att_t, gated, normed1_t],
        [live_own], [tall(b16), line, jax.ShapeDtypeStruct((1, width), f32), jax.ShapeDtypeStruct((slots, 1), f32)],
        finish_ffn, 4, filler=fill_mix,
        filled=[jax.ShapeDtypeStruct((rows, wide_in), b16),
                jax.ShapeDtypeStruct((high, mix.shape[1]), b16)],
        scratch=[pltpu.VMEM((rows, wide_in), b16), pltpu.SemaphoreType.DMA((1,)), *states,
                 *tile_scratch(model_width, mix.shape[1], share, 1)],
    )
    grad_mix = line_scatter(grad_mix)
    live_row = jnp.full((1, model_width), jnp.sum(live_own) / model_width)
    own_row = jnp.concatenate([grad_gain_head.reshape(seq_count, n_gain), grad_bias.reshape(seq_count, n_bias)], axis=1)
    own_row = jnp.pad(own_row, ((0, 0), (0, share - n_gain - n_bias))).reshape(1, model_width)
    nothing = jnp.zeros((1, model_width), f32)
    small = jnp.concatenate(
        [nothing, grad_gain_two, x_squares, mix_squares, ffn_squares, live_row, nothing, own_row], axis=0
    )
    hops = 2 + seq_count.bit_length() - 1
    outputs, input_grad, small = tail_stage(
        hops, skip, grad_in, mix, x_rel, grad_residual, out_own, scale_one, row_one, small, 6
    )
    outputs = outputs.reshape(rows, model_width)
    input_grad = input_grad.reshape(rows, model_width).astype(f32)

    done = grad_mix.astype(f32)
    sums = jnp.sum(small[2:6], axis=1)
    rms_stats = jnp.sqrt(sums[:3] / (sums[3] * model_width))
    own = lax.dynamic_slice(small, (0, seq_pos * share), (SMALL, share))
    grad_gu_w = grad_gu_w.astype(f32)
    return (
        outputs[None],
        input_grad[None],
        own[0],
        done[:, skip : skip + width],
        done[:, skip + width : skip + 2 * width],
        done[:, skip + 2 * width : skip + 3 * width],
        done[:, skip + 3 * width : f_at],
        done[:, f_at:extra_at],
        own[SMALL - 1, n_gain : n_gain + n_bias],
        own[SMALL - 1, :n_gain],
        done[:, :width].T,
        own[1],
        grad_gu_w[:, :hidden_width],
        grad_gu_w[:, hidden_width:],
        grad_down.astype(f32).T,
        rms_stats,
    )


def solution(mesh):
    both = P("seq", "head")
    flat = P(("head", "seq"))
    rows = P("seq", None, None)
    return jax.shard_map(
        functools.partial(on_device, mesh.shape["seq"]),
        mesh=mesh,
        in_specs=(rows, rows, P("seq"), P("seq"), P("seq"), both, both, both, both, both, flat, flat,
                  P("head", "seq"), P("seq"), both, both, P("head", "seq")),
        out_specs=(rows, rows, P("seq"), both, both, both, both, both, flat, flat, P("head", "seq"), P("seq"),
                   both, both, P("head", "seq"), P()),
        check_vma=False,
    )
```

```python
import functools

import jax
import jax.numpy as jnp
import numpy as np
from jax import lax
from jax.experimental import pallas as pl
from jax.experimental.pallas import tpu as pltpu
from jax.sharding import PartitionSpec as P

EPSILON = 1e-06
DAMPING = 8.0
TILE = 128
BLOCKS = 4
HALVES = (64, 32, 16, 8, 4, 2, 1)
NT = (((1,), (1,)), ((), ()))
NN = (((1,), (0,)), ((), ()))
TN = (((0,), (0,)), ((), ()))


def rel_tile(rows, i, h):
    per = rows // BLOCKS // TILE
    return (i // per ^ h[0]) * per + i % per


def mm(left, right, dims):
    return lax.dot_general(left, right, dims, preferred_element_type=jnp.float32)


def span_matrix():
    r = np.arange(TILE)[:, None]
    t = np.arange(TILE)[None, :]
    parts = []
    for h in HALVES:
        base = t // (2 * h) * (2 * h)
        upper = t % (2 * h) >= h
        parts.append(upper & (r >= base + h) & (r <= t))
        parts.append(~upper & (r > t) & (r <= base + h - 1))
    parts.append(r <= t)
    parts.append(r > t)
    return np.concatenate(parts, axis=1).astype(np.float32)


def level_of():
    s = lax.broadcasted_iota(jnp.int32, (TILE, TILE), 0)
    t = lax.broadcasted_iota(jnp.int32, (TILE, TILE), 1)
    return jnp.where(s < t, s ^ t, jnp.where(s == t, 0, -1))


def level_masks():
    x = level_of()
    masks = [(x >= h) & (x < 2 * h) for h in HALVES]
    masks.append(x == 0)
    return masks


def decays(log_keep, keep_in, spans):
    slots = log_keep.shape[0]
    high = log_keep.astype(jnp.bfloat16)
    rest = log_keep - high.astype(jnp.float32)
    mid = rest.astype(jnp.bfloat16)
    both = mm(jnp.concatenate([high, mid], axis=0), spans, NN)
    grown = jnp.exp(both[:slots] + both[slots:])
    n = len(HALVES)
    ones = jnp.ones_like(keep_in)
    e_parts = [grown[:, (2 * i) * TILE : (2 * i + 1) * TILE] for i in range(n)] + [ones]
    f_bare = [grown[:, (2 * i + 1) * TILE : (2 * i + 2) * TILE] for i in range(n)] + [ones]
    e_all = grown[:, 2 * n * TILE : (2 * n + 1) * TILE]
    f_all = grown[:, (2 * n + 1) * TILE : (2 * n + 2) * TILE]
    total = e_all[:, TILE - 1 : TILE]
    return e_parts, f_bare, e_all, f_all, total


def norm_gate(mixed, gain, gate_pre):
    scale = lax.rsqrt(jnp.mean(mixed * mixed, axis=-1, keepdims=True) + EPSILON)
    unit = mixed * scale
    return scale, unit


def fwd_kernel(h_ref, q_ref, k_ref, v_ref, g_ref, lk_ref, w_ref, gain_ref, spans_ref,
               gated_ref, mixed_ref, probs_ref, kst_ref, vst_ref, kacc, vacc):
    @pl.when(pl.program_id(0) == 0)
    def _():
        kacc[...] = jnp.zeros_like(kacc)
        vacc[...] = jnp.zeros_like(vacc)
    width = q_ref.shape[1]
    root = width ** -0.5
    q, k, v = q_ref[...], k_ref[...], v_ref[...]
    keep_in = w_ref[...]
    e_parts, f_bare, e_all, f_all, total = decays(lk_ref[...], keep_in, spans_ref[...])
    masks = level_masks()
    kst, vst = kacc[...], vacc[...]
    kst_b, vst_b = kst.astype(jnp.bfloat16), vst.astype(jnp.bfloat16)
    kst_ref[0] = kst_b
    vst_ref[0] = vst_b
    inner = mm(k, q, NT) * root
    inner_b = inner.astype(jnp.bfloat16)
    zero_b = jnp.zeros_like(inner_b)
    f_parts = [(bare * keep_in).astype(jnp.bfloat16) for bare in f_bare]
    scores = e_all * (mm(kst_b, q, NT) * root)
    for mask, grow, fade in zip(masks, e_parts, f_parts):
        scores += grow * mm(fade, jnp.where(mask, inner_b, zero_b), NN)
    top = jnp.max(scores, axis=0, keepdims=True)
    raised = jnp.exp(scores - top)
    probs = raised / jnp.sum(raised, axis=0, keepdims=True)
    probs_ref[...] = probs
    mixing = jnp.zeros((TILE, TILE), jnp.float32)
    for mask, grow, fade in zip(masks, e_parts, f_parts):
        mixing = jnp.where(mask, mm(fade, (probs * grow).astype(jnp.bfloat16), TN), mixing)
    mixed = mm(mixing.astype(jnp.bfloat16), v, TN) + mm((probs * e_all).astype(jnp.bfloat16), vst_b, TN)
    tail = (f_all * keep_in).astype(jnp.bfloat16)
    kacc[...] = total * kst + mm(tail, k, NN)
    vacc[...] = total * vst + mm(tail, v, NN)
    mixed_ref[...] = mixed
    scale = lax.rsqrt(jnp.mean(mixed * mixed, axis=-1, keepdims=True) + EPSILON)
    gate = g_ref[...].astype(jnp.float32)
    swish = gate * jax.nn.sigmoid(gate)
    gated_ref[...] = (mixed * scale * gain_ref[...] * swish).astype(jnp.bfloat16)


def rec_fwd(head, qkvg, log_keep_t, keep_in_t, gain):
    rows, wide = qkvg.shape
    width = wide // 4
    slots = log_keep_t.shape[0]
    tiles = rows // TILE
    spans = jnp.asarray(span_matrix(), jnp.bfloat16)
    place = functools.partial(rel_tile, rows)
    col = lambda j: pl.BlockSpec((TILE, width), lambda i, h: (place(i, h), j))
    lane = pl.BlockSpec((slots, TILE), lambda i, h: (0, place(i, h)))
    state = pl.BlockSpec((1, slots, width), lambda i, h: (i, 0, 0))
    return pl.pallas_call(
        fwd_kernel,
        grid_spec=pltpu.PrefetchScalarGridSpec(
            num_scalar_prefetch=1,
            grid=(tiles,),
            in_specs=[col(0), col(1), col(2), col(3), lane, lane,
                      pl.BlockSpec((1, width), lambda i, h: (0, 0)),
                      pl.BlockSpec(spans.shape, lambda i, h: (0, 0))],
            out_specs=[col(0), col(0), lane, state, state],
            scratch_shapes=[pltpu.VMEM((slots, width), jnp.float32)] * 2,
        ),
        out_shape=[
            jax.ShapeDtypeStruct((rows, width), jnp.bfloat16),
            jax.ShapeDtypeStruct((rows, width), jnp.float32),
            jax.ShapeDtypeStruct((slots, rows), jnp.float32),
            jax.ShapeDtypeStruct((tiles, slots, width), jnp.bfloat16),
            jax.ShapeDtypeStruct((tiles, slots, width), jnp.bfloat16),
        ],
        compiler_params=pltpu.CompilerParams(dimension_semantics=("arbitrary",), vmem_limit_bytes=60 << 20),
        cost_estimate=pl.CostEstimate(flops=5 * 10**9, bytes_accessed=10 << 20, transcendentals=0),
        name="slot_fwd",
    )(head, qkvg, qkvg, qkvg, qkvg, log_keep_t, keep_in_t, gain, spans)


def bwd_tile(step, q_ref, k_ref, v_ref, g_ref, lk_ref, w_ref, fpre_ref, gain_ref, spans_ref,
               mixed_ref, probs_ref, kst_ref, vst_ref, dg_ref,
               dproj_ref, dgain_ref, dbias_ref, dk_acc, dv_acc, cross):
    width = q_ref.shape[1]
    slots = lk_ref.shape[0]

    @pl.when(step == 0)
    def _():
        dk_acc[...] = jnp.zeros_like(dk_acc)
        dv_acc[...] = jnp.zeros_like(dv_acc)
        cross[...] = jnp.zeros_like(cross)
        dgain_ref[...] = jnp.zeros_like(dgain_ref)
        dbias_ref[...] = jnp.zeros_like(dbias_ref)
    root = width ** -0.5
    q, k, v = q_ref[...], k_ref[...], v_ref[...]
    mixed = mixed_ref[...]
    gate = g_ref[...].astype(jnp.float32)
    gain = gain_ref[...]
    d_gated = dg_ref[...].astype(jnp.float32)
    scale = lax.rsqrt(jnp.mean(mixed * mixed, axis=-1, keepdims=True) + EPSILON)
    unit = mixed * scale
    sigma = jax.nn.sigmoid(gate)
    swish = gate * sigma
    slope = sigma * (1.0 + gate * (1.0 - sigma))
    dproj_ref[:, 3 * width : 4 * width] = (d_gated * unit * gain * slope).astype(jnp.bfloat16)
    d_normed = d_gated * swish
    dgain_ref[...] += jnp.sum(d_normed * unit, axis=0, keepdims=True)
    c = d_normed * gain
    d_mixed = scale * (c - unit * jnp.mean(c * unit, axis=-1, keepdims=True))
    d_out = d_mixed.astype(jnp.bfloat16)

    log_keep, keep_in = lk_ref[...], w_ref[...]
    e_parts, f_bare, e_all, f_all, total = decays(log_keep, keep_in, spans_ref[...])
    masks = level_masks()
    probs = probs_ref[...]
    kst, vst = kst_ref[0], vst_ref[0]
    dkst, dvst = dk_acc[...], dv_acc[...]
    dkst_b, dvst_b = dkst.astype(jnp.bfloat16), dvst.astype(jnp.bfloat16)

    inner_b = (mm(k, q, NT) * root).astype(jnp.bfloat16)
    d_mixing_b = mm(v, d_out, NT).astype(jnp.bfloat16)
    pair = jnp.concatenate([inner_b, d_mixing_b], axis=1)
    zero_b = jnp.zeros_like(pair)
    masks2 = [jnp.concatenate([mask, mask], axis=1) for mask in masks]
    pairs = [jnp.where(mask, pair, zero_b) for mask in masks2]
    f_parts = [(bare * keep_in).astype(jnp.bfloat16) for bare in f_bare]
    both = [mm(fade, two, NN) for fade, two in zip(f_parts, pairs)]
    s_state = mm(kst, q, NT) * root
    p_state = mm(vst, d_out, NT)
    d_probs = e_all * p_state
    for grow, two in zip(e_parts, both):
        d_probs += grow * two[:, TILE:]
    d_scores = probs * (d_probs - jnp.sum(probs * d_probs, axis=0, keepdims=True))

    xy_all = jnp.concatenate([d_scores * e_all, probs * e_all], axis=1).astype(jnp.bfloat16)
    xy_parts = [jnp.concatenate([d_scores * grow, probs * grow], axis=1).astype(jnp.bfloat16) for grow in e_parts]
    x0 = xy_all[:, :TILE]
    y0 = xy_all[:, TILE:]
    change = x0.astype(jnp.float32) * s_state + y0.astype(jnp.float32) * p_state
    into = jnp.zeros((slots, TILE), jnp.float32)
    d_both = jnp.zeros((TILE, 2 * TILE), jnp.float32)
    for i, (grow, bare, fade, two, xy, part, mask) in enumerate(
        zip(e_parts, f_bare, f_parts, both, xy_parts, pairs, masks2)
    ):
        z = mm(xy, part, NT)
        into += bare * z
        if i < len(HALVES):
            mass = xy.astype(jnp.float32) * two
            change += mass[:, :TILE] + mass[:, TILE:] - fade.astype(jnp.float32) * z
        d_both = jnp.where(mask, mm(fade, xy, TN), d_both)
    d_both_b = d_both.astype(jnp.bfloat16)
    d_inner, mixing = d_both_b[:, :TILE], d_both_b[:, TILE:]
    tail = (f_all * keep_in).astype(jnp.bfloat16)
    z_state = mm(dkst_b, k, NT) + mm(dvst_b, v, NT)
    into += f_all * z_state
    change -= tail.astype(jnp.float32) * z_state

    dproj_ref[:, :width] = (root * (mm(d_inner, k, TN) + mm(x0, kst, TN))).astype(jnp.bfloat16)
    dproj_ref[:, width : 2 * width] = (root * mm(d_inner, q, NN) + mm(tail, dkst_b, TN)).astype(jnp.bfloat16)
    dproj_ref[:, 2 * width : 3 * width] = (mm(mixing, d_out, NN) + mm(tail, dvst_b, TN)).astype(jnp.bfloat16)

    later = (lax.broadcasted_iota(jnp.int32, (TILE, TILE), 0) >= lax.broadcasted_iota(jnp.int32, (TILE, TILE), 1)).astype(jnp.bfloat16)
    high = change.astype(jnp.bfloat16)
    rest = change - high.astype(jnp.float32)
    mid = rest.astype(jnp.bfloat16)
    low = (rest - mid.astype(jnp.float32)).astype(jnp.bfloat16)
    sums = mm(jnp.concatenate([high, mid, low], axis=0), later, NN)
    d_log_keep = sums[:slots] + sums[slots : 2 * slots] + sums[2 * slots :] + cross[...] - jnp.exp(log_keep) * into
    d_forget = (d_log_keep * jax.nn.sigmoid(-fpre_ref[...]) / DAMPING).astype(jnp.bfloat16)
    dbias_ref[...] += jnp.sum(d_forget.astype(jnp.float32), axis=1, keepdims=True)
    turned = jnp.transpose(d_forget.astype(jnp.float32))
    dproj_ref[:, 4 * width :] = jnp.concatenate([turned, jnp.zeros_like(turned)], axis=1).astype(jnp.bfloat16)

    dkst_new = total * dkst + root * mm(x0, q, NN)
    dvst_new = total * dvst + mm(y0, d_out, NN)
    dk_acc[...] = dkst_new
    dv_acc[...] = dvst_new
    cross[...] = jnp.sum(kst.astype(jnp.float32) * dkst_new + vst.astype(jnp.float32) * dvst_new, axis=1, keepdims=True)


MESH = pl.DeviceIdType.MESH
CHUNK = 32


def neighbours():
    head = lax.axis_index("head")
    return {"head": head + 1 - 2 * (head % 2)}, {"head": (head + 2) % BLOCKS}


def flipped(index, bit):
    return index + bit - 2 * bit * (index // bit % 2)


def other_core():
    return {"seq": flipped(lax.axis_index("seq"), 1)}


def greet(targets):
    barrier = pltpu.get_barrier_semaphore()
    for target in targets:
        pl.semaphore_signal(barrier, inc=1, device_id=target, device_id_type=MESH)
    pl.semaphore_wait(barrier, len(targets))


LIMIT = 60 << 20
FAR = pl.BlockSpec(memory_space=pl.ANY)
WHOLE = pl.BlockSpec(memory_space=pltpu.VMEM)


class Loads:
    def __init__(self, sem):
        self.sem, self.copies = sem, []

    def add(self, src, dst):
        copy = pltpu.make_async_copy(src, dst, self.sem.at[len(self.copies)])
        copy.start()
        self.copies.append(copy)
        return copy


class Scatter:
    order = (0, 2, 1, 3)

    def __init__(self, left, right, acc, mid, send, got, send_sem, got_sem):
        self.left, self.right, self.acc, self.mid, self.send, self.got = left, right, acc, mid, send, got
        self.size, self.cols = send.shape[1:]
        to_x, to_y = neighbours()
        self.copies = []
        for u in range(2):
            for k, to in enumerate((to_x, to_x, to_y, to_y, to_y, to_x)):
                slot = 6 * u + k
                self.copies.append(
                    pltpu.make_async_remote_copy(
                        src_ref=send.at[slot], dst_ref=got.at[slot], send_sem=send_sem.at[slot],
                        recv_sem=got_sem.at[slot], device_id=to, device_id_type=MESH,
                    )
                )

    def first(self, loads, watch=None):
        size, cols = self.size, self.cols
        for part, load in zip(self.order, loads):
            load.wait()
            value = mm(self.left[...], self.right[part * cols : (part + 1) * cols, :], NT)
            side_at, u = part // 2, part % 2
            here = slice(part * cols, (part + 1) * cols)
            slot = 6 * u + 2 * side_at
            near_block, mid_block = (1, 2) if side_at == 0 else (2, 1)
            self.acc[:, here] = value[:size]
            self.mid[:, here] = value[mid_block * size : (mid_block + 1) * size]
            self.send[slot] = value[3 * size :].astype(jnp.bfloat16)
            self.copies[slot].start()
            self.send[slot + 1] = value[near_block * size : (near_block + 1) * size].astype(jnp.bfloat16)
            self.copies[slot + 1].start()
            if watch is not None:
                watch(here, value)

    def second(self, u):
        cols = self.cols
        for side_at in range(2):
            part = 2 * side_at + u
            first, second = 6 * u + 2 * side_at, 6 * u + 4 + side_at
            here = slice(part * cols, (part + 1) * cols)
            self.copies[first].wait_recv()
            self.send[second] = (self.mid[:, here] + self.got[first].astype(jnp.float32)).astype(jnp.bfloat16)
            self.copies[second].start()

    def last(self, finish):
        for u in range(2):
            for k in (1, 3, 4, 5):
                self.copies[6 * u + k].wait_recv()
        cols = self.cols

        def rows(i, carry):
            here = pl.ds(pl.multiple_of(i * CHUNK, CHUNK), CHUNK)
            sums = []
            for part in range(4):
                side_at, u = part // 2, part % 2
                one, two = self.got[6 * u + 2 * side_at + 1, here, :], self.got[6 * u + 4 + side_at, here, :]
                own = self.acc[here, part * cols : (part + 1) * cols]
                sums.append(own + one.astype(jnp.float32) + two.astype(jnp.float32))
            finish(here, jnp.concatenate(sums, axis=1), i)
            return carry

        lax.fori_loop(0, self.size // CHUNK, rows, 0)

    def close(self):
        for one in self.copies:
            one.wait_send()


def scatter_scratch(rows, depth, high):
    size, cols = rows // BLOCKS, high // 4
    return [
        pltpu.VMEM((rows, depth), jnp.bfloat16),
        pltpu.VMEM((high, depth), jnp.bfloat16),
        pltpu.VMEM((size, high), jnp.float32),
        pltpu.VMEM((size, high), jnp.float32),
        pltpu.VMEM((12, size, cols), jnp.bfloat16),
        pltpu.VMEM((12, size, cols), jnp.bfloat16),
        pltpu.SemaphoreType.DMA((12,)),
        pltpu.SemaphoreType.DMA((12,)),
    ]


def load_parts(loads, right_far, right, skip):
    cols = right.shape[0] // 4
    parts = []
    for part in Scatter.order:
        here = pl.ds(part * cols, cols)
        parts.append(loads.add(right_far.at[here, pl.ds(skip, right.shape[1])], right.at[here, :]))
    return parts


def scatter_kernel(plan, *refs):
    n_far, n_near, n_out, skip, finish, filler = plan
    left_far, right_far, *more_far = refs[:n_far]
    near = refs[n_far : n_far + n_near]
    outs = refs[n_far + n_near : n_far + n_near + n_out]
    load_sem, *rest = refs[n_far + n_near + n_out :]
    scatter, spare = rest[:8], rest[8:]
    left, right = scatter[:2]
    loads = Loads(load_sem)
    load_left = loads.add(left_far, left)
    parts = load_parts(loads, right_far, right, skip)
    more = [(loads.add(src, dst), dst) for src, dst in zip(more_far, spare)]
    spare = spare[len(more_far) :]
    greet(neighbours() if filler is None else (*neighbours(), other_core()))
    sum_heads = Scatter(*scatter)
    load_left.wait()
    sum_heads.first(parts)
    sum_heads.second(0)
    for load, _ in more:
        load.wait()
    side = [dst for _, dst in more]
    if filler is not None:
        steps = filler(left, right, side, outs, spare)
        next(steps)
        sum_heads.second(1)
        for _ in steps:
            pass
    else:
        sum_heads.second(1)
    sum_heads.last(lambda here, total, i: finish(here, total, side, near, outs, i))
    sum_heads.close()


def head_scatter(left, right, far, near, out_shapes, finish, number, filler=None, filled=(), scratch=()):
    rows, depth = left.shape
    plan = (2 + len(far), len(near), len(out_shapes) + len(filled), 0, finish, filler)
    return pl.pallas_call(
        functools.partial(scatter_kernel, plan),
        in_specs=[FAR] * (2 + len(far)) + [WHOLE] * len(near),
        out_specs=[WHOLE] * len(out_shapes) + [FAR] * len(filled),
        out_shape=[*out_shapes, *filled],
        scratch_shapes=[
            pltpu.SemaphoreType.DMA((5 + len(far),)),
            *scatter_scratch(rows, depth, right.shape[0]),
            *[pltpu.VMEM(one.shape, one.dtype) for one in far],
            *scratch,
        ],
        compiler_params=pltpu.CompilerParams(collective_id=number, has_side_effects=True, vmem_limit_bytes=LIMIT),
        cost_estimate=pl.CostEstimate(flops=10**9, bytes_accessed=1 << 20, transcendentals=0),
        name="head_scatter%d" % number,
    )(left, right, *far, *near)


STEP = 512


def weight_tiles(pairs, place, out_ref, room, land, store_sem, send_sem, got_sem, pause=None):
    count, share = land.shape[:2]
    high = 2 * count * share
    core = lax.axis_index("seq") % 2
    per = STEP // (2 * share)

    def row(p, at):
        return (2 * p + at) * share % room.shape[0]

    def swap_shard(p):
        return pltpu.make_async_remote_copy(
            src_ref=room.at[pl.ds(row(p, 0) + (1 - core) * share, share), :], dst_ref=land.at[p],
            send_sem=send_sem.at[p], recv_sem=got_sem.at[p], device_id=other_core(), device_id_type=MESH,
        )

    def store(p):
        return pltpu.make_async_copy(land.at[p], out_ref.at[pl.ds(p * share, share), :], store_sem.at[p])

    def settle(p):
        swap_shard(p).wait_recv()
        own = room[pl.ds(pl.multiple_of(row(p, 0) + core * share, share), share), :]
        land[p] = (own.astype(jnp.float32) + land[p].astype(jnp.float32)).astype(jnp.bfloat16)
        store(p).start()

    sent = []
    for i in range(high // STEP):
        here = slice(i * STEP, (i + 1) * STEP)
        there = slice(i * STEP % room.shape[0], i * STEP % room.shape[0] + STEP)
        if (i + 1) * STEP > room.shape[0]:
            for p in range((i - 2) * per, (i - 1) * per):
                swap_shard(p).wait_send()
                sent.append(p)
        for turned, right, column in pairs:
            for at in range(0, right.shape[1], STEP):
                cols = min(STEP, right.shape[1] - at)
                value = mm(turned[here, :], right[:, at : at + cols], NN).astype(jnp.bfloat16)
                for src, dst, wide in place(column + at, cols):
                    room[there, dst : dst + wide] = value[:, src : src + wide]
        for p in range(i * per, (i + 1) * per):
            swap_shard(p).start()
        if i:
            for p in range((i - 1) * per, i * per):
                settle(p)
        if i == pause:
            yield
    for p in range(count - per, count):
        settle(p)
    for p in range(count):
        store(p).wait()
        if p not in sent:
            swap_shard(p).wait_send()


def tile_scratch(high, width, share, room):
    count = high // (2 * share)
    return [pltpu.VMEM((2 * STEP, width), jnp.bfloat16)] * room + [
        pltpu.VMEM((count, share, width), jnp.bfloat16),
        pltpu.SemaphoreType.DMA((count,)),
        pltpu.SemaphoreType.DMA((count,)),
        pltpu.SemaphoreType.DMA((count,)),
    ]


def fill_gu(left, right, side, outs, spare):
    half = left.shape[1] // 2

    def place(at, cols):
        return [(k, (at + k) // 256 * 128 + (at + k) // 128 % 2 * half, 128) for k in range(0, cols, 128)]

    return weight_tiles([(side[0], left, 0)], place, outs[-1], right, *spare, pause=1)


def mixed_index(block):
    head = lax.axis_index("head")
    return (block + head) % 2 + 2 * ((block // 2 + head // 2) % 2)


def fill_mix(left, right, side, outs, spare):
    qkvg, d_gated, mixed, probs, kst, vst, log_keep, keep_in, forget, spans, gain, _, att_t, gated, normed_t = side
    grad_far, gain_grad, bias_grad, out_ref = outs[-2], outs[2], outs[3], outs[-1]
    grad_in, grad_sem, dk_acc, dv_acc, cross, *spare = spare
    width = gated.shape[1]
    tiles = qkvg.shape[0] // TILE
    per = tiles // BLOCKS

    def tile(i, carry):
        at = tiles - 1 - i
        rel = mixed_index(at // per) * per + at % per
        rows = pl.ds(pl.multiple_of(rel * TILE, TILE), TILE)
        bwd_tile(
            i, *[qkvg.at[rows, pl.ds(k * width, width)] for k in range(4)], log_keep.at[:, rows], keep_in.at[:, rows],
            forget.at[:, rows], gain, spans, mixed.at[rows, :], probs.at[:, rows], kst.at[pl.ds(at, 1)],
            vst.at[pl.ds(at, 1)], d_gated.at[rows, :], grad_in.at[rows, :], gain_grad, bias_grad, dk_acc, dv_acc, cross,
        )
        return carry

    lax.fori_loop(0, tiles, tile, 0)
    keep = pltpu.make_async_copy(grad_in, grad_far, grad_sem.at[0])
    keep.start()
    yield
    place = lambda at, cols: [(0, at, cols)]
    yield from weight_tiles([(att_t, gated, 0), (normed_t, grad_in, width)], place, out_ref, *spare)
    keep.wait()


class Gather:
    def __init__(self, own, blocks, send_sem, got_sem):
        half = own.shape[1] // 2
        to_x, to_y = neighbours()

        def copy(slot, src, block, side_at, target):
            here = pl.ds(side_at * half, half)
            return pltpu.make_async_remote_copy(
                src_ref=src.at[:, here], dst_ref=blocks.at[block, :, here],
                send_sem=send_sem.at[slot], recv_sem=got_sem.at[slot], device_id=target, device_id_type=MESH,
            )

        self.copies = [
            copy(0, own, 1, 0, to_x),
            copy(1, own, 2, 1, to_y),
            copy(2, own, 1, 1, to_x),
            copy(3, own, 2, 0, to_y),
            copy(4, blocks.at[1], 3, 0, to_y),
            copy(5, blocks.at[2], 3, 1, to_x),
        ]

    def first(self):
        for one in self.copies[:4]:
            one.start()

    def second(self):
        for near, far in ((0, 4), (1, 5)):
            self.copies[near].wait_recv()
            self.copies[far].start()

    def last(self):
        for one in self.copies[2:]:
            one.wait_recv()
        for one in self.copies:
            one.wait_send()


def gather_kernel(plan, *refs):
    keep, product, also = plan
    refs = list(refs)
    own_ref = refs.pop(0)
    weight_far = refs.pop(0) if product else None
    also_far = refs.pop(0) if also else None
    out_ref = refs.pop(0) if keep else None
    turned_ref = refs.pop(0)
    product_ref = refs.pop(0) if product else None
    also_ref = refs.pop(0) if also else None
    blocks, turned_buf, send_sem, got_sem, out_sem, load_sem, *refs = refs
    size, half = own_ref.shape[0], own_ref.shape[1] // 2
    loads = Loads(load_sem)
    if product:
        weight = refs.pop(0)
        fetch = loads.add(weight_far.at[:, pl.ds(0, weight.shape[1])], weight)
    if also:
        also_buf, also_turned = refs
        fetch = loads.add(also_far, also_buf)
    greet(neighbours())
    gather = Gather(own_ref, blocks, send_sem, got_sem)
    gather.first()
    if product or also:
        fetch.wait()
    stores = []

    def store(src, dst):
        copy = pltpu.make_async_copy(src, dst, out_sem.at[len(stores)])
        copy.start()
        stores.append(copy)

    def use(block, side_at, src):
        here = slice(side_at * half, (side_at + 1) * half)
        rows = slice(block * size, (block + 1) * size)
        value = src[:, here]
        turned_buf[here, rows] = jnp.transpose(value)
        store(turned_buf.at[here, rows], turned_ref.at[here, rows])
        if keep:
            store(src.at[:, here], out_ref.at[block, :, here])
        if product:
            term = mm(value, weight[here, :], NN)
            if (block, side_at) in ((0, 0), (1, 0), (2, 1), (3, 0)):
                product_ref[rows, :] = term
            else:
                product_ref[rows, :] += term

    use(0, 0, own_ref)
    use(0, 1, own_ref)
    if also:
        also_turned[...] = jnp.transpose(also_buf[: also_buf.shape[0] // 2, :])
        middle = also_buf.shape[0] // 2
        store(also_turned, also_ref.at[:, pl.ds(0, middle)])
    gather.second()
    use(1, 0, blocks.at[1])
    use(2, 1, blocks.at[2])
    if also:
        stores[-1 - 4 * keep - 2 * (not keep)].wait()
        finished = len(stores) - 1 - 4 * keep - 2 * (not keep)
        also_turned[...] = jnp.transpose(also_buf[middle:, :])
        store(also_turned, also_ref.at[:, pl.ds(middle, middle)])
    for slot, block, side_at in ((2, 1, 1), (3, 2, 0), (4, 3, 0), (5, 3, 1)):
        gather.copies[slot].wait_recv()
        use(block, side_at, blocks.at[block])
    for at, one in enumerate(stores):
        if not also or at != finished:
            one.wait()
    for one in gather.copies:
        one.wait_send()


def head_gather(own, number, keep=True, weight=None, width=0, also=None):
    size, wide = own.shape
    rows = BLOCKS * size
    product = weight is not None
    extra = [one for one in (weight, also) if one is not None]
    out_shape, out_specs = [], []
    if keep:
        out_shape.append(jax.ShapeDtypeStruct((BLOCKS, size, wide), own.dtype))
        out_specs.append(FAR)
    out_shape.append(jax.ShapeDtypeStruct((wide, rows), own.dtype))
    out_specs.append(FAR)
    scratch = [
        pltpu.VMEM((BLOCKS, size, wide), own.dtype),
        pltpu.VMEM((wide, rows), own.dtype),
        pltpu.SemaphoreType.DMA((6,)),
        pltpu.SemaphoreType.DMA((6,)),
        pltpu.SemaphoreType.DMA((20,)),
        pltpu.SemaphoreType.DMA((2,)),
    ]
    if product:
        out_shape.append(jax.ShapeDtypeStruct((rows, width), jnp.float32))
        out_specs.append(WHOLE)
        scratch.append(pltpu.VMEM((wide, width), own.dtype))
    if also is not None:
        out_shape.append(jax.ShapeDtypeStruct(also.shape[::-1], also.dtype))
        out_specs.append(FAR)
        scratch += [pltpu.VMEM(also.shape, also.dtype), pltpu.VMEM((also.shape[1], also.shape[0] // 2), also.dtype)]
    return pl.pallas_call(
        functools.partial(gather_kernel, (keep, product, also is not None)),
        in_specs=[WHOLE] + [FAR] * len(extra),
        out_specs=out_specs,
        out_shape=out_shape,
        scratch_shapes=scratch,
        compiler_params=pltpu.CompilerParams(collective_id=number, has_side_effects=True, vmem_limit_bytes=LIMIT),
        cost_estimate=pl.CostEstimate(flops=10**9, bytes_accessed=1 << 20, transcendentals=0),
        name="head_gather%d" % number,
    )(own, *extra)


def unit_of(values):
    scale = lax.rsqrt(jnp.mean(values * values, axis=-1, keepdims=True) + EPSILON)
    return scale, values * scale


def finish_mixer(here, total, side, near, outs, i):
    x = side[0][here, :].astype(jnp.float32)
    gain, live = near[0][...], near[1][here, :]
    residual = x + total
    outs[0][here, :] = residual
    outs[1][here, :] = (unit_of(residual)[1] * gain).astype(jnp.bfloat16)
    add_row(outs[2], jnp.sum(live * x * x, axis=0, keepdims=True), i)
    add_row(outs[3], jnp.sum(live * total * total, axis=0, keepdims=True), i)
    add_row(outs[4], jnp.sum(live / x.shape[1] + jnp.zeros_like(x), axis=0, keepdims=True), i)


def add_row(ref, row, i):
    @pl.when(i == 0)
    def _():
        ref[...] = jnp.zeros_like(ref)

    ref[...] += row


def norm_back(total, gain, scale, unit):
    c = total * gain
    return scale * (c - unit * jnp.mean(c * unit, axis=-1, keepdims=True))


def finish_norm_two(here, total, side, near, outs, i):
    residual, cot = side[1][here, :], side[2][here, :].astype(jnp.float32)
    live, gain = near[0][here, :], near[1][...]
    scale, unit = unit_of(residual)
    add_row(outs[2], jnp.sum(total * unit, axis=0, keepdims=True), i)
    grad = cot * live + norm_back(total, gain, scale, unit)
    outs[0][here, :] = grad
    outs[1][here, :] = grad.astype(jnp.bfloat16)


def finish_ffn(here, total, side, near, outs, i):
    live = near[0][here, :]
    add_row(outs[1], jnp.sum(live * total * total, axis=0, keepdims=True), i)
    outs[0][here, :] = (live * (side[11][here, :] + total)).astype(jnp.bfloat16)


SMALL = 8


def tail_kernel(skip, grad_far, mix_far, normed_far, x_far, res_far, out_own, gain_ref, two_ref, x_sum, mix_sum, ffn_sum,
                live_sum, head_ref, bias_ref, outputs_far, input_far, total_ref, load_sem, store_sem, *rest):
    scatter = rest[:8]
    left, right = scatter[:2]
    normed, x_buf, res_buf, in_own, out_blocks, in_blocks, f_send, f_got, z_send, z_got, s_buf, s_send, s_got = rest[8:]
    loads = Loads(load_sem)
    load_left = loads.add(grad_far, left)
    parts = load_parts(loads, mix_far, right, skip)
    load_normed = loads.add(normed_far, normed)
    load_x = loads.add(x_far.at[pl.ds(0, x_buf.shape[0]), :], x_buf)
    load_res = loads.add(res_far, res_buf)
    size = in_own.shape[0]
    seq = lax.axis_index("seq")
    hops = [*neighbours(), other_core()]
    bit = 2
    while bit < lax.axis_size("seq"):
        hops.append({"seq": flipped(seq, bit)})
        bit *= 2
    greet(hops)
    sum_heads = Scatter(*scatter)

    def watch(here, value):
        term = value * normed[:, here].astype(jnp.float32)
        s_buf[0, 0:1, here] = jnp.sum(term, axis=0, keepdims=True) / gain_ref[:, here]

    f_gather = Gather(out_own, out_blocks, f_send, f_got)
    f_gather.first()
    s_buf[0] = jnp.zeros(s_buf.shape[1:], jnp.float32)
    load_left.wait()
    load_normed.wait()
    sum_heads.first(parts, watch)
    sum_heads.second(0)
    sum_heads.second(1)

    is_own = lax.broadcasted_iota(jnp.int32, (SMALL, 1), 0) >= SMALL - 2
    for k, row in enumerate((two_ref, x_sum, mix_sum, ffn_sum, live_sum)):
        s_buf[0, k + 1 : k + 2, :] = row[...]
    s_buf[0, SMALL - 2 : SMALL - 1, : head_ref.shape[1]] = head_ref[...]
    slots = bias_ref.shape[0]
    s_buf[0, SMALL - 1 : SMALL, :slots] = jnp.transpose(jnp.broadcast_to(bias_ref[...], (slots, 128)))[:1, :]
    small = [
        pltpu.make_async_remote_copy(
            src_ref=s_buf.at[2 * k], dst_ref=s_buf.at[2 * k + 1], send_sem=s_send.at[k], recv_sem=s_got.at[k],
            device_id=hop, device_id_type=MESH,
        )
        for k, hop in enumerate(hops)
    ]

    def hop_done(k):
        small[k].wait_recv()
        arrived = s_buf[2 * k + 1]
        if k < 2:
            arrived = jnp.where(is_own, 0.0, arrived)
        if k + 1 < len(small):
            s_buf[2 * k + 2] = s_buf[2 * k] + arrived
            small[k + 1].start()
        else:
            total_ref[...] = s_buf[2 * k] + arrived

    small[0].start()
    load_x.wait()
    load_res.wait()

    def finish(here, total, i):
        scale, unit = unit_of(x_buf[here, :].astype(jnp.float32))
        in_own[here, :] = (res_buf[here, :] + norm_back(total, gain_ref[...], scale, unit)).astype(jnp.bfloat16)

    f_gather.second()
    hop_done(0)
    sum_heads.last(finish)
    z_gather = Gather(in_own, in_blocks, z_send, z_got)
    z_gather.first()
    head = lax.axis_index("head")
    places = (head, flipped(head, 1), flipped(head, 2), BLOCKS - 1 - head)
    stores = []

    def store(src, far, k):
        copy = pltpu.make_async_copy(src, far.at[places[k]], store_sem.at[len(stores)])
        copy.start()
        stores.append(copy)

    store(out_own, outputs_far, 0)
    store(in_own, input_far, 0)
    hop_done(1)
    z_gather.second()
    for k in range(2, len(small)):
        hop_done(k)
    f_gather.last()
    for k in range(1, BLOCKS):
        store(out_blocks.at[k], outputs_far, k)
    z_gather.last()
    for k in range(1, BLOCKS):
        store(in_blocks.at[k], input_far, k)
    sum_heads.close()
    for one in small:
        one.wait_send()
    for one in stores:
        one.wait()


def tail_stage(hops, skip, grad_in, mix, normed, x_rel, grad_residual, out_own, small, number):
    rows, depth = grad_in.shape
    size, high = out_own.shape
    blocks = jax.ShapeDtypeStruct((BLOCKS, size, high), jnp.bfloat16)
    sems = lambda n: pltpu.SemaphoreType.DMA((n,))
    return pl.pallas_call(
        functools.partial(tail_kernel, skip),
        in_specs=[FAR] * 5 + [WHOLE] * (1 + len(small)),
        out_specs=[FAR, FAR, WHOLE],
        out_shape=[blocks, blocks, jax.ShapeDtypeStruct((SMALL, high), jnp.float32)],
        scratch_shapes=[
            sems(8),
            sems(2 * BLOCKS),
            *scatter_scratch(rows, depth, high),
            pltpu.VMEM((rows, high), jnp.bfloat16),
            pltpu.VMEM((size, high), jnp.bfloat16),
            pltpu.VMEM((size, high), jnp.float32),
            pltpu.VMEM((size, high), jnp.bfloat16),
            pltpu.VMEM((BLOCKS, size, high), jnp.bfloat16),
            pltpu.VMEM((BLOCKS, size, high), jnp.bfloat16),
            sems(6), sems(6), sems(6), sems(6),
            pltpu.VMEM((2 * hops, SMALL, high), jnp.float32),
            sems(hops), sems(hops),
        ],
        compiler_params=pltpu.CompilerParams(collective_id=number, has_side_effects=True, vmem_limit_bytes=LIMIT),
        cost_estimate=pl.CostEstimate(flops=10**9, bytes_accessed=1 << 20, transcendentals=0),
        name="tail_stage",
    )(grad_in, mix, normed, x_rel, grad_residual, out_own, *small)


def last_kernel(counts, seq_ref, input_ref, output_ref, gu_ref, mix_ref, out_w_ref, narrow_ref, down_ref, small_ref,
                input_out, output_out, q_out, k_out, v_out, go_out, f_out, gate_out, up_out, w_out_out, down_out,
                one_out, two_out, head_out, bias_out, rms_out):
    seq_count, skip, n_gain, n_bias = counts
    f32 = jnp.float32
    step = pl.program_id(0)
    input_out[...] = input_ref[...].astype(f32)
    output_out[...] = output_ref[...]
    half = gate_out.shape[1]
    gate_out[...] = gu_ref[:, :half].astype(f32)
    up_out[...] = gu_ref[:, half:].astype(f32)
    width = q_out.shape[1]
    for k, out in enumerate((q_out, k_out, v_out, go_out)):
        out[...] = mix_ref[:, skip + k * width : skip + (k + 1) * width].astype(f32)

    @pl.when(step == 0)
    def _():
        down_out[...] = jnp.transpose(down_ref[...].astype(f32))

    @pl.when(step == 1)
    def _():
        slots = f_out.shape[0]
        f_out[...] = jnp.transpose(narrow_ref[...].astype(f32))[:slots, :]
        w_out_out[...] = jnp.transpose(out_w_ref[...].astype(f32))
        share = one_out.shape[1]
        picks = [(one_out, 0, share), (two_out, 1, share), (head_out, SMALL - 2, n_gain), (bias_out, SMALL - 1, n_bias)]
        for out, row, n in picks:
            value = small_ref[row : row + 1, :n]
            for s in range(1, seq_count):
                value = jnp.where(seq_ref[0] == s, small_ref[row : row + 1, s * n : (s + 1) * n], value)
            out[...] = value
        sums = jnp.sum(small_ref[...], axis=1, keepdims=True)
        roots = jnp.sqrt(sums / (sums[5:6] * small_ref.shape[1]))
        rms_out[...] = jnp.transpose(jnp.broadcast_to(roots, (SMALL, 128)))[:1, 2:5]


def last_stage(seq_pos, seq_count, input_grad, outputs, grad_gu, grad_mix, grad_down, small, width, slots, n_gain, n_bias):
    f32 = jnp.float32
    rows, high = input_grad.shape
    share, wide_gu = grad_gu.shape
    wide_mix, hidden = grad_mix.shape[1], grad_down.shape[1]
    steps = 4
    per, part = rows // steps, share // steps
    tile = lambda a, b: pl.BlockSpec((a, b), lambda i, s: (i, 0))
    fixed = lambda a, b: pl.BlockSpec((a, b), lambda i, s: (0, 0))
    shapes = lambda *dims: [jax.ShapeDtypeStruct(one, f32) for one in dims]
    return pl.pallas_call(
        functools.partial(last_kernel, (seq_count, width, n_gain, n_bias)),
        grid_spec=pltpu.PrefetchScalarGridSpec(
            num_scalar_prefetch=1,
            grid=(steps,),
            in_specs=[tile(per, high), tile(per, high), tile(part, wide_gu), tile(part, wide_mix), fixed(share, width),
                      pl.BlockSpec((share, 2 * slots), lambda i, s: (0, wide_mix // (2 * slots) - 1)), fixed(share, hidden), fixed(SMALL, high)],
            out_specs=[tile(per, high), tile(per, high), *[tile(part, width)] * 4, fixed(slots, share),
                       *[tile(part, hidden)] * 2, fixed(width, share), fixed(hidden, share), fixed(1, share),
                       fixed(1, share), fixed(1, n_gain), fixed(1, n_bias), fixed(1, 3)],
        ),
        out_shape=[
            *shapes((rows, high)), jax.ShapeDtypeStruct((rows, high), jnp.bfloat16),
            *shapes(*[(share, width)] * 4, (slots, share), (share, hidden), (share, hidden), (width, share),
                    (hidden, share), (1, share), (1, share), (1, n_gain), (1, n_bias), (1, 3)),
        ],
        compiler_params=pltpu.CompilerParams(dimension_semantics=("arbitrary",), vmem_limit_bytes=LIMIT),
        cost_estimate=pl.CostEstimate(flops=10**7, bytes_accessed=1 << 20, transcendentals=0),
        name="last_stage",
    )(seq_pos, input_grad, outputs, grad_gu, grad_mix, grad_mix, grad_mix, grad_down, small)


def first_kernel(*refs):
    (out_w, q, k, v, go, *small), mix_ref, (wide_buf, mix, *bufs, turned, sem) = refs[:10], refs[10], refs[11:]
    width = q.shape[1]
    f32 = jnp.float32
    loads = Loads(sem)
    load_out = loads.add(out_w, wide_buf)
    load_small = [loads.add(src, dst) for src, dst in zip(small, bufs)]
    pieces = [loads.add(piece, mix.at[:, pl.ds((at + 1) * width, width)]) for at, piece in enumerate((q, k, v, go))]
    turned[...] = jnp.zeros_like(turned)
    for load in load_small:
        load.wait()
    forget, one, two, head, bias = bufs
    slots, n = forget.shape[0], head.shape[1]
    turned[:slots, :] = forget[...].astype(f32)
    turned[slots : slots + 1, :] = one[...].astype(f32)
    turned[slots + 1 : slots + 2, :] = two[...].astype(f32)
    turned[slots + 2 : slots + 3, :n] = head[...].astype(f32)
    turned[slots + 2 : slots + 3, n : n + bias.shape[1]] = bias[...].astype(f32)
    mix[:, 5 * width :] = jnp.transpose(turned[...]).astype(jnp.bfloat16)
    load_out.wait()
    mix[:, :width] = jnp.transpose(wide_buf[...])
    for piece in pieces:
        piece.wait()
    loads.add(mix, mix_ref).wait()


def first_stage(out_w, q, k, v, go, forget, one, two, head, bias):
    share, width = q.shape
    wide = 2 * forget.shape[0]
    buf = lambda one: pltpu.VMEM(one.shape, jnp.bfloat16)
    return pl.pallas_call(
        first_kernel,
        in_specs=[FAR] * 10,
        out_specs=FAR,
        out_shape=jax.ShapeDtypeStruct((share, 5 * width + wide), jnp.bfloat16),
        scratch_shapes=[
            buf(out_w), pltpu.VMEM((share, 5 * width + wide), jnp.bfloat16), *[buf(one) for one in (forget, one, two, head, bias)],
            pltpu.VMEM((wide, share), jnp.float32), pltpu.SemaphoreType.DMA((12,)),
        ],
        compiler_params=pltpu.CompilerParams(vmem_limit_bytes=LIMIT),
        cost_estimate=pl.CostEstimate(flops=10**6, bytes_accessed=1 << 20, transcendentals=0),
        name="first_stage",
    )(out_w, q, k, v, go, forget, one, two, head, bias)


def ffn_fwd_kernel(x_ref, w_ref, slopes_ref, hidden_ref):
    half = x_ref.shape[0] // 2
    for rows in (slice(0, half), slice(half, 2 * half)):
        value = mm(x_ref[rows, :], w_ref[...], NN)
        gate, up = value[:, :128], value[:, 128:]
        sigma = jax.nn.sigmoid(gate)
        swish = gate * sigma
        slopes_ref[rows, :128] = (up * (sigma + swish * (1.0 - sigma))).astype(jnp.bfloat16)
        slopes_ref[rows, 128:] = swish.astype(jnp.bfloat16)
        hidden_ref[rows, :] = (swish * up).astype(jnp.bfloat16)


def ffn_fwd(x, weight):
    rows, width = x.shape
    wide = weight.shape[1]
    return pl.pallas_call(
        ffn_fwd_kernel,
        grid=(wide // 256,),
        in_specs=[pl.BlockSpec((rows, width), lambda j: (0, 0)), pl.BlockSpec((width, 256), lambda j: (0, j))],
        out_specs=[pl.BlockSpec((rows, 256), lambda j: (0, j)), pl.BlockSpec((rows, 128), lambda j: (0, j))],
        out_shape=[
            jax.ShapeDtypeStruct((rows, wide), jnp.bfloat16),
            jax.ShapeDtypeStruct((rows, wide // 2), jnp.bfloat16),
        ],
        compiler_params=pltpu.CompilerParams(dimension_semantics=("arbitrary",), vmem_limit_bytes=LIMIT),
        cost_estimate=pl.CostEstimate(flops=10**9, bytes_accessed=1 << 20, transcendentals=0),
        name="ffn_fwd",
    )(x, weight)


def ffn_bwd_kernel(grad_ref, w_ref, slopes_ref, out_ref):
    half = grad_ref.shape[0] // 2
    for rows in (slice(0, half), slice(half, 2 * half)):
        value = mm(grad_ref[rows, :], w_ref[...], NN)
        for p in range(4):
            here = slice(p * 128, (p + 1) * 128)
            grad = value[:, p // 2 * 128 : (p // 2 + 1) * 128]
            out_ref[rows, here] = (grad * slopes_ref[rows, here].astype(jnp.float32)).astype(jnp.bfloat16)


def ffn_bwd(grad, weight, gu):
    rows, width = grad.shape
    wide = gu.shape[1]
    return pl.pallas_call(
        ffn_bwd_kernel,
        grid=(pl.cdiv(wide, 512),),
        in_specs=[
            pl.BlockSpec((rows, width), lambda j: (0, 0)),
            pl.BlockSpec((width, 256), lambda j: (0, j)),
            pl.BlockSpec((rows, 512), lambda j: (0, j)),
        ],
        out_specs=pl.BlockSpec((rows, 512), lambda j: (0, j)),
        out_shape=jax.ShapeDtypeStruct((rows, wide), jnp.bfloat16),
        compiler_params=pltpu.CompilerParams(dimension_semantics=("arbitrary",), vmem_limit_bytes=LIMIT),
        cost_estimate=pl.CostEstimate(flops=10**9, bytes_accessed=1 << 20, transcendentals=0),
        name="ffn_bwd",
    )(grad, weight, gu)


def after(values, *earlier):
    return lax.optimization_barrier((values, earlier))[0]


def turn(array, head_pos):
    blocks = array.reshape((BLOCKS, array.shape[0] // BLOCKS) + array.shape[1:])
    picked = [lax.dynamic_index_in_dim(blocks, head_pos ^ k, 0, keepdims=False) for k in range(BLOCKS)]
    return jnp.concatenate(picked, axis=0)


def rms_scale(values):
    return lax.rsqrt(jnp.mean(values * values, axis=-1, keepdims=True) + EPSILON)


def on_device(seq_count, tokens, cotangent, counts, pads, norm1_gain, w_query, w_key, w_value, w_gate_out,
              w_forget, forget_bias, out_gain, w_out, norm2_gain, w_gate, w_up, w_down):
    f32, b16 = jnp.float32, jnp.bfloat16
    rows, model_width = tokens.shape[1:]
    head_pos = lax.axis_index("head")
    head_arr = head_pos.reshape(1).astype(jnp.int32)
    width, slots, hidden_width = w_query.shape[1], w_forget.shape[1], w_gate.shape[1]
    share = w_query.shape[0]
    extra = slots
    size = rows // BLOCKS

    wide = 4 * width
    own_mix = first_stage(
        w_out, w_query, w_key, w_value, w_gate_out, w_forget.T, norm1_gain[None], norm2_gain[None], out_gain[None],
        forget_bias[None],
    )
    mix = lax.all_gather(own_mix, "seq", axis=0, tiled=True)
    own_gu = jnp.stack([w_gate.reshape(share, -1, 128), w_up.reshape(share, -1, 128)], axis=2).reshape(share, -1)
    gu_weight = lax.all_gather(own_gu, "seq", axis=0, tiled=True)
    down_weight = lax.all_gather(w_down.T, "seq", axis=0, tiled=True)

    skip = width
    f_at, extra_at = skip + wide, skip + wide + slots
    gains = mix[:, extra_at : extra_at + 3].astype(f32)
    gain_one, gain_two = gains[:, 0], gains[:, 1]
    small_all = gains[:, 2].reshape(seq_count, share)
    n_gain, n_bias = out_gain.shape[0], forget_bias.shape[0]
    gain_head = small_all[:, :n_gain].reshape(1, width)
    bias = small_all[:, n_gain : n_gain + n_bias].reshape(slots, 1)

    x_rel = turn(tokens[0], head_pos)
    cot_rel = turn(cotangent[0], head_pos)
    block_of = jnp.arange(BLOCKS, dtype=jnp.int32) ^ head_pos
    position = (block_of[:, None] * size + jnp.arange(size, dtype=jnp.int32)[None, :]).reshape(rows, 1)
    live_len = jnp.where(counts[0] > 0, rows - pads[0], 0)
    live = (position < live_len).astype(f32)
    live_own = live[:size]

    x_f = x_rel.astype(f32)
    scale_one = rms_scale(x_f)
    normed1 = lax.optimization_barrier((x_f * scale_one * gain_one).astype(b16))
    grad_ffn = (cot_rel.astype(f32) * live).astype(b16)
    qkvg = mm(normed1, mix[:, skip:f_at], NN).astype(b16)
    forget_t = lax.dot_general(
        mix[:, f_at:extra_at], normed1, (((0,), (1,)), ((), ())), preferred_element_type=f32
    ) + bias
    log_keep = jax.nn.log_sigmoid(forget_t) / DAMPING
    keep_in = -jnp.expm1(log_keep)
    gated, mixed, probs, kst, vst = rec_fwd(head_arr, qkvg, log_keep, keep_in, gain_head)

    row_one, row_two = gain_one[None], gain_two[None]
    x_own = x_rel[:size]
    cot_own = cot_rel[:size]
    tall = lambda kind: jax.ShapeDtypeStruct((size, model_width), kind)
    line = jax.ShapeDtypeStruct((1, model_width), f32)
    seq_pos = lax.axis_index("seq")
    residual, normed_own, x_squares, mix_squares, live_sum = head_scatter(
        gated, mix, [x_own], [row_two, live_own], [tall(f32), tall(b16), line, line, line], finish_mixer, 0
    )
    normed2, normed2_t, normed1_t = head_gather(normed_own, 1, also=normed1)
    gu, hidden = ffn_fwd(normed2.reshape(rows, model_width), gu_weight)

    grad_down = mm(grad_ffn, hidden, TN).astype(b16).reshape(-1, 2, share, hidden_width)
    core = seq_pos % 2
    kept = lax.dynamic_index_in_dim(grad_down, core, 1, keepdims=False)
    given = lax.dynamic_index_in_dim(grad_down, 1 - core, 1, keepdims=False)
    given = lax.ppermute(given, "seq", [(i, i ^ 1) for i in range(seq_count)])
    grad_down = (kept.astype(f32) + given.astype(f32)).astype(b16).reshape(-1, hidden_width)
    down_weight = after(down_weight, grad_down)
    lines = [list(range(c, seq_count, 2)) for c in range(2)]

    def line_scatter(array):
        return lax.psum_scatter(array, "seq", scatter_dimension=0, tiled=True, axis_index_groups=lines)

    grad_down = line_scatter(grad_down)
    grad_gu = ffn_bwd(grad_ffn, down_weight, gu)
    high = model_width // 2
    grad_residual, grad_low, grad_gain_two, grad_gu_w = head_scatter(
        grad_gu, gu_weight, [normed2_t, residual, cot_own], [live_own, row_two], [tall(f32), tall(b16), line],
        finish_norm_two, 2, filler=fill_gu, filled=[jax.ShapeDtypeStruct((high, gu_weight.shape[1]), b16)],
        scratch=tile_scratch(model_width, gu_weight.shape[1], share, 0),
    )
    grad_gu_w = line_scatter(grad_gu_w)
    grad_att_t, grad_gated = head_gather(grad_low, 3, keep=False, weight=mix, width=width)
    grad_gated = after(grad_gated, grad_down)
    wide_in = wide + slots + extra
    states = [pltpu.VMEM((slots, width), f32), pltpu.VMEM((slots, width), f32), pltpu.VMEM((slots, 1), f32)]
    out_own, ffn_squares, grad_gain_head, grad_bias, grad_in, grad_mix = head_scatter(
        hidden, down_weight,
        [qkvg, grad_gated, mixed, probs, kst, vst, log_keep, keep_in, forget_t, jnp.asarray(span_matrix(), b16), gain_head,
         residual, grad_att_t, gated, normed1_t],
        [live_own], [tall(b16), line, jax.ShapeDtypeStruct((1, width), f32), jax.ShapeDtypeStruct((slots, 1), f32)],
        finish_ffn, 4, filler=fill_mix,
        filled=[jax.ShapeDtypeStruct((rows, wide_in), b16),
                jax.ShapeDtypeStruct((high, mix.shape[1]), b16)],
        scratch=[pltpu.VMEM((rows, wide_in), b16), pltpu.SemaphoreType.DMA((1,)), *states,
                 *tile_scratch(model_width, mix.shape[1], share, 1)],
    )
    grad_mix = line_scatter(grad_mix)
    hops = 2 + seq_count.bit_length() - 1
    outputs, input_grad, small = tail_stage(
        hops, skip, grad_in, mix, normed1, x_rel, grad_residual, out_own,
        (row_one, grad_gain_two, x_squares, mix_squares, ffn_squares, live_sum, grad_gain_head, grad_bias), 6,
    )
    (input_grad, outputs, grad_q, grad_k, grad_v, grad_go, grad_f, grad_gate, grad_up, grad_wo, grad_wd, grad_one,
     grad_two, grad_head, grad_fb, rms) = last_stage(
        seq_pos.reshape(1).astype(jnp.int32), seq_count, input_grad.reshape(rows, model_width),
        outputs.reshape(rows, model_width), grad_gu_w, grad_mix, grad_down, small, width, slots, n_gain, n_bias,
    )
    return (
        outputs[None], input_grad[None], grad_one[0], grad_q, grad_k, grad_v, grad_go, grad_f.T, grad_fb[0], grad_head[0],
        grad_wo, grad_two[0], grad_gate, grad_up, grad_wd, rms[0],
    )


def solution(mesh):
    both = P("seq", "head")
    flat = P(("head", "seq"))
    rows = P("seq", None, None)
    return jax.shard_map(
        functools.partial(on_device, mesh.shape["seq"]),
        mesh=mesh,
        in_specs=(rows, rows, P("seq"), P("seq"), P("seq"), both, both, both, both, both, flat, flat,
                  P("head", "seq"), P("seq"), both, both, P("head", "seq")),
        out_specs=(rows, rows, P("seq"), both, both, both, both, both, flat, flat, P("head", "seq"), P("seq"),
                   both, both, P("head", "seq"), P()),
        check_vma=False,
    )
```

```python
import functools

import jax
import jax.numpy as jnp
import numpy as np
from jax import lax
from jax.experimental import pallas as pl
from jax.experimental.pallas import tpu as pltpu
from jax.sharding import PartitionSpec as P

EPSILON = 1e-06
DAMPING = 8.0
TILE = 128
BLOCKS = 4
HALVES = (64, 32, 16, 8, 4, 2, 1)
NT = (((1,), (1,)), ((), ()))
NN = (((1,), (0,)), ((), ()))
TN = (((0,), (0,)), ((), ()))


def rel_tile(rows, i, h):
    per = rows // BLOCKS // TILE
    return (i // per ^ h[0]) * per + i % per


def mm(left, right, dims):
    return lax.dot_general(left, right, dims, preferred_element_type=jnp.float32)


def span_matrix():
    r = np.arange(TILE)[:, None]
    t = np.arange(TILE)[None, :]
    parts = []
    for h in HALVES:
        base = t // (2 * h) * (2 * h)
        upper = t % (2 * h) >= h
        parts.append(upper & (r >= base + h) & (r <= t))
        parts.append(~upper & (r > t) & (r <= base + h - 1))
    parts.append(r <= t)
    parts.append(r > t)
    return np.concatenate(parts, axis=1).astype(np.float32)


def level_of():
    s = lax.broadcasted_iota(jnp.int32, (TILE, TILE), 0)
    t = lax.broadcasted_iota(jnp.int32, (TILE, TILE), 1)
    return jnp.where(s < t, s ^ t, jnp.where(s == t, 0, -1))


def level_masks():
    x = level_of()
    masks = [(x >= h) & (x < 2 * h) for h in HALVES]
    masks.append(x == 0)
    return masks


def decays(log_keep, keep_in, spans):
    slots = log_keep.shape[0]
    high = log_keep.astype(jnp.bfloat16)
    rest = log_keep - high.astype(jnp.float32)
    mid = rest.astype(jnp.bfloat16)
    both = mm(jnp.concatenate([high, mid], axis=0), spans, NN)
    grown = jnp.exp(both[:slots] + both[slots:])
    n = len(HALVES)
    ones = jnp.ones_like(keep_in)
    e_parts = [grown[:, (2 * i) * TILE : (2 * i + 1) * TILE] for i in range(n)] + [ones]
    f_bare = [grown[:, (2 * i + 1) * TILE : (2 * i + 2) * TILE] for i in range(n)] + [ones]
    e_all = grown[:, 2 * n * TILE : (2 * n + 1) * TILE]
    f_all = grown[:, (2 * n + 1) * TILE : (2 * n + 2) * TILE]
    total = e_all[:, TILE - 1 : TILE]
    return e_parts, f_bare, e_all, f_all, total


def norm_gate(mixed, gain, gate_pre):
    scale = lax.rsqrt(jnp.mean(mixed * mixed, axis=-1, keepdims=True) + EPSILON)
    unit = mixed * scale
    return scale, unit


def fwd_kernel(h_ref, q_ref, k_ref, v_ref, g_ref, lk_ref, w_ref, gain_ref, spans_ref,
               gated_ref, mixed_ref, probs_ref, kst_ref, vst_ref, kacc, vacc):
    @pl.when(pl.program_id(0) == 0)
    def _():
        kacc[...] = jnp.zeros_like(kacc)
        vacc[...] = jnp.zeros_like(vacc)
    width = q_ref.shape[1]
    root = width ** -0.5
    q, k, v = q_ref[...], k_ref[...], v_ref[...]
    keep_in = w_ref[...]
    e_parts, f_bare, e_all, f_all, total = decays(lk_ref[...], keep_in, spans_ref[...])
    masks = level_masks()
    kst, vst = kacc[...], vacc[...]
    kst_b, vst_b = kst.astype(jnp.bfloat16), vst.astype(jnp.bfloat16)
    kst_ref[0] = kst_b
    vst_ref[0] = vst_b
    inner = mm(k, q, NT) * root
    inner_b = inner.astype(jnp.bfloat16)
    zero_b = jnp.zeros_like(inner_b)
    f_parts = [(bare * keep_in).astype(jnp.bfloat16) for bare in f_bare]
    scores = e_all * (mm(kst_b, q, NT) * root)
    for mask, grow, fade in zip(masks, e_parts, f_parts):
        scores += grow * mm(fade, jnp.where(mask, inner_b, zero_b), NN)
    top = jnp.max(scores, axis=0, keepdims=True)
    raised = jnp.exp(scores - top)
    probs = raised / jnp.sum(raised, axis=0, keepdims=True)
    probs_ref[...] = probs
    mixing = jnp.zeros((TILE, TILE), jnp.float32)
    for mask, grow, fade in zip(masks, e_parts, f_parts):
        mixing = jnp.where(mask, mm(fade, (probs * grow).astype(jnp.bfloat16), TN), mixing)
    mixed = mm(mixing.astype(jnp.bfloat16), v, TN) + mm((probs * e_all).astype(jnp.bfloat16), vst_b, TN)
    tail = (f_all * keep_in).astype(jnp.bfloat16)
    kacc[...] = total * kst + mm(tail, k, NN)
    vacc[...] = total * vst + mm(tail, v, NN)
    mixed_ref[...] = mixed
    scale = lax.rsqrt(jnp.mean(mixed * mixed, axis=-1, keepdims=True) + EPSILON)
    gate = g_ref[...].astype(jnp.float32)
    swish = gate * jax.nn.sigmoid(gate)
    gated_ref[...] = (mixed * scale * gain_ref[...] * swish).astype(jnp.bfloat16)


def rec_fwd(head, qkvg, log_keep_t, keep_in_t, gain):
    rows, wide = qkvg.shape
    width = wide // 4
    slots = log_keep_t.shape[0]
    tiles = rows // TILE
    spans = jnp.asarray(span_matrix(), jnp.bfloat16)
    place = functools.partial(rel_tile, rows)
    col = lambda j: pl.BlockSpec((TILE, width), lambda i, h: (place(i, h), j))
    lane = pl.BlockSpec((slots, TILE), lambda i, h: (0, place(i, h)))
    state = pl.BlockSpec((1, slots, width), lambda i, h: (i, 0, 0))
    return pl.pallas_call(
        fwd_kernel,
        grid_spec=pltpu.PrefetchScalarGridSpec(
            num_scalar_prefetch=1,
            grid=(tiles,),
            in_specs=[col(0), col(1), col(2), col(3), lane, lane,
                      pl.BlockSpec((1, width), lambda i, h: (0, 0)),
                      pl.BlockSpec(spans.shape, lambda i, h: (0, 0))],
            out_specs=[col(0), col(0), lane, state, state],
            scratch_shapes=[pltpu.VMEM((slots, width), jnp.float32)] * 2,
        ),
        out_shape=[
            jax.ShapeDtypeStruct((rows, width), jnp.bfloat16),
            jax.ShapeDtypeStruct((rows, width), jnp.float32),
            jax.ShapeDtypeStruct((slots, rows), jnp.float32),
            jax.ShapeDtypeStruct((tiles, slots, width), jnp.bfloat16),
            jax.ShapeDtypeStruct((tiles, slots, width), jnp.bfloat16),
        ],
        compiler_params=pltpu.CompilerParams(dimension_semantics=("arbitrary",), vmem_limit_bytes=60 << 20),
        cost_estimate=pl.CostEstimate(flops=5 * 10**9, bytes_accessed=10 << 20, transcendentals=0),
        name="slot_fwd",
    )(head, qkvg, qkvg, qkvg, qkvg, log_keep_t, keep_in_t, gain, spans)


def bwd_tile(step, q_ref, k_ref, v_ref, g_ref, lk_ref, w_ref, fpre_ref, gain_ref, spans_ref,
               mixed_ref, probs_ref, kst_ref, vst_ref, dg_ref,
               dproj_ref, dgain_ref, dbias_ref, dk_acc, dv_acc, cross):
    width = q_ref.shape[1]
    slots = lk_ref.shape[0]

    @pl.when(step == 0)
    def _():
        dk_acc[...] = jnp.zeros_like(dk_acc)
        dv_acc[...] = jnp.zeros_like(dv_acc)
        cross[...] = jnp.zeros_like(cross)
        dgain_ref[...] = jnp.zeros_like(dgain_ref)
        dbias_ref[...] = jnp.zeros_like(dbias_ref)
    root = width ** -0.5
    q, k, v = q_ref[...], k_ref[...], v_ref[...]
    mixed = mixed_ref[...]
    gate = g_ref[...].astype(jnp.float32)
    gain = gain_ref[...]
    d_gated = dg_ref[...].astype(jnp.float32)
    scale = lax.rsqrt(jnp.mean(mixed * mixed, axis=-1, keepdims=True) + EPSILON)
    unit = mixed * scale
    sigma = jax.nn.sigmoid(gate)
    swish = gate * sigma
    slope = sigma * (1.0 + gate * (1.0 - sigma))
    dproj_ref[:, 3 * width : 4 * width] = (d_gated * unit * gain * slope).astype(jnp.bfloat16)
    d_normed = d_gated * swish
    dgain_ref[...] += jnp.sum(d_normed * unit, axis=0, keepdims=True)
    c = d_normed * gain
    d_mixed = scale * (c - unit * jnp.mean(c * unit, axis=-1, keepdims=True))
    d_out = d_mixed.astype(jnp.bfloat16)

    log_keep, keep_in = lk_ref[...], w_ref[...]
    e_parts, f_bare, e_all, f_all, total = decays(log_keep, keep_in, spans_ref[...])
    masks = level_masks()
    probs = probs_ref[...]
    kst, vst = kst_ref[0], vst_ref[0]
    dkst, dvst = dk_acc[...], dv_acc[...]
    dkst_b, dvst_b = dkst.astype(jnp.bfloat16), dvst.astype(jnp.bfloat16)

    inner_b = (mm(k, q, NT) * root).astype(jnp.bfloat16)
    d_mixing_b = mm(v, d_out, NT).astype(jnp.bfloat16)
    pair = jnp.concatenate([inner_b, d_mixing_b], axis=1)
    zero_b = jnp.zeros_like(pair)
    masks2 = [jnp.concatenate([mask, mask], axis=1) for mask in masks]
    pairs = [jnp.where(mask, pair, zero_b) for mask in masks2]
    f_parts = [(bare * keep_in).astype(jnp.bfloat16) for bare in f_bare]
    both = [mm(fade, two, NN) for fade, two in zip(f_parts, pairs)]
    s_state = mm(kst, q, NT) * root
    p_state = mm(vst, d_out, NT)
    d_probs = e_all * p_state
    for grow, two in zip(e_parts, both):
        d_probs += grow * two[:, TILE:]
    d_scores = probs * (d_probs - jnp.sum(probs * d_probs, axis=0, keepdims=True))

    xy_all = jnp.concatenate([d_scores * e_all, probs * e_all], axis=1).astype(jnp.bfloat16)
    xy_parts = [jnp.concatenate([d_scores * grow, probs * grow], axis=1).astype(jnp.bfloat16) for grow in e_parts]
    x0 = xy_all[:, :TILE]
    y0 = xy_all[:, TILE:]
    change = x0.astype(jnp.float32) * s_state + y0.astype(jnp.float32) * p_state
    into = jnp.zeros((slots, TILE), jnp.float32)
    d_both = jnp.zeros((TILE, 2 * TILE), jnp.float32)
    for i, (grow, bare, fade, two, xy, part, mask) in enumerate(
        zip(e_parts, f_bare, f_parts, both, xy_parts, pairs, masks2)
    ):
        z = mm(xy, part, NT)
        into += bare * z
        if i < len(HALVES):
            mass = xy.astype(jnp.float32) * two
            change += mass[:, :TILE] + mass[:, TILE:] - fade.astype(jnp.float32) * z
        d_both = jnp.where(mask, mm(fade, xy, TN), d_both)
    d_both_b = d_both.astype(jnp.bfloat16)
    d_inner, mixing = d_both_b[:, :TILE], d_both_b[:, TILE:]
    tail = (f_all * keep_in).astype(jnp.bfloat16)
    z_state = mm(dkst_b, k, NT) + mm(dvst_b, v, NT)
    into += f_all * z_state
    change -= tail.astype(jnp.float32) * z_state

    dproj_ref[:, :width] = (root * (mm(d_inner, k, TN) + mm(x0, kst, TN))).astype(jnp.bfloat16)
    dproj_ref[:, width : 2 * width] = (root * mm(d_inner, q, NN) + mm(tail, dkst_b, TN)).astype(jnp.bfloat16)
    dproj_ref[:, 2 * width : 3 * width] = (mm(mixing, d_out, NN) + mm(tail, dvst_b, TN)).astype(jnp.bfloat16)

    later = (lax.broadcasted_iota(jnp.int32, (TILE, TILE), 0) >= lax.broadcasted_iota(jnp.int32, (TILE, TILE), 1)).astype(jnp.bfloat16)
    high = change.astype(jnp.bfloat16)
    rest = change - high.astype(jnp.float32)
    mid = rest.astype(jnp.bfloat16)
    low = (rest - mid.astype(jnp.float32)).astype(jnp.bfloat16)
    sums = mm(jnp.concatenate([high, mid, low], axis=0), later, NN)
    d_log_keep = sums[:slots] + sums[slots : 2 * slots] + sums[2 * slots :] + cross[...] - jnp.exp(log_keep) * into
    d_forget = (d_log_keep * jax.nn.sigmoid(-fpre_ref[...]) / DAMPING).astype(jnp.bfloat16)
    dbias_ref[...] += jnp.sum(d_forget.astype(jnp.float32), axis=1, keepdims=True)
    turned = jnp.transpose(d_forget.astype(jnp.float32))
    dproj_ref[:, 4 * width :] = jnp.concatenate([turned, jnp.zeros_like(turned)], axis=1).astype(jnp.bfloat16)

    dkst_new = total * dkst + root * mm(x0, q, NN)
    dvst_new = total * dvst + mm(y0, d_out, NN)
    dk_acc[...] = dkst_new
    dv_acc[...] = dvst_new
    cross[...] = jnp.sum(kst.astype(jnp.float32) * dkst_new + vst.astype(jnp.float32) * dvst_new, axis=1, keepdims=True)


MESH = pl.DeviceIdType.MESH
CHUNK = 32


def neighbours():
    head = lax.axis_index("head")
    return {"head": head + 1 - 2 * (head % 2)}, {"head": (head + 2) % BLOCKS}


def flipped(index, bit):
    return index + bit - 2 * bit * (index // bit % 2)


def other_core():
    return {"seq": flipped(lax.axis_index("seq"), 1)}


def greet(targets):
    barrier = pltpu.get_barrier_semaphore()
    for target in targets:
        pl.semaphore_signal(barrier, inc=1, device_id=target, device_id_type=MESH)
    pl.semaphore_wait(barrier, len(targets))


LIMIT = 60 << 20
FAR = pl.BlockSpec(memory_space=pl.ANY)
WHOLE = pl.BlockSpec(memory_space=pltpu.VMEM)


class Loads:
    def __init__(self, sem):
        self.sem, self.copies = sem, []

    def add(self, src, dst):
        copy = pltpu.make_async_copy(src, dst, self.sem.at[len(self.copies)])
        copy.start()
        self.copies.append(copy)
        return copy


class Scatter:
    order = (0, 2, 1, 3)

    def __init__(self, left, right, acc, mid, send, got, send_sem, got_sem):
        self.left, self.right, self.acc, self.mid, self.send, self.got = left, right, acc, mid, send, got
        self.size, self.cols = send.shape[1:]
        to_x, to_y = neighbours()
        self.copies = []
        for u in range(2):
            for k, to in enumerate((to_x, to_x, to_y, to_y, to_y, to_x)):
                slot = 6 * u + k
                self.copies.append(
                    pltpu.make_async_remote_copy(
                        src_ref=send.at[slot], dst_ref=got.at[slot], send_sem=send_sem.at[slot],
                        recv_sem=got_sem.at[slot], device_id=to, device_id_type=MESH,
                    )
                )

    def first(self, loads, watch=None):
        size, cols = self.size, self.cols
        for part, load in zip(self.order, loads):
            load.wait()
            value = mm(self.left[...], self.right[part * cols : (part + 1) * cols, :], NT)
            side_at, u = part // 2, part % 2
            here = slice(part * cols, (part + 1) * cols)
            slot = 6 * u + 2 * side_at
            near_block, mid_block = (1, 2) if side_at == 0 else (2, 1)
            self.acc[:, here] = value[:size]
            self.mid[:, here] = value[mid_block * size : (mid_block + 1) * size]
            self.send[slot] = value[3 * size :].astype(jnp.bfloat16)
            self.copies[slot].start()
            self.send[slot + 1] = value[near_block * size : (near_block + 1) * size].astype(jnp.bfloat16)
            self.copies[slot + 1].start()
            if watch is not None:
                watch(here, value)

    def second(self, u):
        cols = self.cols
        for side_at in range(2):
            part = 2 * side_at + u
            first, second = 6 * u + 2 * side_at, 6 * u + 4 + side_at
            here = slice(part * cols, (part + 1) * cols)
            self.copies[first].wait_recv()
            self.send[second] = (self.mid[:, here] + self.got[first].astype(jnp.float32)).astype(jnp.bfloat16)
            self.copies[second].start()

    def last(self, finish):
        for u in range(2):
            for k in (1, 3, 4, 5):
                self.copies[6 * u + k].wait_recv()
        cols = self.cols

        def rows(i, carry):
            here = pl.ds(pl.multiple_of(i * CHUNK, CHUNK), CHUNK)
            sums = []
            for part in range(4):
                side_at, u = part // 2, part % 2
                one, two = self.got[6 * u + 2 * side_at + 1, here, :], self.got[6 * u + 4 + side_at, here, :]
                own = self.acc[here, part * cols : (part + 1) * cols]
                sums.append(own + one.astype(jnp.float32) + two.astype(jnp.float32))
            finish(here, jnp.concatenate(sums, axis=1), i)
            return carry

        lax.fori_loop(0, self.size // CHUNK, rows, 0)

    def close(self):
        for one in self.copies:
            one.wait_send()


def scatter_scratch(rows, depth, high):
    size, cols = rows // BLOCKS, high // 4
    return [
        pltpu.VMEM((rows, depth), jnp.bfloat16),
        pltpu.VMEM((high, depth), jnp.bfloat16),
        pltpu.VMEM((size, high), jnp.float32),
        pltpu.VMEM((size, high), jnp.float32),
        pltpu.VMEM((12, size, cols), jnp.bfloat16),
        pltpu.VMEM((12, size, cols), jnp.bfloat16),
        pltpu.SemaphoreType.DMA((12,)),
        pltpu.SemaphoreType.DMA((12,)),
    ]


def load_parts(loads, right_far, right, skip):
    cols = right.shape[0] // 4
    parts = []
    for part in Scatter.order:
        here = pl.ds(part * cols, cols)
        parts.append(loads.add(right_far.at[here, pl.ds(skip, right.shape[1])], right.at[here, :]))
    return parts


def scatter_kernel(plan, *refs):
    n_far, n_near, n_out, skip, finish, filler = plan
    left_far, right_far, *more_far = refs[:n_far]
    near = refs[n_far : n_far + n_near]
    outs = refs[n_far + n_near : n_far + n_near + n_out]
    load_sem, *rest = refs[n_far + n_near + n_out :]
    scatter, spare = rest[:8], rest[8:]
    left, right = scatter[:2]
    loads = Loads(load_sem)
    load_left = loads.add(left_far, left)
    parts = load_parts(loads, right_far, right, skip)
    more = [(loads.add(src, dst), dst) for src, dst in zip(more_far, spare)]
    spare = spare[len(more_far) :]
    greet(neighbours() if filler is None else (*neighbours(), other_core()))
    sum_heads = Scatter(*scatter)
    load_left.wait()
    sum_heads.first(parts)
    sum_heads.second(0)
    for load, _ in more:
        load.wait()
    side = [dst for _, dst in more]
    if filler is not None:
        steps = filler(left, right, side, outs, spare)
        next(steps)
        sum_heads.second(1)
        for _ in steps:
            pass
    else:
        sum_heads.second(1)
    sum_heads.last(lambda here, total, i: finish(here, total, side, near, outs, i))
    sum_heads.close()


def head_scatter(left, right, far, near, out_shapes, finish, number, filler=None, filled=(), scratch=()):
    rows, depth = left.shape
    plan = (2 + len(far), len(near), len(out_shapes) + len(filled), 0, finish, filler)
    return pl.pallas_call(
        functools.partial(scatter_kernel, plan),
        in_specs=[FAR] * (2 + len(far)) + [WHOLE] * len(near),
        out_specs=[WHOLE] * len(out_shapes) + [FAR] * len(filled),
        out_shape=[*out_shapes, *filled],
        scratch_shapes=[
            pltpu.SemaphoreType.DMA((5 + len(far),)),
            *scatter_scratch(rows, depth, right.shape[0]),
            *[pltpu.VMEM(one.shape, one.dtype) for one in far],
            *scratch,
        ],
        compiler_params=pltpu.CompilerParams(collective_id=number, has_side_effects=True, vmem_limit_bytes=LIMIT),
        cost_estimate=pl.CostEstimate(flops=10**9, bytes_accessed=1 << 20, transcendentals=0),
        name="head_scatter%d" % number,
    )(left, right, *far, *near)


STEP = 512


def weight_tiles(pairs, place, out_ref, room, land, store_sem, send_sem, got_sem, pause=None):
    count, share = land.shape[:2]
    high = 2 * count * share
    core = lax.axis_index("seq") % 2
    per = STEP // (2 * share)

    def row(p, at):
        return (2 * p + at) * share % room.shape[0]

    def swap_shard(p):
        return pltpu.make_async_remote_copy(
            src_ref=room.at[pl.ds(row(p, 0) + (1 - core) * share, share), :], dst_ref=land.at[p],
            send_sem=send_sem.at[p], recv_sem=got_sem.at[p], device_id=other_core(), device_id_type=MESH,
        )

    def store(p):
        return pltpu.make_async_copy(land.at[p], out_ref.at[pl.ds(p * share, share), :], store_sem.at[p])

    def settle(p):
        swap_shard(p).wait_recv()
        own = room[pl.ds(pl.multiple_of(row(p, 0) + core * share, share), share), :]
        land[p] = (own.astype(jnp.float32) + land[p].astype(jnp.float32)).astype(jnp.bfloat16)
        store(p).start()

    sent = []
    for i in range(high // STEP):
        here = slice(i * STEP, (i + 1) * STEP)
        there = slice(i * STEP % room.shape[0], i * STEP % room.shape[0] + STEP)
        if (i + 1) * STEP > room.shape[0]:
            for p in range((i - 2) * per, (i - 1) * per):
                swap_shard(p).wait_send()
                sent.append(p)
        for turned, right, column in pairs:
            for at in range(0, right.shape[1], STEP):
                cols = min(STEP, right.shape[1] - at)
                value = mm(turned[here, :], right[:, at : at + cols], NN).astype(jnp.bfloat16)
                for src, dst, wide in place(column + at, cols):
                    room[there, dst : dst + wide] = value[:, src : src + wide]
        for p in range(i * per, (i + 1) * per):
            swap_shard(p).start()
        if i:
            for p in range((i - 1) * per, i * per):
                settle(p)
        if i == pause:
            yield
    for p in range(count - per, count):
        settle(p)
    for p in range(count):
        store(p).wait()
        if p not in sent:
            swap_shard(p).wait_send()


def tile_scratch(high, width, share, room):
    count = high // (2 * share)
    return [pltpu.VMEM((2 * STEP, width), jnp.bfloat16)] * room + [
        pltpu.VMEM((count, share, width), jnp.bfloat16),
        pltpu.SemaphoreType.DMA((count,)),
        pltpu.SemaphoreType.DMA((count,)),
        pltpu.SemaphoreType.DMA((count,)),
    ]


def fill_gu(left, right, side, outs, spare):
    half = left.shape[1] // 2

    def place(at, cols):
        return [(k, (at + k) // 256 * 128 + (at + k) // 128 % 2 * half, 128) for k in range(0, cols, 128)]

    return weight_tiles([(side[0], left, 0)], place, outs[-1], right, *spare, pause=1)


def mixed_index(block):
    head = lax.axis_index("head")
    return (block + head) % 2 + 2 * ((block // 2 + head // 2) % 2)


def fill_mix(left, right, side, outs, spare):
    qkvg, d_gated, mixed, probs, kst, vst, log_keep, keep_in, forget, spans, gain, _, att_t, gated, normed_t = side
    grad_far, gain_grad, bias_grad, out_ref = outs[-2], outs[2], outs[3], outs[-1]
    grad_in, grad_sem, dk_acc, dv_acc, cross, *spare = spare
    width = gated.shape[1]
    tiles = qkvg.shape[0] // TILE
    per = tiles // BLOCKS

    def tile(i, carry):
        at = tiles - 1 - i
        rel = mixed_index(at // per) * per + at % per
        rows = pl.ds(pl.multiple_of(rel * TILE, TILE), TILE)
        bwd_tile(
            i, *[qkvg.at[rows, pl.ds(k * width, width)] for k in range(4)], log_keep.at[:, rows], keep_in.at[:, rows],
            forget.at[:, rows], gain, spans, mixed.at[rows, :], probs.at[:, rows], kst.at[pl.ds(at, 1)],
            vst.at[pl.ds(at, 1)], d_gated.at[rows, :], grad_in.at[rows, :], gain_grad, bias_grad, dk_acc, dv_acc, cross,
        )
        return carry

    lax.fori_loop(0, tiles, tile, 0)
    keep = pltpu.make_async_copy(grad_in, grad_far, grad_sem.at[0])
    keep.start()
    yield
    place = lambda at, cols: [(0, at, cols)]
    yield from weight_tiles([(att_t, gated, 0), (normed_t, grad_in, width)], place, out_ref, *spare)
    keep.wait()


class Gather:
    def __init__(self, own, blocks, send_sem, got_sem):
        half = own.shape[1] // 2
        to_x, to_y = neighbours()

        def copy(slot, src, block, side_at, target):
            here = pl.ds(side_at * half, half)
            return pltpu.make_async_remote_copy(
                src_ref=src.at[:, here], dst_ref=blocks.at[block, :, here],
                send_sem=send_sem.at[slot], recv_sem=got_sem.at[slot], device_id=target, device_id_type=MESH,
            )

        self.copies = [
            copy(0, own, 1, 0, to_x),
            copy(1, own, 2, 1, to_y),
            copy(2, own, 1, 1, to_x),
            copy(3, own, 2, 0, to_y),
            copy(4, blocks.at[1], 3, 0, to_y),
            copy(5, blocks.at[2], 3, 1, to_x),
        ]

    def first(self):
        for one in self.copies[:4]:
            one.start()

    def second(self):
        for near, far in ((0, 4), (1, 5)):
            self.copies[near].wait_recv()
            self.copies[far].start()

    def last(self):
        for one in self.copies[2:]:
            one.wait_recv()
        for one in self.copies:
            one.wait_send()


def gather_kernel(plan, *refs):
    keep, product, also = plan
    refs = list(refs)
    own_ref = refs.pop(0)
    weight_far = refs.pop(0) if product else None
    also_far = refs.pop(0) if also else None
    out_ref = refs.pop(0) if keep else None
    turned_ref = refs.pop(0)
    product_ref = refs.pop(0) if product else None
    also_ref = refs.pop(0) if also else None
    blocks, turned_buf, send_sem, got_sem, out_sem, load_sem, *refs = refs
    size, half = own_ref.shape[0], own_ref.shape[1] // 2
    loads = Loads(load_sem)
    if product:
        weight = refs.pop(0)
        fetch = loads.add(weight_far.at[:, pl.ds(0, weight.shape[1])], weight)
    if also:
        also_buf, also_turned = refs
        fetch = loads.add(also_far, also_buf)
    greet(neighbours())
    gather = Gather(own_ref, blocks, send_sem, got_sem)
    gather.first()
    if product or also:
        fetch.wait()
    stores = []

    def store(src, dst):
        copy = pltpu.make_async_copy(src, dst, out_sem.at[len(stores)])
        copy.start()
        stores.append(copy)

    def use(block, side_at, src):
        here = slice(side_at * half, (side_at + 1) * half)
        rows = slice(block * size, (block + 1) * size)
        value = src[:, here]
        turned_buf[here, rows] = jnp.transpose(value)
        store(turned_buf.at[here, rows], turned_ref.at[here, rows])
        if keep:
            store(src.at[:, here], out_ref.at[block, :, here])
        if product:
            term = mm(value, weight[here, :], NN)
            if (block, side_at) in ((0, 0), (1, 0), (2, 1), (3, 0)):
                product_ref[rows, :] = term
            else:
                product_ref[rows, :] += term

    use(0, 0, own_ref)
    use(0, 1, own_ref)
    if also:
        also_turned[...] = jnp.transpose(also_buf[: also_buf.shape[0] // 2, :])
        middle = also_buf.shape[0] // 2
        store(also_turned, also_ref.at[:, pl.ds(0, middle)])
    gather.second()
    use(1, 0, blocks.at[1])
    use(2, 1, blocks.at[2])
    if also:
        stores[-1 - 4 * keep - 2 * (not keep)].wait()
        finished = len(stores) - 1 - 4 * keep - 2 * (not keep)
        also_turned[...] = jnp.transpose(also_buf[middle:, :])
        store(also_turned, also_ref.at[:, pl.ds(middle, middle)])
    for slot, block, side_at in ((2, 1, 1), (3, 2, 0), (4, 3, 0), (5, 3, 1)):
        gather.copies[slot].wait_recv()
        use(block, side_at, blocks.at[block])
    for at, one in enumerate(stores):
        if not also or at != finished:
            one.wait()
    for one in gather.copies:
        one.wait_send()


def head_gather(own, number, keep=True, weight=None, width=0, also=None):
    size, wide = own.shape
    rows = BLOCKS * size
    product = weight is not None
    extra = [one for one in (weight, also) if one is not None]
    out_shape, out_specs = [], []
    if keep:
        out_shape.append(jax.ShapeDtypeStruct((BLOCKS, size, wide), own.dtype))
        out_specs.append(FAR)
    out_shape.append(jax.ShapeDtypeStruct((wide, rows), own.dtype))
    out_specs.append(FAR)
    scratch = [
        pltpu.VMEM((BLOCKS, size, wide), own.dtype),
        pltpu.VMEM((wide, rows), own.dtype),
        pltpu.SemaphoreType.DMA((6,)),
        pltpu.SemaphoreType.DMA((6,)),
        pltpu.SemaphoreType.DMA((20,)),
        pltpu.SemaphoreType.DMA((2,)),
    ]
    if product:
        out_shape.append(jax.ShapeDtypeStruct((rows, width), jnp.float32))
        out_specs.append(WHOLE)
        scratch.append(pltpu.VMEM((wide, width), own.dtype))
    if also is not None:
        out_shape.append(jax.ShapeDtypeStruct(also.shape[::-1], also.dtype))
        out_specs.append(FAR)
        scratch += [pltpu.VMEM(also.shape, also.dtype), pltpu.VMEM((also.shape[1], also.shape[0] // 2), also.dtype)]
    return pl.pallas_call(
        functools.partial(gather_kernel, (keep, product, also is not None)),
        in_specs=[WHOLE] + [FAR] * len(extra),
        out_specs=out_specs,
        out_shape=out_shape,
        scratch_shapes=scratch,
        compiler_params=pltpu.CompilerParams(collective_id=number, has_side_effects=True, vmem_limit_bytes=LIMIT),
        cost_estimate=pl.CostEstimate(flops=10**9, bytes_accessed=1 << 20, transcendentals=0),
        name="head_gather%d" % number,
    )(own, *extra)


def unit_of(values):
    scale = lax.rsqrt(jnp.mean(values * values, axis=-1, keepdims=True) + EPSILON)
    return scale, values * scale


def finish_mixer(here, total, side, near, outs, i):
    x = side[0][here, :].astype(jnp.float32)
    gain, live = near[0][...], near[1][here, :]
    residual = x + total
    outs[0][here, :] = residual
    outs[1][here, :] = (unit_of(residual)[1] * gain).astype(jnp.bfloat16)
    add_row(outs[2], jnp.sum(live * x * x, axis=0, keepdims=True), i)
    add_row(outs[3], jnp.sum(live * total * total, axis=0, keepdims=True), i)
    add_row(outs[4], jnp.sum(live / x.shape[1] + jnp.zeros_like(x), axis=0, keepdims=True), i)


def add_row(ref, row, i):
    @pl.when(i == 0)
    def _():
        ref[...] = jnp.zeros_like(ref)

    ref[...] += row


def norm_back(total, gain, scale, unit):
    c = total * gain
    return scale * (c - unit * jnp.mean(c * unit, axis=-1, keepdims=True))


def finish_norm_two(here, total, side, near, outs, i):
    residual, cot = side[1][here, :], side[2][here, :].astype(jnp.float32)
    live, gain = near[0][here, :], near[1][...]
    scale, unit = unit_of(residual)
    add_row(outs[2], jnp.sum(total * unit, axis=0, keepdims=True), i)
    grad = cot * live + norm_back(total, gain, scale, unit)
    outs[0][here, :] = grad
    outs[1][here, :] = grad.astype(jnp.bfloat16)


def finish_ffn(here, total, side, near, outs, i):
    live = near[0][here, :]
    add_row(outs[1], jnp.sum(live * total * total, axis=0, keepdims=True), i)
    outs[0][here, :] = (live * (side[11][here, :] + total)).astype(jnp.bfloat16)


SMALL = 8


def tail_kernel(skip, grad_far, mix_far, normed_far, x_far, res_far, out_own, gain_ref, two_ref, x_sum, mix_sum, ffn_sum,
                live_sum, head_ref, bias_ref, outputs_far, input_far, total_ref, load_sem, store_sem, *rest):
    scatter = rest[:8]
    left, right = scatter[:2]
    normed, x_buf, res_buf, in_own, out_blocks, in_blocks, f_send, f_got, z_send, z_got, s_buf, s_send, s_got = rest[8:]
    loads = Loads(load_sem)
    load_left = loads.add(grad_far, left)
    parts = load_parts(loads, mix_far, right, skip)
    load_normed = loads.add(normed_far, normed)
    load_x = loads.add(x_far.at[pl.ds(0, x_buf.shape[0]), :], x_buf)
    load_res = loads.add(res_far, res_buf)
    size = in_own.shape[0]
    seq = lax.axis_index("seq")
    hops = [*neighbours(), other_core()]
    bit = 2
    while bit < lax.axis_size("seq"):
        hops.append({"seq": flipped(seq, bit)})
        bit *= 2
    greet(hops)
    sum_heads = Scatter(*scatter)

    def watch(here, value):
        term = value * normed[:, here].astype(jnp.float32)
        s_buf[0, 0:1, here] = jnp.sum(term, axis=0, keepdims=True) / gain_ref[:, here]

    f_gather = Gather(out_own, out_blocks, f_send, f_got)
    f_gather.first()
    s_buf[0] = jnp.zeros(s_buf.shape[1:], jnp.float32)
    load_left.wait()
    load_normed.wait()
    sum_heads.first(parts, watch)
    sum_heads.second(0)
    sum_heads.second(1)

    is_own = lax.broadcasted_iota(jnp.int32, (SMALL, 1), 0) >= SMALL - 2
    for k, row in enumerate((two_ref, x_sum, mix_sum, ffn_sum, live_sum)):
        s_buf[0, k + 1 : k + 2, :] = row[...]
    s_buf[0, SMALL - 2 : SMALL - 1, : head_ref.shape[1]] = head_ref[...]
    slots = bias_ref.shape[0]
    s_buf[0, SMALL - 1 : SMALL, :slots] = jnp.transpose(jnp.broadcast_to(bias_ref[...], (slots, 128)))[:1, :]
    small = [
        pltpu.make_async_remote_copy(
            src_ref=s_buf.at[2 * k], dst_ref=s_buf.at[2 * k + 1], send_sem=s_send.at[k], recv_sem=s_got.at[k],
            device_id=hop, device_id_type=MESH,
        )
        for k, hop in enumerate(hops)
    ]

    def hop_done(k):
        small[k].wait_recv()
        arrived = s_buf[2 * k + 1]
        if k < 2:
            arrived = jnp.where(is_own, 0.0, arrived)
        if k + 1 < len(small):
            s_buf[2 * k + 2] = s_buf[2 * k] + arrived
            small[k + 1].start()
        else:
            total_ref[...] = s_buf[2 * k] + arrived

    small[0].start()
    load_x.wait()
    load_res.wait()

    def finish(here, total, i):
        scale, unit = unit_of(x_buf[here, :].astype(jnp.float32))
        in_own[here, :] = (res_buf[here, :] + norm_back(total, gain_ref[...], scale, unit)).astype(jnp.bfloat16)

    f_gather.second()
    hop_done(0)
    sum_heads.last(finish)
    z_gather = Gather(in_own, in_blocks, z_send, z_got)
    z_gather.first()
    head = lax.axis_index("head")
    places = (head, flipped(head, 1), flipped(head, 2), BLOCKS - 1 - head)
    stores = []

    def store(src, far, k):
        copy = pltpu.make_async_copy(src, far.at[places[k]], store_sem.at[len(stores)])
        copy.start()
        stores.append(copy)

    store(out_own, outputs_far, 0)
    store(in_own, input_far, 0)
    hop_done(1)
    z_gather.second()
    for k in range(2, len(small)):
        hop_done(k)
    f_gather.last()
    for k in range(1, BLOCKS):
        store(out_blocks.at[k], outputs_far, k)
    z_gather.last()
    for k in range(1, BLOCKS):
        store(in_blocks.at[k], input_far, k)
    sum_heads.close()
    for one in small:
        one.wait_send()
    for one in stores:
        one.wait()


def tail_stage(hops, skip, grad_in, mix, normed, x_rel, grad_residual, out_own, small, number):
    rows, depth = grad_in.shape
    size, high = out_own.shape
    blocks = jax.ShapeDtypeStruct((BLOCKS, size, high), jnp.bfloat16)
    sems = lambda n: pltpu.SemaphoreType.DMA((n,))
    return pl.pallas_call(
        functools.partial(tail_kernel, skip),
        in_specs=[FAR] * 5 + [WHOLE] * (1 + len(small)),
        out_specs=[FAR, FAR, WHOLE],
        out_shape=[blocks, blocks, jax.ShapeDtypeStruct((SMALL, high), jnp.float32)],
        scratch_shapes=[
            sems(8),
            sems(2 * BLOCKS),
            *scatter_scratch(rows, depth, high),
            pltpu.VMEM((rows, high), jnp.bfloat16),
            pltpu.VMEM((size, high), jnp.bfloat16),
            pltpu.VMEM((size, high), jnp.float32),
            pltpu.VMEM((size, high), jnp.bfloat16),
            pltpu.VMEM((BLOCKS, size, high), jnp.bfloat16),
            pltpu.VMEM((BLOCKS, size, high), jnp.bfloat16),
            sems(6), sems(6), sems(6), sems(6),
            pltpu.VMEM((2 * hops, SMALL, high), jnp.float32),
            sems(hops), sems(hops),
        ],
        compiler_params=pltpu.CompilerParams(collective_id=number, has_side_effects=True, vmem_limit_bytes=LIMIT),
        cost_estimate=pl.CostEstimate(flops=10**9, bytes_accessed=1 << 20, transcendentals=0),
        name="tail_stage",
    )(grad_in, mix, normed, x_rel, grad_residual, out_own, *small)


def last_kernel(counts, seq_ref, input_ref, output_ref, gu_ref, mix_ref, out_w_ref, narrow_ref, down_ref, small_ref,
                input_out, output_out, q_out, k_out, v_out, go_out, f_out, gate_out, up_out, w_out_out, down_out,
                one_out, two_out, head_out, bias_out, rms_out):
    seq_count, skip, n_gain, n_bias = counts
    f32 = jnp.float32
    step = pl.program_id(0)
    input_out[...] = input_ref[...].astype(f32)
    output_out[...] = output_ref[...]
    half = gate_out.shape[1]
    gate_out[...] = gu_ref[:, :half].astype(f32)
    up_out[...] = gu_ref[:, half:].astype(f32)
    width = q_out.shape[1]
    for k, out in enumerate((q_out, k_out, v_out, go_out)):
        out[...] = mix_ref[:, skip + k * width : skip + (k + 1) * width].astype(f32)

    @pl.when(step == 0)
    def _():
        down_out[...] = jnp.transpose(down_ref[...].astype(f32))

    @pl.when(step == 1)
    def _():
        slots = f_out.shape[0]
        f_out[...] = jnp.transpose(narrow_ref[...].astype(f32))[:slots, :]
        w_out_out[...] = jnp.transpose(out_w_ref[...].astype(f32))
        share = one_out.shape[1]
        picks = [(one_out, 0, share), (two_out, 1, share), (head_out, SMALL - 2, n_gain), (bias_out, SMALL - 1, n_bias)]
        for out, row, n in picks:
            value = small_ref[row : row + 1, :n]
            for s in range(1, seq_count):
                value = jnp.where(seq_ref[0] == s, small_ref[row : row + 1, s * n : (s + 1) * n], value)
            out[...] = value
        sums = jnp.sum(small_ref[...], axis=1, keepdims=True)
        roots = jnp.sqrt(sums / (sums[5:6] * small_ref.shape[1]))
        rms_out[...] = jnp.transpose(jnp.broadcast_to(roots, (SMALL, 128)))[:1, 2:5]


def last_stage(seq_pos, seq_count, input_grad, outputs, grad_gu, grad_mix, grad_down, small, width, slots, n_gain, n_bias):
    f32 = jnp.float32
    rows, high = input_grad.shape
    share, wide_gu = grad_gu.shape
    wide_mix, hidden = grad_mix.shape[1], grad_down.shape[1]
    steps = 4
    per, part = rows // steps, share // steps
    tile = lambda a, b: pl.BlockSpec((a, b), lambda i, s: (i, 0))
    fixed = lambda a, b: pl.BlockSpec((a, b), lambda i, s: (0, 0))
    shapes = lambda *dims: [jax.ShapeDtypeStruct(one, f32) for one in dims]
    return pl.pallas_call(
        functools.partial(last_kernel, (seq_count, width, n_gain, n_bias)),
        grid_spec=pltpu.PrefetchScalarGridSpec(
            num_scalar_prefetch=1,
            grid=(steps,),
            in_specs=[tile(per, high), tile(per, high), tile(part, wide_gu), tile(part, wide_mix), fixed(share, width),
                      pl.BlockSpec((share, 2 * slots), lambda i, s: (0, wide_mix // (2 * slots) - 1)), fixed(share, hidden), fixed(SMALL, high)],
            out_specs=[tile(per, high), tile(per, high), *[tile(part, width)] * 4, fixed(slots, share),
                       *[tile(part, hidden)] * 2, fixed(width, share), fixed(hidden, share), fixed(1, share),
                       fixed(1, share), fixed(1, n_gain), fixed(1, n_bias), fixed(1, 3)],
        ),
        out_shape=[
            *shapes((rows, high)), jax.ShapeDtypeStruct((rows, high), jnp.bfloat16),
            *shapes(*[(share, width)] * 4, (slots, share), (share, hidden), (share, hidden), (width, share),
                    (hidden, share), (1, share), (1, share), (1, n_gain), (1, n_bias), (1, 3)),
        ],
        compiler_params=pltpu.CompilerParams(dimension_semantics=("arbitrary",), vmem_limit_bytes=LIMIT),
        cost_estimate=pl.CostEstimate(flops=10**7, bytes_accessed=1 << 20, transcendentals=0),
        name="last_stage",
    )(seq_pos, input_grad, outputs, grad_gu, grad_mix, grad_mix, grad_mix, grad_down, small)


def enter_kernel(count, *refs):
    (out_w, q, k, v, go, forget_w, one, two, head_gain, bias, tokens, cot, gate_w, up_w, down_w, counts, pads) = refs[:17]
    (mix_out, normed_out, grad_out, x_out, cot_out, gu_out, down_out, qkvg_out, forget_out, rows_out) = refs[17:27]
    (buf, wide_buf, f_buf, one_buf, two_buf, head_buf, bias_buf, turned, x_buf, cot_buf, scale, normed, acc, gate_buf,
     up_buf, gu_buf, downw_buf, down_buf, load_sem, mix_sem, norm_sem, out_sem, r_send, r_got, l_send, l_got, x_send,
     x_got) = refs[27:]
    f32, b16 = jnp.float32, jnp.bfloat16
    seq = lax.axis_index("seq")
    place, core = seq // 2, seq % 2
    chips = count // 2
    rows = x_buf.shape[0]
    size = rows // BLOCKS
    share, width = q.shape
    slots = f_buf.shape[0]
    part, pair = share // 2, 2 * share
    own = buf.at[pl.ds(pl.multiple_of(seq * share, share), share), :]

    loads = Loads(load_sem)
    load_small = [loads.add(src, dst) for src, dst in (
        (forget_w, f_buf), (one, one_buf), (two, two_buf), (head_gain, head_buf), (bias, bias_buf))]
    load_out = loads.add(out_w, wide_buf)
    pieces = [loads.add(piece, own.at[:, pl.ds((at + 1) * width, width)]) for at, piece in enumerate((q, k, v, go))]
    load_x, load_cot = [], []
    for block in range(BLOCKS):
        there = pl.ds(pl.multiple_of(mixed_index(block) * size, size), size)
        load_x.append(loads.add(tokens.at[there, :], x_buf.at[pl.ds(block * size, size), :]))
        load_cot.append(loads.add(cot.at[there, :], cot_buf.at[pl.ds(block * size, size), :]))
    load_ffn = [loads.add(src, dst) for src, dst in ((gate_w, gate_buf), (up_w, up_buf), (down_w, downw_buf))]
    at_seq = lambda chip: {"seq": 2 * (chip % chips) + core}
    greet([at_seq(place + 1), at_seq(place + chips - 1), other_core()])

    turned[...] = jnp.zeros_like(turned)
    for load in load_small:
        load.wait()
    n = head_buf.shape[1]
    turned[:slots, :] = f_buf[...].astype(f32)
    turned[slots : slots + 1, :] = one_buf[...].astype(f32)
    turned[slots + 1 : slots + 2, :] = two_buf[...].astype(f32)
    turned[slots + 2 : slots + 3, :n] = head_buf[...].astype(f32)
    turned[slots + 2 : slots + 3, n : n + bias_buf.shape[1]] = bias_buf[...].astype(f32)
    own[:, 5 * width :] = jnp.transpose(turned[...]).astype(b16)
    load_out.wait()
    own[:, :width] = jnp.transpose(wide_buf[...])
    for load in pieces:
        load.wait()

    def remote(shard, ch, send, got, target):
        there = buf.at[pl.ds(pl.multiple_of(shard * share + ch * part, part), part), :]
        return pltpu.make_async_remote_copy(
            src_ref=there, dst_ref=there, send_sem=send, recv_sem=got, device_id=target, device_id_type=MESH
        )

    def right(d, ch):
        return remote(2 * (place - d) + core, ch, r_send.at[d, ch], r_got.at[d, ch], at_seq(place + 1))

    def left(d, ch):
        return remote(2 * (place + d) + core, ch, l_send.at[d, ch], l_got.at[d, ch], at_seq(place + chips - 1))

    def across(chip, ch):
        return remote(2 * chip + core, ch, x_send.at[chip, ch], x_got.at[chip, ch], other_core())

    for ch in range(2):
        pl.when(place < chips - 1)(right(0, ch).start)
        pl.when(place > 0)(left(0, ch).start)
    for ch in range(2):
        across(place, ch).start()

    acc[...] = jnp.zeros_like(acc)
    for load in load_x:
        load.wait()
    outs = []

    def leave(src, dst):
        copy = pltpu.make_async_copy(src, dst, out_sem.at[len(outs)])
        copy.start()
        outs.append(copy)

    leave(x_buf.at[pl.ds(0, size), :], x_out)

    def row_scale(i, carry):
        here = pl.ds(pl.multiple_of(i * CHUNK, CHUNK), CHUNK)
        scale[here, :] = unit_of(x_buf[here, :].astype(f32))[0]
        return carry

    lax.fori_loop(0, rows // CHUNK, row_scale, 0)
    for load in load_cot:
        load.wait()
    live_len = jnp.where(counts[0] > 0, rows - pads[0], 0)
    per = size // CHUNK

    def mask(i, carry):
        here = pl.ds(pl.multiple_of(i * CHUNK, CHUNK), CHUNK)
        start = mixed_index(i // per) * size + i % per * CHUNK
        live = start + lax.broadcasted_iota(jnp.int32, (CHUNK, 1), 0) < live_len
        cot_buf[here, :] = (cot_buf[here, :].astype(f32) * live.astype(f32)).astype(b16)
        return carry

    lax.fori_loop(0, rows // CHUNK, mask, 0)
    leave(cot_buf, grad_out)
    leave(cot_buf.at[pl.ds(0, size), :], cot_out)
    for load in load_ffn:
        load.wait()
    for at in range(0, gate_buf.shape[1], 128):
        gu_buf[:, 2 * at : 2 * at + 128] = gate_buf[:, at : at + 128]
        gu_buf[:, 2 * at + 128 : 2 * at + 256] = up_buf[:, at : at + 128]
    leave(gu_buf, gu_out)
    down_buf[...] = jnp.transpose(downw_buf[...])
    leave(down_buf, down_out)

    def chip_rows(chip):
        return pl.ds(pl.multiple_of(chip * pair, pair), pair)

    def mix_store(chip):
        return pltpu.make_async_copy(buf.at[chip_rows(chip), :], mix_out.at[chip_rows(chip), :], mix_sem.at[chip])

    def norm_store(chip):
        return pltpu.make_async_copy(normed.at[:, chip_rows(chip)], normed_out.at[:, chip_rows(chip)], norm_sem.at[chip])

    def use(chip):
        for ch in range(2):
            across(chip, ch).wait_recv()
        mix_store(chip).start()
        here = chip_rows(chip)
        narrow = jnp.transpose(buf[here, 5 * width :].astype(f32))[slots : slots + 8, :]
        rows_out[:, here] = narrow
        normed[:, here] = (x_buf[:, here].astype(f32) * scale[...] * narrow[:1, :]).astype(b16)
        norm_store(chip).start()
        for at in range(width, buf.shape[1], 512):
            cols = min(512, buf.shape[1] - at)
            acc[:, at - width : at - width + cols] += mm(normed[:, here], buf[here, at : at + cols], NN)

    use(place)

    def step(d, carry):
        on_left, on_right = place >= d, place + d < chips

        @pl.when(on_left)
        def _():
            for ch in range(2):
                right(d - 1, ch).wait_recv()
                pl.when((d < chips - 1) & (place < chips - 1))(right(d, ch).start)
                across(place - d, ch).start()

        @pl.when(on_right)
        def _():
            for ch in range(2):
                left(d - 1, ch).wait_recv()
                pl.when((d < chips - 1) & (place > 0))(left(d, ch).start)
                across(place + d, ch).start()

        @pl.when(on_left)
        def _():
            use(place - d)

        @pl.when(on_right)
        def _():
            use(place + d)

        return carry

    lax.fori_loop(1, chips, step, 0)
    forget_out[...] = jnp.transpose(acc[:, 4 * width :])[:slots, :]
    outs[0].wait()
    for at in range(0, 4 * width, width):
        x_buf[:, at : at + width] = acc[:, at : at + width].astype(b16)
        leave(x_buf.at[:, pl.ds(at, width)], qkvg_out.at[:, pl.ds(at, width)])

    def close(d, carry):
        for ch in range(2):
            pl.when((place >= d) & (place < chips - 1))(right(d, ch).wait_send)
            pl.when((place + d < chips) & (place > 0))(left(d, ch).wait_send)
        return carry

    lax.fori_loop(0, chips - 1, close, 0)

    def settle(chip, carry):
        for ch in range(2):
            across(chip, ch).wait_send()
        mix_store(chip).wait()
        norm_store(chip).wait()
        return carry

    lax.fori_loop(0, chips, settle, 0)
    for one_out in outs[1:]:
        one_out.wait()


def enter_stage(count, out_w, q, k, v, go, forget, one, two, head, bias, tokens, cot, gate, up, down, counts, pads, number):
    f32, b16 = jnp.float32, jnp.bfloat16
    share, width = q.shape
    slots, hidden = forget.shape[0], gate.shape[1]
    rows, high = tokens.shape
    size, chips = rows // BLOCKS, count // 2
    mix_width = 5 * width + 2 * slots
    shape = jax.ShapeDtypeStruct
    buf = lambda array: pltpu.VMEM(array.shape, b16)
    sems = lambda *dims: pltpu.SemaphoreType.DMA(dims)
    return pl.pallas_call(
        functools.partial(enter_kernel, count),
        in_specs=[FAR] * 15 + [pl.BlockSpec(memory_space=pltpu.SMEM)] * 2,
        out_specs=[FAR] * 8 + [WHOLE] * 2,
        out_shape=[
            shape((high, mix_width), b16), shape((rows, high), b16), shape((rows, high), b16), shape((size, high), b16),
            shape((size, high), b16), shape((share, 2 * hidden), b16), shape((share, hidden), b16),
            shape((rows, 4 * width), b16), shape((slots, rows), f32), shape((8, high), f32),
        ],
        scratch_shapes=[
            pltpu.VMEM((high, mix_width), b16), buf(out_w), *[buf(array) for array in (forget, one, two, head, bias)],
            pltpu.VMEM((2 * slots, share), f32), buf(tokens), buf(cot), pltpu.VMEM((rows, 1), f32), buf(tokens),
            pltpu.VMEM((rows, 4 * width + 2 * slots), f32), buf(gate), buf(up), pltpu.VMEM((share, 2 * hidden), b16),
            buf(down), pltpu.VMEM((share, hidden), b16), sems(21), sems(chips), sems(chips), sems(9),
            *[sems(chips, 2)] * 6,
        ],
        compiler_params=pltpu.CompilerParams(collective_id=number, has_side_effects=True, vmem_limit_bytes=LIMIT),
        cost_estimate=pl.CostEstimate(flops=10**9, bytes_accessed=1 << 20, transcendentals=0),
        name="enter_stage",
    )(out_w, q, k, v, go, forget, one, two, head, bias, tokens, cot, gate, up, down, counts, pads)


def ffn_fwd_kernel(x_ref, w_ref, slopes_ref, hidden_ref):
    half = x_ref.shape[0] // 2
    for rows in (slice(0, half), slice(half, 2 * half)):
        value = mm(x_ref[rows, :], w_ref[...], NN)
        gate, up = value[:, :128], value[:, 128:]
        sigma = jax.nn.sigmoid(gate)
        swish = gate * sigma
        slopes_ref[rows, :128] = (up * (sigma + swish * (1.0 - sigma))).astype(jnp.bfloat16)
        slopes_ref[rows, 128:] = swish.astype(jnp.bfloat16)
        hidden_ref[rows, :] = (swish * up).astype(jnp.bfloat16)


def ffn_fwd(x, weight):
    rows, width = x.shape
    wide = weight.shape[1]
    return pl.pallas_call(
        ffn_fwd_kernel,
        grid=(wide // 256,),
        in_specs=[pl.BlockSpec((rows, width), lambda j: (0, 0)), pl.BlockSpec((width, 256), lambda j: (0, j))],
        out_specs=[pl.BlockSpec((rows, 256), lambda j: (0, j)), pl.BlockSpec((rows, 128), lambda j: (0, j))],
        out_shape=[
            jax.ShapeDtypeStruct((rows, wide), jnp.bfloat16),
            jax.ShapeDtypeStruct((rows, wide // 2), jnp.bfloat16),
        ],
        compiler_params=pltpu.CompilerParams(dimension_semantics=("arbitrary",), vmem_limit_bytes=LIMIT),
        cost_estimate=pl.CostEstimate(flops=10**9, bytes_accessed=1 << 20, transcendentals=0),
        name="ffn_fwd",
    )(x, weight)


def ffn_bwd_kernel(grad_ref, w_ref, slopes_ref, out_ref):
    half = grad_ref.shape[0] // 2
    for rows in (slice(0, half), slice(half, 2 * half)):
        value = mm(grad_ref[rows, :], w_ref[...], NN)
        for p in range(4):
            here = slice(p * 128, (p + 1) * 128)
            grad = value[:, p // 2 * 128 : (p // 2 + 1) * 128]
            out_ref[rows, here] = (grad * slopes_ref[rows, here].astype(jnp.float32)).astype(jnp.bfloat16)


def ffn_bwd(grad, weight, gu):
    rows, width = grad.shape
    wide = gu.shape[1]
    return pl.pallas_call(
        ffn_bwd_kernel,
        grid=(pl.cdiv(wide, 512),),
        in_specs=[
            pl.BlockSpec((rows, width), lambda j: (0, 0)),
            pl.BlockSpec((width, 256), lambda j: (0, j)),
            pl.BlockSpec((rows, 512), lambda j: (0, j)),
        ],
        out_specs=pl.BlockSpec((rows, 512), lambda j: (0, j)),
        out_shape=jax.ShapeDtypeStruct((rows, wide), jnp.bfloat16),
        compiler_params=pltpu.CompilerParams(dimension_semantics=("arbitrary",), vmem_limit_bytes=LIMIT),
        cost_estimate=pl.CostEstimate(flops=10**9, bytes_accessed=1 << 20, transcendentals=0),
        name="ffn_bwd",
    )(grad, weight, gu)


def after(values, *earlier):
    return lax.optimization_barrier((values, earlier))[0]


def on_device(seq_count, tokens, cotangent, counts, pads, norm1_gain, w_query, w_key, w_value, w_gate_out,
              w_forget, forget_bias, out_gain, w_out, norm2_gain, w_gate, w_up, w_down):
    f32, b16 = jnp.float32, jnp.bfloat16
    rows, model_width = tokens.shape[1:]
    head_pos = lax.axis_index("head")
    head_arr = head_pos.reshape(1).astype(jnp.int32)
    width, slots, hidden_width = w_query.shape[1], w_forget.shape[1], w_gate.shape[1]
    share = w_query.shape[0]
    extra = slots
    size = rows // BLOCKS

    wide = 4 * width
    mix, normed1, grad_ffn, x_own, cot_own, own_gu, own_down, qkvg, forget_raw, gain_rows = enter_stage(
        seq_count, w_out, w_query, w_key, w_value, w_gate_out, w_forget.T, norm1_gain[None], norm2_gain[None],
        out_gain[None], forget_bias[None], tokens[0], cotangent[0], w_gate, w_up, w_down, counts, pads, 7,
    )
    gu_weight = lax.all_gather(own_gu, "seq", axis=0, tiled=True)
    down_weight = lax.all_gather(own_down, "seq", axis=0, tiled=True)

    skip = width
    row_one, row_two = gain_rows[0:1], gain_rows[1:2]
    small_all = gain_rows[2].reshape(seq_count, share)
    n_gain, n_bias = out_gain.shape[0], forget_bias.shape[0]
    gain_head = small_all[:, :n_gain].reshape(1, width)
    bias = small_all[:, n_gain : n_gain + n_bias].reshape(slots, 1)
    position = head_pos * size + jnp.arange(size, dtype=jnp.int32)[:, None]
    live_own = (position < jnp.where(counts[0] > 0, rows - pads[0], 0)).astype(f32)
    forget_t = forget_raw + bias
    log_keep = jax.nn.log_sigmoid(forget_t) / DAMPING
    keep_in = -jnp.expm1(log_keep)
    gated, mixed, probs, kst, vst = rec_fwd(head_arr, qkvg, log_keep, keep_in, gain_head)

    tall = lambda kind: jax.ShapeDtypeStruct((size, model_width), kind)
    line = jax.ShapeDtypeStruct((1, model_width), f32)
    seq_pos = lax.axis_index("seq")
    residual, normed_own, x_squares, mix_squares, live_sum = head_scatter(
        gated, mix, [x_own], [row_two, live_own], [tall(f32), tall(b16), line, line, line], finish_mixer, 0
    )
    normed2, normed2_t, normed1_t = head_gather(normed_own, 1, also=normed1)
    gu, hidden = ffn_fwd(normed2.reshape(rows, model_width), gu_weight)

    grad_down = mm(grad_ffn, hidden, TN).astype(b16).reshape(-1, 2, share, hidden_width)
    core = seq_pos % 2
    kept = lax.dynamic_index_in_dim(grad_down, core, 1, keepdims=False)
    given = lax.dynamic_index_in_dim(grad_down, 1 - core, 1, keepdims=False)
    given = lax.ppermute(given, "seq", [(i, i ^ 1) for i in range(seq_count)])
    grad_down = (kept.astype(f32) + given.astype(f32)).astype(b16).reshape(-1, hidden_width)
    down_weight = after(down_weight, grad_down)
    lines = [list(range(c, seq_count, 2)) for c in range(2)]

    def line_scatter(array):
        return lax.psum_scatter(array, "seq", scatter_dimension=0, tiled=True, axis_index_groups=lines)

    grad_down = line_scatter(grad_down)
    grad_gu = ffn_bwd(grad_ffn, down_weight, gu)
    high = model_width // 2
    grad_residual, grad_low, grad_gain_two, grad_gu_w = head_scatter(
        grad_gu, gu_weight, [normed2_t, residual, cot_own], [live_own, row_two], [tall(f32), tall(b16), line],
        finish_norm_two, 2, filler=fill_gu, filled=[jax.ShapeDtypeStruct((high, gu_weight.shape[1]), b16)],
        scratch=tile_scratch(model_width, gu_weight.shape[1], share, 0),
    )
    grad_gu_w = line_scatter(grad_gu_w)
    grad_att_t, grad_gated = head_gather(grad_low, 3, keep=False, weight=mix, width=width)
    grad_gated = after(grad_gated, grad_down)
    wide_in = wide + slots + extra
    states = [pltpu.VMEM((slots, width), f32), pltpu.VMEM((slots, width), f32), pltpu.VMEM((slots, 1), f32)]
    out_own, ffn_squares, grad_gain_head, grad_bias, grad_in, grad_mix = head_scatter(
        hidden, down_weight,
        [qkvg, grad_gated, mixed, probs, kst, vst, log_keep, keep_in, forget_t, jnp.asarray(span_matrix(), b16), gain_head,
         residual, grad_att_t, gated, normed1_t],
        [live_own], [tall(b16), line, jax.ShapeDtypeStruct((1, width), f32), jax.ShapeDtypeStruct((slots, 1), f32)],
        finish_ffn, 4, filler=fill_mix,
        filled=[jax.ShapeDtypeStruct((rows, wide_in), b16),
                jax.ShapeDtypeStruct((high, mix.shape[1]), b16)],
        scratch=[pltpu.VMEM((rows, wide_in), b16), pltpu.SemaphoreType.DMA((1,)), *states,
                 *tile_scratch(model_width, mix.shape[1], share, 1)],
    )
    grad_mix = line_scatter(grad_mix)
    hops = 2 + seq_count.bit_length() - 1
    outputs, input_grad, small = tail_stage(
        hops, skip, grad_in, mix, normed1, x_own, grad_residual, out_own,
        (row_one, grad_gain_two, x_squares, mix_squares, ffn_squares, live_sum, grad_gain_head, grad_bias), 6,
    )
    (input_grad, outputs, grad_q, grad_k, grad_v, grad_go, grad_f, grad_gate, grad_up, grad_wo, grad_wd, grad_one,
     grad_two, grad_head, grad_fb, rms) = last_stage(
        seq_pos.reshape(1).astype(jnp.int32), seq_count, input_grad.reshape(rows, model_width),
        outputs.reshape(rows, model_width), grad_gu_w, grad_mix, grad_down, small, width, slots, n_gain, n_bias,
    )
    return (
        outputs[None], input_grad[None], grad_one[0], grad_q, grad_k, grad_v, grad_go, grad_f.T, grad_fb[0], grad_head[0],
        grad_wo, grad_two[0], grad_gate, grad_up, grad_wd, rms[0],
    )


def solution(mesh):
    both = P("seq", "head")
    flat = P(("head", "seq"))
    rows = P("seq", None, None)
    return jax.shard_map(
        functools.partial(on_device, mesh.shape["seq"]),
        mesh=mesh,
        in_specs=(rows, rows, P("seq"), P("seq"), P("seq"), both, both, both, both, both, flat, flat,
                  P("head", "seq"), P("seq"), both, both, P("head", "seq")),
        out_specs=(rows, rows, P("seq"), both, both, both, both, both, flat, flat, P("head", "seq"), P("seq"),
                   both, both, P("head", "seq"), P()),
        check_vma=False,
    )
```

```python
import functools

import jax
import jax.numpy as jnp
import numpy as np
from jax import lax
from jax.experimental import pallas as pl
from jax.experimental.pallas import tpu as pltpu
from jax.sharding import PartitionSpec as P

EPSILON = 1e-06
DAMPING = 8.0
TILE = 128
BLOCKS = 4
HALVES = (64, 32, 16, 8, 4, 2, 1)
NT = (((1,), (1,)), ((), ()))
NN = (((1,), (0,)), ((), ()))
TN = (((0,), (0,)), ((), ()))


def rel_tile(rows, i, h):
    per = rows // BLOCKS // TILE
    return (i // per ^ h[0]) * per + i % per


def mm(left, right, dims):
    return lax.dot_general(left, right, dims, preferred_element_type=jnp.float32)


def span_matrix():
    r = np.arange(TILE)[:, None]
    t = np.arange(TILE)[None, :]
    parts = []
    for h in HALVES:
        base = t // (2 * h) * (2 * h)
        upper = t % (2 * h) >= h
        parts.append(upper & (r >= base + h) & (r <= t))
        parts.append(~upper & (r > t) & (r <= base + h - 1))
    parts.append(r <= t)
    parts.append(r > t)
    return np.concatenate(parts, axis=1).astype(np.float32)


def level_of():
    s = lax.broadcasted_iota(jnp.int32, (TILE, TILE), 0)
    t = lax.broadcasted_iota(jnp.int32, (TILE, TILE), 1)
    return jnp.where(s < t, s ^ t, jnp.where(s == t, 0, -1))


def level_masks():
    x = level_of()
    masks = [(x >= h) & (x < 2 * h) for h in HALVES]
    masks.append(x == 0)
    return masks


def decays(log_keep, keep_in, spans):
    slots = log_keep.shape[0]
    high = log_keep.astype(jnp.bfloat16)
    rest = log_keep - high.astype(jnp.float32)
    mid = rest.astype(jnp.bfloat16)
    both = mm(jnp.concatenate([high, mid], axis=0), spans, NN)
    grown = jnp.exp(both[:slots] + both[slots:])
    n = len(HALVES)
    ones = jnp.ones_like(keep_in)
    e_parts = [grown[:, (2 * i) * TILE : (2 * i + 1) * TILE] for i in range(n)] + [ones]
    f_bare = [grown[:, (2 * i + 1) * TILE : (2 * i + 2) * TILE] for i in range(n)] + [ones]
    e_all = grown[:, 2 * n * TILE : (2 * n + 1) * TILE]
    f_all = grown[:, (2 * n + 1) * TILE : (2 * n + 2) * TILE]
    total = e_all[:, TILE - 1 : TILE]
    return e_parts, f_bare, e_all, f_all, total


def norm_gate(mixed, gain, gate_pre):
    scale = lax.rsqrt(jnp.mean(mixed * mixed, axis=-1, keepdims=True) + EPSILON)
    unit = mixed * scale
    return scale, unit


def fwd_tile(step, q_ref, k_ref, v_ref, g_ref, lk_ref, w_ref, gain_ref, spans_ref,
               gated_ref, mixed_ref, probs_ref, kst_ref, vst_ref, kacc, vacc):
    @pl.when(step == 0)
    def _():
        kacc[...] = jnp.zeros_like(kacc)
        vacc[...] = jnp.zeros_like(vacc)
    width = q_ref.shape[1]
    root = width ** -0.5
    q, k, v = q_ref[...], k_ref[...], v_ref[...]
    keep_in = w_ref[...]
    e_parts, f_bare, e_all, f_all, total = decays(lk_ref[...], keep_in, spans_ref[...])
    masks = level_masks()
    kst, vst = kacc[...], vacc[...]
    kst_b, vst_b = kst.astype(jnp.bfloat16), vst.astype(jnp.bfloat16)
    kst_ref[0] = kst_b
    vst_ref[0] = vst_b
    inner = mm(k, q, NT) * root
    inner_b = inner.astype(jnp.bfloat16)
    zero_b = jnp.zeros_like(inner_b)
    f_parts = [(bare * keep_in).astype(jnp.bfloat16) for bare in f_bare]
    scores = e_all * (mm(kst_b, q, NT) * root)
    for mask, grow, fade in zip(masks, e_parts, f_parts):
        scores += grow * mm(fade, jnp.where(mask, inner_b, zero_b), NN)
    top = jnp.max(scores, axis=0, keepdims=True)
    raised = jnp.exp(scores - top)
    probs = raised / jnp.sum(raised, axis=0, keepdims=True)
    probs_ref[...] = probs
    mixing = jnp.zeros((TILE, TILE), jnp.float32)
    for mask, grow, fade in zip(masks, e_parts, f_parts):
        mixing = jnp.where(mask, mm(fade, (probs * grow).astype(jnp.bfloat16), TN), mixing)
    mixed = mm(mixing.astype(jnp.bfloat16), v, TN) + mm((probs * e_all).astype(jnp.bfloat16), vst_b, TN)
    tail = (f_all * keep_in).astype(jnp.bfloat16)
    kacc[...] = total * kst + mm(tail, k, NN)
    vacc[...] = total * vst + mm(tail, v, NN)
    mixed_ref[...] = mixed
    scale = lax.rsqrt(jnp.mean(mixed * mixed, axis=-1, keepdims=True) + EPSILON)
    gate = g_ref[...].astype(jnp.float32)
    swish = gate * jax.nn.sigmoid(gate)
    gated_ref[...] = (mixed * scale * gain_ref[...] * swish).astype(jnp.bfloat16)


def bwd_tile(step, q_ref, k_ref, v_ref, g_ref, lk_ref, w_ref, fpre_ref, gain_ref, spans_ref,
               mixed_ref, probs_ref, kst_ref, vst_ref, dg_ref,
               dproj_ref, dgain_ref, dbias_ref, dk_acc, dv_acc, cross):
    width = q_ref.shape[1]
    slots = lk_ref.shape[0]

    @pl.when(step == 0)
    def _():
        dk_acc[...] = jnp.zeros_like(dk_acc)
        dv_acc[...] = jnp.zeros_like(dv_acc)
        cross[...] = jnp.zeros_like(cross)
        dgain_ref[...] = jnp.zeros_like(dgain_ref)
        dbias_ref[...] = jnp.zeros_like(dbias_ref)
    root = width ** -0.5
    q, k, v = q_ref[...], k_ref[...], v_ref[...]
    mixed = mixed_ref[...]
    gate = g_ref[...].astype(jnp.float32)
    gain = gain_ref[...]
    d_gated = dg_ref[...].astype(jnp.float32)
    scale = lax.rsqrt(jnp.mean(mixed * mixed, axis=-1, keepdims=True) + EPSILON)
    unit = mixed * scale
    sigma = jax.nn.sigmoid(gate)
    swish = gate * sigma
    slope = sigma * (1.0 + gate * (1.0 - sigma))
    dproj_ref[:, 3 * width : 4 * width] = (d_gated * unit * gain * slope).astype(jnp.bfloat16)
    d_normed = d_gated * swish
    dgain_ref[...] += jnp.sum(d_normed * unit, axis=0, keepdims=True)
    c = d_normed * gain
    d_mixed = scale * (c - unit * jnp.mean(c * unit, axis=-1, keepdims=True))
    d_out = d_mixed.astype(jnp.bfloat16)

    log_keep, keep_in = lk_ref[...], w_ref[...]
    e_parts, f_bare, e_all, f_all, total = decays(log_keep, keep_in, spans_ref[...])
    masks = level_masks()
    probs = probs_ref[...]
    kst, vst = kst_ref[0], vst_ref[0]
    dkst, dvst = dk_acc[...], dv_acc[...]
    dkst_b, dvst_b = dkst.astype(jnp.bfloat16), dvst.astype(jnp.bfloat16)

    inner_b = (mm(k, q, NT) * root).astype(jnp.bfloat16)
    d_mixing_b = mm(v, d_out, NT).astype(jnp.bfloat16)
    pair = jnp.concatenate([inner_b, d_mixing_b], axis=1)
    zero_b = jnp.zeros_like(pair)
    masks2 = [jnp.concatenate([mask, mask], axis=1) for mask in masks]
    pairs = [jnp.where(mask, pair, zero_b) for mask in masks2]
    f_parts = [(bare * keep_in).astype(jnp.bfloat16) for bare in f_bare]
    both = [mm(fade, two, NN) for fade, two in zip(f_parts, pairs)]
    s_state = mm(kst, q, NT) * root
    p_state = mm(vst, d_out, NT)
    d_probs = e_all * p_state
    for grow, two in zip(e_parts, both):
        d_probs += grow * two[:, TILE:]
    d_scores = probs * (d_probs - jnp.sum(probs * d_probs, axis=0, keepdims=True))

    xy_all = jnp.concatenate([d_scores * e_all, probs * e_all], axis=1).astype(jnp.bfloat16)
    xy_parts = [jnp.concatenate([d_scores * grow, probs * grow], axis=1).astype(jnp.bfloat16) for grow in e_parts]
    x0 = xy_all[:, :TILE]
    y0 = xy_all[:, TILE:]
    change = x0.astype(jnp.float32) * s_state + y0.astype(jnp.float32) * p_state
    into = jnp.zeros((slots, TILE), jnp.float32)
    d_both = jnp.zeros((TILE, 2 * TILE), jnp.float32)
    for i, (grow, bare, fade, two, xy, part, mask) in enumerate(
        zip(e_parts, f_bare, f_parts, both, xy_parts, pairs, masks2)
    ):
        z = mm(xy, part, NT)
        into += bare * z
        if i < len(HALVES):
            mass = xy.astype(jnp.float32) * two
            change += mass[:, :TILE] + mass[:, TILE:] - fade.astype(jnp.float32) * z
        d_both = jnp.where(mask, mm(fade, xy, TN), d_both)
    d_both_b = d_both.astype(jnp.bfloat16)
    d_inner, mixing = d_both_b[:, :TILE], d_both_b[:, TILE:]
    tail = (f_all * keep_in).astype(jnp.bfloat16)
    z_state = mm(dkst_b, k, NT) + mm(dvst_b, v, NT)
    into += f_all * z_state
    change -= tail.astype(jnp.float32) * z_state

    dproj_ref[:, :width] = (root * (mm(d_inner, k, TN) + mm(x0, kst, TN))).astype(jnp.bfloat16)
    dproj_ref[:, width : 2 * width] = (root * mm(d_inner, q, NN) + mm(tail, dkst_b, TN)).astype(jnp.bfloat16)
    dproj_ref[:, 2 * width : 3 * width] = (mm(mixing, d_out, NN) + mm(tail, dvst_b, TN)).astype(jnp.bfloat16)

    later = (lax.broadcasted_iota(jnp.int32, (TILE, TILE), 0) >= lax.broadcasted_iota(jnp.int32, (TILE, TILE), 1)).astype(jnp.bfloat16)
    high = change.astype(jnp.bfloat16)
    rest = change - high.astype(jnp.float32)
    mid = rest.astype(jnp.bfloat16)
    low = (rest - mid.astype(jnp.float32)).astype(jnp.bfloat16)
    sums = mm(jnp.concatenate([high, mid, low], axis=0), later, NN)
    d_log_keep = sums[:slots] + sums[slots : 2 * slots] + sums[2 * slots :] + cross[...] - jnp.exp(log_keep) * into
    d_forget = (d_log_keep * jax.nn.sigmoid(-fpre_ref[...]) / DAMPING).astype(jnp.bfloat16)
    dbias_ref[...] += jnp.sum(d_forget.astype(jnp.float32), axis=1, keepdims=True)
    turned = jnp.transpose(d_forget.astype(jnp.float32))
    dproj_ref[:, 4 * width :] = jnp.concatenate([turned, jnp.zeros_like(turned)], axis=1).astype(jnp.bfloat16)

    dkst_new = total * dkst + root * mm(x0, q, NN)
    dvst_new = total * dvst + mm(y0, d_out, NN)
    dk_acc[...] = dkst_new
    dv_acc[...] = dvst_new
    cross[...] = jnp.sum(kst.astype(jnp.float32) * dkst_new + vst.astype(jnp.float32) * dvst_new, axis=1, keepdims=True)


MESH = pl.DeviceIdType.MESH
CHUNK = 32


def neighbours():
    head = lax.axis_index("head")
    return {"head": head + 1 - 2 * (head % 2)}, {"head": (head + 2) % BLOCKS}


def flipped(index, bit):
    return index + bit - 2 * bit * (index // bit % 2)


def other_core():
    return {"seq": flipped(lax.axis_index("seq"), 1)}


def greet(targets):
    barrier = pltpu.get_barrier_semaphore()
    for target in targets:
        pl.semaphore_signal(barrier, inc=1, device_id=target, device_id_type=MESH)
    pl.semaphore_wait(barrier, len(targets))


LIMIT = 60 << 20
FAR = pl.BlockSpec(memory_space=pl.ANY)
WHOLE = pl.BlockSpec(memory_space=pltpu.VMEM)


class Loads:
    def __init__(self, sem):
        self.sem, self.copies = sem, []

    def add(self, src, dst):
        copy = pltpu.make_async_copy(src, dst, self.sem.at[len(self.copies)])
        copy.start()
        self.copies.append(copy)
        return copy


class Scatter:
    order = (0, 2, 1, 3)

    def __init__(self, left, right, acc, mid, send, got, send_sem, got_sem):
        self.left, self.right, self.acc, self.mid, self.send, self.got = left, right, acc, mid, send, got
        self.size, self.cols = send.shape[1:]
        to_x, to_y = neighbours()
        self.copies = []
        for u in range(2):
            for k, to in enumerate((to_x, to_x, to_y, to_y, to_y, to_x)):
                slot = 6 * u + k
                self.copies.append(
                    pltpu.make_async_remote_copy(
                        src_ref=send.at[slot], dst_ref=got.at[slot], send_sem=send_sem.at[slot],
                        recv_sem=got_sem.at[slot], device_id=to, device_id_type=MESH,
                    )
                )

    def first(self, loads, watch=None):
        size, cols = self.size, self.cols
        for part, load in zip(self.order, loads):
            load.wait()
            value = mm(self.left[...], self.right[part * cols : (part + 1) * cols, :], NT)
            side_at, u = part // 2, part % 2
            here = slice(part * cols, (part + 1) * cols)
            slot = 6 * u + 2 * side_at
            near_block, mid_block = (1, 2) if side_at == 0 else (2, 1)
            self.acc[:, here] = value[:size]
            self.mid[:, here] = value[mid_block * size : (mid_block + 1) * size]
            self.send[slot] = value[3 * size :].astype(jnp.bfloat16)
            self.copies[slot].start()
            self.send[slot + 1] = value[near_block * size : (near_block + 1) * size].astype(jnp.bfloat16)
            self.copies[slot + 1].start()
            if watch is not None:
                watch(here, value)

    def second(self, u):
        cols = self.cols
        for side_at in range(2):
            part = 2 * side_at + u
            first, second = 6 * u + 2 * side_at, 6 * u + 4 + side_at
            here = slice(part * cols, (part + 1) * cols)
            self.copies[first].wait_recv()
            self.send[second] = (self.mid[:, here] + self.got[first].astype(jnp.float32)).astype(jnp.bfloat16)
            self.copies[second].start()

    def last(self, finish):
        for u in range(2):
            for k in (1, 3, 4, 5):
                self.copies[6 * u + k].wait_recv()
        cols = self.cols

        def rows(i, carry):
            here = pl.ds(pl.multiple_of(i * CHUNK, CHUNK), CHUNK)
            sums = []
            for part in range(4):
                side_at, u = part // 2, part % 2
                one, two = self.got[6 * u + 2 * side_at + 1, here, :], self.got[6 * u + 4 + side_at, here, :]
                own = self.acc[here, part * cols : (part + 1) * cols]
                sums.append(own + one.astype(jnp.float32) + two.astype(jnp.float32))
            finish(here, jnp.concatenate(sums, axis=1), i)
            return carry

        lax.fori_loop(0, self.size // CHUNK, rows, 0)

    def close(self):
        for one in self.copies:
            one.wait_send()


def scatter_scratch(rows, depth, high):
    size, cols = rows // BLOCKS, high // 4
    return [
        pltpu.VMEM((rows, depth), jnp.bfloat16),
        pltpu.VMEM((high, depth), jnp.bfloat16),
        pltpu.VMEM((size, high), jnp.float32),
        pltpu.VMEM((size, high), jnp.float32),
        pltpu.VMEM((12, size, cols), jnp.bfloat16),
        pltpu.VMEM((12, size, cols), jnp.bfloat16),
        pltpu.SemaphoreType.DMA((12,)),
        pltpu.SemaphoreType.DMA((12,)),
    ]


def load_parts(loads, right_far, right, skip):
    cols = right.shape[0] // 4
    parts = []
    for part in Scatter.order:
        here = pl.ds(part * cols, cols)
        parts.append(loads.add(right_far.at[here, pl.ds(skip, right.shape[1])], right.at[here, :]))
    return parts


def scatter_kernel(plan, *refs):
    n_far, n_near, n_out, skip, finish, filler = plan
    left_far, right_far, *more_far = refs[:n_far]
    near = refs[n_far : n_far + n_near]
    outs = refs[n_far + n_near : n_far + n_near + n_out]
    load_sem, *rest = refs[n_far + n_near + n_out :]
    scatter, spare = rest[:8], rest[8:]
    left, right = scatter[:2]
    loads = Loads(load_sem)
    load_left = loads.add(left_far, left)
    parts = load_parts(loads, right_far, right, skip)
    more = [(loads.add(src, dst), dst) for src, dst in zip(more_far, spare)]
    spare = spare[len(more_far) :]
    greet(neighbours() if filler is None else (*neighbours(), other_core()))
    sum_heads = Scatter(*scatter)
    load_left.wait()
    sum_heads.first(parts)
    sum_heads.second(0)
    for load, _ in more:
        load.wait()
    side = [dst for _, dst in more]
    if filler is not None:
        steps = filler(left, right, side, outs, spare)
        next(steps)
        sum_heads.second(1)
        for _ in steps:
            pass
    else:
        sum_heads.second(1)
    sum_heads.last(lambda here, total, i: finish(here, total, side, near, outs, i))
    sum_heads.close()


def head_scatter(left, right, far, near, out_shapes, finish, number, filler=None, filled=(), scratch=()):
    rows, depth = left.shape
    plan = (2 + len(far), len(near), len(out_shapes) + len(filled), 0, finish, filler)
    return pl.pallas_call(
        functools.partial(scatter_kernel, plan),
        in_specs=[FAR] * (2 + len(far)) + [WHOLE] * len(near),
        out_specs=[WHOLE] * len(out_shapes) + [FAR] * len(filled),
        out_shape=[*out_shapes, *filled],
        scratch_shapes=[
            pltpu.SemaphoreType.DMA((5 + len(far),)),
            *scatter_scratch(rows, depth, right.shape[0]),
            *[pltpu.VMEM(one.shape, one.dtype) for one in far],
            *scratch,
        ],
        compiler_params=pltpu.CompilerParams(collective_id=number, has_side_effects=True, vmem_limit_bytes=LIMIT),
        cost_estimate=pl.CostEstimate(flops=10**9, bytes_accessed=1 << 20, transcendentals=0),
        name="head_scatter%d" % number,
    )(left, right, *far, *near)


STEP = 512


def weight_tiles(pairs, place, out_ref, room, land, store_sem, send_sem, got_sem, pause=()):
    count, share = land.shape[:2]
    high = 2 * count * share
    core = lax.axis_index("seq") % 2
    per = STEP // (2 * share)

    def row(p, at):
        return (2 * p + at) * share % room.shape[0]

    def swap_shard(p):
        return pltpu.make_async_remote_copy(
            src_ref=room.at[pl.ds(row(p, 0) + (1 - core) * share, share), :], dst_ref=land.at[p],
            send_sem=send_sem.at[p], recv_sem=got_sem.at[p], device_id=other_core(), device_id_type=MESH,
        )

    def store(p):
        return pltpu.make_async_copy(land.at[p], out_ref.at[pl.ds(p * share, share), :], store_sem.at[p])

    def settle(p):
        swap_shard(p).wait_recv()
        own = room[pl.ds(pl.multiple_of(row(p, 0) + core * share, share), share), :]
        land[p] = (own.astype(jnp.float32) + land[p].astype(jnp.float32)).astype(jnp.bfloat16)
        store(p).start()

    sent = []
    for i in range(high // STEP):
        here = slice(i * STEP, (i + 1) * STEP)
        there = slice(i * STEP % room.shape[0], i * STEP % room.shape[0] + STEP)
        if (i + 1) * STEP > room.shape[0]:
            for p in range((i - 2) * per, (i - 1) * per):
                swap_shard(p).wait_send()
                sent.append(p)
        for turned, right, column in pairs:
            for at in range(0, right.shape[1], STEP):
                cols = min(STEP, right.shape[1] - at)
                value = mm(turned[here, :], right[:, at : at + cols], NN).astype(jnp.bfloat16)
                for src, dst, wide in place(column + at, cols):
                    room[there, dst : dst + wide] = value[:, src : src + wide]
        for p in range(i * per, (i + 1) * per):
            swap_shard(p).start()
        if i:
            for p in range((i - 1) * per, i * per):
                settle(p)
        if i in pause:
            yield
    for p in range(count - per, count):
        settle(p)
    for p in range(count):
        store(p).wait()
        if p not in sent:
            swap_shard(p).wait_send()


def tile_scratch(high, width, share, room):
    count = high // (2 * share)
    return [pltpu.VMEM((2 * STEP, width), jnp.bfloat16)] * room + [
        pltpu.VMEM((count, share, width), jnp.bfloat16),
        pltpu.SemaphoreType.DMA((count,)),
        pltpu.SemaphoreType.DMA((count,)),
        pltpu.SemaphoreType.DMA((count,)),
    ]


def fill_gu(left, right, side, outs, spare):
    half = left.shape[1] // 2

    def place(at, cols):
        return [(k, (at + k) // 256 * 128 + (at + k) // 128 % 2 * half, 128) for k in range(0, cols, 128)]

    return weight_tiles([(side[0], left, 0)], place, outs[-1], right, *spare, pause=(1,))


def mixed_index(block):
    head = lax.axis_index("head")
    return (block + head) % 2 + 2 * ((block // 2 + head // 2) % 2)


def fill_mix(left, right, side, outs, spare):
    qkvg, d_gated, mixed, probs, kst, vst, log_keep, keep_in, forget, spans, gain, _, att_t, gated, normed_t = side
    grad_far, gain_grad, bias_grad, out_ref = outs[-2], outs[2], outs[3], outs[-1]
    grad_in, grad_sem, dk_acc, dv_acc, cross, *spare = spare
    width = gated.shape[1]
    tiles = qkvg.shape[0] // TILE
    per = tiles // BLOCKS

    def tile(i, carry):
        at = tiles - 1 - i
        rel = mixed_index(at // per) * per + at % per
        rows = pl.ds(pl.multiple_of(rel * TILE, TILE), TILE)
        bwd_tile(
            i, *[qkvg.at[rows, pl.ds(k * width, width)] for k in range(4)], log_keep.at[:, rows], keep_in.at[:, rows],
            forget.at[:, rows], gain, spans, mixed.at[rows, :], probs.at[:, rows], kst.at[pl.ds(at, 1)],
            vst.at[pl.ds(at, 1)], d_gated.at[rows, :], grad_in.at[rows, :], gain_grad, bias_grad, dk_acc, dv_acc, cross,
        )
        return carry

    lax.fori_loop(0, tiles, tile, 0)
    keep = pltpu.make_async_copy(grad_in, grad_far, grad_sem.at[0])
    keep.start()
    yield
    place = lambda at, cols: [(0, at, cols)]
    yield from weight_tiles([(att_t, gated, 0), (normed_t, grad_in, width)], place, out_ref, *spare)
    keep.wait()


class Gather:
    def __init__(self, own, blocks, send_sem, got_sem):
        half = own.shape[1] // 2
        to_x, to_y = neighbours()

        def copy(slot, src, block, side_at, target):
            here = pl.ds(side_at * half, half)
            return pltpu.make_async_remote_copy(
                src_ref=src.at[:, here], dst_ref=blocks.at[block, :, here],
                send_sem=send_sem.at[slot], recv_sem=got_sem.at[slot], device_id=target, device_id_type=MESH,
            )

        self.copies = [
            copy(0, own, 1, 0, to_x),
            copy(1, own, 2, 1, to_y),
            copy(2, own, 1, 1, to_x),
            copy(3, own, 2, 0, to_y),
            copy(4, blocks.at[1], 3, 0, to_y),
            copy(5, blocks.at[2], 3, 1, to_x),
        ]

    def first(self):
        for one in self.copies[:4]:
            one.start()

    def second(self):
        for near, far in ((0, 4), (1, 5)):
            self.copies[near].wait_recv()
            self.copies[far].start()

    def last(self):
        for one in self.copies[2:]:
            one.wait_recv()
        for one in self.copies:
            one.wait_send()


def gather_kernel(plan, *refs):
    keep, product, also = plan
    refs = list(refs)
    own_ref = refs.pop(0)
    weight_far = refs.pop(0) if product else None
    also_far = refs.pop(0) if also else None
    out_ref = refs.pop(0) if keep else None
    turned_ref = refs.pop(0)
    product_ref = refs.pop(0) if product else None
    also_ref = refs.pop(0) if also else None
    blocks, turned_buf, send_sem, got_sem, out_sem, load_sem, *refs = refs
    size, half = own_ref.shape[0], own_ref.shape[1] // 2
    loads = Loads(load_sem)
    if product:
        weight = refs.pop(0)
        fetch = loads.add(weight_far.at[:, pl.ds(0, weight.shape[1])], weight)
    if also:
        also_buf, also_turned = refs
        fetch = loads.add(also_far, also_buf)
    greet(neighbours())
    gather = Gather(own_ref, blocks, send_sem, got_sem)
    gather.first()
    if product or also:
        fetch.wait()
    stores = []

    def store(src, dst):
        copy = pltpu.make_async_copy(src, dst, out_sem.at[len(stores)])
        copy.start()
        stores.append(copy)

    def use(block, side_at, src):
        here = slice(side_at * half, (side_at + 1) * half)
        rows = slice(block * size, (block + 1) * size)
        value = src[:, here]
        turned_buf[here, rows] = jnp.transpose(value)
        store(turned_buf.at[here, rows], turned_ref.at[here, rows])
        if keep:
            store(src.at[:, here], out_ref.at[block, :, here])
        if product:
            term = mm(value, weight[here, :], NN)
            if (block, side_at) in ((0, 0), (1, 0), (2, 1), (3, 0)):
                product_ref[rows, :] = term
            else:
                product_ref[rows, :] += term

    use(0, 0, own_ref)
    use(0, 1, own_ref)
    if also:
        also_turned[...] = jnp.transpose(also_buf[: also_buf.shape[0] // 2, :])
        middle = also_buf.shape[0] // 2
        store(also_turned, also_ref.at[:, pl.ds(0, middle)])
    gather.second()
    use(1, 0, blocks.at[1])
    use(2, 1, blocks.at[2])
    if also:
        stores[-1 - 4 * keep - 2 * (not keep)].wait()
        finished = len(stores) - 1 - 4 * keep - 2 * (not keep)
        also_turned[...] = jnp.transpose(also_buf[middle:, :])
        store(also_turned, also_ref.at[:, pl.ds(middle, middle)])
    for slot, block, side_at in ((2, 1, 1), (3, 2, 0), (4, 3, 0), (5, 3, 1)):
        gather.copies[slot].wait_recv()
        use(block, side_at, blocks.at[block])
    for at, one in enumerate(stores):
        if not also or at != finished:
            one.wait()
    for one in gather.copies:
        one.wait_send()


def head_gather(own, number, keep=True, weight=None, width=0, also=None):
    size, wide = own.shape
    rows = BLOCKS * size
    product = weight is not None
    extra = [one for one in (weight, also) if one is not None]
    out_shape, out_specs = [], []
    if keep:
        out_shape.append(jax.ShapeDtypeStruct((BLOCKS, size, wide), own.dtype))
        out_specs.append(FAR)
    out_shape.append(jax.ShapeDtypeStruct((wide, rows), own.dtype))
    out_specs.append(FAR)
    scratch = [
        pltpu.VMEM((BLOCKS, size, wide), own.dtype),
        pltpu.VMEM((wide, rows), own.dtype),
        pltpu.SemaphoreType.DMA((6,)),
        pltpu.SemaphoreType.DMA((6,)),
        pltpu.SemaphoreType.DMA((20,)),
        pltpu.SemaphoreType.DMA((2,)),
    ]
    if product:
        out_shape.append(jax.ShapeDtypeStruct((rows, width), jnp.float32))
        out_specs.append(WHOLE)
        scratch.append(pltpu.VMEM((wide, width), own.dtype))
    if also is not None:
        out_shape.append(jax.ShapeDtypeStruct(also.shape[::-1], also.dtype))
        out_specs.append(FAR)
        scratch += [pltpu.VMEM(also.shape, also.dtype), pltpu.VMEM((also.shape[1], also.shape[0] // 2), also.dtype)]
    return pl.pallas_call(
        functools.partial(gather_kernel, (keep, product, also is not None)),
        in_specs=[WHOLE] + [FAR] * len(extra),
        out_specs=out_specs,
        out_shape=out_shape,
        scratch_shapes=scratch,
        compiler_params=pltpu.CompilerParams(collective_id=number, has_side_effects=True, vmem_limit_bytes=LIMIT),
        cost_estimate=pl.CostEstimate(flops=10**9, bytes_accessed=1 << 20, transcendentals=0),
        name="head_gather%d" % number,
    )(own, *extra)


def unit_of(values):
    scale = lax.rsqrt(jnp.mean(values * values, axis=-1, keepdims=True) + EPSILON)
    return scale, values * scale


def finish_mixer(here, total, side, near, outs, i):
    x = side[0][here, :].astype(jnp.float32)
    gain, live = near[0][...], near[1][here, :]
    residual = x + total
    outs[0][here, :] = residual
    outs[1][here, :] = (unit_of(residual)[1] * gain).astype(jnp.bfloat16)
    add_row(outs[2], jnp.sum(live * x * x, axis=0, keepdims=True), i)
    add_row(outs[3], jnp.sum(live * total * total, axis=0, keepdims=True), i)
    add_row(outs[4], jnp.sum(live / x.shape[1] + jnp.zeros_like(x), axis=0, keepdims=True), i)


def add_row(ref, row, i):
    @pl.when(i == 0)
    def _():
        ref[...] = jnp.zeros_like(ref)

    ref[...] += row


def norm_back(total, gain, scale, unit):
    c = total * gain
    return scale * (c - unit * jnp.mean(c * unit, axis=-1, keepdims=True))


def finish_norm_two(here, total, side, near, outs, i):
    residual, cot = side[1][here, :], side[2][here, :].astype(jnp.float32)
    live, gain = near[0][here, :], near[1][...]
    scale, unit = unit_of(residual)
    add_row(outs[2], jnp.sum(total * unit, axis=0, keepdims=True), i)
    grad = cot * live + norm_back(total, gain, scale, unit)
    outs[0][here, :] = grad
    outs[1][here, :] = grad.astype(jnp.bfloat16)


def finish_ffn(here, total, side, near, outs, i):
    live = near[0][here, :]
    add_row(outs[1], jnp.sum(live * total * total, axis=0, keepdims=True), i)
    outs[0][here, :] = (live * (side[11][here, :] + total)).astype(jnp.bfloat16)


SMALL = 8


def tail_kernel(skip, grad_far, mix_far, normed_far, x_far, res_far, out_own, gain_ref, two_ref, x_sum, mix_sum, ffn_sum,
                live_sum, head_ref, bias_ref, outputs_far, input_far, total_ref, load_sem, store_sem, *rest):
    scatter = rest[:8]
    left, right = scatter[:2]
    normed, x_buf, res_buf, in_own, out_blocks, in_blocks, f_send, f_got, z_send, z_got, s_buf, s_send, s_got = rest[8:]
    loads = Loads(load_sem)
    load_left = loads.add(grad_far, left)
    parts = load_parts(loads, mix_far, right, skip)
    load_normed = loads.add(normed_far, normed)
    load_x = loads.add(x_far.at[pl.ds(0, x_buf.shape[0]), :], x_buf)
    load_res = loads.add(res_far, res_buf)
    size = in_own.shape[0]
    seq = lax.axis_index("seq")
    hops = [*neighbours(), other_core()]
    bit = 2
    while bit < lax.axis_size("seq"):
        hops.append({"seq": flipped(seq, bit)})
        bit *= 2
    greet(hops)
    sum_heads = Scatter(*scatter)

    def watch(here, value):
        term = value * normed[:, here].astype(jnp.float32)
        s_buf[0, 0:1, here] = jnp.sum(term, axis=0, keepdims=True) / gain_ref[:, here]

    f_gather = Gather(out_own, out_blocks, f_send, f_got)
    f_gather.first()
    s_buf[0] = jnp.zeros(s_buf.shape[1:], jnp.float32)
    load_left.wait()
    load_normed.wait()
    sum_heads.first(parts, watch)
    sum_heads.second(0)
    sum_heads.second(1)

    is_own = lax.broadcasted_iota(jnp.int32, (SMALL, 1), 0) >= SMALL - 2
    for k, row in enumerate((two_ref, x_sum, mix_sum, ffn_sum, live_sum)):
        s_buf[0, k + 1 : k + 2, :] = row[...]
    s_buf[0, SMALL - 2 : SMALL - 1, : head_ref.shape[1]] = head_ref[...]
    slots = bias_ref.shape[0]
    s_buf[0, SMALL - 1 : SMALL, :slots] = jnp.transpose(jnp.broadcast_to(bias_ref[...], (slots, 128)))[:1, :]
    small = [
        pltpu.make_async_remote_copy(
            src_ref=s_buf.at[2 * k], dst_ref=s_buf.at[2 * k + 1], send_sem=s_send.at[k], recv_sem=s_got.at[k],
            device_id=hop, device_id_type=MESH,
        )
        for k, hop in enumerate(hops)
    ]

    def hop_done(k):
        small[k].wait_recv()
        arrived = s_buf[2 * k + 1]
        if k < 2:
            arrived = jnp.where(is_own, 0.0, arrived)
        if k + 1 < len(small):
            s_buf[2 * k + 2] = s_buf[2 * k] + arrived
            small[k + 1].start()
        else:
            total_ref[...] = s_buf[2 * k] + arrived

    small[0].start()
    load_x.wait()
    load_res.wait()

    def finish(here, total, i):
        scale, unit = unit_of(x_buf[here, :].astype(jnp.float32))
        in_own[here, :] = (res_buf[here, :] + norm_back(total, gain_ref[...], scale, unit)).astype(jnp.bfloat16)

    f_gather.second()
    hop_done(0)
    sum_heads.last(finish)
    z_gather = Gather(in_own, in_blocks, z_send, z_got)
    z_gather.first()
    head = lax.axis_index("head")
    places = (head, flipped(head, 1), flipped(head, 2), BLOCKS - 1 - head)
    stores = []

    def store(src, far, k):
        copy = pltpu.make_async_copy(src, far.at[places[k]], store_sem.at[len(stores)])
        copy.start()
        stores.append(copy)

    store(out_own, outputs_far, 0)
    store(in_own, input_far, 0)
    hop_done(1)
    z_gather.second()
    for k in range(2, len(small)):
        hop_done(k)
    f_gather.last()
    for k in range(1, BLOCKS):
        store(out_blocks.at[k], outputs_far, k)
    z_gather.last()
    for k in range(1, BLOCKS):
        store(in_blocks.at[k], input_far, k)
    sum_heads.close()
    for one in small:
        one.wait_send()
    for one in stores:
        one.wait()


def tail_stage(hops, skip, grad_in, mix, normed, x_rel, grad_residual, out_own, small, number):
    rows, depth = grad_in.shape
    size, high = out_own.shape
    blocks = jax.ShapeDtypeStruct((BLOCKS, size, high), jnp.bfloat16)
    sems = lambda n: pltpu.SemaphoreType.DMA((n,))
    return pl.pallas_call(
        functools.partial(tail_kernel, skip),
        in_specs=[FAR] * 5 + [WHOLE] * (1 + len(small)),
        out_specs=[FAR, FAR, WHOLE],
        out_shape=[blocks, blocks, jax.ShapeDtypeStruct((SMALL, high), jnp.float32)],
        scratch_shapes=[
            sems(8),
            sems(2 * BLOCKS),
            *scatter_scratch(rows, depth, high),
            pltpu.VMEM((rows, high), jnp.bfloat16),
            pltpu.VMEM((size, high), jnp.bfloat16),
            pltpu.VMEM((size, high), jnp.float32),
            pltpu.VMEM((size, high), jnp.bfloat16),
            pltpu.VMEM((BLOCKS, size, high), jnp.bfloat16),
            pltpu.VMEM((BLOCKS, size, high), jnp.bfloat16),
            sems(6), sems(6), sems(6), sems(6),
            pltpu.VMEM((2 * hops, SMALL, high), jnp.float32),
            sems(hops), sems(hops),
        ],
        compiler_params=pltpu.CompilerParams(collective_id=number, has_side_effects=True, vmem_limit_bytes=LIMIT),
        cost_estimate=pl.CostEstimate(flops=10**9, bytes_accessed=1 << 20, transcendentals=0),
        name="tail_stage",
    )(grad_in, mix, normed, x_rel, grad_residual, out_own, *small)


def last_kernel(counts, seq_ref, input_ref, output_ref, gu_ref, mix_ref, out_w_ref, narrow_ref, down_ref, small_ref,
                input_out, output_out, q_out, k_out, v_out, go_out, f_out, gate_out, up_out, w_out_out, down_out,
                one_out, two_out, head_out, bias_out, rms_out):
    seq_count, skip, n_gain, n_bias = counts
    f32 = jnp.float32
    step = pl.program_id(0)
    input_out[...] = input_ref[...].astype(f32)
    output_out[...] = output_ref[...]
    half = gate_out.shape[1]
    gate_out[...] = gu_ref[:, :half].astype(f32)
    up_out[...] = gu_ref[:, half:].astype(f32)
    width = q_out.shape[1]
    for k, out in enumerate((q_out, k_out, v_out, go_out)):
        out[...] = mix_ref[:, skip + k * width : skip + (k + 1) * width].astype(f32)

    @pl.when(step == 0)
    def _():
        down_out[...] = jnp.transpose(down_ref[...].astype(f32))

    @pl.when(step == 1)
    def _():
        slots = f_out.shape[0]
        f_out[...] = jnp.transpose(narrow_ref[...].astype(f32))[:slots, :]
        w_out_out[...] = jnp.transpose(out_w_ref[...].astype(f32))
        share = one_out.shape[1]
        picks = [(one_out, 0, share), (two_out, 1, share), (head_out, SMALL - 2, n_gain), (bias_out, SMALL - 1, n_bias)]
        for out, row, n in picks:
            value = small_ref[row : row + 1, :n]
            for s in range(1, seq_count):
                value = jnp.where(seq_ref[0] == s, small_ref[row : row + 1, s * n : (s + 1) * n], value)
            out[...] = value
        sums = jnp.sum(small_ref[...], axis=1, keepdims=True)
        roots = jnp.sqrt(sums / (sums[5:6] * small_ref.shape[1]))
        rms_out[...] = jnp.transpose(jnp.broadcast_to(roots, (SMALL, 128)))[:1, 2:5]


def last_stage(seq_pos, seq_count, input_grad, outputs, grad_gu, grad_mix, grad_down, small, width, slots, n_gain, n_bias):
    f32 = jnp.float32
    rows, high = input_grad.shape
    share, wide_gu = grad_gu.shape
    wide_mix, hidden = grad_mix.shape[1], grad_down.shape[1]
    steps = 4
    per, part = rows // steps, share // steps
    tile = lambda a, b: pl.BlockSpec((a, b), lambda i, s: (i, 0))
    fixed = lambda a, b: pl.BlockSpec((a, b), lambda i, s: (0, 0))
    shapes = lambda *dims: [jax.ShapeDtypeStruct(one, f32) for one in dims]
    return pl.pallas_call(
        functools.partial(last_kernel, (seq_count, width, n_gain, n_bias)),
        grid_spec=pltpu.PrefetchScalarGridSpec(
            num_scalar_prefetch=1,
            grid=(steps,),
            in_specs=[tile(per, high), tile(per, high), tile(part, wide_gu), tile(part, wide_mix), fixed(share, width),
                      pl.BlockSpec((share, 2 * slots), lambda i, s: (0, wide_mix // (2 * slots) - 1)), fixed(share, hidden), fixed(SMALL, high)],
            out_specs=[tile(per, high), tile(per, high), *[tile(part, width)] * 4, fixed(slots, share),
                       *[tile(part, hidden)] * 2, fixed(width, share), fixed(hidden, share), fixed(1, share),
                       fixed(1, share), fixed(1, n_gain), fixed(1, n_bias), fixed(1, 3)],
        ),
        out_shape=[
            *shapes((rows, high)), jax.ShapeDtypeStruct((rows, high), jnp.bfloat16),
            *shapes(*[(share, width)] * 4, (slots, share), (share, hidden), (share, hidden), (width, share),
                    (hidden, share), (1, share), (1, share), (1, n_gain), (1, n_bias), (1, 3)),
        ],
        compiler_params=pltpu.CompilerParams(dimension_semantics=("arbitrary",), vmem_limit_bytes=LIMIT),
        cost_estimate=pl.CostEstimate(flops=10**7, bytes_accessed=1 << 20, transcendentals=0),
        name="last_stage",
    )(seq_pos, input_grad, outputs, grad_gu, grad_mix, grad_mix, grad_mix, grad_down, small)


def enter_kernel(count, *refs):
    (out_w, q, k, v, go, forget_w, one, two, head_gain, bias, tokens, cot, gate_w, up_w, down_w, counts, pads) = refs[:17]
    (mix_out, normed_out, grad_out, turned_out, x_out, cot_out, gu_out, down_out, qkvg_out, forget_out, rows_out) = refs[17:28]
    (buf, wide_buf, f_buf, one_buf, two_buf, head_buf, bias_buf, turned, x_buf, cot_buf, scale, normed, acc, gate_buf,
     up_buf, gu_buf, downw_buf, down_buf, cot_turned, load_sem, mix_sem, norm_sem, out_sem, r_send, r_got, l_send, l_got, x_send,
     x_got) = refs[28:]
    f32, b16 = jnp.float32, jnp.bfloat16
    seq = lax.axis_index("seq")
    place, core = seq // 2, seq % 2
    chips = count // 2
    rows = x_buf.shape[0]
    size = rows // BLOCKS
    share, width = q.shape
    slots = f_buf.shape[0]
    part, pair = share // 2, 2 * share
    own = buf.at[pl.ds(pl.multiple_of(seq * share, share), share), :]

    loads = Loads(load_sem)
    load_small = [loads.add(src, dst) for src, dst in (
        (forget_w, f_buf), (one, one_buf), (two, two_buf), (head_gain, head_buf), (bias, bias_buf))]
    load_out = loads.add(out_w, wide_buf)
    pieces = [loads.add(piece, own.at[:, pl.ds((at + 1) * width, width)]) for at, piece in enumerate((q, k, v, go))]
    load_x, load_cot = [], []
    for block in range(BLOCKS):
        there = pl.ds(pl.multiple_of(mixed_index(block) * size, size), size)
        load_x.append(loads.add(tokens.at[there, :], x_buf.at[pl.ds(block * size, size), :]))
        load_cot.append(loads.add(cot.at[there, :], cot_buf.at[pl.ds(block * size, size), :]))
    load_ffn = [loads.add(src, dst) for src, dst in ((gate_w, gate_buf), (up_w, up_buf), (down_w, downw_buf))]
    at_seq = lambda chip: {"seq": 2 * (chip % chips) + core}
    greet([at_seq(place + 1), at_seq(place + chips - 1), other_core()])

    turned[...] = jnp.zeros_like(turned)
    for load in load_small:
        load.wait()
    n = head_buf.shape[1]
    turned[:slots, :] = f_buf[...].astype(f32)
    turned[slots : slots + 1, :] = one_buf[...].astype(f32)
    turned[slots + 1 : slots + 2, :] = two_buf[...].astype(f32)
    turned[slots + 2 : slots + 3, :n] = head_buf[...].astype(f32)
    turned[slots + 2 : slots + 3, n : n + bias_buf.shape[1]] = bias_buf[...].astype(f32)
    own[:, 5 * width :] = jnp.transpose(turned[...]).astype(b16)
    load_out.wait()
    own[:, :width] = jnp.transpose(wide_buf[...])
    for load in pieces:
        load.wait()

    def remote(shard, ch, send, got, target):
        there = buf.at[pl.ds(pl.multiple_of(shard * share + ch * part, part), part), :]
        return pltpu.make_async_remote_copy(
            src_ref=there, dst_ref=there, send_sem=send, recv_sem=got, device_id=target, device_id_type=MESH
        )

    def right(d, ch):
        return remote(2 * (place - d) + core, ch, r_send.at[d, ch], r_got.at[d, ch], at_seq(place + 1))

    def left(d, ch):
        return remote(2 * (place + d) + core, ch, l_send.at[d, ch], l_got.at[d, ch], at_seq(place + chips - 1))

    def across(chip, ch):
        return remote(2 * chip + core, ch, x_send.at[chip, ch], x_got.at[chip, ch], other_core())

    for ch in range(2):
        pl.when(place < chips - 1)(right(0, ch).start)
        pl.when(place > 0)(left(0, ch).start)
    for ch in range(2):
        across(place, ch).start()

    acc[...] = jnp.zeros_like(acc)
    for load in load_x:
        load.wait()
    outs = []

    def leave(src, dst):
        copy = pltpu.make_async_copy(src, dst, out_sem.at[len(outs)])
        copy.start()
        outs.append(copy)

    leave(x_buf.at[pl.ds(0, size), :], x_out)

    def row_scale(i, carry):
        here = pl.ds(pl.multiple_of(i * CHUNK, CHUNK), CHUNK)
        scale[here, :] = unit_of(x_buf[here, :].astype(f32))[0]
        return carry

    lax.fori_loop(0, rows // CHUNK, row_scale, 0)
    for load in load_cot:
        load.wait()
    live_len = jnp.where(counts[0] > 0, rows - pads[0], 0)
    per = size // CHUNK

    def mask(i, carry):
        here = pl.ds(pl.multiple_of(i * CHUNK, CHUNK), CHUNK)
        start = mixed_index(i // per) * size + i % per * CHUNK
        live = start + lax.broadcasted_iota(jnp.int32, (CHUNK, 1), 0) < live_len
        cot_buf[here, :] = (cot_buf[here, :].astype(f32) * live.astype(f32)).astype(b16)
        return carry

    lax.fori_loop(0, rows // CHUNK, mask, 0)
    leave(cot_buf, grad_out)
    leave(cot_buf.at[pl.ds(0, size), :], cot_out)
    for load in load_ffn:
        load.wait()
    for at in range(0, gate_buf.shape[1], 128):
        gu_buf[:, 2 * at : 2 * at + 128] = gate_buf[:, at : at + 128]
        gu_buf[:, 2 * at + 128 : 2 * at + 256] = up_buf[:, at : at + 128]
    leave(gu_buf, gu_out)
    down_buf[...] = jnp.transpose(downw_buf[...])
    leave(down_buf, down_out)
    for block in range(BLOCKS):
        here = slice(block * size, (block + 1) * size)
        cot_turned[:, here] = jnp.transpose(cot_buf[here, :])
    leave(cot_turned, turned_out)

    def chip_rows(chip):
        return pl.ds(pl.multiple_of(chip * pair, pair), pair)

    def mix_store(chip):
        return pltpu.make_async_copy(buf.at[chip_rows(chip), :], mix_out.at[chip_rows(chip), :], mix_sem.at[chip])

    def norm_store(chip):
        return pltpu.make_async_copy(normed.at[:, chip_rows(chip)], normed_out.at[:, chip_rows(chip)], norm_sem.at[chip])

    def use(chip):
        for ch in range(2):
            across(chip, ch).wait_recv()
        mix_store(chip).start()
        here = chip_rows(chip)
        narrow = jnp.transpose(buf[here, 5 * width :].astype(f32))[slots : slots + 8, :]
        rows_out[:, here] = narrow
        normed[:, here] = (x_buf[:, here].astype(f32) * scale[...] * narrow[:1, :]).astype(b16)
        norm_store(chip).start()
        for at in range(width, buf.shape[1], 512):
            cols = min(512, buf.shape[1] - at)
            acc[:, at - width : at - width + cols] += mm(normed[:, here], buf[here, at : at + cols], NN)

    use(place)

    def step(d, carry):
        on_left, on_right = place >= d, place + d < chips

        @pl.when(on_left)
        def _():
            for ch in range(2):
                right(d - 1, ch).wait_recv()
                pl.when((d < chips - 1) & (place < chips - 1))(right(d, ch).start)
                across(place - d, ch).start()

        @pl.when(on_right)
        def _():
            for ch in range(2):
                left(d - 1, ch).wait_recv()
                pl.when((d < chips - 1) & (place > 0))(left(d, ch).start)
                across(place + d, ch).start()

        @pl.when(on_left)
        def _():
            use(place - d)

        @pl.when(on_right)
        def _():
            use(place + d)

        return carry

    lax.fori_loop(1, chips, step, 0)
    forget_out[...] = jnp.transpose(acc[:, 4 * width :])[:slots, :]
    outs[0].wait()
    for at in range(0, 4 * width, width):
        x_buf[:, at : at + width] = acc[:, at : at + width].astype(b16)
        leave(x_buf.at[:, pl.ds(at, width)], qkvg_out.at[:, pl.ds(at, width)])

    def close(d, carry):
        for ch in range(2):
            pl.when((place >= d) & (place < chips - 1))(right(d, ch).wait_send)
            pl.when((place + d < chips) & (place > 0))(left(d, ch).wait_send)
        return carry

    lax.fori_loop(0, chips - 1, close, 0)

    def settle(chip, carry):
        for ch in range(2):
            across(chip, ch).wait_send()
        mix_store(chip).wait()
        norm_store(chip).wait()
        return carry

    lax.fori_loop(0, chips, settle, 0)
    for one_out in outs[1:]:
        one_out.wait()


def enter_stage(count, out_w, q, k, v, go, forget, one, two, head, bias, tokens, cot, gate, up, down, counts, pads, number):
    f32, b16 = jnp.float32, jnp.bfloat16
    share, width = q.shape
    slots, hidden = forget.shape[0], gate.shape[1]
    rows, high = tokens.shape
    size, chips = rows // BLOCKS, count // 2
    mix_width = 5 * width + 2 * slots
    shape = jax.ShapeDtypeStruct
    buf = lambda array: pltpu.VMEM(array.shape, b16)
    sems = lambda *dims: pltpu.SemaphoreType.DMA(dims)
    return pl.pallas_call(
        functools.partial(enter_kernel, count),
        in_specs=[FAR] * 15 + [pl.BlockSpec(memory_space=pltpu.SMEM)] * 2,
        out_specs=[FAR] * 9 + [WHOLE] * 2,
        out_shape=[
            shape((high, mix_width), b16), shape((rows, high), b16), shape((rows, high), b16), shape((high, rows), b16), shape((size, high), b16),
            shape((size, high), b16), shape((share, 2 * hidden), b16), shape((share, hidden), b16),
            shape((rows, 4 * width), b16), shape((slots, rows), f32), shape((8, high), f32),
        ],
        scratch_shapes=[
            pltpu.VMEM((high, mix_width), b16), buf(out_w), *[buf(array) for array in (forget, one, two, head, bias)],
            pltpu.VMEM((2 * slots, share), f32), buf(tokens), buf(cot), pltpu.VMEM((rows, 1), f32), buf(tokens),
            pltpu.VMEM((rows, 4 * width + 2 * slots), f32), buf(gate), buf(up), pltpu.VMEM((share, 2 * hidden), b16),
            buf(down), pltpu.VMEM((share, hidden), b16), pltpu.VMEM((high, rows), b16), sems(21), sems(chips), sems(chips), sems(10),
            *[sems(chips, 2)] * 6,
        ],
        compiler_params=pltpu.CompilerParams(collective_id=number, has_side_effects=True, vmem_limit_bytes=LIMIT),
        cost_estimate=pl.CostEstimate(flops=10**9, bytes_accessed=1 << 20, transcendentals=0),
        name="enter_stage",
    )(out_w, q, k, v, go, forget, one, two, head, bias, tokens, cot, gate, up, down, counts, pads)


class LineGather:
    def __init__(self, count, out, own, r_send, r_got, l_send, l_got, x_send, x_got, own_sem):
        self.seq = lax.axis_index("seq")
        self.place, self.core, self.chips = self.seq // 2, self.seq % 2, count // 2
        self.out, self.own, self.share = out, own, own.shape[0]
        self.sems = r_send, r_got, l_send, l_got, x_send, x_got
        self.keep = pltpu.make_async_copy(own, out.at[pl.ds(pl.multiple_of(self.seq * self.share, self.share), self.share), :], own_sem.at[0])
        self.steps = [(d, ch) for d in range(1, self.chips) for ch in range(2)]

    def remote(self, shard, ch, is_own, send, got, target):
        part = self.share // 2
        there = self.out.at[pl.ds(pl.multiple_of(shard * self.share + ch * part, part), part), :]
        return pltpu.make_async_remote_copy(
            src_ref=self.own.at[pl.ds(ch * part, part), :] if is_own else there, dst_ref=there, send_sem=send, recv_sem=got,
            device_id=target, device_id_type=MESH,
        )

    def at_seq(self, chip):
        return {"seq": 2 * ((chip + self.chips) % self.chips) + self.core}

    def right(self, d, ch):
        send, got = self.sems[:2]
        return self.remote(2 * (self.place - d) + self.core, ch, d == 0, send.at[d, ch], got.at[d, ch], self.at_seq(self.place + 1))

    def left(self, d, ch):
        send, got = self.sems[2:4]
        return self.remote(2 * (self.place + d) + self.core, ch, d == 0, send.at[d, ch], got.at[d, ch], self.at_seq(self.place - 1))

    def across(self, chip, ch, is_own=False):
        send, got = self.sems[4:]
        return self.remote(2 * chip + self.core, ch, is_own, send.at[chip, ch], got.at[chip, ch], other_core())

    def begin(self):
        for ch in range(2):
            pl.when(self.place < self.chips - 1)(self.right(0, ch).start)
            pl.when(self.place > 0)(self.left(0, ch).start)
        for ch in range(2):
            self.across(self.place, ch, True).start()
        self.keep.start()

    def serve(self, n):
        now, self.steps = self.steps[:n], self.steps[n:]
        place, chips = self.place, self.chips
        for d, ch in now:

            @pl.when(place >= d)
            def _():
                self.right(d - 1, ch).wait_recv()
                if d < chips - 1:
                    pl.when(place < chips - 1)(self.right(d, ch).start)
                self.across(place - d, ch).start()

            @pl.when(place + d < chips)
            def _():
                self.left(d - 1, ch).wait_recv()
                if d < chips - 1:
                    pl.when(place > 0)(self.left(d, ch).start)
                self.across(place + d, ch).start()

    def finish(self):
        self.serve(len(self.steps))
        for chip in range(self.chips):
            for ch in range(2):
                self.across(chip, ch).wait_recv()
        self.keep.wait()

    def close(self):
        place, chips = self.place, self.chips
        for d in range(chips - 1):
            for ch in range(2):
                pl.when((place >= d) & (place < chips - 1))(self.right(d, ch).wait_send)
                pl.when((place + d < chips) & (place > 0))(self.left(d, ch).wait_send)
        for chip in range(chips):
            for ch in range(2):
                self.across(chip, ch).wait_send()


def mid_kernel(count, *refs):
    (qkvg_far, lk_far, keep_far, spans_far, mix_far, x_far, normed_far, gu_far, down_far, grad_far, gain_row, live_ref,
     head_gain) = refs[:13]
    (residual_ref, x_sum, mix_sum, live_sum, gated_out, mixed_out, probs_out, kst_out, vst_out, n2t_out, n1t_out, gu_out,
     downw_out, slopes_out, hidden_out, gdown_out) = refs[13:29]
    (qkvg, lk, keep_in, spans, mixed, probs, kst, vst, kacc, vacc, *rest) = refs[29:]
    scatter, rest = rest[:8], rest[8:]
    (x_buf, own, blocks, n2t, n1t, own_g, own_d, w_tiles, slopes, hidden, grad_t, room, land, store_sem, t_send, t_got,
     load_sem, out_sem, g_send, g_got, w_sem, s_sem, *z_sems) = rest
    left, right = scatter[:2]
    rows, width = left.shape
    size, high = own.shape
    half = high // 2
    f32, b16 = jnp.float32, jnp.bfloat16
    loads = Loads(load_sem)
    load_g = loads.add(gu_far, own_g)
    load_slot = [loads.add(src, dst) for src, dst in ((qkvg_far, qkvg), (lk_far, lk), (keep_far, keep_in), (spans_far, spans))]
    parts = load_parts(loads, mix_far, right, 0)
    load_x = loads.add(x_far, x_buf)
    load_d = loads.add(down_far, own_d)
    load_t = loads.add(grad_far, grad_t)
    gu = LineGather(count, gu_out, own_g, *z_sems[:7])
    down = LineGather(count, downw_out, own_d, *z_sems[7:])
    greet([*neighbours(), other_core(), gu.at_seq(gu.place + 1), gu.at_seq(gu.place - 1)])
    load_g.wait()
    gu.begin()
    pace = max(len(gu.steps) // 6, 1)
    for load in load_slot:
        load.wait()
    tiles = rows // TILE
    per = tiles // BLOCKS

    def tile(i, carry):
        rel = mixed_index(i // per) * per + i % per
        here = pl.ds(pl.multiple_of(rel * TILE, TILE), TILE)
        fwd_tile(
            i, *[qkvg.at[here, pl.ds(k * width, width)] for k in range(4)], lk.at[:, here], keep_in.at[:, here], head_gain,
            spans, left.at[here, :], mixed.at[here, :], probs.at[:, here], kst.at[pl.ds(i, 1)], vst.at[pl.ds(i, 1)], kacc,
            vacc,
        )
        return carry

    lax.fori_loop(0, tiles, tile, 0)
    outs = []

    def leave(src, dst):
        copy = pltpu.make_async_copy(src, dst, out_sem.at[len(outs)])
        copy.start()
        outs.append(copy)
        return copy

    for src, dst in ((left, gated_out), (mixed, mixed_out), (probs, probs_out), (kst, kst_out), (vst, vst_out)):
        leave(src, dst)
    load_n = loads.add(normed_far, qkvg)
    sum_heads = Scatter(*scatter)
    sum_heads.first(parts)
    gu.serve(pace)
    sum_heads.second(0)
    gu.serve(pace)
    sum_heads.second(1)
    load_x.wait()
    gu.serve(pace)
    sum_heads.last(lambda here, total, i: finish_mixer(
        here, total, [x_buf], [gain_row, live_ref], [residual_ref, own, x_sum, mix_sum, live_sum], i))
    gather = Gather(own, blocks, g_send, g_got)
    gather.first()
    gu.serve(pace)
    load_d.wait()
    down.begin()

    def use(block, side_at, src):
        here = slice(side_at * half, (side_at + 1) * half)
        there = slice(block * size, (block + 1) * size)
        n2t[here, there] = jnp.transpose(src[:, here])

    blocks[0] = own[...]
    use(0, 0, own)
    use(0, 1, own)
    load_n.wait()
    middle = rows // 2
    n1t[...] = jnp.transpose(qkvg[:middle, :])
    first_half = leave(n1t, n1t_out.at[:, pl.ds(0, middle)])
    gather.second()
    use(1, 0, blocks.at[1])
    use(2, 1, blocks.at[2])
    gu.serve(pace)
    first_half.wait()
    n1t[...] = jnp.transpose(qkvg[middle:, :])
    leave(n1t, n1t_out.at[:, pl.ds(middle, middle)])
    for slot, block, side_at in ((2, 1, 1), (3, 2, 0), (4, 3, 0), (5, 3, 1)):
        gather.copies[slot].wait_recv()
        use(block, side_at, blocks.at[block])
    leave(n2t, n2t_out)
    gu.finish()

    count_w = gu_out.shape[1] // 256

    def w_copy(j):
        return pltpu.make_async_copy(gu_out.at[:, pl.ds(pl.multiple_of(j * 256, 256), 256)], w_tiles.at[j % 2], w_sem.at[j % 2])

    def s_copy(j):
        return pltpu.make_async_copy(slopes.at[j % 2], slopes_out.at[:, pl.ds(pl.multiple_of(j * 256, 256), 256)], s_sem.at[j % 2])

    def ffn(j, carry):
        pl.when(j + 1 < count_w)(w_copy(j + 1).start)
        w_copy(j).wait()

        @pl.when(j >= 2)
        def _():
            s_copy(j - 2).wait()

        there = pl.ds(pl.multiple_of(j * 128, 128), 128)
        for k in range(2):
            here = slice(k * middle, (k + 1) * middle)
            rows_in = blocks[k * BLOCKS // 2 : (k + 1) * BLOCKS // 2].reshape(middle, high)
            value = mm(rows_in, w_tiles[j % 2], NN)
            gate, up = value[:, :128], value[:, 128:]
            sigma = jax.nn.sigmoid(gate)
            swish = gate * sigma
            slopes[j % 2, here, :128] = (up * (sigma + swish * (1.0 - sigma))).astype(b16)
            slopes[j % 2, here, 128:] = swish.astype(b16)
            hidden[here, there] = (swish * up).astype(b16)
        s_copy(j).start()
        return carry

    w_copy(0).start()
    third = count_w // 3
    lax.fori_loop(0, third, ffn, 0)
    down.serve(pace)
    lax.fori_loop(third, 2 * third, ffn, 0)
    down.serve(pace)
    lax.fori_loop(2 * third, count_w, ffn, 0)
    s_copy(count_w - 2).wait()
    s_copy(count_w - 1).wait()
    leave(hidden, hidden_out)
    load_t.wait()
    down.serve(pace)
    place = lambda at, cols: [(0, at, cols)]
    for _ in weight_tiles([(grad_t, hidden, 0)], place, gdown_out, room, land, store_sem, t_send, t_got, pause=(1,)):
        down.serve(pace)
    down.finish()
    gather_done = gather.copies
    for one in gather_done:
        one.wait_send()
    sum_heads.close()
    gu.close()
    down.close()
    for k, one in enumerate(outs):
        if one is not first_half:
            one.wait()


def mid_stage(count, qkvg, log_keep, keep_in, mix, x_own, normed1, own_gu, own_down, grad_t, gain_row, live_own, head_gain,
              number):
    f32, b16 = jnp.float32, jnp.bfloat16
    rows, width = qkvg.shape[0], qkvg.shape[1] // 4
    slots = log_keep.shape[0]
    size, high = x_own.shape
    share, wide = own_gu.shape
    chips, tiles, narrow = count // 2, rows // TILE, wide // 2
    spans = jnp.asarray(span_matrix(), b16)
    shape = jax.ShapeDtypeStruct
    buf = lambda *dims: pltpu.VMEM(dims, b16)
    full = lambda *dims: pltpu.VMEM(dims, f32)
    sems = lambda *dims: pltpu.SemaphoreType.DMA(dims)
    line = shape((1, high), f32)
    z_sems = [*[sems(chips, 2)] * 6, sems(1)]
    return pl.pallas_call(
        functools.partial(mid_kernel, count),
        in_specs=[FAR] * 10 + [WHOLE] * 3,
        out_specs=[WHOLE] * 4 + [FAR] * 12,
        out_shape=[
            shape((size, high), f32), line, line, line, shape((rows, width), b16), shape((rows, width), f32),
            shape((slots, rows), f32), shape((tiles, slots, width), b16), shape((tiles, slots, width), b16),
            shape((high, rows), b16), shape((high, rows), b16), shape((high, wide), b16), shape((high, narrow), b16),
            shape((rows, wide), b16), shape((rows, narrow), b16), shape((high // 2, narrow), b16),
        ],
        scratch_shapes=[
            buf(rows, 4 * width), full(slots, rows), full(slots, rows), buf(*spans.shape), full(rows, width),
            full(slots, rows), buf(tiles, slots, width), buf(tiles, slots, width), full(slots, width), full(slots, width),
            *scatter_scratch(rows, width, high), buf(size, high), buf(size, high), buf(BLOCKS, size, high),
            buf(high, rows), buf(high, rows // 2), buf(share, wide), buf(share, narrow), buf(2, high, 256),
            buf(2, rows, 256), buf(rows, narrow), buf(high, rows), *tile_scratch(high, narrow, share, 1), sems(13), sems(10),
            sems(6), sems(6), sems(2), sems(2), *z_sems, *z_sems,
        ],
        compiler_params=pltpu.CompilerParams(collective_id=number, has_side_effects=True, vmem_limit_bytes=LIMIT),
        cost_estimate=pl.CostEstimate(flops=10**9, bytes_accessed=1 << 20, transcendentals=0),
        name="mid_stage",
    )(qkvg, log_keep, keep_in, spans, mix, x_own, normed1, own_gu, own_down, grad_t, gain_row, live_own, head_gain)


def ffn_bwd_kernel(grad_ref, w_ref, slopes_ref, out_ref):
    half = grad_ref.shape[0] // 2
    for rows in (slice(0, half), slice(half, 2 * half)):
        value = mm(grad_ref[rows, :], w_ref[...], NN)
        for p in range(4):
            here = slice(p * 128, (p + 1) * 128)
            grad = value[:, p // 2 * 128 : (p // 2 + 1) * 128]
            out_ref[rows, here] = (grad * slopes_ref[rows, here].astype(jnp.float32)).astype(jnp.bfloat16)


def ffn_bwd(grad, weight, gu):
    rows, width = grad.shape
    wide = gu.shape[1]
    return pl.pallas_call(
        ffn_bwd_kernel,
        grid=(pl.cdiv(wide, 512),),
        in_specs=[
            pl.BlockSpec((rows, width), lambda j: (0, 0)),
            pl.BlockSpec((width, 256), lambda j: (0, j)),
            pl.BlockSpec((rows, 512), lambda j: (0, j)),
        ],
        out_specs=pl.BlockSpec((rows, 512), lambda j: (0, j)),
        out_shape=jax.ShapeDtypeStruct((rows, wide), jnp.bfloat16),
        compiler_params=pltpu.CompilerParams(dimension_semantics=("arbitrary",), vmem_limit_bytes=LIMIT),
        cost_estimate=pl.CostEstimate(flops=10**9, bytes_accessed=1 << 20, transcendentals=0),
        name="ffn_bwd",
    )(grad, weight, gu)


def after(values, *earlier):
    return lax.optimization_barrier((values, earlier))[0]


def on_device(seq_count, tokens, cotangent, counts, pads, norm1_gain, w_query, w_key, w_value, w_gate_out,
              w_forget, forget_bias, out_gain, w_out, norm2_gain, w_gate, w_up, w_down):
    f32, b16 = jnp.float32, jnp.bfloat16
    rows, model_width = tokens.shape[1:]
    head_pos = lax.axis_index("head")
    width, slots, hidden_width = w_query.shape[1], w_forget.shape[1], w_gate.shape[1]
    share = w_query.shape[0]
    extra = slots
    size = rows // BLOCKS

    wide = 4 * width
    mix, normed1, grad_ffn, grad_ffn_t, x_own, cot_own, own_gu, own_down, qkvg, forget_raw, gain_rows = enter_stage(
        seq_count, w_out, w_query, w_key, w_value, w_gate_out, w_forget.T, norm1_gain[None], norm2_gain[None],
        out_gain[None], forget_bias[None], tokens[0], cotangent[0], w_gate, w_up, w_down, counts, pads, 7,
    )

    skip = width
    row_one, row_two = gain_rows[0:1], gain_rows[1:2]
    small_all = gain_rows[2].reshape(seq_count, share)
    n_gain, n_bias = out_gain.shape[0], forget_bias.shape[0]
    gain_head = small_all[:, :n_gain].reshape(1, width)
    bias = small_all[:, n_gain : n_gain + n_bias].reshape(slots, 1)
    position = head_pos * size + jnp.arange(size, dtype=jnp.int32)[:, None]
    live_own = (position < jnp.where(counts[0] > 0, rows - pads[0], 0)).astype(f32)
    forget_t = forget_raw + bias
    log_keep = jax.nn.log_sigmoid(forget_t) / DAMPING
    keep_in = -jnp.expm1(log_keep)
    tall = lambda kind: jax.ShapeDtypeStruct((size, model_width), kind)
    line = jax.ShapeDtypeStruct((1, model_width), f32)
    seq_pos = lax.axis_index("seq")
    (residual, x_squares, mix_squares, live_sum, gated, mixed, probs, kst, vst, normed2_t, normed1_t, gu_weight,
     down_weight, gu, hidden, grad_down) = mid_stage(
        seq_count, qkvg, log_keep, keep_in, mix, x_own, normed1, own_gu, own_down, grad_ffn_t, row_two, live_own, gain_head, 0
    )
    lines = [list(range(c, seq_count, 2)) for c in range(2)]

    def line_scatter(array):
        return lax.psum_scatter(array, "seq", scatter_dimension=0, tiled=True, axis_index_groups=lines)

    grad_down = line_scatter(grad_down)
    grad_gu = ffn_bwd(grad_ffn, down_weight, gu)
    high = model_width // 2
    grad_residual, grad_low, grad_gain_two, grad_gu_w = head_scatter(
        grad_gu, gu_weight, [normed2_t, residual, cot_own], [live_own, row_two], [tall(f32), tall(b16), line],
        finish_norm_two, 2, filler=fill_gu, filled=[jax.ShapeDtypeStruct((high, gu_weight.shape[1]), b16)],
        scratch=tile_scratch(model_width, gu_weight.shape[1], share, 0),
    )
    grad_gu_w = line_scatter(grad_gu_w)
    grad_att_t, grad_gated = head_gather(grad_low, 3, keep=False, weight=mix, width=width)
    grad_gated = after(grad_gated, grad_down)
    wide_in = wide + slots + extra
    states = [pltpu.VMEM((slots, width), f32), pltpu.VMEM((slots, width), f32), pltpu.VMEM((slots, 1), f32)]
    out_own, ffn_squares, grad_gain_head, grad_bias, grad_in, grad_mix = head_scatter(
        hidden, down_weight,
        [qkvg, grad_gated, mixed, probs, kst, vst, log_keep, keep_in, forget_t, jnp.asarray(span_matrix(), b16), gain_head,
         residual, grad_att_t, gated, normed1_t],
        [live_own], [tall(b16), line, jax.ShapeDtypeStruct((1, width), f32), jax.ShapeDtypeStruct((slots, 1), f32)],
        finish_ffn, 4, filler=fill_mix,
        filled=[jax.ShapeDtypeStruct((rows, wide_in), b16),
                jax.ShapeDtypeStruct((high, mix.shape[1]), b16)],
        scratch=[pltpu.VMEM((rows, wide_in), b16), pltpu.SemaphoreType.DMA((1,)), *states,
                 *tile_scratch(model_width, mix.shape[1], share, 1)],
    )
    grad_mix = line_scatter(grad_mix)
    hops = 2 + seq_count.bit_length() - 1
    outputs, input_grad, small = tail_stage(
        hops, skip, grad_in, mix, normed1, x_own, grad_residual, out_own,
        (row_one, grad_gain_two, x_squares, mix_squares, ffn_squares, live_sum, grad_gain_head, grad_bias), 6,
    )
    (input_grad, outputs, grad_q, grad_k, grad_v, grad_go, grad_f, grad_gate, grad_up, grad_wo, grad_wd, grad_one,
     grad_two, grad_head, grad_fb, rms) = last_stage(
        seq_pos.reshape(1).astype(jnp.int32), seq_count, input_grad.reshape(rows, model_width),
        outputs.reshape(rows, model_width), grad_gu_w, grad_mix, grad_down, small, width, slots, n_gain, n_bias,
    )
    return (
        outputs[None], input_grad[None], grad_one[0], grad_q, grad_k, grad_v, grad_go, grad_f.T, grad_fb[0], grad_head[0],
        grad_wo, grad_two[0], grad_gate, grad_up, grad_wd, rms[0],
    )


def solution(mesh):
    both = P("seq", "head")
    flat = P(("head", "seq"))
    rows = P("seq", None, None)
    return jax.shard_map(
        functools.partial(on_device, mesh.shape["seq"]),
        mesh=mesh,
        in_specs=(rows, rows, P("seq"), P("seq"), P("seq"), both, both, both, both, both, flat, flat,
                  P("head", "seq"), P("seq"), both, both, P("head", "seq")),
        out_specs=(rows, rows, P("seq"), both, both, both, both, both, flat, flat, P("head", "seq"), P("seq"),
                   both, both, P("head", "seq"), P()),
        check_vma=False,
    )
```

```python
import functools

import jax
import jax.numpy as jnp
import numpy as np
from jax import lax
from jax.experimental import pallas as pl
from jax.experimental.pallas import tpu as pltpu
from jax.sharding import PartitionSpec as P

EPSILON = 1e-06
DAMPING = 8.0
TILE = 128
BLOCKS = 4
HALVES = (64, 32, 16, 8, 4, 2, 1)
NT = (((1,), (1,)), ((), ()))
NN = (((1,), (0,)), ((), ()))
TN = (((0,), (0,)), ((), ()))


def rel_tile(rows, i, h):
    per = rows // BLOCKS // TILE
    return (i // per ^ h[0]) * per + i % per


def mm(left, right, dims):
    return lax.dot_general(left, right, dims, preferred_element_type=jnp.float32)


def span_matrix():
    r = np.arange(TILE)[:, None]
    t = np.arange(TILE)[None, :]
    parts = []
    for h in HALVES:
        base = t // (2 * h) * (2 * h)
        upper = t % (2 * h) >= h
        parts.append(upper & (r >= base + h) & (r <= t))
        parts.append(~upper & (r > t) & (r <= base + h - 1))
    parts.append(r <= t)
    parts.append(r > t)
    return np.concatenate(parts, axis=1).astype(np.float32)


def level_of():
    s = lax.broadcasted_iota(jnp.int32, (TILE, TILE), 0)
    t = lax.broadcasted_iota(jnp.int32, (TILE, TILE), 1)
    return jnp.where(s < t, s ^ t, jnp.where(s == t, 0, -1))


def level_masks():
    x = level_of()
    masks = [(x >= h) & (x < 2 * h) for h in HALVES]
    masks.append(x == 0)
    return masks


def decays(log_keep, keep_in, spans):
    slots = log_keep.shape[0]
    high = log_keep.astype(jnp.bfloat16)
    rest = log_keep - high.astype(jnp.float32)
    mid = rest.astype(jnp.bfloat16)
    both = mm(jnp.concatenate([high, mid], axis=0), spans, NN)
    grown = jnp.exp(both[:slots] + both[slots:])
    n = len(HALVES)
    ones = jnp.ones_like(keep_in)
    e_parts = [grown[:, (2 * i) * TILE : (2 * i + 1) * TILE] for i in range(n)] + [ones]
    f_bare = [grown[:, (2 * i + 1) * TILE : (2 * i + 2) * TILE] for i in range(n)] + [ones]
    e_all = grown[:, 2 * n * TILE : (2 * n + 1) * TILE]
    f_all = grown[:, (2 * n + 1) * TILE : (2 * n + 2) * TILE]
    total = e_all[:, TILE - 1 : TILE]
    return e_parts, f_bare, e_all, f_all, total


def norm_gate(mixed, gain, gate_pre):
    scale = lax.rsqrt(jnp.mean(mixed * mixed, axis=-1, keepdims=True) + EPSILON)
    unit = mixed * scale
    return scale, unit


def fwd_tile(step, q_ref, k_ref, v_ref, g_ref, lk_ref, w_ref, gain_ref, spans_ref,
               gated_ref, mixed_ref, probs_ref, kst_ref, vst_ref, kacc, vacc):
    @pl.when(step == 0)
    def _():
        kacc[...] = jnp.zeros_like(kacc)
        vacc[...] = jnp.zeros_like(vacc)
    width = q_ref.shape[1]
    root = width ** -0.5
    q, k, v = q_ref[...], k_ref[...], v_ref[...]
    keep_in = w_ref[...]
    e_parts, f_bare, e_all, f_all, total = decays(lk_ref[...], keep_in, spans_ref[...])
    masks = level_masks()
    kst, vst = kacc[...], vacc[...]
    kst_b, vst_b = kst.astype(jnp.bfloat16), vst.astype(jnp.bfloat16)
    kst_ref[0] = kst_b
    vst_ref[0] = vst_b
    inner = mm(k, q, NT) * root
    inner_b = inner.astype(jnp.bfloat16)
    zero_b = jnp.zeros_like(inner_b)
    f_parts = [(bare * keep_in).astype(jnp.bfloat16) for bare in f_bare]
    scores = e_all * (mm(kst_b, q, NT) * root)
    for mask, grow, fade in zip(masks, e_parts, f_parts):
        scores += grow * mm(fade, jnp.where(mask, inner_b, zero_b), NN)
    top = jnp.max(scores, axis=0, keepdims=True)
    raised = jnp.exp(scores - top)
    probs = raised / jnp.sum(raised, axis=0, keepdims=True)
    probs_ref[...] = probs
    mixing = jnp.zeros((TILE, TILE), jnp.float32)
    for mask, grow, fade in zip(masks, e_parts, f_parts):
        mixing = jnp.where(mask, mm(fade, (probs * grow).astype(jnp.bfloat16), TN), mixing)
    mixed = mm(mixing.astype(jnp.bfloat16), v, TN) + mm((probs * e_all).astype(jnp.bfloat16), vst_b, TN)
    tail = (f_all * keep_in).astype(jnp.bfloat16)
    kacc[...] = total * kst + mm(tail, k, NN)
    vacc[...] = total * vst + mm(tail, v, NN)
    mixed_ref[...] = mixed
    scale = lax.rsqrt(jnp.mean(mixed * mixed, axis=-1, keepdims=True) + EPSILON)
    gate = g_ref[...].astype(jnp.float32)
    swish = gate * jax.nn.sigmoid(gate)
    gated_ref[...] = (mixed * scale * gain_ref[...] * swish).astype(jnp.bfloat16)


def bwd_tile(step, q_ref, k_ref, v_ref, g_ref, lk_ref, w_ref, fpre_ref, gain_ref, spans_ref,
               mixed_ref, probs_ref, kst_ref, vst_ref, dg_ref,
               dproj_ref, dgain_ref, dbias_ref, dk_acc, dv_acc, cross):
    width = q_ref.shape[1]
    slots = lk_ref.shape[0]

    @pl.when(step == 0)
    def _():
        dk_acc[...] = jnp.zeros_like(dk_acc)
        dv_acc[...] = jnp.zeros_like(dv_acc)
        cross[...] = jnp.zeros_like(cross)
        dgain_ref[...] = jnp.zeros_like(dgain_ref)
        dbias_ref[...] = jnp.zeros_like(dbias_ref)
    root = width ** -0.5
    q, k, v = q_ref[...], k_ref[...], v_ref[...]
    mixed = mixed_ref[...]
    gate = g_ref[...].astype(jnp.float32)
    gain = gain_ref[...]
    d_gated = dg_ref[...].astype(jnp.float32)
    scale = lax.rsqrt(jnp.mean(mixed * mixed, axis=-1, keepdims=True) + EPSILON)
    unit = mixed * scale
    sigma = jax.nn.sigmoid(gate)
    swish = gate * sigma
    slope = sigma * (1.0 + gate * (1.0 - sigma))
    dproj_ref[:, 3 * width : 4 * width] = (d_gated * unit * gain * slope).astype(jnp.bfloat16)
    d_normed = d_gated * swish
    dgain_ref[...] += jnp.sum(d_normed * unit, axis=0, keepdims=True)
    c = d_normed * gain
    d_mixed = scale * (c - unit * jnp.mean(c * unit, axis=-1, keepdims=True))
    d_out = d_mixed.astype(jnp.bfloat16)

    log_keep, keep_in = lk_ref[...], w_ref[...]
    e_parts, f_bare, e_all, f_all, total = decays(log_keep, keep_in, spans_ref[...])
    masks = level_masks()
    probs = probs_ref[...]
    kst, vst = kst_ref[0], vst_ref[0]
    dkst, dvst = dk_acc[...], dv_acc[...]
    dkst_b, dvst_b = dkst.astype(jnp.bfloat16), dvst.astype(jnp.bfloat16)

    inner_b = (mm(k, q, NT) * root).astype(jnp.bfloat16)
    d_mixing_b = mm(v, d_out, NT).astype(jnp.bfloat16)
    pair = jnp.concatenate([inner_b, d_mixing_b], axis=1)
    zero_b = jnp.zeros_like(pair)
    masks2 = [jnp.concatenate([mask, mask], axis=1) for mask in masks]
    pairs = [jnp.where(mask, pair, zero_b) for mask in masks2]
    f_parts = [(bare * keep_in).astype(jnp.bfloat16) for bare in f_bare]
    both = [mm(fade, two, NN) for fade, two in zip(f_parts, pairs)]
    s_state = mm(kst, q, NT) * root
    p_state = mm(vst, d_out, NT)
    d_probs = e_all * p_state
    for grow, two in zip(e_parts, both):
        d_probs += grow * two[:, TILE:]
    d_scores = probs * (d_probs - jnp.sum(probs * d_probs, axis=0, keepdims=True))

    xy_all = jnp.concatenate([d_scores * e_all, probs * e_all], axis=1).astype(jnp.bfloat16)
    xy_parts = [jnp.concatenate([d_scores * grow, probs * grow], axis=1).astype(jnp.bfloat16) for grow in e_parts]
    x0 = xy_all[:, :TILE]
    y0 = xy_all[:, TILE:]
    change = x0.astype(jnp.float32) * s_state + y0.astype(jnp.float32) * p_state
    into = jnp.zeros((slots, TILE), jnp.float32)
    d_both = jnp.zeros((TILE, 2 * TILE), jnp.float32)
    for i, (grow, bare, fade, two, xy, part, mask) in enumerate(
        zip(e_parts, f_bare, f_parts, both, xy_parts, pairs, masks2)
    ):
        z = mm(xy, part, NT)
        into += bare * z
        if i < len(HALVES):
            mass = xy.astype(jnp.float32) * two
            change += mass[:, :TILE] + mass[:, TILE:] - fade.astype(jnp.float32) * z
        d_both = jnp.where(mask, mm(fade, xy, TN), d_both)
    d_both_b = d_both.astype(jnp.bfloat16)
    d_inner, mixing = d_both_b[:, :TILE], d_both_b[:, TILE:]
    tail = (f_all * keep_in).astype(jnp.bfloat16)
    z_state = mm(dkst_b, k, NT) + mm(dvst_b, v, NT)
    into += f_all * z_state
    change -= tail.astype(jnp.float32) * z_state

    dproj_ref[:, :width] = (root * (mm(d_inner, k, TN) + mm(x0, kst, TN))).astype(jnp.bfloat16)
    dproj_ref[:, width : 2 * width] = (root * mm(d_inner, q, NN) + mm(tail, dkst_b, TN)).astype(jnp.bfloat16)
    dproj_ref[:, 2 * width : 3 * width] = (mm(mixing, d_out, NN) + mm(tail, dvst_b, TN)).astype(jnp.bfloat16)

    later = (lax.broadcasted_iota(jnp.int32, (TILE, TILE), 0) >= lax.broadcasted_iota(jnp.int32, (TILE, TILE), 1)).astype(jnp.bfloat16)
    high = change.astype(jnp.bfloat16)
    rest = change - high.astype(jnp.float32)
    mid = rest.astype(jnp.bfloat16)
    low = (rest - mid.astype(jnp.float32)).astype(jnp.bfloat16)
    sums = mm(jnp.concatenate([high, mid, low], axis=0), later, NN)
    d_log_keep = sums[:slots] + sums[slots : 2 * slots] + sums[2 * slots :] + cross[...] - jnp.exp(log_keep) * into
    d_forget = (d_log_keep * jax.nn.sigmoid(-fpre_ref[...]) / DAMPING).astype(jnp.bfloat16)
    dbias_ref[...] += jnp.sum(d_forget.astype(jnp.float32), axis=1, keepdims=True)
    turned = jnp.transpose(d_forget.astype(jnp.float32))
    dproj_ref[:, 4 * width :] = jnp.concatenate([turned, jnp.zeros_like(turned)], axis=1).astype(jnp.bfloat16)

    dkst_new = total * dkst + root * mm(x0, q, NN)
    dvst_new = total * dvst + mm(y0, d_out, NN)
    dk_acc[...] = dkst_new
    dv_acc[...] = dvst_new
    cross[...] = jnp.sum(kst.astype(jnp.float32) * dkst_new + vst.astype(jnp.float32) * dvst_new, axis=1, keepdims=True)


MESH = pl.DeviceIdType.MESH
CHUNK = 32


def neighbours():
    head = lax.axis_index("head")
    return {"head": head + 1 - 2 * (head % 2)}, {"head": (head + 2) % BLOCKS}


def flipped(index, bit):
    return index + bit - 2 * bit * (index // bit % 2)


def other_core():
    return {"seq": flipped(lax.axis_index("seq"), 1)}


def greet(targets):
    barrier = pltpu.get_barrier_semaphore()
    for target in targets:
        pl.semaphore_signal(barrier, inc=1, device_id=target, device_id_type=MESH)
    pl.semaphore_wait(barrier, len(targets))


LIMIT = 60 << 20
FAR = pl.BlockSpec(memory_space=pl.ANY)
WHOLE = pl.BlockSpec(memory_space=pltpu.VMEM)


class Loads:
    def __init__(self, sem):
        self.sem, self.copies = sem, []

    def add(self, src, dst):
        copy = pltpu.make_async_copy(src, dst, self.sem.at[len(self.copies)])
        copy.start()
        self.copies.append(copy)
        return copy


SPLIT = 2


class Scatter:
    order = tuple(side * SPLIT + u for u in range(SPLIT) for side in range(2))

    def __init__(self, left, right, acc, mid, send, got, send_sem, got_sem):
        self.left, self.right, self.acc, self.mid, self.send, self.got = left, right, acc, mid, send, got
        self.size, self.cols = send.shape[1:]
        to_x, to_y = neighbours()
        self.copies = []
        for u in range(SPLIT):
            for k, to in enumerate((to_x, to_x, to_y, to_y, to_y, to_x)):
                slot = 6 * u + k
                self.copies.append(
                    pltpu.make_async_remote_copy(
                        src_ref=send.at[slot], dst_ref=got.at[slot], send_sem=send_sem.at[slot],
                        recv_sem=got_sem.at[slot], device_id=to, device_id_type=MESH,
                    )
                )

    def first(self, loads, watch=None):
        size, cols = self.size, self.cols
        for part, load in zip(self.order, loads):
            load.wait()
            value = mm(self.left[...], self.right[part * cols : (part + 1) * cols, :], NT)
            side_at, u = part // SPLIT, part % SPLIT
            here = slice(part * cols, (part + 1) * cols)
            slot = 6 * u + 2 * side_at
            near_block, mid_block = (1, 2) if side_at == 0 else (2, 1)
            self.acc[:, here] = value[:size]
            self.mid[:, here] = value[mid_block * size : (mid_block + 1) * size]
            self.send[slot] = value[3 * size :].astype(jnp.bfloat16)
            self.copies[slot].start()
            self.send[slot + 1] = value[near_block * size : (near_block + 1) * size].astype(jnp.bfloat16)
            self.copies[slot + 1].start()
            if watch is not None:
                watch(here, value)

    def second(self, u):
        cols = self.cols
        for side_at in range(2):
            part = SPLIT * side_at + u
            first, second = 6 * u + 2 * side_at, 6 * u + 4 + side_at
            here = slice(part * cols, (part + 1) * cols)
            self.copies[first].wait_recv()
            self.send[second] = (self.mid[:, here] + self.got[first].astype(jnp.float32)).astype(jnp.bfloat16)
            self.copies[second].start()

    def last(self, finish):
        for u in range(SPLIT):
            for k in (1, 3, 4, 5):
                self.copies[6 * u + k].wait_recv()
        cols = self.cols

        def rows(i, carry):
            here = pl.ds(pl.multiple_of(i * CHUNK, CHUNK), CHUNK)
            sums = []
            for part in range(2 * SPLIT):
                side_at, u = part // SPLIT, part % SPLIT
                one, two = self.got[6 * u + 2 * side_at + 1, here, :], self.got[6 * u + 4 + side_at, here, :]
                own = self.acc[here, part * cols : (part + 1) * cols]
                sums.append(own + one.astype(jnp.float32) + two.astype(jnp.float32))
            finish(here, jnp.concatenate(sums, axis=1), i)
            return carry

        lax.fori_loop(0, self.size // CHUNK, rows, 0)

    def close(self):
        for one in self.copies:
            one.wait_send()


def scatter_scratch(rows, depth, high):
    size, cols = rows // BLOCKS, high // (2 * SPLIT)
    return [
        pltpu.VMEM((rows, depth), jnp.bfloat16),
        pltpu.VMEM((high, depth), jnp.bfloat16),
        pltpu.VMEM((size, high), jnp.float32),
        pltpu.VMEM((size, high), jnp.float32),
        pltpu.VMEM((6 * SPLIT, size, cols), jnp.bfloat16),
        pltpu.VMEM((6 * SPLIT, size, cols), jnp.bfloat16),
        pltpu.SemaphoreType.DMA((6 * SPLIT,)),
        pltpu.SemaphoreType.DMA((6 * SPLIT,)),
    ]


def load_parts(loads, right_far, right, skip):
    cols = right.shape[0] // (2 * SPLIT)
    parts = []
    for part in Scatter.order:
        here = pl.ds(part * cols, cols)
        parts.append(loads.add(right_far.at[here, pl.ds(skip, right.shape[1])], right.at[here, :]))
    return parts


def scatter_kernel(plan, *refs):
    n_far, n_near, n_out, skip, finish, filler = plan
    left_far, right_far, *more_far = refs[:n_far]
    near = refs[n_far : n_far + n_near]
    outs = refs[n_far + n_near : n_far + n_near + n_out]
    load_sem, *rest = refs[n_far + n_near + n_out :]
    scatter, spare = rest[:8], rest[8:]
    left, right = scatter[:2]
    loads = Loads(load_sem)
    load_left = loads.add(left_far, left)
    parts = load_parts(loads, right_far, right, skip)
    more = [(loads.add(src, dst), dst) for src, dst in zip(more_far, spare)]
    spare = spare[len(more_far) :]
    greet(neighbours() if filler is None else (*neighbours(), other_core()))
    sum_heads = Scatter(*scatter)
    load_left.wait()
    sum_heads.first(parts)
    for u in range(SPLIT // 2):
        sum_heads.second(u)
    for load, _ in more:
        load.wait()
    side = [dst for _, dst in more]
    if filler is not None:
        steps = filler(left, right, side, outs, spare)
        next(steps)
        for u in range(SPLIT // 2, SPLIT):
            sum_heads.second(u)
        for _ in steps:
            pass
    else:
        for u in range(SPLIT // 2, SPLIT):
            sum_heads.second(u)
    sum_heads.last(lambda here, total, i: finish(here, total, side, near, outs, i))
    sum_heads.close()


def head_scatter(left, right, far, near, out_shapes, finish, number, filler=None, filled=(), scratch=()):
    rows, depth = left.shape
    plan = (2 + len(far), len(near), len(out_shapes) + len(filled), 0, finish, filler)
    return pl.pallas_call(
        functools.partial(scatter_kernel, plan),
        in_specs=[FAR] * (2 + len(far)) + [WHOLE] * len(near),
        out_specs=[WHOLE] * len(out_shapes) + [FAR] * len(filled),
        out_shape=[*out_shapes, *filled],
        scratch_shapes=[
            pltpu.SemaphoreType.DMA((1 + 2 * SPLIT + len(far),)),
            *scatter_scratch(rows, depth, right.shape[0]),
            *[pltpu.VMEM(one.shape, one.dtype) for one in far],
            *scratch,
        ],
        compiler_params=pltpu.CompilerParams(collective_id=number, has_side_effects=True, vmem_limit_bytes=LIMIT),
        cost_estimate=pl.CostEstimate(flops=10**9, bytes_accessed=1 << 20, transcendentals=0),
        name="head_scatter%d" % number,
    )(left, right, *far, *near)


STEP = 512


def weight_tiles(pairs, place, out_ref, room, land, store_sem, send_sem, got_sem, pause=()):
    count, share = land.shape[:2]
    high = 2 * count * share
    core = lax.axis_index("seq") % 2
    per = STEP // (2 * share)

    def row(p, at):
        return (2 * p + at) * share % room.shape[0]

    def swap_shard(p):
        return pltpu.make_async_remote_copy(
            src_ref=room.at[pl.ds(row(p, 0) + (1 - core) * share, share), :], dst_ref=land.at[p],
            send_sem=send_sem.at[p], recv_sem=got_sem.at[p], device_id=other_core(), device_id_type=MESH,
        )

    def store(p):
        return pltpu.make_async_copy(land.at[p], out_ref.at[pl.ds(p * share, share), :], store_sem.at[p])

    def settle(p):
        swap_shard(p).wait_recv()
        own = room[pl.ds(pl.multiple_of(row(p, 0) + core * share, share), share), :]
        land[p] = (own.astype(jnp.float32) + land[p].astype(jnp.float32)).astype(jnp.bfloat16)
        store(p).start()

    sent = []
    for i in range(high // STEP):
        here = slice(i * STEP, (i + 1) * STEP)
        there = slice(i * STEP % room.shape[0], i * STEP % room.shape[0] + STEP)
        if (i + 1) * STEP > room.shape[0]:
            for p in range((i - 2) * per, (i - 1) * per):
                swap_shard(p).wait_send()
                sent.append(p)
        for turned, right, column in pairs:
            for at in range(0, right.shape[1], STEP):
                cols = min(STEP, right.shape[1] - at)
                value = mm(turned[here, :], right[:, at : at + cols], NN).astype(jnp.bfloat16)
                for src, dst, wide in place(column + at, cols):
                    room[there, dst : dst + wide] = value[:, src : src + wide]
        for p in range(i * per, (i + 1) * per):
            swap_shard(p).start()
        if i:
            for p in range((i - 1) * per, i * per):
                settle(p)
        if i in pause:
            yield
    for p in range(count - per, count):
        settle(p)
    for p in range(count):
        store(p).wait()
        if p not in sent:
            swap_shard(p).wait_send()


def tile_scratch(high, width, share, room):
    count = high // (2 * share)
    return [pltpu.VMEM((2 * STEP, width), jnp.bfloat16)] * room + [
        pltpu.VMEM((count, share, width), jnp.bfloat16),
        pltpu.SemaphoreType.DMA((count,)),
        pltpu.SemaphoreType.DMA((count,)),
        pltpu.SemaphoreType.DMA((count,)),
    ]


def fill_gu(left, right, side, outs, spare):
    half = left.shape[1] // 2

    def place(at, cols):
        return [(k, (at + k) // 256 * 128 + (at + k) // 128 % 2 * half, 128) for k in range(0, cols, 128)]

    return weight_tiles([(side[0], left, 0)], place, outs[-1], right, *spare, pause=(1,))


def mixed_index(block):
    head = lax.axis_index("head")
    return (block + head) % 2 + 2 * ((block // 2 + head // 2) % 2)


def fill_mix(left, right, side, outs, spare):
    qkvg, d_gated, mixed, probs, kst, vst, log_keep, keep_in, forget, spans, gain, _, att_t, gated, normed_t = side
    grad_far, gain_grad, bias_grad, out_ref = outs[-2], outs[2], outs[3], outs[-1]
    grad_in, grad_sem, dk_acc, dv_acc, cross, *spare = spare
    width = gated.shape[1]
    tiles = qkvg.shape[0] // TILE
    per = tiles // BLOCKS

    def tile(i, carry):
        at = tiles - 1 - i
        rel = mixed_index(at // per) * per + at % per
        rows = pl.ds(pl.multiple_of(rel * TILE, TILE), TILE)
        bwd_tile(
            i, *[qkvg.at[rows, pl.ds(k * width, width)] for k in range(4)], log_keep.at[:, rows], keep_in.at[:, rows],
            forget.at[:, rows], gain, spans, mixed.at[rows, :], probs.at[:, rows], kst.at[pl.ds(at, 1)],
            vst.at[pl.ds(at, 1)], d_gated.at[rows, :], grad_in.at[rows, :], gain_grad, bias_grad, dk_acc, dv_acc, cross,
        )
        return carry

    lax.fori_loop(0, tiles, tile, 0)
    keep = pltpu.make_async_copy(grad_in, grad_far, grad_sem.at[0])
    keep.start()
    yield
    place = lambda at, cols: [(0, at, cols)]
    yield from weight_tiles([(att_t, gated, 0), (normed_t, grad_in, width)], place, out_ref, *spare)
    keep.wait()


class Gather:
    def __init__(self, own, blocks, send_sem, got_sem):
        half = own.shape[1] // 2
        to_x, to_y = neighbours()

        def copy(slot, src, block, side_at, target):
            here = pl.ds(side_at * half, half)
            return pltpu.make_async_remote_copy(
                src_ref=src.at[:, here], dst_ref=blocks.at[block, :, here],
                send_sem=send_sem.at[slot], recv_sem=got_sem.at[slot], device_id=target, device_id_type=MESH,
            )

        self.copies = [
            copy(0, own, 1, 0, to_x),
            copy(1, own, 2, 1, to_y),
            copy(2, own, 1, 1, to_x),
            copy(3, own, 2, 0, to_y),
            copy(4, blocks.at[1], 3, 0, to_y),
            copy(5, blocks.at[2], 3, 1, to_x),
        ]

    def first(self):
        for one in self.copies[:4]:
            one.start()

    def second(self):
        for near, far in ((0, 4), (1, 5)):
            self.copies[near].wait_recv()
            self.copies[far].start()

    def last(self):
        for one in self.copies[2:]:
            one.wait_recv()
        for one in self.copies:
            one.wait_send()


def gather_kernel(plan, *refs):
    keep, product, also = plan
    refs = list(refs)
    own_ref = refs.pop(0)
    weight_far = refs.pop(0) if product else None
    also_far = refs.pop(0) if also else None
    out_ref = refs.pop(0) if keep else None
    turned_ref = refs.pop(0)
    product_ref = refs.pop(0) if product else None
    also_ref = refs.pop(0) if also else None
    blocks, turned_buf, send_sem, got_sem, out_sem, load_sem, *refs = refs
    size, half = own_ref.shape[0], own_ref.shape[1] // 2
    loads = Loads(load_sem)
    if product:
        weight = refs.pop(0)
        fetch = loads.add(weight_far.at[:, pl.ds(0, weight.shape[1])], weight)
    if also:
        also_buf, also_turned = refs
        fetch = loads.add(also_far, also_buf)
    greet(neighbours())
    gather = Gather(own_ref, blocks, send_sem, got_sem)
    gather.first()
    if product or also:
        fetch.wait()
    stores = []

    def store(src, dst):
        copy = pltpu.make_async_copy(src, dst, out_sem.at[len(stores)])
        copy.start()
        stores.append(copy)

    def use(block, side_at, src):
        here = slice(side_at * half, (side_at + 1) * half)
        rows = slice(block * size, (block + 1) * size)
        value = src[:, here]
        turned_buf[here, rows] = jnp.transpose(value)
        store(turned_buf.at[here, rows], turned_ref.at[here, rows])
        if keep:
            store(src.at[:, here], out_ref.at[block, :, here])
        if product:
            term = mm(value, weight[here, :], NN)
            if (block, side_at) in ((0, 0), (1, 0), (2, 1), (3, 0)):
                product_ref[rows, :] = term
            else:
                product_ref[rows, :] += term

    use(0, 0, own_ref)
    use(0, 1, own_ref)
    if also:
        also_turned[...] = jnp.transpose(also_buf[: also_buf.shape[0] // 2, :])
        middle = also_buf.shape[0] // 2
        store(also_turned, also_ref.at[:, pl.ds(0, middle)])
    gather.second()
    use(1, 0, blocks.at[1])
    use(2, 1, blocks.at[2])
    if also:
        stores[-1 - 4 * keep - 2 * (not keep)].wait()
        finished = len(stores) - 1 - 4 * keep - 2 * (not keep)
        also_turned[...] = jnp.transpose(also_buf[middle:, :])
        store(also_turned, also_ref.at[:, pl.ds(middle, middle)])
    for slot, block, side_at in ((2, 1, 1), (3, 2, 0), (4, 3, 0), (5, 3, 1)):
        gather.copies[slot].wait_recv()
        use(block, side_at, blocks.at[block])
    for at, one in enumerate(stores):
        if not also or at != finished:
            one.wait()
    for one in gather.copies:
        one.wait_send()


def head_gather(own, number, keep=True, weight=None, width=0, also=None):
    size, wide = own.shape
    rows = BLOCKS * size
    product = weight is not None
    extra = [one for one in (weight, also) if one is not None]
    out_shape, out_specs = [], []
    if keep:
        out_shape.append(jax.ShapeDtypeStruct((BLOCKS, size, wide), own.dtype))
        out_specs.append(FAR)
    out_shape.append(jax.ShapeDtypeStruct((wide, rows), own.dtype))
    out_specs.append(FAR)
    scratch = [
        pltpu.VMEM((BLOCKS, size, wide), own.dtype),
        pltpu.VMEM((wide, rows), own.dtype),
        pltpu.SemaphoreType.DMA((6,)),
        pltpu.SemaphoreType.DMA((6,)),
        pltpu.SemaphoreType.DMA((20,)),
        pltpu.SemaphoreType.DMA((2,)),
    ]
    if product:
        out_shape.append(jax.ShapeDtypeStruct((rows, width), jnp.float32))
        out_specs.append(WHOLE)
        scratch.append(pltpu.VMEM((wide, width), own.dtype))
    if also is not None:
        out_shape.append(jax.ShapeDtypeStruct(also.shape[::-1], also.dtype))
        out_specs.append(FAR)
        scratch += [pltpu.VMEM(also.shape, also.dtype), pltpu.VMEM((also.shape[1], also.shape[0] // 2), also.dtype)]
    return pl.pallas_call(
        functools.partial(gather_kernel, (keep, product, also is not None)),
        in_specs=[WHOLE] + [FAR] * len(extra),
        out_specs=out_specs,
        out_shape=out_shape,
        scratch_shapes=scratch,
        compiler_params=pltpu.CompilerParams(collective_id=number, has_side_effects=True, vmem_limit_bytes=LIMIT),
        cost_estimate=pl.CostEstimate(flops=10**9, bytes_accessed=1 << 20, transcendentals=0),
        name="head_gather%d" % number,
    )(own, *extra)


def unit_of(values):
    scale = lax.rsqrt(jnp.mean(values * values, axis=-1, keepdims=True) + EPSILON)
    return scale, values * scale


def finish_mixer(here, total, side, near, outs, i):
    x = side[0][here, :].astype(jnp.float32)
    gain, live = near[0][...], near[1][here, :]
    residual = x + total
    outs[0][here, :] = residual
    outs[1][here, :] = (unit_of(residual)[1] * gain).astype(jnp.bfloat16)
    add_row(outs[2], jnp.sum(live * x * x, axis=0, keepdims=True), i)
    add_row(outs[3], jnp.sum(live * total * total, axis=0, keepdims=True), i)
    add_row(outs[4], jnp.sum(live / x.shape[1] + jnp.zeros_like(x), axis=0, keepdims=True), i)


def add_row(ref, row, i):
    @pl.when(i == 0)
    def _():
        ref[...] = jnp.zeros_like(ref)

    ref[...] += row


def norm_back(total, gain, scale, unit):
    c = total * gain
    return scale * (c - unit * jnp.mean(c * unit, axis=-1, keepdims=True))


def finish_norm_two(here, total, side, near, outs, i):
    residual, cot = side[1][here, :], side[2][here, :].astype(jnp.float32)
    live, gain = near[0][here, :], near[1][1:2, :]
    scale, unit = unit_of(residual)
    add_row(outs[2], jnp.sum(total * unit, axis=0, keepdims=True), i)
    grad = cot * live + norm_back(total, gain, scale, unit)
    outs[0][here, :] = grad
    outs[1][here, :] = grad.astype(jnp.bfloat16)


def finish_ffn(here, total, side, near, outs, i):
    live = near[0][here, :]
    add_row(outs[1], jnp.sum(live * total * total, axis=0, keepdims=True), i)
    outs[0][here, :] = (live * (side[11][here, :] + total)).astype(jnp.bfloat16)


SMALL = 8


def tail_kernel(skip, grad_far, mix_far, normed_far, x_far, res_far, out_own, gain_ref, two_ref, x_sum, mix_sum, ffn_sum,
                live_sum, head_ref, bias_ref, outputs_far, input_far, total_ref, load_sem, store_sem, *rest):
    scatter = rest[:8]
    left, right = scatter[:2]
    normed, x_buf, res_buf, in_own, out_blocks, in_blocks, f_send, f_got, z_send, z_got, s_buf, s_send, s_got = rest[8:]
    loads = Loads(load_sem)
    load_left = loads.add(grad_far, left)
    parts = load_parts(loads, mix_far, right, skip)
    load_normed = loads.add(normed_far, normed)
    load_x = loads.add(x_far.at[pl.ds(0, x_buf.shape[0]), :], x_buf)
    load_res = loads.add(res_far, res_buf)
    size = in_own.shape[0]
    seq = lax.axis_index("seq")
    hops = [*neighbours(), other_core()]
    bit = 2
    while bit < lax.axis_size("seq"):
        hops.append({"seq": flipped(seq, bit)})
        bit *= 2
    greet(hops)
    sum_heads = Scatter(*scatter)

    def watch(here, value):
        term = value * normed[:, here].astype(jnp.float32)
        s_buf[0, 0:1, here] = jnp.sum(term, axis=0, keepdims=True) / gain_ref[0:1, here]

    f_gather = Gather(out_own, out_blocks, f_send, f_got)
    f_gather.first()
    s_buf[0] = jnp.zeros(s_buf.shape[1:], jnp.float32)
    load_left.wait()
    load_normed.wait()
    sum_heads.first(parts, watch)
    for u in range(SPLIT):
        sum_heads.second(u)

    is_own = lax.broadcasted_iota(jnp.int32, (SMALL, 1), 0) >= SMALL - 2
    for k, row in enumerate((two_ref, x_sum, mix_sum, ffn_sum, live_sum)):
        s_buf[0, k + 1 : k + 2, :] = row[...]
    s_buf[0, SMALL - 2 : SMALL - 1, : head_ref.shape[1]] = head_ref[...]
    slots = bias_ref.shape[0]
    s_buf[0, SMALL - 1 : SMALL, :slots] = jnp.transpose(jnp.broadcast_to(bias_ref[...], (slots, 128)))[:1, :]
    small = [
        pltpu.make_async_remote_copy(
            src_ref=s_buf.at[2 * k], dst_ref=s_buf.at[2 * k + 1], send_sem=s_send.at[k], recv_sem=s_got.at[k],
            device_id=hop, device_id_type=MESH,
        )
        for k, hop in enumerate(hops)
    ]

    def hop_done(k):
        small[k].wait_recv()
        arrived = s_buf[2 * k + 1]
        if k < 2:
            arrived = jnp.where(is_own, 0.0, arrived)
        if k + 1 < len(small):
            s_buf[2 * k + 2] = s_buf[2 * k] + arrived
            small[k + 1].start()
        else:
            total_ref[...] = s_buf[2 * k] + arrived

    small[0].start()
    load_x.wait()
    load_res.wait()

    def finish(here, total, i):
        scale, unit = unit_of(x_buf[here, :].astype(jnp.float32))
        in_own[here, :] = (res_buf[here, :] + norm_back(total, gain_ref[0:1, :], scale, unit)).astype(jnp.bfloat16)

    f_gather.second()
    hop_done(0)
    sum_heads.last(finish)
    z_gather = Gather(in_own, in_blocks, z_send, z_got)
    z_gather.first()
    head = lax.axis_index("head")
    places = (head, flipped(head, 1), flipped(head, 2), BLOCKS - 1 - head)
    stores = []

    def store(src, far, k):
        copy = pltpu.make_async_copy(src, far.at[places[k]], store_sem.at[len(stores)])
        copy.start()
        stores.append(copy)

    store(out_own, outputs_far, 0)
    store(in_own, input_far, 0)
    hop_done(1)
    z_gather.second()
    for k in range(2, len(small)):
        hop_done(k)
    f_gather.last()
    for k in range(1, BLOCKS):
        store(out_blocks.at[k], outputs_far, k)
    z_gather.last()
    for k in range(1, BLOCKS):
        store(in_blocks.at[k], input_far, k)
    sum_heads.close()
    for one in small:
        one.wait_send()
    for one in stores:
        one.wait()


def tail_stage(hops, skip, grad_in, mix, normed, x_rel, grad_residual, out_own, small, number):
    rows, depth = grad_in.shape
    size, high = out_own.shape
    blocks = jax.ShapeDtypeStruct((BLOCKS, size, high), jnp.bfloat16)
    sems = lambda n: pltpu.SemaphoreType.DMA((n,))
    return pl.pallas_call(
        functools.partial(tail_kernel, skip),
        in_specs=[FAR] * 5 + [WHOLE] * (1 + len(small)),
        out_specs=[FAR, FAR, WHOLE],
        out_shape=[blocks, blocks, jax.ShapeDtypeStruct((SMALL, high), jnp.float32)],
        scratch_shapes=[
            sems(4 + 2 * SPLIT),
            sems(2 * BLOCKS),
            *scatter_scratch(rows, depth, high),
            pltpu.VMEM((rows, high), jnp.bfloat16),
            pltpu.VMEM((size, high), jnp.bfloat16),
            pltpu.VMEM((size, high), jnp.float32),
            pltpu.VMEM((size, high), jnp.bfloat16),
            pltpu.VMEM((BLOCKS, size, high), jnp.bfloat16),
            pltpu.VMEM((BLOCKS, size, high), jnp.bfloat16),
            sems(6), sems(6), sems(6), sems(6),
            pltpu.VMEM((2 * hops, SMALL, high), jnp.float32),
            sems(hops), sems(hops),
        ],
        compiler_params=pltpu.CompilerParams(collective_id=number, has_side_effects=True, vmem_limit_bytes=LIMIT),
        cost_estimate=pl.CostEstimate(flops=10**9, bytes_accessed=1 << 20, transcendentals=0),
        name="tail_stage",
    )(grad_in, mix, normed, x_rel, grad_residual, out_own, *small)


def last_kernel(counts, seq_ref, input_ref, output_ref, gu_ref, mix_ref, out_w_ref, narrow_ref, down_ref, small_ref,
                input_out, output_out, q_out, k_out, v_out, go_out, f_out, gate_out, up_out, w_out_out, down_out,
                one_out, two_out, head_out, bias_out, rms_out):
    seq_count, skip, n_gain, n_bias = counts
    f32 = jnp.float32
    step = pl.program_id(0)
    input_out[...] = input_ref[...].astype(f32)
    output_out[...] = output_ref[...]
    half = gate_out.shape[1]
    gate_out[...] = gu_ref[:, :half].astype(f32)
    up_out[...] = gu_ref[:, half:].astype(f32)
    width = q_out.shape[1]
    for k, out in enumerate((q_out, k_out, v_out, go_out)):
        out[...] = mix_ref[:, skip + k * width : skip + (k + 1) * width].astype(f32)

    @pl.when(step == 0)
    def _():
        down_out[...] = jnp.transpose(down_ref[...].astype(f32))

    @pl.when(step == 1)
    def _():
        slots = f_out.shape[0]
        f_out[...] = jnp.transpose(narrow_ref[...].astype(f32))[:slots, :]
        w_out_out[...] = jnp.transpose(out_w_ref[...].astype(f32))
        share = one_out.shape[1]
        picks = [(one_out, 0, share), (two_out, 1, share), (head_out, SMALL - 2, n_gain), (bias_out, SMALL - 1, n_bias)]
        for out, row, n in picks:
            value = small_ref[row : row + 1, :n]
            for s in range(1, seq_count):
                value = jnp.where(seq_ref[0] == s, small_ref[row : row + 1, s * n : (s + 1) * n], value)
            out[...] = value
        sums = jnp.sum(small_ref[...], axis=1, keepdims=True)
        roots = jnp.sqrt(sums / (sums[5:6] * small_ref.shape[1]))
        rms_out[...] = jnp.transpose(jnp.broadcast_to(roots, (SMALL, 128)))[:1, 2:5]


def last_stage(seq_pos, seq_count, input_grad, outputs, grad_gu, grad_mix, grad_down, small, width, slots, n_gain, n_bias):
    f32 = jnp.float32
    rows, high = input_grad.shape
    share, wide_gu = grad_gu.shape
    wide_mix, hidden = grad_mix.shape[1], grad_down.shape[1]
    steps = 4
    per, part = rows // steps, share // steps
    tile = lambda a, b: pl.BlockSpec((a, b), lambda i, s: (i, 0))
    fixed = lambda a, b: pl.BlockSpec((a, b), lambda i, s: (0, 0))
    shapes = lambda *dims: [jax.ShapeDtypeStruct(one, f32) for one in dims]
    return pl.pallas_call(
        functools.partial(last_kernel, (seq_count, width, n_gain, n_bias)),
        grid_spec=pltpu.PrefetchScalarGridSpec(
            num_scalar_prefetch=1,
            grid=(steps,),
            in_specs=[tile(per, high), tile(per, high), tile(part, wide_gu), tile(part, wide_mix), fixed(share, width),
                      pl.BlockSpec((share, 2 * slots), lambda i, s: (0, wide_mix // (2 * slots) - 1)), fixed(share, hidden), fixed(SMALL, high)],
            out_specs=[tile(per, high), tile(per, high), *[tile(part, width)] * 4, fixed(slots, share),
                       *[tile(part, hidden)] * 2, fixed(width, share), fixed(hidden, share), fixed(1, share),
                       fixed(1, share), fixed(1, n_gain), fixed(1, n_bias), fixed(1, 3)],
        ),
        out_shape=[
            *shapes((rows, high)), jax.ShapeDtypeStruct((rows, high), jnp.bfloat16),
            *shapes(*[(share, width)] * 4, (slots, share), (share, hidden), (share, hidden), (width, share),
                    (hidden, share), (1, share), (1, share), (1, n_gain), (1, n_bias), (1, 3)),
        ],
        compiler_params=pltpu.CompilerParams(dimension_semantics=("arbitrary",), vmem_limit_bytes=LIMIT),
        cost_estimate=pl.CostEstimate(flops=10**7, bytes_accessed=1 << 20, transcendentals=0),
        name="last_stage",
    )(seq_pos, input_grad, outputs, grad_gu, grad_mix, grad_mix, grad_mix, grad_down, small)


def enter_kernel(count, *refs):
    (out_w, q, k, v, go, forget_w, small_far, tokens, cot, gate_w, up_w, down_w, counts, pads) = refs[:14]
    (mix_out, normed_out, grad_out, turned_out, x_out, cot_out, gu_out, down_out, qkvg_out, forget_out, rows_out) = refs[14:25]
    (buf, wide_buf, f_buf, small_buf, turned, x_buf, cot_buf, scale, normed, acc, gate_buf,
     up_buf, gu_buf, downw_buf, down_buf, cot_turned, load_sem, mix_sem, norm_sem, out_sem, r_send, r_got, l_send, l_got, x_send,
     x_got) = refs[25:]
    f32, b16 = jnp.float32, jnp.bfloat16
    seq = lax.axis_index("seq")
    place, core = seq // 2, seq % 2
    chips = count // 2
    rows = x_buf.shape[0]
    size = rows // BLOCKS
    share, width = q.shape
    slots = f_buf.shape[0]
    part, pair = share // 2, 2 * share
    own = buf.at[pl.ds(pl.multiple_of(seq * share, share), share), :]

    loads = Loads(load_sem)
    load_small = [loads.add(forget_w, f_buf), loads.add(small_far, small_buf)]
    load_out = loads.add(out_w, wide_buf)
    pieces = [loads.add(piece, own.at[:, pl.ds((at + 1) * width, width)]) for at, piece in enumerate((q, k, v, go))]
    load_x, load_cot = [], []
    for block in range(BLOCKS):
        there = pl.ds(pl.multiple_of(mixed_index(block) * size, size), size)
        load_x.append(loads.add(tokens.at[there, :], x_buf.at[pl.ds(block * size, size), :]))
        load_cot.append(loads.add(cot.at[there, :], cot_buf.at[pl.ds(block * size, size), :]))
    load_ffn = [loads.add(src, dst) for src, dst in ((gate_w, gate_buf), (up_w, up_buf), (down_w, downw_buf))]
    at_seq = lambda chip: {"seq": 2 * (chip % chips) + core}
    greet([at_seq(place + 1), at_seq(place + chips - 1), other_core()])

    turned[...] = jnp.zeros_like(turned)
    for load in load_small:
        load.wait()
    turned[:slots, :] = f_buf[...].astype(f32)
    for at in range(3):
        turned[slots + at : slots + at + 1, :] = small_buf[:, at * share : (at + 1) * share].astype(f32)
    own[:, 5 * width :] = jnp.transpose(turned[...]).astype(b16)
    load_out.wait()
    own[:, :width] = jnp.transpose(wide_buf[...])
    for load in pieces:
        load.wait()

    def remote(shard, ch, send, got, target):
        there = buf.at[pl.ds(pl.multiple_of(shard * share + ch * part, part), part), :]
        return pltpu.make_async_remote_copy(
            src_ref=there, dst_ref=there, send_sem=send, recv_sem=got, device_id=target, device_id_type=MESH
        )

    def right(d, ch):
        return remote(2 * (place - d) + core, ch, r_send.at[d, ch], r_got.at[d, ch], at_seq(place + 1))

    def left(d, ch):
        return remote(2 * (place + d) + core, ch, l_send.at[d, ch], l_got.at[d, ch], at_seq(place + chips - 1))

    def across(chip, ch):
        return remote(2 * chip + core, ch, x_send.at[chip, ch], x_got.at[chip, ch], other_core())

    for ch in range(2):
        pl.when(place < chips - 1)(right(0, ch).start)
        pl.when(place > 0)(left(0, ch).start)
    for ch in range(2):
        across(place, ch).start()

    acc[...] = jnp.zeros_like(acc)
    for load in load_x:
        load.wait()
    outs = []

    def leave(src, dst):
        copy = pltpu.make_async_copy(src, dst, out_sem.at[len(outs)])
        copy.start()
        outs.append(copy)

    leave(x_buf.at[pl.ds(0, size), :], x_out)

    def row_scale(i, carry):
        here = pl.ds(pl.multiple_of(i * CHUNK, CHUNK), CHUNK)
        scale[here, :] = unit_of(x_buf[here, :].astype(f32))[0]
        return carry

    lax.fori_loop(0, rows // CHUNK, row_scale, 0)
    for load in load_cot:
        load.wait()
    live_len = jnp.where(counts[0] > 0, rows - pads[0], 0)
    per = size // CHUNK

    def mask(i, carry):
        here = pl.ds(pl.multiple_of(i * CHUNK, CHUNK), CHUNK)
        start = mixed_index(i // per) * size + i % per * CHUNK
        live = start + lax.broadcasted_iota(jnp.int32, (CHUNK, 1), 0) < live_len
        cot_buf[here, :] = (cot_buf[here, :].astype(f32) * live.astype(f32)).astype(b16)
        return carry

    lax.fori_loop(0, rows // CHUNK, mask, 0)
    leave(cot_buf, grad_out)
    leave(cot_buf.at[pl.ds(0, size), :], cot_out)
    for load in load_ffn:
        load.wait()
    for at in range(0, gate_buf.shape[1], 128):
        gu_buf[:, 2 * at : 2 * at + 128] = gate_buf[:, at : at + 128]
        gu_buf[:, 2 * at + 128 : 2 * at + 256] = up_buf[:, at : at + 128]
    leave(gu_buf, gu_out)
    down_buf[...] = jnp.transpose(downw_buf[...])
    leave(down_buf, down_out)
    for block in range(BLOCKS):
        here = slice(block * size, (block + 1) * size)
        cot_turned[:, here] = jnp.transpose(cot_buf[here, :])
    leave(cot_turned, turned_out)

    def chip_rows(chip):
        return pl.ds(pl.multiple_of(chip * pair, pair), pair)

    def mix_store(chip):
        return pltpu.make_async_copy(buf.at[chip_rows(chip), :], mix_out.at[chip_rows(chip), :], mix_sem.at[chip])

    def norm_store(chip):
        return pltpu.make_async_copy(normed.at[:, chip_rows(chip)], normed_out.at[:, chip_rows(chip)], norm_sem.at[chip])

    def use(chip):
        for ch in range(2):
            across(chip, ch).wait_recv()
        mix_store(chip).start()
        here = chip_rows(chip)
        narrow = jnp.transpose(buf[here, 5 * width :].astype(f32))[slots : slots + 8, :]
        rows_out[:, here] = narrow
        normed[:, here] = (x_buf[:, here].astype(f32) * scale[...] * narrow[:1, :]).astype(b16)
        norm_store(chip).start()
        for at in range(width, buf.shape[1], 512):
            cols = min(512, buf.shape[1] - at)
            acc[:, at - width : at - width + cols] += mm(normed[:, here], buf[here, at : at + cols], NN)

    use(place)

    def step(d, carry):
        on_left, on_right = place >= d, place + d < chips

        @pl.when(on_left)
        def _():
            for ch in range(2):
                right(d - 1, ch).wait_recv()
                pl.when((d < chips - 1) & (place < chips - 1))(right(d, ch).start)
                across(place - d, ch).start()

        @pl.when(on_right)
        def _():
            for ch in range(2):
                left(d - 1, ch).wait_recv()
                pl.when((d < chips - 1) & (place > 0))(left(d, ch).start)
                across(place + d, ch).start()

        @pl.when(on_left)
        def _():
            use(place - d)

        @pl.when(on_right)
        def _():
            use(place + d)

        return carry

    lax.fori_loop(1, chips, step, 0)
    forget_out[...] = jnp.transpose(acc[:, 4 * width :])[:slots, :]
    outs[0].wait()
    for at in range(0, 4 * width, width):
        x_buf[:, at : at + width] = acc[:, at : at + width].astype(b16)
        leave(x_buf.at[:, pl.ds(at, width)], qkvg_out.at[:, pl.ds(at, width)])

    def close(d, carry):
        for ch in range(2):
            pl.when((place >= d) & (place < chips - 1))(right(d, ch).wait_send)
            pl.when((place + d < chips) & (place > 0))(left(d, ch).wait_send)
        return carry

    lax.fori_loop(0, chips - 1, close, 0)

    def settle(chip, carry):
        for ch in range(2):
            across(chip, ch).wait_send()
        mix_store(chip).wait()
        norm_store(chip).wait()
        return carry

    lax.fori_loop(0, chips, settle, 0)
    for one_out in outs[1:]:
        one_out.wait()


def enter_stage(count, out_w, q, k, v, go, forget, small, tokens, cot, gate, up, down, counts, pads, number):
    f32, b16 = jnp.float32, jnp.bfloat16
    share, width = q.shape
    slots, hidden = forget.shape[0], gate.shape[1]
    rows, high = tokens.shape
    size, chips = rows // BLOCKS, count // 2
    mix_width = 5 * width + 2 * slots
    shape = jax.ShapeDtypeStruct
    buf = lambda array: pltpu.VMEM(array.shape, b16)
    sems = lambda *dims: pltpu.SemaphoreType.DMA(dims)
    return pl.pallas_call(
        functools.partial(enter_kernel, count),
        in_specs=[FAR] * 12 + [pl.BlockSpec(memory_space=pltpu.SMEM)] * 2,
        out_specs=[FAR] * 9 + [WHOLE] * 2,
        out_shape=[
            shape((high, mix_width), b16), shape((rows, high), b16), shape((rows, high), b16), shape((high, rows), b16), shape((size, high), b16),
            shape((size, high), b16), shape((share, 2 * hidden), b16), shape((share, hidden), b16),
            shape((rows, 4 * width), b16), shape((slots, rows), f32), shape((8, high), f32),
        ],
        scratch_shapes=[
            pltpu.VMEM((high, mix_width), b16), buf(out_w), buf(forget), buf(small),
            pltpu.VMEM((2 * slots, share), f32), buf(tokens), buf(cot), pltpu.VMEM((rows, 1), f32), buf(tokens),
            pltpu.VMEM((rows, 4 * width + 2 * slots), f32), buf(gate), buf(up), pltpu.VMEM((share, 2 * hidden), b16),
            buf(down), pltpu.VMEM((share, hidden), b16), pltpu.VMEM((high, rows), b16), sems(21), sems(chips), sems(chips), sems(10),
            *[sems(chips, 2)] * 6,
        ],
        compiler_params=pltpu.CompilerParams(collective_id=number, has_side_effects=True, vmem_limit_bytes=LIMIT),
        cost_estimate=pl.CostEstimate(flops=10**9, bytes_accessed=1 << 20, transcendentals=0),
        name="enter_stage",
    )(out_w, q, k, v, go, forget, small, tokens, cot, gate, up, down, counts, pads)


class LineGather:
    def __init__(self, count, out, own, r_send, r_got, l_send, l_got, x_send, x_got, own_sem):
        self.seq = lax.axis_index("seq")
        self.place, self.core, self.chips = self.seq // 2, self.seq % 2, count // 2
        self.out, self.own, self.share = out, own, own.shape[0]
        self.sems = r_send, r_got, l_send, l_got, x_send, x_got
        self.keep = pltpu.make_async_copy(own, out.at[pl.ds(pl.multiple_of(self.seq * self.share, self.share), self.share), :], own_sem.at[0])
        self.steps = [(d, ch) for d in range(1, self.chips) for ch in range(2)]

    def remote(self, shard, ch, is_own, send, got, target):
        part = self.share // 2
        there = self.out.at[pl.ds(pl.multiple_of(shard * self.share + ch * part, part), part), :]
        return pltpu.make_async_remote_copy(
            src_ref=self.own.at[pl.ds(ch * part, part), :] if is_own else there, dst_ref=there, send_sem=send, recv_sem=got,
            device_id=target, device_id_type=MESH,
        )

    def at_seq(self, chip):
        return {"seq": 2 * ((chip + self.chips) % self.chips) + self.core}

    def right(self, d, ch):
        send, got = self.sems[:2]
        return self.remote(2 * (self.place - d) + self.core, ch, d == 0, send.at[d, ch], got.at[d, ch], self.at_seq(self.place + 1))

    def left(self, d, ch):
        send, got = self.sems[2:4]
        return self.remote(2 * (self.place + d) + self.core, ch, d == 0, send.at[d, ch], got.at[d, ch], self.at_seq(self.place - 1))

    def across(self, chip, ch, is_own=False):
        send, got = self.sems[4:]
        return self.remote(2 * chip + self.core, ch, is_own, send.at[chip, ch], got.at[chip, ch], other_core())

    def begin(self):
        for ch in range(2):
            pl.when(self.place < self.chips - 1)(self.right(0, ch).start)
            pl.when(self.place > 0)(self.left(0, ch).start)
        for ch in range(2):
            self.across(self.place, ch, True).start()
        self.keep.start()

    def serve(self, n):
        now, self.steps = self.steps[:n], self.steps[n:]
        place, chips = self.place, self.chips
        for d, ch in now:

            @pl.when(place >= d)
            def _():
                self.right(d - 1, ch).wait_recv()
                if d < chips - 1:
                    pl.when(place < chips - 1)(self.right(d, ch).start)
                self.across(place - d, ch).start()

            @pl.when(place + d < chips)
            def _():
                self.left(d - 1, ch).wait_recv()
                if d < chips - 1:
                    pl.when(place > 0)(self.left(d, ch).start)
                self.across(place + d, ch).start()

    def finish(self):
        self.serve(len(self.steps))
        for chip in range(self.chips):
            for ch in range(2):
                self.across(chip, ch).wait_recv()
        self.keep.wait()

    def close(self):
        place, chips = self.place, self.chips
        for d in range(chips - 1):
            for ch in range(2):
                pl.when((place >= d) & (place < chips - 1))(self.right(d, ch).wait_send)
                pl.when((place + d < chips) & (place > 0))(self.left(d, ch).wait_send)
        for chip in range(chips):
            for ch in range(2):
                self.across(chip, ch).wait_send()


def gate_decays(forget):
    small = jnp.exp(-jnp.abs(forget))
    series = small * (1.0 - small * (0.5 - small * (1.0 / 3.0 - small * (0.25 - small * 0.2))))
    soft = jnp.where(small < 0.05, series, jnp.log(1.0 + small))
    log_keep = (jnp.minimum(forget, 0.0) - soft) / DAMPING
    grown = 1.0 + log_keep * (0.25 + log_keep * 0.05)
    series = -log_keep * (1.0 + log_keep * (0.5 + log_keep * (1.0 / 6.0) * grown))
    return log_keep, jnp.where(log_keep > -0.1, series, 1.0 - jnp.exp(log_keep))


def mid_kernel(count, *refs):
    (qkvg_far, forget_far, spans_far, mix_far, x_far, normed_far, gu_far, down_far, grad_far, gain_rows, live_ref) = refs[:11]
    (residual_ref, x_sum, mix_sum, live_sum, head_gain, gated_out, mixed_out, probs_out, kst_out, vst_out, n2t_out, n1t_out,
     gu_out, downw_out, slopes_out, hidden_out, gdown_out, forget_out, lk_out, keep_out) = refs[11:31]
    (qkvg, forget, lk, keep_in, spans, mixed, probs, kst, vst, kacc, vacc, *rest) = refs[31:]
    scatter, rest = rest[:8], rest[8:]
    (x_buf, own, blocks, n2t, n1t, own_g, own_d, w_tiles, slopes, hidden, grad_t, room, land, store_sem, t_send, t_got,
     load_sem, out_sem, g_send, g_got, w_sem, s_sem, *z_sems) = rest
    left, right = scatter[:2]
    rows, width = left.shape
    size, high = own.shape
    half = high // 2
    f32, b16 = jnp.float32, jnp.bfloat16
    loads = Loads(load_sem)
    load_g = loads.add(gu_far, own_g)
    load_slot = [loads.add(src, dst) for src, dst in ((forget_far, forget), (qkvg_far, qkvg), (spans_far, spans))]
    parts = load_parts(loads, mix_far, right, 0)
    load_x = loads.add(x_far, x_buf)
    load_d = loads.add(down_far, own_d)
    load_t = loads.add(grad_far, grad_t)
    gu = LineGather(count, gu_out, own_g, *z_sems[:7])
    down = LineGather(count, downw_out, own_d, *z_sems[7:])
    greet([*neighbours(), other_core(), gu.at_seq(gu.place + 1), gu.at_seq(gu.place - 1)])
    load_g.wait()
    gu.begin()
    pace = max(len(gu.steps) // 6, 1)
    small = gain_rows[2:3, :]
    share = own_g.shape[0]
    n_gain, n_bias = width // count, forget.shape[0] // count
    head_gain[...] = jnp.concatenate([small[:, s * share : s * share + n_gain] for s in range(count)], axis=1)
    bias = jnp.concatenate([small[:, s * share + n_gain : s * share + n_gain + n_bias] for s in range(count)], axis=1)
    for load in load_slot:
        load.wait()
    forget[...] += jnp.transpose(jnp.broadcast_to(bias, (8, bias.shape[1])))[:, :1]
    lk[...], keep_in[...] = gate_decays(forget[...])
    tiles = rows // TILE
    per = tiles // BLOCKS

    def tile(i, carry):
        rel = mixed_index(i // per) * per + i % per
        here = pl.ds(pl.multiple_of(rel * TILE, TILE), TILE)
        fwd_tile(
            i, *[qkvg.at[here, pl.ds(k * width, width)] for k in range(4)], lk.at[:, here], keep_in.at[:, here], head_gain,
            spans, left.at[here, :], mixed.at[here, :], probs.at[:, here], kst.at[pl.ds(i, 1)], vst.at[pl.ds(i, 1)], kacc,
            vacc,
        )
        return carry

    lax.fori_loop(0, tiles, tile, 0)
    outs = []

    def leave(src, dst):
        copy = pltpu.make_async_copy(src, dst, out_sem.at[len(outs)])
        copy.start()
        outs.append(copy)
        return copy

    for src, dst in ((left, gated_out), (mixed, mixed_out), (probs, probs_out), (kst, kst_out), (vst, vst_out),
                     (forget, forget_out), (lk, lk_out), (keep_in, keep_out)):
        leave(src, dst)
    load_n = loads.add(normed_far, qkvg)
    sum_heads = Scatter(*scatter)
    sum_heads.first(parts)
    gu.serve(pace)
    for u in range(SPLIT // 2):
        sum_heads.second(u)
    gu.serve(pace)
    for u in range(SPLIT // 2, SPLIT):
        sum_heads.second(u)
    load_x.wait()
    gu.serve(pace)
    sum_heads.last(lambda here, total, i: finish_mixer(
        here, total, [x_buf], [gain_rows.at[pl.ds(1, 1), :], live_ref], [residual_ref, own, x_sum, mix_sum, live_sum], i))
    gather = Gather(own, blocks, g_send, g_got)
    gather.first()
    gu.serve(pace)
    load_d.wait()
    down.begin()

    def use(block, side_at, src):
        here = slice(side_at * half, (side_at + 1) * half)
        there = slice(block * size, (block + 1) * size)
        n2t[here, there] = jnp.transpose(src[:, here])

    blocks[0] = own[...]
    use(0, 0, own)
    use(0, 1, own)
    load_n.wait()
    middle = rows // 2
    n1t[...] = jnp.transpose(qkvg[:middle, :])
    first_half = leave(n1t, n1t_out.at[:, pl.ds(0, middle)])
    gather.second()
    use(1, 0, blocks.at[1])
    use(2, 1, blocks.at[2])
    gu.serve(pace)
    first_half.wait()
    n1t[...] = jnp.transpose(qkvg[middle:, :])
    leave(n1t, n1t_out.at[:, pl.ds(middle, middle)])
    for slot, block, side_at in ((2, 1, 1), (3, 2, 0), (4, 3, 0), (5, 3, 1)):
        gather.copies[slot].wait_recv()
        use(block, side_at, blocks.at[block])
    leave(n2t, n2t_out)
    gu.finish()

    count_w = gu_out.shape[1] // 256

    def w_copy(j):
        return pltpu.make_async_copy(gu_out.at[:, pl.ds(pl.multiple_of(j * 256, 256), 256)], w_tiles.at[j % 2], w_sem.at[j % 2])

    def s_copy(j):
        return pltpu.make_async_copy(slopes.at[j % 2], slopes_out.at[:, pl.ds(pl.multiple_of(j * 256, 256), 256)], s_sem.at[j % 2])

    def ffn(j, carry):
        pl.when(j + 1 < count_w)(w_copy(j + 1).start)
        w_copy(j).wait()

        @pl.when(j >= 2)
        def _():
            s_copy(j - 2).wait()

        there = pl.ds(pl.multiple_of(j * 128, 128), 128)
        for k in range(2):
            here = slice(k * middle, (k + 1) * middle)
            rows_in = blocks[k * BLOCKS // 2 : (k + 1) * BLOCKS // 2].reshape(middle, high)
            value = mm(rows_in, w_tiles[j % 2], NN)
            gate, up = value[:, :128], value[:, 128:]
            sigma = jax.nn.sigmoid(gate)
            swish = gate * sigma
            slopes[j % 2, here, :128] = (up * (sigma + swish * (1.0 - sigma))).astype(b16)
            slopes[j % 2, here, 128:] = swish.astype(b16)
            hidden[here, there] = (swish * up).astype(b16)
        s_copy(j).start()
        return carry

    w_copy(0).start()
    third = count_w // 3
    lax.fori_loop(0, third, ffn, 0)
    down.serve(pace)
    lax.fori_loop(third, 2 * third, ffn, 0)
    down.serve(pace)
    lax.fori_loop(2 * third, count_w, ffn, 0)
    s_copy(count_w - 2).wait()
    s_copy(count_w - 1).wait()
    leave(hidden, hidden_out)
    load_t.wait()
    down.serve(pace)
    place = lambda at, cols: [(0, at, cols)]
    for _ in weight_tiles([(grad_t, hidden, 0)], place, gdown_out, room, land, store_sem, t_send, t_got, pause=(1,)):
        down.serve(pace)
    down.finish()
    gather_done = gather.copies
    for one in gather_done:
        one.wait_send()
    sum_heads.close()
    gu.close()
    down.close()
    for k, one in enumerate(outs):
        if one is not first_half:
            one.wait()


def mid_stage(count, qkvg, forget, mix, x_own, normed1, own_gu, own_down, grad_t, gain_rows, live_own, number):
    f32, b16 = jnp.float32, jnp.bfloat16
    rows, width = qkvg.shape[0], qkvg.shape[1] // 4
    slots = forget.shape[0]
    size, high = x_own.shape
    share, wide = own_gu.shape
    chips, tiles, narrow = count // 2, rows // TILE, wide // 2
    spans = jnp.asarray(span_matrix(), b16)
    shape = jax.ShapeDtypeStruct
    buf = lambda *dims: pltpu.VMEM(dims, b16)
    full = lambda *dims: pltpu.VMEM(dims, f32)
    sems = lambda *dims: pltpu.SemaphoreType.DMA(dims)
    line = shape((1, high), f32)
    z_sems = [*[sems(chips, 2)] * 6, sems(1)]
    return pl.pallas_call(
        functools.partial(mid_kernel, count),
        in_specs=[FAR] * 9 + [WHOLE] * 2,
        out_specs=[WHOLE] * 5 + [FAR] * 15,
        out_shape=[
            shape((size, high), f32), line, line, line, shape((1, width), f32), shape((rows, width), b16), shape((rows, width), f32),
            shape((slots, rows), f32), shape((tiles, slots, width), b16), shape((tiles, slots, width), b16),
            shape((high, rows), b16), shape((high, rows), b16), shape((high, wide), b16), shape((high, narrow), b16),
            shape((rows, wide), b16), shape((rows, narrow), b16), shape((high // 2, narrow), b16),
            *[shape((slots, rows), f32)] * 3,
        ],
        scratch_shapes=[
            buf(rows, 4 * width), full(slots, rows), full(slots, rows), full(slots, rows), buf(*spans.shape), full(rows, width),
            full(slots, rows), buf(tiles, slots, width), buf(tiles, slots, width), full(slots, width), full(slots, width),
            *scatter_scratch(rows, width, high), buf(size, high), buf(size, high), buf(BLOCKS, size, high),
            buf(high, rows), buf(high, rows // 2), buf(share, wide), buf(share, narrow), buf(2, high, 256),
            buf(2, rows, 256), buf(rows, narrow), buf(high, rows), *tile_scratch(high, narrow, share, 1), sems(8 + 2 * SPLIT), sems(13),
            sems(6), sems(6), sems(2), sems(2), *z_sems, *z_sems,
        ],
        compiler_params=pltpu.CompilerParams(collective_id=number, has_side_effects=True, vmem_limit_bytes=LIMIT),
        cost_estimate=pl.CostEstimate(flops=10**9, bytes_accessed=1 << 20, transcendentals=0),
        name="mid_stage",
    )(qkvg, forget, spans, mix, x_own, normed1, own_gu, own_down, grad_t, gain_rows, live_own)


def ffn_bwd_kernel(grad_ref, w_ref, slopes_ref, out_ref):
    value = mm(grad_ref[...], w_ref[...], NN)
    for p in range(4):
        here = slice(p * 128, (p + 1) * 128)
        grad = value[:, p // 2 * 128 : (p // 2 + 1) * 128]
        out_ref[:, here] = (grad * slopes_ref[:, here].astype(jnp.float32)).astype(jnp.bfloat16)


def ffn_bwd(grad, weight, gu):
    rows, width = grad.shape
    wide = gu.shape[1]
    return pl.pallas_call(
        ffn_bwd_kernel,
        grid=(pl.cdiv(wide, 512),),
        in_specs=[
            pl.BlockSpec((rows, width), lambda j: (0, 0)),
            pl.BlockSpec((width, 256), lambda j: (0, j)),
            pl.BlockSpec((rows, 512), lambda j: (0, j)),
        ],
        out_specs=pl.BlockSpec((rows, 512), lambda j: (0, j)),
        out_shape=jax.ShapeDtypeStruct((rows, wide), jnp.bfloat16),
        compiler_params=pltpu.CompilerParams(dimension_semantics=("arbitrary",), vmem_limit_bytes=LIMIT),
        cost_estimate=pl.CostEstimate(flops=10**9, bytes_accessed=1 << 20, transcendentals=0),
        name="ffn_bwd",
    )(grad, weight, gu)


def after(values, *earlier):
    return lax.optimization_barrier((values, earlier))[0]


def on_device(seq_count, tokens, cotangent, counts, pads, norm1_gain, w_query, w_key, w_value, w_gate_out,
              w_forget, forget_bias, out_gain, w_out, norm2_gain, w_gate, w_up, w_down):
    f32, b16 = jnp.float32, jnp.bfloat16
    rows, model_width = tokens.shape[1:]
    head_pos = lax.axis_index("head")
    width, slots, hidden_width = w_query.shape[1], w_forget.shape[1], w_gate.shape[1]
    share = w_query.shape[0]
    extra = slots
    size = rows // BLOCKS

    wide = 4 * width
    small = jnp.concatenate([norm1_gain, norm2_gain, out_gain, forget_bias])
    small = jnp.pad(small, (0, 3 * share - small.shape[0]))
    mix, normed1, grad_ffn, grad_ffn_t, x_own, cot_own, own_gu, own_down, qkvg, forget_raw, gain_rows = enter_stage(
        seq_count, w_out, w_query, w_key, w_value, w_gate_out, w_forget.T, small[None], tokens[0], cotangent[0], w_gate, w_up, w_down, counts, pads, 7,
    )

    skip = width
    n_gain, n_bias = out_gain.shape[0], forget_bias.shape[0]
    position = head_pos * size + jnp.arange(size, dtype=jnp.int32)[:, None]
    live_own = (position < jnp.where(counts[0] > 0, rows - pads[0], 0)).astype(f32)
    tall = lambda kind: jax.ShapeDtypeStruct((size, model_width), kind)
    line = jax.ShapeDtypeStruct((1, model_width), f32)
    seq_pos = lax.axis_index("seq")
    (residual, x_squares, mix_squares, live_sum, gain_head, gated, mixed, probs, kst, vst, normed2_t, normed1_t, gu_weight,
     down_weight, gu, hidden, grad_down, forget_t, log_keep, keep_in) = mid_stage(
        seq_count, qkvg, forget_raw, mix, x_own, normed1, own_gu, own_down, grad_ffn_t, gain_rows, live_own, 0
    )
    lines = [list(range(c, seq_count, 2)) for c in range(2)]

    def line_scatter(array):
        return lax.psum_scatter(array, "seq", scatter_dimension=0, tiled=True, axis_index_groups=lines)

    grad_down = line_scatter(grad_down)
    grad_gu = ffn_bwd(grad_ffn, down_weight, gu)
    high = model_width // 2
    grad_residual, grad_low, grad_gain_two, grad_gu_w = head_scatter(
        grad_gu, gu_weight, [normed2_t, residual, cot_own], [live_own, gain_rows], [tall(f32), tall(b16), line],
        finish_norm_two, 2, filler=fill_gu, filled=[jax.ShapeDtypeStruct((high, gu_weight.shape[1]), b16)],
        scratch=tile_scratch(model_width, gu_weight.shape[1], share, 0),
    )
    grad_gu_w = line_scatter(grad_gu_w)
    grad_att_t, grad_gated = head_gather(grad_low, 3, keep=False, weight=mix, width=width)
    grad_gated = after(grad_gated, grad_down)
    wide_in = wide + slots + extra
    states = [pltpu.VMEM((slots, width), f32), pltpu.VMEM((slots, width), f32), pltpu.VMEM((slots, 1), f32)]
    out_own, ffn_squares, grad_gain_head, grad_bias, grad_in, grad_mix = head_scatter(
        hidden, down_weight,
        [qkvg, grad_gated, mixed, probs, kst, vst, log_keep, keep_in, forget_t, jnp.asarray(span_matrix(), b16), gain_head,
         residual, grad_att_t, gated, normed1_t],
        [live_own], [tall(b16), line, jax.ShapeDtypeStruct((1, width), f32), jax.ShapeDtypeStruct((slots, 1), f32)],
        finish_ffn, 4, filler=fill_mix,
        filled=[jax.ShapeDtypeStruct((rows, wide_in), b16),
                jax.ShapeDtypeStruct((high, mix.shape[1]), b16)],
        scratch=[pltpu.VMEM((rows, wide_in), b16), pltpu.SemaphoreType.DMA((1,)), *states,
                 *tile_scratch(model_width, mix.shape[1], share, 1)],
    )
    grad_mix = line_scatter(grad_mix)
    hops = 2 + seq_count.bit_length() - 1
    outputs, input_grad, small = tail_stage(
        hops, skip, grad_in, mix, normed1, x_own, grad_residual, out_own,
        (gain_rows, grad_gain_two, x_squares, mix_squares, ffn_squares, live_sum, grad_gain_head, grad_bias), 6,
    )
    (input_grad, outputs, grad_q, grad_k, grad_v, grad_go, grad_f, grad_gate, grad_up, grad_wo, grad_wd, grad_one,
     grad_two, grad_head, grad_fb, rms) = last_stage(
        seq_pos.reshape(1).astype(jnp.int32), seq_count, input_grad.reshape(rows, model_width),
        outputs.reshape(rows, model_width), grad_gu_w, grad_mix, grad_down, small, width, slots, n_gain, n_bias,
    )
    return (
        outputs[None], input_grad[None], grad_one[0], grad_q, grad_k, grad_v, grad_go, grad_f.T, grad_fb[0], grad_head[0],
        grad_wo, grad_two[0], grad_gate, grad_up, grad_wd, rms[0],
    )


def solution(mesh):
    both = P("seq", "head")
    flat = P(("head", "seq"))
    rows = P("seq", None, None)
    return jax.shard_map(
        functools.partial(on_device, mesh.shape["seq"]),
        mesh=mesh,
        in_specs=(rows, rows, P("seq"), P("seq"), P("seq"), both, both, both, both, both, flat, flat,
                  P("head", "seq"), P("seq"), both, both, P("head", "seq")),
        out_specs=(rows, rows, P("seq"), both, both, both, both, both, flat, flat, P("head", "seq"), P("seq"),
                   both, both, P("head", "seq"), P()),
        check_vma=False,
    )
```

```python
import functools

import jax
import jax.numpy as jnp
import numpy as np
from jax import lax
from jax.experimental import pallas as pl
from jax.experimental.pallas import tpu as pltpu
from jax.sharding import PartitionSpec as P

EPSILON = 1e-06
DAMPING = 8.0
TILE = 128
BLOCKS = 4
HALVES = (64, 32, 16, 8, 4, 2, 1)
NT = (((1,), (1,)), ((), ()))
NN = (((1,), (0,)), ((), ()))
TN = (((0,), (0,)), ((), ()))


def rel_tile(rows, i, h):
    per = rows // BLOCKS // TILE
    return (i // per ^ h[0]) * per + i % per


def mm(left, right, dims):
    return lax.dot_general(left, right, dims, preferred_element_type=jnp.float32)


def span_matrix():
    r = np.arange(TILE)[:, None]
    t = np.arange(TILE)[None, :]
    parts = []
    for h in HALVES:
        base = t // (2 * h) * (2 * h)
        upper = t % (2 * h) >= h
        parts.append(upper & (r >= base + h) & (r <= t))
        parts.append(~upper & (r > t) & (r <= base + h - 1))
    parts.append(r <= t)
    parts.append(r > t)
    return np.concatenate(parts, axis=1).astype(np.float32)


def level_of():
    s = lax.broadcasted_iota(jnp.int32, (TILE, TILE), 0)
    t = lax.broadcasted_iota(jnp.int32, (TILE, TILE), 1)
    return jnp.where(s < t, s ^ t, jnp.where(s == t, 0, -1))


def level_masks():
    x = level_of()
    masks = [(x >= h) & (x < 2 * h) for h in HALVES]
    masks.append(x == 0)
    return masks


def decays(log_keep, keep_in, spans):
    slots = log_keep.shape[0]
    high = log_keep.astype(jnp.bfloat16)
    rest = log_keep - high.astype(jnp.float32)
    mid = rest.astype(jnp.bfloat16)
    both = mm(jnp.concatenate([high, mid], axis=0), spans, NN)
    grown = jnp.exp(both[:slots] + both[slots:])
    n = len(HALVES)
    ones = jnp.ones_like(keep_in)
    e_parts = [grown[:, (2 * i) * TILE : (2 * i + 1) * TILE] for i in range(n)] + [ones]
    f_bare = [grown[:, (2 * i + 1) * TILE : (2 * i + 2) * TILE] for i in range(n)] + [ones]
    e_all = grown[:, 2 * n * TILE : (2 * n + 1) * TILE]
    f_all = grown[:, (2 * n + 1) * TILE : (2 * n + 2) * TILE]
    total = e_all[:, TILE - 1 : TILE]
    return e_parts, f_bare, e_all, f_all, total


def norm_gate(mixed, gain, gate_pre):
    scale = lax.rsqrt(jnp.mean(mixed * mixed, axis=-1, keepdims=True) + EPSILON)
    unit = mixed * scale
    return scale, unit


def fwd_tile(step, q_ref, k_ref, v_ref, g_ref, lk_ref, w_ref, gain_ref, spans_ref,
               gated_ref, mixed_ref, probs_ref, kst_ref, vst_ref, kacc, vacc):
    @pl.when(step == 0)
    def _():
        kacc[...] = jnp.zeros_like(kacc)
        vacc[...] = jnp.zeros_like(vacc)
    width = q_ref.shape[1]
    root = width ** -0.5
    q, k, v = q_ref[...], k_ref[...], v_ref[...]
    keep_in = w_ref[...]
    e_parts, f_bare, e_all, f_all, total = decays(lk_ref[...], keep_in, spans_ref[...])
    masks = level_masks()
    kst, vst = kacc[...], vacc[...]
    kst_b, vst_b = kst.astype(jnp.bfloat16), vst.astype(jnp.bfloat16)
    kst_ref[0] = kst_b
    vst_ref[0] = vst_b
    inner = mm(k, q, NT) * root
    inner_b = inner.astype(jnp.bfloat16)
    zero_b = jnp.zeros_like(inner_b)
    f_parts = [(bare * keep_in).astype(jnp.bfloat16) for bare in f_bare]
    scores = e_all * (mm(kst_b, q, NT) * root)
    for mask, grow, fade in zip(masks, e_parts, f_parts):
        scores += grow * mm(fade, jnp.where(mask, inner_b, zero_b), NN)
    top = jnp.max(scores, axis=0, keepdims=True)
    raised = jnp.exp(scores - top)
    probs = raised / jnp.sum(raised, axis=0, keepdims=True)
    probs_ref[...] = probs
    mixing = jnp.zeros((TILE, TILE), jnp.float32)
    for mask, grow, fade in zip(masks, e_parts, f_parts):
        mixing = jnp.where(mask, mm(fade, (probs * grow).astype(jnp.bfloat16), TN), mixing)
    mixed = mm(mixing.astype(jnp.bfloat16), v, TN) + mm((probs * e_all).astype(jnp.bfloat16), vst_b, TN)
    tail = (f_all * keep_in).astype(jnp.bfloat16)
    kacc[...] = total * kst + mm(tail, k, NN)
    vacc[...] = total * vst + mm(tail, v, NN)
    mixed_ref[...] = mixed
    scale = lax.rsqrt(jnp.mean(mixed * mixed, axis=-1, keepdims=True) + EPSILON)
    gate = g_ref[...].astype(jnp.float32)
    swish = gate * jax.nn.sigmoid(gate)
    gated_ref[...] = (mixed * scale * gain_ref[...] * swish).astype(jnp.bfloat16)


def bwd_tile(step, q_ref, k_ref, v_ref, g_ref, lk_ref, w_ref, fpre_ref, gain_ref, spans_ref,
               mixed_ref, probs_ref, kst_ref, vst_ref, dg_ref,
               dproj_ref, dgain_ref, dbias_ref, dk_acc, dv_acc, cross):
    width = q_ref.shape[1]
    slots = lk_ref.shape[0]

    @pl.when(step == 0)
    def _():
        dk_acc[...] = jnp.zeros_like(dk_acc)
        dv_acc[...] = jnp.zeros_like(dv_acc)
        cross[...] = jnp.zeros_like(cross)
        dgain_ref[...] = jnp.zeros_like(dgain_ref)
        dbias_ref[...] = jnp.zeros_like(dbias_ref)
    root = width ** -0.5
    q, k, v = q_ref[...], k_ref[...], v_ref[...]
    mixed = mixed_ref[...]
    gate = g_ref[...].astype(jnp.float32)
    gain = gain_ref[...]
    d_gated = dg_ref[...].astype(jnp.float32)
    scale = lax.rsqrt(jnp.mean(mixed * mixed, axis=-1, keepdims=True) + EPSILON)
    unit = mixed * scale
    sigma = jax.nn.sigmoid(gate)
    swish = gate * sigma
    slope = sigma * (1.0 + gate * (1.0 - sigma))
    dproj_ref[:, 3 * width : 4 * width] = (d_gated * unit * gain * slope).astype(jnp.bfloat16)
    d_normed = d_gated * swish
    dgain_ref[...] += jnp.sum(d_normed * unit, axis=0, keepdims=True)
    c = d_normed * gain
    d_mixed = scale * (c - unit * jnp.mean(c * unit, axis=-1, keepdims=True))
    d_out = d_mixed.astype(jnp.bfloat16)

    log_keep, keep_in = lk_ref[...], w_ref[...]
    e_parts, f_bare, e_all, f_all, total = decays(log_keep, keep_in, spans_ref[...])
    masks = level_masks()
    probs = probs_ref[...]
    kst, vst = kst_ref[0], vst_ref[0]
    dkst, dvst = dk_acc[...], dv_acc[...]
    dkst_b, dvst_b = dkst.astype(jnp.bfloat16), dvst.astype(jnp.bfloat16)

    inner_b = (mm(k, q, NT) * root).astype(jnp.bfloat16)
    d_mixing_b = mm(v, d_out, NT).astype(jnp.bfloat16)
    pair = jnp.concatenate([inner_b, d_mixing_b], axis=1)
    zero_b = jnp.zeros_like(pair)
    masks2 = [jnp.concatenate([mask, mask], axis=1) for mask in masks]
    pairs = [jnp.where(mask, pair, zero_b) for mask in masks2]
    f_parts = [(bare * keep_in).astype(jnp.bfloat16) for bare in f_bare]
    both = [mm(fade, two, NN) for fade, two in zip(f_parts, pairs)]
    s_state = mm(kst, q, NT) * root
    p_state = mm(vst, d_out, NT)
    d_probs = e_all * p_state
    for grow, two in zip(e_parts, both):
        d_probs += grow * two[:, TILE:]
    d_scores = probs * (d_probs - jnp.sum(probs * d_probs, axis=0, keepdims=True))

    xy_all = jnp.concatenate([d_scores * e_all, probs * e_all], axis=1).astype(jnp.bfloat16)
    xy_parts = [jnp.concatenate([d_scores * grow, probs * grow], axis=1).astype(jnp.bfloat16) for grow in e_parts]
    x0 = xy_all[:, :TILE]
    y0 = xy_all[:, TILE:]
    change = x0.astype(jnp.float32) * s_state + y0.astype(jnp.float32) * p_state
    into = jnp.zeros((slots, TILE), jnp.float32)
    d_both = jnp.zeros((TILE, 2 * TILE), jnp.float32)
    for i, (grow, bare, fade, two, xy, part, mask) in enumerate(
        zip(e_parts, f_bare, f_parts, both, xy_parts, pairs, masks2)
    ):
        z = mm(xy, part, NT)
        into += bare * z
        if i < len(HALVES):
            mass = xy.astype(jnp.float32) * two
            change += mass[:, :TILE] + mass[:, TILE:] - fade.astype(jnp.float32) * z
        d_both = jnp.where(mask, mm(fade, xy, TN), d_both)
    d_both_b = d_both.astype(jnp.bfloat16)
    d_inner, mixing = d_both_b[:, :TILE], d_both_b[:, TILE:]
    tail = (f_all * keep_in).astype(jnp.bfloat16)
    z_state = mm(dkst_b, k, NT) + mm(dvst_b, v, NT)
    into += f_all * z_state
    change -= tail.astype(jnp.float32) * z_state

    dproj_ref[:, :width] = (root * (mm(d_inner, k, TN) + mm(x0, kst, TN))).astype(jnp.bfloat16)
    dproj_ref[:, width : 2 * width] = (root * mm(d_inner, q, NN) + mm(tail, dkst_b, TN)).astype(jnp.bfloat16)
    dproj_ref[:, 2 * width : 3 * width] = (mm(mixing, d_out, NN) + mm(tail, dvst_b, TN)).astype(jnp.bfloat16)

    later = (lax.broadcasted_iota(jnp.int32, (TILE, TILE), 0) >= lax.broadcasted_iota(jnp.int32, (TILE, TILE), 1)).astype(jnp.bfloat16)
    high = change.astype(jnp.bfloat16)
    rest = change - high.astype(jnp.float32)
    mid = rest.astype(jnp.bfloat16)
    low = (rest - mid.astype(jnp.float32)).astype(jnp.bfloat16)
    sums = mm(jnp.concatenate([high, mid, low], axis=0), later, NN)
    d_log_keep = sums[:slots] + sums[slots : 2 * slots] + sums[2 * slots :] + cross[...] - jnp.exp(log_keep) * into
    d_forget = (d_log_keep * jax.nn.sigmoid(-fpre_ref[...]) / DAMPING).astype(jnp.bfloat16)
    dbias_ref[...] += jnp.sum(d_forget.astype(jnp.float32), axis=1, keepdims=True)
    turned = jnp.transpose(d_forget.astype(jnp.float32))
    dproj_ref[:, 4 * width :] = jnp.concatenate([turned, jnp.zeros_like(turned)], axis=1).astype(jnp.bfloat16)

    dkst_new = total * dkst + root * mm(x0, q, NN)
    dvst_new = total * dvst + mm(y0, d_out, NN)
    dk_acc[...] = dkst_new
    dv_acc[...] = dvst_new
    cross[...] = jnp.sum(kst.astype(jnp.float32) * dkst_new + vst.astype(jnp.float32) * dvst_new, axis=1, keepdims=True)


MESH = pl.DeviceIdType.MESH
CHUNK = 32


def neighbours():
    head = lax.axis_index("head")
    return {"head": head + 1 - 2 * (head % 2)}, {"head": (head + 2) % BLOCKS}


def flipped(index, bit):
    return index + bit - 2 * bit * (index // bit % 2)


def other_core():
    return {"seq": flipped(lax.axis_index("seq"), 1)}


def greet(targets):
    barrier = pltpu.get_barrier_semaphore()
    for target in targets:
        pl.semaphore_signal(barrier, inc=1, device_id=target, device_id_type=MESH)
    pl.semaphore_wait(barrier, len(targets))


LIMIT = 60 << 20
FAR = pl.BlockSpec(memory_space=pl.ANY)
WHOLE = pl.BlockSpec(memory_space=pltpu.VMEM)


class Loads:
    def __init__(self, sem):
        self.sem, self.copies = sem, []

    def add(self, src, dst):
        copy = pltpu.make_async_copy(src, dst, self.sem.at[len(self.copies)])
        copy.start()
        self.copies.append(copy)
        return copy


SPLIT = 2


class Scatter:
    order = tuple(side * SPLIT + u for u in range(SPLIT) for side in range(2))

    def __init__(self, left, right, acc, mid, send, got, send_sem, got_sem):
        self.left, self.right, self.acc, self.mid, self.send, self.got = left, right, acc, mid, send, got
        self.size, self.cols = send.shape[1:]
        to_x, to_y = neighbours()
        self.copies = []
        for u in range(SPLIT):
            for k, to in enumerate((to_x, to_x, to_y, to_y, to_y, to_x)):
                slot = 6 * u + k
                self.copies.append(
                    pltpu.make_async_remote_copy(
                        src_ref=send.at[slot], dst_ref=got.at[slot], send_sem=send_sem.at[slot],
                        recv_sem=got_sem.at[slot], device_id=to, device_id_type=MESH,
                    )
                )

    def first(self, loads, watch=None):
        size, cols = self.size, self.cols
        for part, load in zip(self.order, loads):
            load.wait()
            value = mm(self.left[...], self.right[part * cols : (part + 1) * cols, :], NT)
            side_at, u = part // SPLIT, part % SPLIT
            here = slice(part * cols, (part + 1) * cols)
            slot = 6 * u + 2 * side_at
            near_block, mid_block = (1, 2) if side_at == 0 else (2, 1)
            self.acc[:, here] = value[:size]
            self.mid[:, here] = value[mid_block * size : (mid_block + 1) * size]
            self.send[slot] = value[3 * size :].astype(jnp.bfloat16)
            self.copies[slot].start()
            self.send[slot + 1] = value[near_block * size : (near_block + 1) * size].astype(jnp.bfloat16)
            self.copies[slot + 1].start()
            if watch is not None:
                watch(here, value)

    def second(self, u):
        cols = self.cols
        for side_at in range(2):
            part = SPLIT * side_at + u
            first, second = 6 * u + 2 * side_at, 6 * u + 4 + side_at
            here = slice(part * cols, (part + 1) * cols)
            self.copies[first].wait_recv()
            self.send[second] = (self.mid[:, here] + self.got[first].astype(jnp.float32)).astype(jnp.bfloat16)
            self.copies[second].start()

    def last(self, finish):
        for u in range(SPLIT):
            for k in (1, 3, 4, 5):
                self.copies[6 * u + k].wait_recv()
        cols = self.cols

        def rows(i, carry):
            here = pl.ds(pl.multiple_of(i * CHUNK, CHUNK), CHUNK)
            sums = []
            for part in range(2 * SPLIT):
                side_at, u = part // SPLIT, part % SPLIT
                one, two = self.got[6 * u + 2 * side_at + 1, here, :], self.got[6 * u + 4 + side_at, here, :]
                own = self.acc[here, part * cols : (part + 1) * cols]
                sums.append(own + one.astype(jnp.float32) + two.astype(jnp.float32))
            finish(here, jnp.concatenate(sums, axis=1), i)
            return carry

        lax.fori_loop(0, self.size // CHUNK, rows, 0)

    def close(self):
        for one in self.copies:
            one.wait_send()


def scatter_scratch(rows, depth, high):
    size, cols = rows // BLOCKS, high // (2 * SPLIT)
    return [
        pltpu.VMEM((rows, depth), jnp.bfloat16),
        pltpu.VMEM((high, depth), jnp.bfloat16),
        pltpu.VMEM((size, high), jnp.float32),
        pltpu.VMEM((size, high), jnp.float32),
        pltpu.VMEM((6 * SPLIT, size, cols), jnp.bfloat16),
        pltpu.VMEM((6 * SPLIT, size, cols), jnp.bfloat16),
        pltpu.SemaphoreType.DMA((6 * SPLIT,)),
        pltpu.SemaphoreType.DMA((6 * SPLIT,)),
    ]


def load_parts(loads, right_far, right, skip):
    cols = right.shape[0] // (2 * SPLIT)
    parts = []
    for part in Scatter.order:
        here = pl.ds(part * cols, cols)
        parts.append(loads.add(right_far.at[here, pl.ds(skip, right.shape[1])], right.at[here, :]))
    return parts


def scatter_kernel(plan, *refs):
    n_far, n_near, n_out, skip, finish, filler = plan
    left_far, right_far, *more_far = refs[:n_far]
    near = refs[n_far : n_far + n_near]
    outs = refs[n_far + n_near : n_far + n_near + n_out]
    load_sem, *rest = refs[n_far + n_near + n_out :]
    scatter, spare = rest[:8], rest[8:]
    left, right = scatter[:2]
    loads = Loads(load_sem)
    load_left = loads.add(left_far, left)
    parts = load_parts(loads, right_far, right, skip)
    more = [(loads.add(src, dst), dst) for src, dst in zip(more_far, spare)]
    spare = spare[len(more_far) :]
    greet(neighbours() if filler is None else (*neighbours(), other_core()))
    sum_heads = Scatter(*scatter)
    load_left.wait()
    sum_heads.first(parts)
    for u in range(SPLIT // 2):
        sum_heads.second(u)
    for load, _ in more:
        load.wait()
    side = [dst for _, dst in more]
    if filler is not None:
        steps = filler(left, right, side, outs, spare)
        next(steps)
        for u in range(SPLIT // 2, SPLIT):
            sum_heads.second(u)
        for _ in steps:
            pass
    else:
        for u in range(SPLIT // 2, SPLIT):
            sum_heads.second(u)
    sum_heads.last(lambda here, total, i: finish(here, total, side, near, outs, i))
    sum_heads.close()


def head_scatter(left, right, far, near, out_shapes, finish, number, filler=None, filled=(), scratch=()):
    rows, depth = left.shape
    plan = (2 + len(far), len(near), len(out_shapes) + len(filled), 0, finish, filler)
    return pl.pallas_call(
        functools.partial(scatter_kernel, plan),
        in_specs=[FAR] * (2 + len(far)) + [WHOLE] * len(near),
        out_specs=[WHOLE] * len(out_shapes) + [FAR] * len(filled),
        out_shape=[*out_shapes, *filled],
        scratch_shapes=[
            pltpu.SemaphoreType.DMA((1 + 2 * SPLIT + len(far),)),
            *scatter_scratch(rows, depth, right.shape[0]),
            *[pltpu.VMEM(one.shape, one.dtype) for one in far],
            *scratch,
        ],
        compiler_params=pltpu.CompilerParams(collective_id=number, has_side_effects=True, vmem_limit_bytes=LIMIT),
        cost_estimate=pl.CostEstimate(flops=10**9, bytes_accessed=1 << 20, transcendentals=0),
        name="head_scatter%d" % number,
    )(left, right, *far, *near)


STEP = 512


def weight_tiles(pairs, place, out_ref, room, land, store_sem, send_sem, got_sem, pause=()):
    count, share = land.shape[:2]
    high = 2 * count * share
    core = lax.axis_index("seq") % 2
    per = STEP // (2 * share)

    def row(p, at):
        return (2 * p + at) * share % room.shape[0]

    def swap_shard(p):
        return pltpu.make_async_remote_copy(
            src_ref=room.at[pl.ds(row(p, 0) + (1 - core) * share, share), :], dst_ref=land.at[p],
            send_sem=send_sem.at[p], recv_sem=got_sem.at[p], device_id=other_core(), device_id_type=MESH,
        )

    def store(p):
        return pltpu.make_async_copy(land.at[p], out_ref.at[pl.ds(p * share, share), :], store_sem.at[p])

    def settle(p):
        swap_shard(p).wait_recv()
        own = room[pl.ds(pl.multiple_of(row(p, 0) + core * share, share), share), :]
        land[p] = (own.astype(jnp.float32) + land[p].astype(jnp.float32)).astype(jnp.bfloat16)
        store(p).start()

    sent = []
    for i in range(high // STEP):
        here = slice(i * STEP, (i + 1) * STEP)
        there = slice(i * STEP % room.shape[0], i * STEP % room.shape[0] + STEP)
        if (i + 1) * STEP > room.shape[0]:
            for p in range((i - 2) * per, (i - 1) * per):
                swap_shard(p).wait_send()
                sent.append(p)
        for turned, right, column in pairs:

            def chunk(at, cols):
                value = mm(turned[here, :], right[:, pl.ds(at, cols)], NN).astype(jnp.bfloat16)
                for src, dst, wide in place(column + at, cols):
                    dst = dst if isinstance(dst, int) else pl.multiple_of(dst, 128)
                    room[there, pl.ds(dst, wide)] = value[:, src : src + wide]

            def chunks(c, carry):
                chunk(pl.multiple_of(c * STEP, STEP), STEP)
                return carry

            whole = right.shape[1] // STEP
            lax.fori_loop(0, whole, chunks, 0)
            if right.shape[1] % STEP:
                chunk(whole * STEP, right.shape[1] % STEP)
        for p in range(i * per, (i + 1) * per):
            swap_shard(p).start()
        if i:
            for p in range((i - 1) * per, i * per):
                settle(p)
        if i in pause:
            yield
    for p in range(count - per, count):
        settle(p)
    for p in range(count):
        store(p).wait()
        if p not in sent:
            swap_shard(p).wait_send()


def tile_scratch(high, width, share, room):
    count = high // (2 * share)
    return [pltpu.VMEM((2 * STEP, width), jnp.bfloat16)] * room + [
        pltpu.VMEM((count, share, width), jnp.bfloat16),
        pltpu.SemaphoreType.DMA((count,)),
        pltpu.SemaphoreType.DMA((count,)),
        pltpu.SemaphoreType.DMA((count,)),
    ]


def fill_gu(left, right, side, outs, spare):
    half = left.shape[1] // 2

    def place(at, cols):
        return [(k, at // 2 + k // 256 * 128 + k // 128 % 2 * half, 128) for k in range(0, cols, 128)]

    return weight_tiles([(side[0], left, 0)], place, outs[-1], right, *spare, pause=(1,))


def mixed_index(block):
    head = lax.axis_index("head")
    return (block + head) % 2 + 2 * ((block // 2 + head // 2) % 2)


def fill_mix(left, right, side, outs, spare):
    qkvg, d_gated, mixed, probs, kst, vst, log_keep, keep_in, forget, spans, gain, _, att_t, gated, normed_t = side
    grad_far, gain_grad, bias_grad, out_ref = outs[-2], outs[2], outs[3], outs[-1]
    grad_in, grad_sem, dk_acc, dv_acc, cross, *spare = spare
    width = gated.shape[1]
    tiles = qkvg.shape[0] // TILE
    per = tiles // BLOCKS

    def tile(i, carry):
        at = tiles - 1 - i
        rel = mixed_index(at // per) * per + at % per
        rows = pl.ds(pl.multiple_of(rel * TILE, TILE), TILE)
        bwd_tile(
            i, *[qkvg.at[rows, pl.ds(k * width, width)] for k in range(4)], log_keep.at[:, rows], keep_in.at[:, rows],
            forget.at[:, rows], gain, spans, mixed.at[rows, :], probs.at[:, rows], kst.at[pl.ds(at, 1)],
            vst.at[pl.ds(at, 1)], d_gated.at[rows, :], grad_in.at[rows, :], gain_grad, bias_grad, dk_acc, dv_acc, cross,
        )
        return carry

    lax.fori_loop(0, tiles, tile, 0)
    keep = pltpu.make_async_copy(grad_in, grad_far, grad_sem.at[0])
    keep.start()
    yield
    place = lambda at, cols: [(0, at, cols)]
    yield from weight_tiles([(att_t, gated, 0), (normed_t, grad_in, width)], place, out_ref, *spare)
    keep.wait()


class Gather:
    def __init__(self, own, blocks, send_sem, got_sem):
        half = own.shape[1] // 2
        to_x, to_y = neighbours()

        def copy(slot, src, block, side_at, target):
            here = pl.ds(side_at * half, half)
            return pltpu.make_async_remote_copy(
                src_ref=src.at[:, here], dst_ref=blocks.at[block, :, here],
                send_sem=send_sem.at[slot], recv_sem=got_sem.at[slot], device_id=target, device_id_type=MESH,
            )

        self.copies = [
            copy(0, own, 1, 0, to_x),
            copy(1, own, 2, 1, to_y),
            copy(2, own, 1, 1, to_x),
            copy(3, own, 2, 0, to_y),
            copy(4, blocks.at[1], 3, 0, to_y),
            copy(5, blocks.at[2], 3, 1, to_x),
        ]

    def first(self):
        for one in self.copies[:4]:
            one.start()

    def second(self):
        for near, far in ((0, 4), (1, 5)):
            self.copies[near].wait_recv()
            self.copies[far].start()

    def last(self):
        for one in self.copies[2:]:
            one.wait_recv()
        for one in self.copies:
            one.wait_send()


def gather_kernel(plan, *refs):
    keep, product, also = plan
    refs = list(refs)
    own_ref = refs.pop(0)
    weight_far = refs.pop(0) if product else None
    also_far = refs.pop(0) if also else None
    out_ref = refs.pop(0) if keep else None
    turned_ref = refs.pop(0)
    product_ref = refs.pop(0) if product else None
    also_ref = refs.pop(0) if also else None
    blocks, turned_buf, send_sem, got_sem, out_sem, load_sem, *refs = refs
    size, half = own_ref.shape[0], own_ref.shape[1] // 2
    loads = Loads(load_sem)
    if product:
        weight = refs.pop(0)
        fetch = loads.add(weight_far.at[:, pl.ds(0, weight.shape[1])], weight)
    if also:
        also_buf, also_turned = refs
        fetch = loads.add(also_far, also_buf)
    greet(neighbours())
    gather = Gather(own_ref, blocks, send_sem, got_sem)
    gather.first()
    if product or also:
        fetch.wait()
    stores = []

    def store(src, dst):
        copy = pltpu.make_async_copy(src, dst, out_sem.at[len(stores)])
        copy.start()
        stores.append(copy)

    def use(block, side_at, src):
        here = slice(side_at * half, (side_at + 1) * half)
        rows = slice(block * size, (block + 1) * size)
        value = src[:, here]
        turned_buf[here, rows] = jnp.transpose(value)
        store(turned_buf.at[here, rows], turned_ref.at[here, rows])
        if keep:
            store(src.at[:, here], out_ref.at[block, :, here])
        if product:
            term = mm(value, weight[here, :], NN)
            if (block, side_at) in ((0, 0), (1, 0), (2, 1), (3, 0)):
                product_ref[rows, :] = term
            else:
                product_ref[rows, :] += term

    use(0, 0, own_ref)
    use(0, 1, own_ref)
    if also:
        also_turned[...] = jnp.transpose(also_buf[: also_buf.shape[0] // 2, :])
        middle = also_buf.shape[0] // 2
        store(also_turned, also_ref.at[:, pl.ds(0, middle)])
    gather.second()
    use(1, 0, blocks.at[1])
    use(2, 1, blocks.at[2])
    if also:
        stores[-1 - 4 * keep - 2 * (not keep)].wait()
        finished = len(stores) - 1 - 4 * keep - 2 * (not keep)
        also_turned[...] = jnp.transpose(also_buf[middle:, :])
        store(also_turned, also_ref.at[:, pl.ds(middle, middle)])
    for slot, block, side_at in ((2, 1, 1), (3, 2, 0), (4, 3, 0), (5, 3, 1)):
        gather.copies[slot].wait_recv()
        use(block, side_at, blocks.at[block])
    for at, one in enumerate(stores):
        if not also or at != finished:
            one.wait()
    for one in gather.copies:
        one.wait_send()


def head_gather(own, number, keep=True, weight=None, width=0, also=None):
    size, wide = own.shape
    rows = BLOCKS * size
    product = weight is not None
    extra = [one for one in (weight, also) if one is not None]
    out_shape, out_specs = [], []
    if keep:
        out_shape.append(jax.ShapeDtypeStruct((BLOCKS, size, wide), own.dtype))
        out_specs.append(FAR)
    out_shape.append(jax.ShapeDtypeStruct((wide, rows), own.dtype))
    out_specs.append(FAR)
    scratch = [
        pltpu.VMEM((BLOCKS, size, wide), own.dtype),
        pltpu.VMEM((wide, rows), own.dtype),
        pltpu.SemaphoreType.DMA((6,)),
        pltpu.SemaphoreType.DMA((6,)),
        pltpu.SemaphoreType.DMA((20,)),
        pltpu.SemaphoreType.DMA((2,)),
    ]
    if product:
        out_shape.append(jax.ShapeDtypeStruct((rows, width), jnp.float32))
        out_specs.append(WHOLE)
        scratch.append(pltpu.VMEM((wide, width), own.dtype))
    if also is not None:
        out_shape.append(jax.ShapeDtypeStruct(also.shape[::-1], also.dtype))
        out_specs.append(FAR)
        scratch += [pltpu.VMEM(also.shape, also.dtype), pltpu.VMEM((also.shape[1], also.shape[0] // 2), also.dtype)]
    return pl.pallas_call(
        functools.partial(gather_kernel, (keep, product, also is not None)),
        in_specs=[WHOLE] + [FAR] * len(extra),
        out_specs=out_specs,
        out_shape=out_shape,
        scratch_shapes=scratch,
        compiler_params=pltpu.CompilerParams(collective_id=number, has_side_effects=True, vmem_limit_bytes=LIMIT),
        cost_estimate=pl.CostEstimate(flops=10**9, bytes_accessed=1 << 20, transcendentals=0),
        name="head_gather%d" % number,
    )(own, *extra)


def unit_of(values):
    scale = lax.rsqrt(jnp.mean(values * values, axis=-1, keepdims=True) + EPSILON)
    return scale, values * scale


def finish_mixer(here, total, side, near, outs, i):
    x = side[0][here, :].astype(jnp.float32)
    gain, live = near[0][...], near[1][here, :]
    residual = x + total
    outs[0][here, :] = residual
    outs[1][here, :] = (unit_of(residual)[1] * gain).astype(jnp.bfloat16)
    add_row(outs[2], jnp.sum(live * x * x, axis=0, keepdims=True), i)
    add_row(outs[3], jnp.sum(live * total * total, axis=0, keepdims=True), i)
    add_row(outs[4], jnp.sum(live / x.shape[1] + jnp.zeros_like(x), axis=0, keepdims=True), i)


def add_row(ref, row, i):
    @pl.when(i == 0)
    def _():
        ref[...] = jnp.zeros_like(ref)

    ref[...] += row


def norm_back(total, gain, scale, unit):
    c = total * gain
    return scale * (c - unit * jnp.mean(c * unit, axis=-1, keepdims=True))


def finish_norm_two(here, total, side, near, outs, i):
    residual, cot = side[1][here, :], side[2][here, :].astype(jnp.float32)
    live, gain = near[0][here, :], near[1][1:2, :]
    scale, unit = unit_of(residual)
    add_row(outs[2], jnp.sum(total * unit, axis=0, keepdims=True), i)
    grad = cot * live + norm_back(total, gain, scale, unit)
    outs[0][here, :] = grad
    outs[1][here, :] = grad.astype(jnp.bfloat16)


def finish_ffn(here, total, side, near, outs, i):
    live = near[0][here, :]
    add_row(outs[1], jnp.sum(live * total * total, axis=0, keepdims=True), i)
    outs[0][here, :] = (live * (side[11][here, :] + total)).astype(jnp.bfloat16)


SMALL = 8


def tail_kernel(skip, grad_far, mix_far, normed_far, x_far, res_far, out_own, gain_ref, two_ref, x_sum, mix_sum, ffn_sum,
                live_sum, head_ref, bias_ref, outputs_far, input_far, total_ref, load_sem, store_sem, *rest):
    scatter = rest[:8]
    left, right = scatter[:2]
    normed, x_buf, res_buf, in_own, out_blocks, in_blocks, f_send, f_got, z_send, z_got, s_buf, s_send, s_got = rest[8:]
    loads = Loads(load_sem)
    load_left = loads.add(grad_far, left)
    parts = load_parts(loads, mix_far, right, skip)
    load_normed = loads.add(normed_far, normed)
    load_x = loads.add(x_far.at[pl.ds(0, x_buf.shape[0]), :], x_buf)
    load_res = loads.add(res_far, res_buf)
    size = in_own.shape[0]
    seq = lax.axis_index("seq")
    hops = [*neighbours(), other_core()]
    bit = 2
    while bit < lax.axis_size("seq"):
        hops.append({"seq": flipped(seq, bit)})
        bit *= 2
    greet(hops)
    sum_heads = Scatter(*scatter)

    def watch(here, value):
        term = value * normed[:, here].astype(jnp.float32)
        s_buf[0, 0:1, here] = jnp.sum(term, axis=0, keepdims=True) / gain_ref[0:1, here]

    f_gather = Gather(out_own, out_blocks, f_send, f_got)
    f_gather.first()
    s_buf[0] = jnp.zeros(s_buf.shape[1:], jnp.float32)
    load_left.wait()
    load_normed.wait()
    sum_heads.first(parts, watch)
    for u in range(SPLIT):
        sum_heads.second(u)

    is_own = lax.broadcasted_iota(jnp.int32, (SMALL, 1), 0) >= SMALL - 2
    for k, row in enumerate((two_ref, x_sum, mix_sum, ffn_sum, live_sum)):
        s_buf[0, k + 1 : k + 2, :] = row[...]
    s_buf[0, SMALL - 2 : SMALL - 1, : head_ref.shape[1]] = head_ref[...]
    slots = bias_ref.shape[0]
    s_buf[0, SMALL - 1 : SMALL, :slots] = jnp.transpose(jnp.broadcast_to(bias_ref[...], (slots, 128)))[:1, :]
    small = [
        pltpu.make_async_remote_copy(
            src_ref=s_buf.at[2 * k], dst_ref=s_buf.at[2 * k + 1], send_sem=s_send.at[k], recv_sem=s_got.at[k],
            device_id=hop, device_id_type=MESH,
        )
        for k, hop in enumerate(hops)
    ]

    def hop_done(k):
        small[k].wait_recv()
        arrived = s_buf[2 * k + 1]
        if k < 2:
            arrived = jnp.where(is_own, 0.0, arrived)
        if k + 1 < len(small):
            s_buf[2 * k + 2] = s_buf[2 * k] + arrived
            small[k + 1].start()
        else:
            total_ref[...] = s_buf[2 * k] + arrived

    small[0].start()
    load_x.wait()
    load_res.wait()

    def finish(here, total, i):
        scale, unit = unit_of(x_buf[here, :].astype(jnp.float32))
        in_own[here, :] = (res_buf[here, :] + norm_back(total, gain_ref[0:1, :], scale, unit)).astype(jnp.bfloat16)

    f_gather.second()
    hop_done(0)
    sum_heads.last(finish)
    z_gather = Gather(in_own, in_blocks, z_send, z_got)
    z_gather.first()
    head = lax.axis_index("head")
    places = (head, flipped(head, 1), flipped(head, 2), BLOCKS - 1 - head)
    stores = []

    def store(src, far, k):
        copy = pltpu.make_async_copy(src, far.at[places[k]], store_sem.at[len(stores)])
        copy.start()
        stores.append(copy)

    store(out_own, outputs_far, 0)
    store(in_own, input_far, 0)
    hop_done(1)
    z_gather.second()
    for k in range(2, len(small)):
        hop_done(k)
    f_gather.last()
    for k in range(1, BLOCKS):
        store(out_blocks.at[k], outputs_far, k)
    z_gather.last()
    for k in range(1, BLOCKS):
        store(in_blocks.at[k], input_far, k)
    sum_heads.close()
    for one in small:
        one.wait_send()
    for one in stores:
        one.wait()


def tail_stage(hops, skip, grad_in, mix, normed, x_rel, grad_residual, out_own, small, number):
    rows, depth = grad_in.shape
    size, high = out_own.shape
    blocks = jax.ShapeDtypeStruct((BLOCKS, size, high), jnp.bfloat16)
    sems = lambda n: pltpu.SemaphoreType.DMA((n,))
    return pl.pallas_call(
        functools.partial(tail_kernel, skip),
        in_specs=[FAR] * 5 + [WHOLE] * (1 + len(small)),
        out_specs=[FAR, FAR, WHOLE],
        out_shape=[blocks, blocks, jax.ShapeDtypeStruct((SMALL, high), jnp.float32)],
        scratch_shapes=[
            sems(4 + 2 * SPLIT),
            sems(2 * BLOCKS),
            *scatter_scratch(rows, depth, high),
            pltpu.VMEM((rows, high), jnp.bfloat16),
            pltpu.VMEM((size, high), jnp.bfloat16),
            pltpu.VMEM((size, high), jnp.float32),
            pltpu.VMEM((size, high), jnp.bfloat16),
            pltpu.VMEM((BLOCKS, size, high), jnp.bfloat16),
            pltpu.VMEM((BLOCKS, size, high), jnp.bfloat16),
            sems(6), sems(6), sems(6), sems(6),
            pltpu.VMEM((2 * hops, SMALL, high), jnp.float32),
            sems(hops), sems(hops),
        ],
        compiler_params=pltpu.CompilerParams(collective_id=number, has_side_effects=True, vmem_limit_bytes=LIMIT),
        cost_estimate=pl.CostEstimate(flops=10**9, bytes_accessed=1 << 20, transcendentals=0),
        name="tail_stage",
    )(grad_in, mix, normed, x_rel, grad_residual, out_own, *small)


def last_kernel(counts, seq_ref, input_ref, output_ref, gu_ref, mix_ref, out_w_ref, narrow_ref, down_ref, small_ref,
                input_out, output_out, q_out, k_out, v_out, go_out, f_out, gate_out, up_out, w_out_out, down_out,
                one_out, two_out, head_out, bias_out, rms_out):
    seq_count, skip, n_gain, n_bias = counts
    f32 = jnp.float32
    step = pl.program_id(0)
    input_out[...] = input_ref[...].astype(f32)
    output_out[...] = output_ref[...]
    half = gate_out.shape[1]
    gate_out[...] = gu_ref[:, :half].astype(f32)
    up_out[...] = gu_ref[:, half:].astype(f32)
    width = q_out.shape[1]
    for k, out in enumerate((q_out, k_out, v_out, go_out)):
        out[...] = mix_ref[:, skip + k * width : skip + (k + 1) * width].astype(f32)

    @pl.when(step == 0)
    def _():
        down_out[...] = jnp.transpose(down_ref[...].astype(f32))

    @pl.when(step == 1)
    def _():
        slots = f_out.shape[0]
        f_out[...] = jnp.transpose(narrow_ref[...].astype(f32))[:slots, :]
        w_out_out[...] = jnp.transpose(out_w_ref[...].astype(f32))
        share = one_out.shape[1]
        picks = [(one_out, 0, share), (two_out, 1, share), (head_out, SMALL - 2, n_gain), (bias_out, SMALL - 1, n_bias)]
        for out, row, n in picks:
            value = small_ref[row : row + 1, :n]
            for s in range(1, seq_count):
                value = jnp.where(seq_ref[0] == s, small_ref[row : row + 1, s * n : (s + 1) * n], value)
            out[...] = value
        sums = jnp.sum(small_ref[...], axis=1, keepdims=True)
        roots = jnp.sqrt(sums / (sums[5:6] * small_ref.shape[1]))
        rms_out[...] = jnp.transpose(jnp.broadcast_to(roots, (SMALL, 128)))[:1, 2:5]


def last_stage(seq_pos, seq_count, input_grad, outputs, grad_gu, grad_mix, grad_down, small, width, slots, n_gain, n_bias):
    f32 = jnp.float32
    rows, high = input_grad.shape
    share, wide_gu = grad_gu.shape
    wide_mix, hidden = grad_mix.shape[1], grad_down.shape[1]
    steps = 4
    per, part = rows // steps, share // steps
    tile = lambda a, b: pl.BlockSpec((a, b), lambda i, s: (i, 0))
    fixed = lambda a, b: pl.BlockSpec((a, b), lambda i, s: (0, 0))
    shapes = lambda *dims: [jax.ShapeDtypeStruct(one, f32) for one in dims]
    return pl.pallas_call(
        functools.partial(last_kernel, (seq_count, width, n_gain, n_bias)),
        grid_spec=pltpu.PrefetchScalarGridSpec(
            num_scalar_prefetch=1,
            grid=(steps,),
            in_specs=[tile(per, high), tile(per, high), tile(part, wide_gu), tile(part, wide_mix), fixed(share, width),
                      pl.BlockSpec((share, 2 * slots), lambda i, s: (0, wide_mix // (2 * slots) - 1)), fixed(share, hidden), fixed(SMALL, high)],
            out_specs=[tile(per, high), tile(per, high), *[tile(part, width)] * 4, fixed(slots, share),
                       *[tile(part, hidden)] * 2, fixed(width, share), fixed(hidden, share), fixed(1, share),
                       fixed(1, share), fixed(1, n_gain), fixed(1, n_bias), fixed(1, 3)],
        ),
        out_shape=[
            *shapes((rows, high)), jax.ShapeDtypeStruct((rows, high), jnp.bfloat16),
            *shapes(*[(share, width)] * 4, (slots, share), (share, hidden), (share, hidden), (width, share),
                    (hidden, share), (1, share), (1, share), (1, n_gain), (1, n_bias), (1, 3)),
        ],
        compiler_params=pltpu.CompilerParams(dimension_semantics=("arbitrary",), vmem_limit_bytes=LIMIT),
        cost_estimate=pl.CostEstimate(flops=10**7, bytes_accessed=1 << 20, transcendentals=0),
        name="last_stage",
    )(seq_pos, input_grad, outputs, grad_gu, grad_mix, grad_mix, grad_mix, grad_down, small)


def enter_kernel(count, *refs):
    (out_w, q, k, v, go, forget_w, small_far, tokens, cot, gate_w, up_w, down_w, counts, pads) = refs[:14]
    (mix_out, normed_out, grad_out, turned_out, x_out, cot_out, gu_out, down_out, qkvg_out, forget_out, rows_out) = refs[14:25]
    (buf, wide_buf, f_buf, small_buf, turned, x_buf, cot_buf, scale, normed, acc, gate_buf,
     up_buf, gu_buf, downw_buf, down_buf, cot_turned, load_sem, mix_sem, norm_sem, out_sem, r_send, r_got, l_send, l_got, x_send,
     x_got) = refs[25:]
    f32, b16 = jnp.float32, jnp.bfloat16
    seq = lax.axis_index("seq")
    place, core = seq // 2, seq % 2
    chips = count // 2
    rows = x_buf.shape[0]
    size = rows // BLOCKS
    share, width = q.shape
    slots = f_buf.shape[0]
    part, pair = share // 2, 2 * share
    own = buf.at[pl.ds(pl.multiple_of(seq * share, share), share), :]

    loads = Loads(load_sem)
    load_small = [loads.add(forget_w, f_buf), loads.add(small_far, small_buf)]
    load_out = loads.add(out_w, wide_buf)
    pieces = [loads.add(piece, own.at[:, pl.ds((at + 1) * width, width)]) for at, piece in enumerate((q, k, v, go))]
    load_x, load_cot = [], []
    for block in range(BLOCKS):
        there = pl.ds(pl.multiple_of(mixed_index(block) * size, size), size)
        load_x.append(loads.add(tokens.at[there, :], x_buf.at[pl.ds(block * size, size), :]))
        load_cot.append(loads.add(cot.at[there, :], cot_buf.at[pl.ds(block * size, size), :]))
    load_ffn = [loads.add(src, dst) for src, dst in ((gate_w, gate_buf), (up_w, up_buf), (down_w, downw_buf))]
    at_seq = lambda chip: {"seq": 2 * (chip % chips) + core}
    greet([at_seq(place + 1), at_seq(place + chips - 1), other_core()])

    turned[...] = jnp.zeros_like(turned)
    for load in load_small:
        load.wait()
    turned[:slots, :] = f_buf[...].astype(f32)
    for at in range(3):
        turned[slots + at : slots + at + 1, :] = small_buf[:, at * share : (at + 1) * share].astype(f32)
    own[:, 5 * width :] = jnp.transpose(turned[...]).astype(b16)
    load_out.wait()
    own[:, :width] = jnp.transpose(wide_buf[...])
    for load in pieces:
        load.wait()

    def remote(shard, ch, send, got, target):
        there = buf.at[pl.ds(pl.multiple_of(shard * share + ch * part, part), part), :]
        return pltpu.make_async_remote_copy(
            src_ref=there, dst_ref=there, send_sem=send, recv_sem=got, device_id=target, device_id_type=MESH
        )

    def right(d, ch):
        return remote(2 * (place - d) + core, ch, r_send.at[d, ch], r_got.at[d, ch], at_seq(place + 1))

    def left(d, ch):
        return remote(2 * (place + d) + core, ch, l_send.at[d, ch], l_got.at[d, ch], at_seq(place + chips - 1))

    def across(chip, ch):
        return remote(2 * chip + core, ch, x_send.at[chip, ch], x_got.at[chip, ch], other_core())

    for ch in range(2):
        pl.when(place < chips - 1)(right(0, ch).start)
        pl.when(place > 0)(left(0, ch).start)
    for ch in range(2):
        across(place, ch).start()

    acc[...] = jnp.zeros_like(acc)
    for load in load_x:
        load.wait()
    outs = []

    def leave(src, dst):
        copy = pltpu.make_async_copy(src, dst, out_sem.at[len(outs)])
        copy.start()
        outs.append(copy)

    leave(x_buf.at[pl.ds(0, size), :], x_out)

    def row_scale(i, carry):
        here = pl.ds(pl.multiple_of(i * CHUNK, CHUNK), CHUNK)
        scale[here, :] = unit_of(x_buf[here, :].astype(f32))[0]
        return carry

    lax.fori_loop(0, rows // CHUNK, row_scale, 0)
    for load in load_cot:
        load.wait()
    live_len = jnp.where(counts[0] > 0, rows - pads[0], 0)
    per = size // CHUNK

    def mask(i, carry):
        here = pl.ds(pl.multiple_of(i * CHUNK, CHUNK), CHUNK)
        start = mixed_index(i // per) * size + i % per * CHUNK
        live = start + lax.broadcasted_iota(jnp.int32, (CHUNK, 1), 0) < live_len
        cot_buf[here, :] = (cot_buf[here, :].astype(f32) * live.astype(f32)).astype(b16)
        return carry

    lax.fori_loop(0, rows // CHUNK, mask, 0)
    leave(cot_buf, grad_out)
    leave(cot_buf.at[pl.ds(0, size), :], cot_out)
    for load in load_ffn:
        load.wait()
    for at in range(0, gate_buf.shape[1], 128):
        gu_buf[:, 2 * at : 2 * at + 128] = gate_buf[:, at : at + 128]
        gu_buf[:, 2 * at + 128 : 2 * at + 256] = up_buf[:, at : at + 128]
    leave(gu_buf, gu_out)
    down_buf[...] = jnp.transpose(downw_buf[...])
    leave(down_buf, down_out)
    for block in range(BLOCKS):
        here = slice(block * size, (block + 1) * size)
        cot_turned[:, here] = jnp.transpose(cot_buf[here, :])
    leave(cot_turned, turned_out)

    def chip_rows(chip):
        return pl.ds(pl.multiple_of(chip * pair, pair), pair)

    def mix_store(chip):
        return pltpu.make_async_copy(buf.at[chip_rows(chip), :], mix_out.at[chip_rows(chip), :], mix_sem.at[chip])

    def norm_store(chip):
        return pltpu.make_async_copy(normed.at[:, chip_rows(chip)], normed_out.at[:, chip_rows(chip)], norm_sem.at[chip])

    def use(chip):
        for ch in range(2):
            across(chip, ch).wait_recv()
        mix_store(chip).start()
        here = chip_rows(chip)
        narrow = jnp.transpose(buf[here, 5 * width :].astype(f32))[slots : slots + 8, :]
        rows_out[:, here] = narrow
        normed[:, here] = (x_buf[:, here].astype(f32) * scale[...] * narrow[:1, :]).astype(b16)
        norm_store(chip).start()
        for at in range(width, buf.shape[1], 512):
            cols = min(512, buf.shape[1] - at)
            acc[:, at - width : at - width + cols] += mm(normed[:, here], buf[here, at : at + cols], NN)

    use(place)

    def step(d, carry):
        on_left, on_right = place >= d, place + d < chips

        @pl.when(on_left)
        def _():
            for ch in range(2):
                right(d - 1, ch).wait_recv()
                pl.when((d < chips - 1) & (place < chips - 1))(right(d, ch).start)
                across(place - d, ch).start()

        @pl.when(on_right)
        def _():
            for ch in range(2):
                left(d - 1, ch).wait_recv()
                pl.when((d < chips - 1) & (place > 0))(left(d, ch).start)
                across(place + d, ch).start()

        @pl.when(on_left)
        def _():
            use(place - d)

        @pl.when(on_right)
        def _():
            use(place + d)

        return carry

    lax.fori_loop(1, chips, step, 0)
    forget_out[...] = jnp.transpose(acc[:, 4 * width :])[:slots, :]
    outs[0].wait()
    for at in range(0, 4 * width, width):
        x_buf[:, at : at + width] = acc[:, at : at + width].astype(b16)
        leave(x_buf.at[:, pl.ds(at, width)], qkvg_out.at[:, pl.ds(at, width)])

    def close(d, carry):
        for ch in range(2):
            pl.when((place >= d) & (place < chips - 1))(right(d, ch).wait_send)
            pl.when((place + d < chips) & (place > 0))(left(d, ch).wait_send)
        return carry

    lax.fori_loop(0, chips - 1, close, 0)

    def settle(chip, carry):
        for ch in range(2):
            across(chip, ch).wait_send()
        mix_store(chip).wait()
        norm_store(chip).wait()
        return carry

    lax.fori_loop(0, chips, settle, 0)
    for one_out in outs[1:]:
        one_out.wait()


def enter_stage(count, out_w, q, k, v, go, forget, small, tokens, cot, gate, up, down, counts, pads, number):
    f32, b16 = jnp.float32, jnp.bfloat16
    share, width = q.shape
    slots, hidden = forget.shape[0], gate.shape[1]
    rows, high = tokens.shape
    size, chips = rows // BLOCKS, count // 2
    mix_width = 5 * width + 2 * slots
    shape = jax.ShapeDtypeStruct
    buf = lambda array: pltpu.VMEM(array.shape, b16)
    sems = lambda *dims: pltpu.SemaphoreType.DMA(dims)
    return pl.pallas_call(
        functools.partial(enter_kernel, count),
        in_specs=[FAR] * 12 + [pl.BlockSpec(memory_space=pltpu.SMEM)] * 2,
        out_specs=[FAR] * 9 + [WHOLE] * 2,
        out_shape=[
            shape((high, mix_width), b16), shape((rows, high), b16), shape((rows, high), b16), shape((high, rows), b16), shape((size, high), b16),
            shape((size, high), b16), shape((share, 2 * hidden), b16), shape((share, hidden), b16),
            shape((rows, 4 * width), b16), shape((slots, rows), f32), shape((8, high), f32),
        ],
        scratch_shapes=[
            pltpu.VMEM((high, mix_width), b16), buf(out_w), buf(forget), buf(small),
            pltpu.VMEM((2 * slots, share), f32), buf(tokens), buf(cot), pltpu.VMEM((rows, 1), f32), buf(tokens),
            pltpu.VMEM((rows, 4 * width + 2 * slots), f32), buf(gate), buf(up), pltpu.VMEM((share, 2 * hidden), b16),
            buf(down), pltpu.VMEM((share, hidden), b16), pltpu.VMEM((high, rows), b16), sems(21), sems(chips), sems(chips), sems(10),
            *[sems(chips, 2)] * 6,
        ],
        compiler_params=pltpu.CompilerParams(collective_id=number, has_side_effects=True, vmem_limit_bytes=LIMIT),
        cost_estimate=pl.CostEstimate(flops=10**9, bytes_accessed=1 << 20, transcendentals=0),
        name="enter_stage",
    )(out_w, q, k, v, go, forget, small, tokens, cot, gate, up, down, counts, pads)


class LineGather:
    def __init__(self, count, out, own, r_send, r_got, l_send, l_got, x_send, x_got, own_sem):
        self.seq = lax.axis_index("seq")
        self.place, self.core, self.chips = self.seq // 2, self.seq % 2, count // 2
        self.out, self.own, self.share = out, own, own.shape[0]
        self.sems = r_send, r_got, l_send, l_got, x_send, x_got
        self.keep = pltpu.make_async_copy(own, out.at[pl.ds(pl.multiple_of(self.seq * self.share, self.share), self.share), :], own_sem.at[0])
        self.steps = [(d, ch) for d in range(1, self.chips) for ch in range(2)]

    def remote(self, shard, ch, is_own, send, got, target):
        part = self.share // 2
        there = self.out.at[pl.ds(pl.multiple_of(shard * self.share + ch * part, part), part), :]
        return pltpu.make_async_remote_copy(
            src_ref=self.own.at[pl.ds(ch * part, part), :] if is_own else there, dst_ref=there, send_sem=send, recv_sem=got,
            device_id=target, device_id_type=MESH,
        )

    def at_seq(self, chip):
        return {"seq": 2 * ((chip + self.chips) % self.chips) + self.core}

    def right(self, d, ch):
        send, got = self.sems[:2]
        return self.remote(2 * (self.place - d) + self.core, ch, d == 0, send.at[d, ch], got.at[d, ch], self.at_seq(self.place + 1))

    def left(self, d, ch):
        send, got = self.sems[2:4]
        return self.remote(2 * (self.place + d) + self.core, ch, d == 0, send.at[d, ch], got.at[d, ch], self.at_seq(self.place - 1))

    def across(self, chip, ch, is_own=False):
        send, got = self.sems[4:]
        return self.remote(2 * chip + self.core, ch, is_own, send.at[chip, ch], got.at[chip, ch], other_core())

    def begin(self):
        for ch in range(2):
            pl.when(self.place < self.chips - 1)(self.right(0, ch).start)
            pl.when(self.place > 0)(self.left(0, ch).start)
        for ch in range(2):
            self.across(self.place, ch, True).start()
        self.keep.start()

    def serve(self, n):
        now, self.steps = self.steps[:n], self.steps[n:]
        place, chips = self.place, self.chips
        for d, ch in now:

            @pl.when(place >= d)
            def _():
                self.right(d - 1, ch).wait_recv()
                if d < chips - 1:
                    pl.when(place < chips - 1)(self.right(d, ch).start)
                self.across(place - d, ch).start()

            @pl.when(place + d < chips)
            def _():
                self.left(d - 1, ch).wait_recv()
                if d < chips - 1:
                    pl.when(place > 0)(self.left(d, ch).start)
                self.across(place + d, ch).start()

    def finish(self):
        self.serve(len(self.steps))
        for chip in range(self.chips):
            for ch in range(2):
                self.across(chip, ch).wait_recv()
        self.keep.wait()

    def close(self):
        place, chips = self.place, self.chips
        for d in range(chips - 1):
            for ch in range(2):
                pl.when((place >= d) & (place < chips - 1))(self.right(d, ch).wait_send)
                pl.when((place + d < chips) & (place > 0))(self.left(d, ch).wait_send)
        for chip in range(chips):
            for ch in range(2):
                self.across(chip, ch).wait_send()


def gate_decays(forget):
    small = jnp.exp(-jnp.abs(forget))
    series = small * (1.0 - small * (0.5 - small * (1.0 / 3.0 - small * (0.25 - small * 0.2))))
    soft = jnp.where(small < 0.05, series, jnp.log(1.0 + small))
    log_keep = (jnp.minimum(forget, 0.0) - soft) / DAMPING
    grown = 1.0 + log_keep * (0.25 + log_keep * 0.05)
    series = -log_keep * (1.0 + log_keep * (0.5 + log_keep * (1.0 / 6.0) * grown))
    return log_keep, jnp.where(log_keep > -0.1, series, 1.0 - jnp.exp(log_keep))


def mid_kernel(count, *refs):
    (qkvg_far, forget_far, spans_far, mix_far, x_far, normed_far, gu_far, down_far, grad_far, gain_rows, live_ref) = refs[:11]
    (residual_ref, x_sum, mix_sum, live_sum, head_gain, gated_out, mixed_out, probs_out, kst_out, vst_out, n2t_out, n1t_out,
     gu_out, downw_out, slopes_out, hidden_out, gdown_out, forget_out, lk_out, keep_out) = refs[11:31]
    (qkvg, forget, lk, keep_in, spans, mixed, probs, kst, vst, kacc, vacc, *rest) = refs[31:]
    scatter, rest = rest[:8], rest[8:]
    (x_buf, own, blocks, n2t, n1t, own_g, own_d, w_tiles, slopes, hidden, grad_t, room, land, store_sem, t_send, t_got,
     load_sem, out_sem, g_send, g_got, w_sem, s_sem, *z_sems) = rest
    left, right = scatter[:2]
    rows, width = left.shape
    size, high = own.shape
    half = high // 2
    f32, b16 = jnp.float32, jnp.bfloat16
    loads = Loads(load_sem)
    load_g = loads.add(gu_far, own_g)
    load_slot = [loads.add(src, dst) for src, dst in ((forget_far, forget), (qkvg_far, qkvg), (spans_far, spans))]
    parts = load_parts(loads, mix_far, right, 0)
    load_x = loads.add(x_far, x_buf)
    load_d = loads.add(down_far, own_d)
    load_t = loads.add(grad_far, grad_t)
    gu = LineGather(count, gu_out, own_g, *z_sems[:7])
    down = LineGather(count, downw_out, own_d, *z_sems[7:])
    greet([*neighbours(), other_core(), gu.at_seq(gu.place + 1), gu.at_seq(gu.place - 1)])
    load_g.wait()
    gu.begin()
    pace = max(len(gu.steps) // 6, 1)
    small = gain_rows[2:3, :]
    share = own_g.shape[0]
    n_gain, n_bias = width // count, forget.shape[0] // count
    head_gain[...] = jnp.concatenate([small[:, s * share : s * share + n_gain] for s in range(count)], axis=1)
    bias = jnp.concatenate([small[:, s * share + n_gain : s * share + n_gain + n_bias] for s in range(count)], axis=1)
    for load in load_slot:
        load.wait()
    forget[...] += jnp.transpose(jnp.broadcast_to(bias, (8, bias.shape[1])))[:, :1]
    lk[...], keep_in[...] = gate_decays(forget[...])
    tiles = rows // TILE
    per = tiles // BLOCKS

    def tile(i, carry):
        rel = mixed_index(i // per) * per + i % per
        here = pl.ds(pl.multiple_of(rel * TILE, TILE), TILE)
        fwd_tile(
            i, *[qkvg.at[here, pl.ds(k * width, width)] for k in range(4)], lk.at[:, here], keep_in.at[:, here], head_gain,
            spans, left.at[here, :], mixed.at[here, :], probs.at[:, here], kst.at[pl.ds(i, 1)], vst.at[pl.ds(i, 1)], kacc,
            vacc,
        )
        return carry

    lax.fori_loop(0, tiles, tile, 0)
    outs = []

    def leave(src, dst):
        copy = pltpu.make_async_copy(src, dst, out_sem.at[len(outs)])
        copy.start()
        outs.append(copy)
        return copy

    for src, dst in ((left, gated_out), (mixed, mixed_out), (probs, probs_out), (kst, kst_out), (vst, vst_out),
                     (forget, forget_out), (lk, lk_out), (keep_in, keep_out)):
        leave(src, dst)
    load_n = loads.add(normed_far, qkvg)
    sum_heads = Scatter(*scatter)
    sum_heads.first(parts)
    gu.serve(pace)
    for u in range(SPLIT // 2):
        sum_heads.second(u)
    gu.serve(pace)
    for u in range(SPLIT // 2, SPLIT):
        sum_heads.second(u)
    load_x.wait()
    gu.serve(pace)
    sum_heads.last(lambda here, total, i: finish_mixer(
        here, total, [x_buf], [gain_rows.at[pl.ds(1, 1), :], live_ref], [residual_ref, own, x_sum, mix_sum, live_sum], i))
    gather = Gather(own, blocks, g_send, g_got)
    gather.first()
    gu.serve(pace)
    load_d.wait()
    down.begin()

    def use(block, side_at, src):
        here = slice(side_at * half, (side_at + 1) * half)
        there = slice(block * size, (block + 1) * size)
        n2t[here, there] = jnp.transpose(src[:, here])

    blocks[0] = own[...]
    use(0, 0, own)
    use(0, 1, own)
    load_n.wait()
    middle = rows // 2
    n1t[...] = jnp.transpose(qkvg[:middle, :])
    first_half = leave(n1t, n1t_out.at[:, pl.ds(0, middle)])
    gather.second()
    use(1, 0, blocks.at[1])
    use(2, 1, blocks.at[2])
    gu.serve(pace)
    first_half.wait()
    n1t[...] = jnp.transpose(qkvg[middle:, :])
    leave(n1t, n1t_out.at[:, pl.ds(middle, middle)])
    for slot, block, side_at in ((2, 1, 1), (3, 2, 0), (4, 3, 0), (5, 3, 1)):
        gather.copies[slot].wait_recv()
        use(block, side_at, blocks.at[block])
    leave(n2t, n2t_out)
    gu.finish()

    count_w = gu_out.shape[1] // 256

    def w_copy(j):
        return pltpu.make_async_copy(gu_out.at[:, pl.ds(pl.multiple_of(j * 256, 256), 256)], w_tiles.at[j % 2], w_sem.at[j % 2])

    def s_copy(j):
        return pltpu.make_async_copy(slopes.at[j % 2], slopes_out.at[:, pl.ds(pl.multiple_of(j * 256, 256), 256)], s_sem.at[j % 2])

    def ffn(j, carry):
        pl.when(j + 1 < count_w)(w_copy(j + 1).start)
        w_copy(j).wait()

        @pl.when(j >= 2)
        def _():
            s_copy(j - 2).wait()

        there = pl.ds(pl.multiple_of(j * 128, 128), 128)
        for k in range(2):
            here = slice(k * middle, (k + 1) * middle)
            rows_in = blocks[k * BLOCKS // 2 : (k + 1) * BLOCKS // 2].reshape(middle, high)
            value = mm(rows_in, w_tiles[j % 2], NN)
            gate, up = value[:, :128], value[:, 128:]
            sigma = jax.nn.sigmoid(gate)
            swish = gate * sigma
            slopes[j % 2, here, :128] = (up * (sigma + swish * (1.0 - sigma))).astype(b16)
            slopes[j % 2, here, 128:] = swish.astype(b16)
            hidden[here, there] = (swish * up).astype(b16)
        s_copy(j).start()
        return carry

    w_copy(0).start()
    third = count_w // 3
    lax.fori_loop(0, third, ffn, 0)
    down.serve(pace)
    lax.fori_loop(third, 2 * third, ffn, 0)
    down.serve(pace)
    lax.fori_loop(2 * third, count_w, ffn, 0)
    s_copy(count_w - 2).wait()
    s_copy(count_w - 1).wait()
    leave(hidden, hidden_out)
    load_t.wait()
    down.serve(pace)
    place = lambda at, cols: [(0, at, cols)]
    for _ in weight_tiles([(grad_t, hidden, 0)], place, gdown_out, room, land, store_sem, t_send, t_got, pause=(1,)):
        down.serve(pace)
    down.finish()
    gather_done = gather.copies
    for one in gather_done:
        one.wait_send()
    sum_heads.close()
    gu.close()
    down.close()
    for k, one in enumerate(outs):
        if one is not first_half:
            one.wait()


def mid_stage(count, qkvg, forget, mix, x_own, normed1, own_gu, own_down, grad_t, gain_rows, live_own, number):
    f32, b16 = jnp.float32, jnp.bfloat16
    rows, width = qkvg.shape[0], qkvg.shape[1] // 4
    slots = forget.shape[0]
    size, high = x_own.shape
    share, wide = own_gu.shape
    chips, tiles, narrow = count // 2, rows // TILE, wide // 2
    spans = jnp.asarray(span_matrix(), b16)
    shape = jax.ShapeDtypeStruct
    buf = lambda *dims: pltpu.VMEM(dims, b16)
    full = lambda *dims: pltpu.VMEM(dims, f32)
    sems = lambda *dims: pltpu.SemaphoreType.DMA(dims)
    line = shape((1, high), f32)
    z_sems = [*[sems(chips, 2)] * 6, sems(1)]
    return pl.pallas_call(
        functools.partial(mid_kernel, count),
        in_specs=[FAR] * 9 + [WHOLE] * 2,
        out_specs=[WHOLE] * 5 + [FAR] * 15,
        out_shape=[
            shape((size, high), f32), line, line, line, shape((1, width), f32), shape((rows, width), b16), shape((rows, width), f32),
            shape((slots, rows), f32), shape((tiles, slots, width), b16), shape((tiles, slots, width), b16),
            shape((high, rows), b16), shape((high, rows), b16), shape((high, wide), b16), shape((high, narrow), b16),
            shape((rows, wide), b16), shape((rows, narrow), b16), shape((high // 2, narrow), b16),
            *[shape((slots, rows), f32)] * 3,
        ],
        scratch_shapes=[
            buf(rows, 4 * width), full(slots, rows), full(slots, rows), full(slots, rows), buf(*spans.shape), full(rows, width),
            full(slots, rows), buf(tiles, slots, width), buf(tiles, slots, width), full(slots, width), full(slots, width),
            *scatter_scratch(rows, width, high), buf(size, high), buf(size, high), buf(BLOCKS, size, high),
            buf(high, rows), buf(high, rows // 2), buf(share, wide), buf(share, narrow), buf(2, high, 256),
            buf(2, rows, 256), buf(rows, narrow), buf(high, rows), *tile_scratch(high, narrow, share, 1), sems(8 + 2 * SPLIT), sems(13),
            sems(6), sems(6), sems(2), sems(2), *z_sems, *z_sems,
        ],
        compiler_params=pltpu.CompilerParams(collective_id=number, has_side_effects=True, vmem_limit_bytes=LIMIT),
        cost_estimate=pl.CostEstimate(flops=10**9, bytes_accessed=1 << 20, transcendentals=0),
        name="mid_stage",
    )(qkvg, forget, spans, mix, x_own, normed1, own_gu, own_down, grad_t, gain_rows, live_own)


def ffn_bwd_kernel(grad_ref, w_ref, slopes_ref, out_ref):
    value = mm(grad_ref[...], w_ref[...], NN)
    for p in range(4):
        here = slice(p * 128, (p + 1) * 128)
        grad = value[:, p // 2 * 128 : (p // 2 + 1) * 128]
        out_ref[:, here] = (grad * slopes_ref[:, here].astype(jnp.float32)).astype(jnp.bfloat16)


def ffn_bwd(grad, weight, gu):
    rows, width = grad.shape
    wide = gu.shape[1]
    return pl.pallas_call(
        ffn_bwd_kernel,
        grid=(pl.cdiv(wide, 512),),
        in_specs=[
            pl.BlockSpec((rows, width), lambda j: (0, 0)),
            pl.BlockSpec((width, 256), lambda j: (0, j)),
            pl.BlockSpec((rows, 512), lambda j: (0, j)),
        ],
        out_specs=pl.BlockSpec((rows, 512), lambda j: (0, j)),
        out_shape=jax.ShapeDtypeStruct((rows, wide), jnp.bfloat16),
        compiler_params=pltpu.CompilerParams(dimension_semantics=("arbitrary",), vmem_limit_bytes=LIMIT),
        cost_estimate=pl.CostEstimate(flops=10**9, bytes_accessed=1 << 20, transcendentals=0),
        name="ffn_bwd",
    )(grad, weight, gu)


def after(values, *earlier):
    return lax.optimization_barrier((values, earlier))[0]


def on_device(seq_count, tokens, cotangent, counts, pads, norm1_gain, w_query, w_key, w_value, w_gate_out,
              w_forget, forget_bias, out_gain, w_out, norm2_gain, w_gate, w_up, w_down):
    f32, b16 = jnp.float32, jnp.bfloat16
    rows, model_width = tokens.shape[1:]
    head_pos = lax.axis_index("head")
    width, slots, hidden_width = w_query.shape[1], w_forget.shape[1], w_gate.shape[1]
    share = w_query.shape[0]
    extra = slots
    size = rows // BLOCKS

    wide = 4 * width
    small = jnp.concatenate([norm1_gain, norm2_gain, out_gain, forget_bias])
    small = jnp.pad(small, (0, 3 * share - small.shape[0]))
    mix, normed1, grad_ffn, grad_ffn_t, x_own, cot_own, own_gu, own_down, qkvg, forget_raw, gain_rows = enter_stage(
        seq_count, w_out, w_query, w_key, w_value, w_gate_out, w_forget.T, small[None], tokens[0], cotangent[0], w_gate, w_up, w_down, counts, pads, 7,
    )

    skip = width
    n_gain, n_bias = out_gain.shape[0], forget_bias.shape[0]
    position = head_pos * size + jnp.arange(size, dtype=jnp.int32)[:, None]
    live_own = (position < jnp.where(counts[0] > 0, rows - pads[0], 0)).astype(f32)
    tall = lambda kind: jax.ShapeDtypeStruct((size, model_width), kind)
    line = jax.ShapeDtypeStruct((1, model_width), f32)
    seq_pos = lax.axis_index("seq")
    (residual, x_squares, mix_squares, live_sum, gain_head, gated, mixed, probs, kst, vst, normed2_t, normed1_t, gu_weight,
     down_weight, gu, hidden, grad_down, forget_t, log_keep, keep_in) = mid_stage(
        seq_count, qkvg, forget_raw, mix, x_own, normed1, own_gu, own_down, grad_ffn_t, gain_rows, live_own, 0
    )
    lines = [list(range(c, seq_count, 2)) for c in range(2)]

    def line_scatter(array):
        return lax.psum_scatter(array, "seq", scatter_dimension=0, tiled=True, axis_index_groups=lines)

    grad_down = line_scatter(grad_down)
    grad_gu = ffn_bwd(grad_ffn, down_weight, gu)
    high = model_width // 2
    grad_residual, grad_low, grad_gain_two, grad_gu_w = head_scatter(
        grad_gu, gu_weight, [normed2_t, residual, cot_own], [live_own, gain_rows], [tall(f32), tall(b16), line],
        finish_norm_two, 2, filler=fill_gu, filled=[jax.ShapeDtypeStruct((high, gu_weight.shape[1]), b16)],
        scratch=tile_scratch(model_width, gu_weight.shape[1], share, 0),
    )
    grad_gu_w = line_scatter(grad_gu_w)
    grad_att_t, grad_gated = head_gather(grad_low, 3, keep=False, weight=mix, width=width)
    grad_gated = after(grad_gated, grad_down)
    wide_in = wide + slots + extra
    states = [pltpu.VMEM((slots, width), f32), pltpu.VMEM((slots, width), f32), pltpu.VMEM((slots, 1), f32)]
    out_own, ffn_squares, grad_gain_head, grad_bias, grad_in, grad_mix = head_scatter(
        hidden, down_weight,
        [qkvg, grad_gated, mixed, probs, kst, vst, log_keep, keep_in, forget_t, jnp.asarray(span_matrix(), b16), gain_head,
         residual, grad_att_t, gated, normed1_t],
        [live_own], [tall(b16), line, jax.ShapeDtypeStruct((1, width), f32), jax.ShapeDtypeStruct((slots, 1), f32)],
        finish_ffn, 4, filler=fill_mix,
        filled=[jax.ShapeDtypeStruct((rows, wide_in), b16),
                jax.ShapeDtypeStruct((high, mix.shape[1]), b16)],
        scratch=[pltpu.VMEM((rows, wide_in), b16), pltpu.SemaphoreType.DMA((1,)), *states,
                 *tile_scratch(model_width, mix.shape[1], share, 1)],
    )
    grad_mix = line_scatter(grad_mix)
    hops = 2 + seq_count.bit_length() - 1
    outputs, input_grad, small = tail_stage(
        hops, skip, grad_in, mix, normed1, x_own, grad_residual, out_own,
        (gain_rows, grad_gain_two, x_squares, mix_squares, ffn_squares, live_sum, grad_gain_head, grad_bias), 6,
    )
    (input_grad, outputs, grad_q, grad_k, grad_v, grad_go, grad_f, grad_gate, grad_up, grad_wo, grad_wd, grad_one,
     grad_two, grad_head, grad_fb, rms) = last_stage(
        seq_pos.reshape(1).astype(jnp.int32), seq_count, input_grad.reshape(rows, model_width),
        outputs.reshape(rows, model_width), grad_gu_w, grad_mix, grad_down, small, width, slots, n_gain, n_bias,
    )
    return (
        outputs[None], input_grad[None], grad_one[0], grad_q, grad_k, grad_v, grad_go, grad_f.T, grad_fb[0], grad_head[0],
        grad_wo, grad_two[0], grad_gate, grad_up, grad_wd, rms[0],
    )


def solution(mesh):
    both = P("seq", "head")
    flat = P(("head", "seq"))
    rows = P("seq", None, None)
    return jax.shard_map(
        functools.partial(on_device, mesh.shape["seq"]),
        mesh=mesh,
        in_specs=(rows, rows, P("seq"), P("seq"), P("seq"), both, both, both, both, both, flat, flat,
                  P("head", "seq"), P("seq"), both, both, P("head", "seq")),
        out_specs=(rows, rows, P("seq"), both, both, both, both, both, flat, flat, P("head", "seq"), P("seq"),
                   both, both, P("head", "seq"), P()),
        check_vma=False,
    )
```
